128 devices in a mesh: tensor: 8 (over y, core), context: 16 (over z, x).
Axes of the slice: x: 4, y: 4, z: 4, core: 2. Of those that a mesh axis runs over, the one named last changes fastest.
Arguments:
- tokens: bfloat16 [4096, 5120], P('context', 'tensor'), may hold values from -6 to 6
- query_weight: bfloat16 [5120, 5120], P('context', 'tensor'), may hold values from -0.078125 to 0.078125
- key_weight: bfloat16 [5120, 5120], P('context', 'tensor'), may hold values from -0.078125 to 0.078125
- value_weight: bfloat16 [5120, 5120], P('context', 'tensor'), may hold values from -0.078125 to 0.078125
- cache_keys: bfloat16 [512, 64, 5120], P('context', None, 'tensor'), may hold values from -160 to 160
- cache_values: bfloat16 [512, 64, 5120], P('context', None, 'tensor'), may hold values from -6 to 6
- selected: int32 [32, 32], P('context'), may hold values from -1 to 511, as said below
- counts: int32 [32], P('context'), may hold values from 24 to 32, as said below
- block_slot: int32 [512], replicated, may hold values from 0 to 511, as said below
Outputs:
- attended: bfloat16 [4096, 5120], P('context', 'tensor')
The draws below stay inside these ranges and needn't reach their ends.
Inputs may be any that keep to these rules, and one draw needn't show every extreme that they name: `selected`: row c names different block ids in its first counts[c] entries and -1 in the others. Among the valid entries of the 2 query blocks of one context device, at most 8 name blocks stored on one context device (block_slot[b] // 32), and exactly 8 do for some device in every draw. `counts`: some query block has 32 valid entries in every draw. `block_slot`: each row of the cache arrays stores exactly one block id.
All inputs are finite; a program needn't handle non-finite values.
Results may differ from the reference program's by a relative error of at most 0.012.
The reference program's roundings to bfloat16 on the way (of `queries` and `weights`) count: a program that leaves them out, or rounds other values in their place, can miss the bound.
Values may be sent and summed in bfloat16 or wider, within the bound.
A program may use at most 192 MiB of HBM per device.

```python
import jax
import jax.numpy as jnp
from jax import lax

D = 5120
HEADS = 40
HDIM = 128
BLK_DEV = 32
SPAN = 128
BLOCK = 64
SELECT = 32
SPAN_DEV = 2
SPANS = 32
TOKENS = 4096
BLOCKS = 512
OWNERS = 16
CAP = 8


def make_plan(key):
    per_device = SPAN_DEV * SELECT
    tickets = OWNERS * CAP
    seed_perm = jax.random.fold_in(key, 101)
    seed_count = jax.random.fold_in(key, 102)
    seed_busy = jax.random.fold_in(key, 103)
    seed_device = jax.random.fold_in(key, 104)
    seed_full = jax.random.fold_in(key, 105)
    placement_map = jax.random.permutation(seed_perm, BLOCKS).astype(jnp.int32)
    inverse = jnp.argsort(placement_map).astype(jnp.int32)
    counts = jax.random.randint(seed_count, (OWNERS, SPAN_DEV), 3 * SELECT // 4, SELECT + 1).astype(jnp.int32)
    full_device = jax.random.randint(seed_full, (), 0, OWNERS)
    counts = counts.at[full_device, 0].set(SELECT)
    valid_rows = (jnp.arange(SELECT)[None, None, :] < counts[:, :, None]).reshape(OWNERS, per_device)
    busy_owner = jax.random.randint(seed_busy, (OWNERS,), 0, OWNERS)

    def device_plan(device_seed, busiest, valid_row):
        seed_shuffle = jax.random.fold_in(device_seed, 1)
        seed_priority = jax.random.fold_in(device_seed, 2)
        seed_local = jax.random.fold_in(device_seed, 3)
        shuffle = jax.random.permutation(seed_shuffle, tickets)
        ticket_owner = jnp.arange(tickets) // CAP
        ranking = jnp.where(ticket_owner == busiest, shuffle, shuffle + tickets)
        ticket_order = jnp.argsort(ranking)
        priority = jax.random.permutation(seed_priority, per_device)
        second = jnp.where(valid_row, priority, priority + per_device)
        entry_rank = jnp.argsort(jnp.argsort(second))
        ticket_pick = ticket_order[jnp.minimum(entry_rank, tickets - 1)]
        owner_pick = ticket_pick // CAP
        within = ticket_pick % CAP
        local_tables = jax.vmap(lambda owner_seed: jax.random.permutation(owner_seed, BLK_DEV))(jax.random.split(seed_local, OWNERS))
        local_row = local_tables[owner_pick, within]
        return (owner_pick * BLK_DEV + local_row).astype(jnp.int32)
    slot_rows = jax.vmap(device_plan)(jax.random.split(seed_device, OWNERS), busy_owner, valid_rows)
    block_ids = inverse[slot_rows]
    chosen = jnp.where(valid_rows, block_ids, -1).reshape(SPANS, SELECT).astype(jnp.int32)
    return (placement_map, counts.reshape(SPANS), chosen)


def draw_selected(key, part):
    return make_plan(key)[2]


def draw_counts(key, part):
    return make_plan(key)[1]


def draw_block_slot(key, part):
    return make_plan(key)[0]


def draw_cache_keys(key, part):
    seed_normal = jax.random.fold_in(key, 201)
    normal_part = jnp.clip(jax.random.normal(seed_normal, (BLOCKS, BLOCK, HEADS * HDIM), jnp.float32), -4.0, 4.0)
    return normal_part.astype(jnp.bfloat16)


def level_of(key, dims, cuts, low, top_value):
    def one(dim, shards_of):
        heights = jax.random.uniform(jax.random.fold_in(jax.random.fold_in(key, 6), dim), (shards_of,), jnp.float32, low / len(cuts), top_value / len(cuts))
        return jnp.repeat(jnp.exp(heights), dims[dim] // shards_of).reshape((-1,) + (1,) * (len(dims) - dim - 1))

    loudness = one(*cuts[0])
    for cut in cuts[1:]:
        loudness = loudness * one(*cut)
    return loudness


def bell_draw(key, shape, scale, limit, cuts=(), kind=jnp.bfloat16):
    values = scale * jax.random.normal(key, shape, jnp.float32)
    if cuts:
        values = values * level_of(key, shape, cuts, -0.22, 0.18)
    return jnp.clip(values, -limit, limit).astype(kind)


def setup_inputs(seed: int = 0) -> dict:
    seeds = jax.random.split(jax.random.key(seed), 10)
    return {
        "tokens": bell_draw(seeds[0], (TOKENS, D), 1.0, 6.0, ((0, 16), (1, 8))),
        "query_weight": bell_draw(seeds[1], (D, HEADS * HDIM), D ** -0.5, 0.078125, ((0, 16), (1, 8))),
        "key_weight": bell_draw(seeds[2], (D, HEADS * HDIM), D ** -0.5, 0.078125, ((0, 16), (1, 8))),
        "value_weight": bell_draw(seeds[3], (D, HEADS * HDIM), D ** -0.5, 0.078125, ((0, 16), (1, 8))),
        "cache_keys": draw_cache_keys(jax.random.fold_in(seeds[9], 71), 0),
        "cache_values": bell_draw(seeds[5], (BLOCKS, BLOCK, HEADS * HDIM), 1.0, 6.0, ((0, 16), (2, 8))),
        "selected": draw_selected(jax.random.fold_in(seeds[9], 71), 0),
        "counts": draw_counts(jax.random.fold_in(seeds[9], 71), 0),
        "block_slot": draw_block_slot(jax.random.fold_in(seeds[9], 71), 0),
    }


NEGATIVE = -1.0e30


def reference(tokens, query_weight, key_weight, value_weight, cache_keys, cache_values, selected, counts, block_slot):
    head_width = HEADS * HDIM
    score_scale = HDIM ** -0.5
    queries = jnp.dot(tokens, query_weight, preferred_element_type=jnp.float32).astype(jnp.bfloat16)
    new_keys = jnp.dot(tokens, key_weight, preferred_element_type=jnp.float32).astype(jnp.bfloat16)
    new_values = jnp.dot(tokens, value_weight, preferred_element_type=jnp.float32).astype(jnp.bfloat16)
    query_spans = queries.reshape(SPANS, SPAN, HEADS, HDIM)
    key_spans = new_keys.reshape(SPANS, SPAN, head_width)
    value_spans = new_values.reshape(SPANS, SPAN, head_width)
    blank = jnp.zeros((1, SPAN, head_width), jnp.bfloat16)
    prior_keys = jnp.concatenate([blank, key_spans[:-1]], 0)
    prior_values = jnp.concatenate([blank, value_spans[:-1]], 0)
    position = jnp.arange(SPAN)
    causal = position[None, :] <= position[:, None]
    entry_index = jnp.arange(SELECT)

    def one_span(packed):
        span_index, chosen, live_count, query_block, prior_key_block, own_key_block, prior_value_block, own_value_block = packed
        slot_rows = block_slot[jnp.clip(chosen, 0, BLOCKS - 1)]
        far_keys = cache_keys[slot_rows].reshape(SELECT * BLOCK, head_width)
        far_values = cache_values[slot_rows].reshape(SELECT * BLOCK, head_width)
        all_keys = jnp.concatenate([far_keys, prior_key_block, own_key_block], 0).astype(jnp.float32).reshape(-1, HEADS, HDIM)
        all_values = jnp.concatenate([far_values, prior_value_block, own_value_block], 0).astype(jnp.float32).reshape(-1, HEADS, HDIM)
        scores = jnp.einsum("qhd,khd->hqk", query_block.astype(jnp.float32), all_keys) * score_scale
        far_open = jnp.repeat(entry_index < live_count, BLOCK)
        allowed = jnp.concatenate([
            jnp.broadcast_to(far_open[None, :], (SPAN, SELECT * BLOCK)),
            jnp.broadcast_to(span_index > 0, (SPAN, SPAN)),
            causal], 1)
        masked = jnp.where(allowed[None], scores, NEGATIVE)
        highest = jnp.max(masked, axis=2, keepdims=True)
        weights = jnp.where(allowed[None], jnp.exp(masked - highest), 0.0)
        totals = jnp.sum(weights, axis=2)
        rounded = lax.optimization_barrier(weights.astype(jnp.bfloat16)).astype(jnp.float32)
        summed = jnp.einsum("hqk,khd->qhd", rounded, all_values)
        return (summed / jnp.transpose(totals)[:, :, None]).astype(jnp.bfloat16).reshape(SPAN, head_width)

    attended = lax.map(one_span, (jnp.arange(SPANS), selected, counts, query_spans, prior_keys, key_spans, prior_values, value_spans))
    return attended.reshape(TOKENS, head_width)
```

```python
import functools

import jax
import jax.numpy as jnp
from jax import lax
from jax.experimental import pallas as pl
from jax.experimental.pallas import tpu as pltpu
from jax.sharding import PartitionSpec as P

HDIM = 128
NEG = -1e30
SCALE = HDIM ** (-0.5) * 1.4426950408889634


def dot_nt(a, b):
    return lax.dot_general(a, b, (((1,), (1,)), ((), ())), preferred_element_type=jnp.float32)


def dot_tn(a, b):
    return lax.dot_general(a, b, (((0,), (0,)), ((), ())), preferred_element_type=jnp.float32)


def owner_kernel(heads, cap, rows_ref, n_ref, q_ref, k_ref, v_ref, o_ref, st_ref, acc_ref):
    src = pl.program_id(0)
    span_count = o_ref.shape[1]
    span = q_ref.shape[1] // span_count
    block = k_ref.shape[1]
    for half in range(span_count):
        c = src * span_count + half
        n = n_ref[c]
        rows = slice(half * span, (half + 1) * span)

        def pair(j, first):
            r0 = rows_ref[c * cap + 2 * j]
            r1 = rows_ref[c * cap + jnp.minimum(2 * j + 1, cap - 1)]
            bias = jnp.where(2 * j + 1 < n, 0.0, NEG)
            for h in range(heads):
                cols = slice(h * HDIM, (h + 1) * HDIM)
                q = q_ref[0, rows, cols]
                k = jnp.concatenate([k_ref[r0, :, cols], k_ref[r1, :, cols]], 0)
                v = jnp.concatenate([v_ref[r0, :, cols], v_ref[r1, :, cols]], 0)
                s = dot_nt(k, q) * SCALE
                s = jnp.concatenate([s[:block], s[block:] + bias], 0)
                m = jnp.max(s, axis=0, keepdims=True)
                if not first:
                    old = st_ref[0, half, h : h + 1, :]
                    m = jnp.maximum(m, old)
                    decay = jnp.exp2(old - m)
                p = jnp.exp2(s - m)
                l = jnp.sum(p, axis=0, keepdims=True)
                a = dot_tn(v, p.astype(jnp.bfloat16))
                if not first:
                    l = l + st_ref[0, half, 8 + h : 9 + h, :] * decay
                    a = a + acc_ref[cols, :] * decay
                st_ref[0, half, h : h + 1, :] = m
                st_ref[0, half, 8 + h : 9 + h, :] = l
                acc_ref[cols, :] = a

        @pl.when(n == 0)
        def _():
            o_ref[0, half] = jnp.zeros_like(o_ref[0, half])
            st_ref[0, half, 0:8, :] = jnp.full_like(st_ref[0, half, 0:8, :], NEG)
            st_ref[0, half, 8:16, :] = jnp.zeros_like(st_ref[0, half, 8:16, :])

        @pl.when(n > 0)
        def _():
            pair(0, True)

            @pl.loop(1, (n + 1) // 2)
            def _(j):
                pair(j, False)

            for h in range(heads):
                cols = slice(h * HDIM, (h + 1) * HDIM)
                o_ref[0, half, cols, :] = (
                    acc_ref[cols, :] / st_ref[0, half, 8 + h : 9 + h, :]
                ).astype(jnp.bfloat16)


def owner_attention(rows, n, q_all, cache_keys, cache_values, heads, cap):
    devices, tokens, width = q_all.shape
    span_count = n.shape[0] // devices
    span = tokens // span_count
    whole = pl.BlockSpec(cache_keys.shape, lambda s, *_: (0, 0, 0), pipeline_mode=pl.Buffered(1))
    return pl.pallas_call(
        functools.partial(owner_kernel, heads, cap),
        grid_spec=pltpu.PrefetchScalarGridSpec(
            num_scalar_prefetch=2,
            grid=(devices,),
            in_specs=[
                pl.BlockSpec((1, tokens, width), lambda s, *_: (s, 0, 0)),
                whole,
                whole,
            ],
            out_specs=[
                pl.BlockSpec((1, span_count, width, span), lambda s, *_: (s, 0, 0, 0)),
                pl.BlockSpec((1, span_count, 16, span), lambda s, *_: (s, 0, 0, 0)),
            ],
            scratch_shapes=[pltpu.VMEM((width, span), jnp.float32)],
        ),
        out_shape=[
            jax.ShapeDtypeStruct((devices, span_count, width, span), jnp.bfloat16),
            jax.ShapeDtypeStruct((devices, span_count, 16, span), jnp.float32),
        ],
    )(rows, n, q_all, cache_keys, cache_values)


def local_kernel(heads, first_ref, q_ref, pk_ref, pv_ref, k_ref, v_ref, o_ref, st_ref, out_ref):
    half = pl.program_id(0)
    span = q_ref.shape[0]
    bias = jnp.where((first_ref[0] + half) > 0, 0.0, NEG)
    key = lax.broadcasted_iota(jnp.int32, (span, span), 0)
    row = lax.broadcasted_iota(jnp.int32, (span, span), 1)
    for h in range(heads):
        cols = slice(h * HDIM, (h + 1) * HDIM)
        q = q_ref[:, cols]
        s0 = dot_nt(pk_ref[0, :, cols], q) * SCALE + bias
        s1 = jnp.where(key <= row, dot_nt(k_ref[:, cols], q) * SCALE, NEG)
        far_m = st_ref[:, 0, h, :]
        far_l = st_ref[:, 0, 8 + h, :]
        m = jnp.maximum(
            jnp.maximum(jnp.max(s0, axis=0, keepdims=True), jnp.max(s1, axis=0, keepdims=True)),
            jnp.max(far_m, axis=0, keepdims=True),
        )
        p0 = jnp.exp2(s0 - m)
        p1 = jnp.exp2(s1 - m)
        w = far_l * jnp.exp2(far_m - m)
        total = (
            jnp.sum(p0, axis=0, keepdims=True)
            + jnp.sum(p1, axis=0, keepdims=True)
            + jnp.sum(w, axis=0, keepdims=True)
        )
        a = dot_tn(pv_ref[0, :, cols], p0.astype(jnp.bfloat16))
        a = a + dot_tn(v_ref[:, cols], p1.astype(jnp.bfloat16))
        for i in range(o_ref.shape[0]):
            a = a + o_ref[i, 0, cols, :].astype(jnp.float32) * w[i : i + 1, :]
        out_ref[:, cols] = jnp.transpose(a / total).astype(out_ref.dtype)


def local_attention(first, q, prior_k, prior_v, k, v, o, st, heads):
    devices, span_count, width, span = o.shape
    rows = pl.BlockSpec((span, width), lambda c, *_: (c, 0))
    before = pl.BlockSpec((1, span, width), lambda c, *_: (c, 0, 0))
    return pl.pallas_call(
        functools.partial(local_kernel, heads),
        grid_spec=pltpu.PrefetchScalarGridSpec(
            num_scalar_prefetch=1,
            grid=(span_count,),
            in_specs=[
                rows,
                before,
                before,
                rows,
                rows,
                pl.BlockSpec((devices, 1, width, span), lambda c, *_: (0, c, 0, 0)),
                pl.BlockSpec((devices, 1, 16, span), lambda c, *_: (0, c, 0, 0)),
            ],
            out_specs=rows,
        ),
        out_shape=jax.ShapeDtypeStruct(q.shape, jnp.bfloat16),
    )(first, q, prior_k, prior_v, k, v, o, st)


def from_behind(block, axis, distance):
    devices = range(lax.axis_size(axis))
    route = [(i - distance, i) for i in devices if i - distance in devices]
    return lax.ppermute(block, axis, route)


def owner_table(selected, counts, block_slot, stored, cap):
    select_count = selected.shape[1]
    live = jnp.arange(select_count)[None, :] < counts[:, None]
    hit = selected[:, :, None] == jnp.arange(block_slot.shape[0])[None, None, :]
    slot = jnp.sum(jnp.where(hit, block_slot[None, None, :], 0), axis=2)
    slot = jnp.where(live, slot, -1).astype(jnp.int32)
    slots = lax.all_gather(slot, "context", axis=0, tiled=True)
    low = lax.axis_index("context") * stored
    mine = (slots >= low) & (slots < low + stored)
    position = jnp.arange(select_count)
    earlier = position[None, :] < position[:, None]
    rank = jnp.sum(jnp.where(mine[:, None, :] & earlier[None], 1, 0), axis=2)
    place = mine[:, :, None] & (rank[:, :, None] == jnp.arange(cap)[None, None, :])
    rows = jnp.sum(jnp.where(place, (slots - low)[:, :, None], 0), axis=1)
    return rows.reshape(-1).astype(jnp.int32), jnp.sum(mine, axis=1).astype(jnp.int32)


def shards(
    tokens,
    query_weight,
    key_weight,
    value_weight,
    cache_keys,
    cache_values,
    selected,
    counts,
    block_slot,
):
    token_count = tokens.shape[0]
    width = query_weight.shape[1]
    heads = width // HDIM
    span_count, select_count = selected.shape
    devices = lax.axis_size("context")
    cap = max(2, 2 * span_count * select_count // devices)
    span = token_count // span_count

    features = lax.all_gather(tokens, "tensor", axis=1, tiled=True)

    def project(weight):
        whole = lax.all_gather(weight, "context", axis=0, tiled=True)
        return jnp.dot(features, whole, preferred_element_type=jnp.float32).astype(jnp.bfloat16)

    q = project(query_weight)
    q_all = lax.all_gather(q, "context", axis=0, tiled=False)
    rows, n = owner_table(selected, counts, block_slot, cache_keys.shape[0], cap)
    o, st = owner_attention(rows, n, q_all, cache_keys, cache_values, heads, cap)
    o = lax.all_to_all(o, "context", split_axis=0, concat_axis=0, tiled=True)
    st = lax.all_to_all(st, "context", split_axis=0, concat_axis=0, tiled=True)
    k = project(key_weight)
    v = project(value_weight)
    last = token_count - span
    before_k, before_v = from_behind((k[last:], v[last:]), "context", 1)

    def prior(before, own):
        return jnp.concatenate([before, own[:last]], 0).reshape(span_count, span, width)

    first = (lax.axis_index("context") * span_count).astype(jnp.int32).reshape(1)
    return local_attention(first, q, prior(before_k, k), prior(before_v, v), k, v, o, st, heads)


def solution(mesh):
    placed = (
        P("context", "tensor"),
        P("context", "tensor"),
        P("context", "tensor"),
        P("context", "tensor"),
        P("context", None, "tensor"),
        P("context", None, "tensor"),
        P("context", None),
        P("context"),
        P(),
    )
    return jax.shard_map(
        shards, mesh=mesh, in_specs=placed, out_specs=P("context", "tensor"), check_vma=False
    )
```

```python
import functools

import jax
import jax.numpy as jnp
from jax import lax
from jax.experimental import pallas as pl
from jax.experimental.pallas import tpu as pltpu
from jax.sharding import PartitionSpec as P

HDIM = 128
NEG = -1e30
MESH = pl.DeviceIdType.MESH
EXTRA = 16
SCALE = HDIM ** (-0.5) * 1.4426950408889634


def dot_nt(a, b):
    return lax.dot_general(a, b, (((1,), (1,)), ((), ())), preferred_element_type=jnp.float32)


def dot_tn(a, b):
    return lax.dot_general(a, b, (((0,), (0,)), ((), ())), preferred_element_type=jnp.float32)


RING = 4
OFFSETS = (0, -1, 1, 2)


def halves(total, extra):
    half = (total - extra) // 2
    part = half // 2
    first = ((0, half), (0, part), (part, half - part))
    second = ((half, half + extra), (half, part), (half + part, half - part + extra))
    return (first, second)


class ContextGather:
    def __init__(self, buf, ranges, send, recv, zpos, xpos):
        self.buf, self.ranges, self.send, self.recv = buf, ranges, send, recv
        self.zpos, self.xpos = zpos, xpos
        self.waited, self.sent = set(), []

    def on_x(self, half, phase):
        return (half == 0) == (phase == 0)

    def chunk(self, half, phase, step):
        first = 0 if phase == 0 else OFFSETS[phase - 1]
        if self.on_x(half, phase):
            dz, dx = (0, step) if phase == 0 else (first, step)
        else:
            dz, dx = (step, 0) if phase == 0 else (step, first)
        return context_of(self.zpos + dz, self.xpos + dx)

    def copy(self, half, phase, index, step):
        start, size = self.ranges[half][max(0, index - 1)]
        ref = self.buf.at[self.chunk(half, phase, step), pl.ds(start, size), :]
        way = 1 if index % 2 == 0 else -1
        if self.on_x(half, phase):
            to = context_of(self.zpos, self.xpos + way)
        else:
            to = context_of(self.zpos + way, self.xpos)
        slot = half * 20 + phase * 4 + index
        return pltpu.make_async_remote_copy(
            src_ref=ref,
            dst_ref=ref,
            send_sem=self.send.at[slot],
            recv_sem=self.recv.at[slot],
            device_id={"context": to},
            device_id_type=MESH,
        )

    def start(self, half, phase, index):
        copy = self.copy(half, phase, index, (0, 0, -1, 1)[index])
        copy.start()
        self.sent.append(copy)

    def arrive(self, half, phase, index):
        if (half, phase, index) not in self.waited:
            self.waited.add((half, phase, index))
            self.copy(half, phase, index, (-1, 1, 2, 2)[index]).wait_recv()

    def whole(self, half, phase):
        self.start(half, phase, 0)
        self.start(half, phase, 1)

    def onward(self, half, phase):
        self.arrive(half, phase, 0)
        self.start(half, phase, 2)
        self.arrive(half, phase, 1)
        self.start(half, phase, 3)

    def opposite(self, half, phase):
        self.arrive(half, phase, 2)
        self.arrive(half, phase, 3)

    def stages(self):
        def own():
            for half in (0, 1):
                self.whole(half, 0)
                self.whole(half, 1)

        def neighbours():
            for half in (0, 1):
                self.onward(half, 0)
                self.whole(half, 2)
                self.whole(half, 3)
            for half in (0, 1):
                self.onward(half, 1)

        def far():
            for half in (0, 1):
                self.opposite(half, 0)
                self.whole(half, 4)

        def corners():
            for half in (0, 1):
                self.onward(half, 2)
                self.onward(half, 3)

        def last():
            for half in (0, 1):
                self.onward(half, 4)

        def rest():
            for half in (0, 1):
                for phase in (1, 2, 3, 4):
                    self.opposite(half, phase)

        return [own, neighbours, far, corners, last, rest]

    def drain(self):
        for copy in self.sent:
            copy.wait_send()


def context_of(zpos, xpos):
    return lax.rem(zpos + RING, RING) * RING + lax.rem(xpos + RING, RING)


def project_kernel(
    tok_ref, wq_ref, wk_ref, wv_ref, ex_ref,
    q_ref, k_ref, v_ref,
    tok, wq, wk, wv, acc,
    wsend, wrecv, tsend, trecv, local_sem,
):
    me = lax.axis_index("context")
    zpos, xpos = me // RING, lax.rem(me, RING)
    col = lax.axis_index("tensor")
    ypos, core = col // 2, lax.rem(col, 2)
    mate = ypos * 2 + 1 - core
    up = lax.rem(ypos + 1, RING) * 2 + core
    down = lax.rem(ypos + RING - 1, RING) * 2 + core
    token_count = tok.shape[1]

    loads = [
        pltpu.make_async_copy(tok_ref, tok.at[col], local_sem.at[0]),
        pltpu.make_async_copy(wq_ref, wq.at[me], local_sem.at[1]),
        pltpu.make_async_copy(wk_ref, wk.at[me], local_sem.at[2]),
        pltpu.make_async_copy(wv_ref, wv.at[me], local_sem.at[3]),
        pltpu.make_async_copy(
            ex_ref, q_ref.at[me, pl.ds(token_count, EXTRA), :], local_sem.at[4]
        ),
    ]
    for load in loads:
        load.start()

    barrier = pltpu.get_barrier_semaphore()
    for dz, dx in ((1, 0), (-1, 0), (0, 1), (0, -1)):
        pl.semaphore_signal(
            barrier,
            inc=1,
            device_id={"context": context_of(zpos + dz, xpos + dx)},
            device_id_type=MESH,
        )
    for other in (up, down, mate):
        pl.semaphore_signal(barrier, inc=1, device_id={"tensor": other}, device_id_type=MESH)
    pl.semaphore_wait(barrier, 7)

    tsent = []
    part = token_count // 2

    def tcopy(index, block, rows, to):
        ref = tok.at[block, rows, :]
        return pltpu.make_async_remote_copy(
            src_ref=ref, dst_ref=ref, send_sem=tsend.at[index], recv_sem=trecv.at[index],
            device_id={"tensor": to}, device_id_type=MESH,
        )

    def tstart(index, block, rows, to):
        copy = tcopy(index, block, rows, to)
        copy.start()
        tsent.append(copy)

    every = pl.ds(0, token_count)
    low, high = pl.ds(0, part), pl.ds(part, part)
    across = lax.rem(ypos + 2, RING) * 2 + core

    gathers = [
        ContextGather(buf, halves(buf.shape[1], extra), wsend.at[i], wrecv.at[i], zpos, xpos)
        for i, (buf, extra) in enumerate(((wq, 0), (q_ref, EXTRA), (wk, 0), (wv, 0)))
    ]
    for_q, for_all, for_k, for_v = [g.stages() for g in gathers]

    loads[0].wait()
    loads[1].wait()
    tstart(0, col, every, up)
    tstart(1, col, every, down)
    tstart(4, col, every, mate)
    for_q[0]()
    tcopy(0, down, every, up).wait_recv()
    tstart(2, down, low, up)
    tcopy(1, up, every, down).wait_recv()
    tstart(3, up, high, down)
    tstart(5, down, every, mate)
    tstart(6, up, every, mate)
    for_q[1]()
    tcopy(2, across, low, up).wait_recv()
    tcopy(3, across, high, down).wait_recv()
    tstart(7, across, every, mate)
    for stage in for_q[2:5]:
        stage()
    loads[2].wait()
    for_k[0]()
    for index, block in ((4, mate), (5, down), (6, up), (7, across)):
        other = lax.rem(block, 2) * 0 + block // 2 * 2 + 1 - core
        tcopy(index, other, every, mate).wait_recv()
    for_q[5]()

    def project(w):
        @pl.loop(0, tok.shape[0])
        def _(t):
            base = pl.multiple_of(t * 2, 2)
            piece = w[pl.ds(base, 2)].reshape(tok.shape[2], w.shape[2])
            new = jnp.dot(tok[t], piece, preferred_element_type=jnp.float32)

            @pl.when(t == 0)
            def _():
                acc[...] = new

            @pl.when(t > 0)
            def _():
                acc[...] += new

    project(wq)
    q_ref[me, 0:token_count, :] = acc[...].astype(jnp.bfloat16)
    loads[4].wait()
    for_all[0]()
    for step in range(1, 6):
        for_all[step]()
        for_k[step]()
        if step == 3:
            loads[3].wait()
            for_v[0]()
    project(wk)
    k_ref[...] = acc[...].astype(jnp.bfloat16)
    for step in range(1, 6):
        for_v[step]()
    project(wv)
    v_ref[...] = acc[...].astype(jnp.bfloat16)
    for copy in tsent:
        copy.wait_send()
    for gather in gathers:
        gather.drain()


def gather_project(tokens, wq, wk, wv, extra):
    token_count, depth = tokens.shape
    rows, width = wq.shape
    devices = lax.axis_size("context")
    columns = lax.axis_size("tensor")
    hbm = pl.BlockSpec(memory_space=pl.ANY)
    vmem = pl.BlockSpec(memory_space=pltpu.VMEM)
    weight = pltpu.VMEM((devices, rows, width), jnp.bfloat16)
    return pl.pallas_call(
        project_kernel,
        in_specs=[hbm] * 5,
        out_specs=[vmem] * 3,
        out_shape=[
            jax.ShapeDtypeStruct((devices, token_count + EXTRA, width), jnp.bfloat16),
            jax.ShapeDtypeStruct((token_count, width), jnp.bfloat16),
            jax.ShapeDtypeStruct((token_count, width), jnp.bfloat16),
        ],
        scratch_shapes=[
            pltpu.VMEM((columns, token_count, depth), jnp.bfloat16),
            weight,
            weight,
            weight,
            pltpu.VMEM((token_count, width), jnp.float32),
            pltpu.SemaphoreType.DMA((4, 40)),
            pltpu.SemaphoreType.DMA((4, 40)),
            pltpu.SemaphoreType.DMA((8,)),
            pltpu.SemaphoreType.DMA((8,)),
            pltpu.SemaphoreType.DMA((5,)),
        ],
        compiler_params=pltpu.CompilerParams(
            collective_id=0, has_side_effects=True, vmem_limit_bytes=60 << 20
        ),
        name="gather_project",
    )(tokens, wq, wk, wv, extra)


def owner_kernel(heads, cap, rows_ref, n_ref, q_ref, k_ref, v_ref, o_ref, st_ref, acc_ref):
    src = pl.program_id(0)
    span_count = o_ref.shape[1]
    span = o_ref.shape[3]
    block = k_ref.shape[1]
    for half in range(span_count):
        c = src * span_count + half
        n = n_ref[c]
        rows = slice(half * span, (half + 1) * span)

        def pair(j, first):
            r0 = rows_ref[c * cap + 2 * j]
            r1 = rows_ref[c * cap + jnp.minimum(2 * j + 1, cap - 1)]
            bias = jnp.where(2 * j + 1 < n, 0.0, NEG)
            for h in range(heads):
                cols = slice(h * HDIM, (h + 1) * HDIM)
                q = q_ref[0, rows, cols]
                k = jnp.concatenate([k_ref[r0, :, cols], k_ref[r1, :, cols]], 0)
                v = jnp.concatenate([v_ref[r0, :, cols], v_ref[r1, :, cols]], 0)
                s = dot_nt(k, q) * SCALE
                s = jnp.concatenate([s[:block], s[block:] + bias], 0)
                m = jnp.max(s, axis=0, keepdims=True)
                if not first:
                    old = st_ref[0, half, h : h + 1, :]
                    m = jnp.maximum(m, old)
                    decay = jnp.exp2(old - m)
                p = jnp.exp2(s - m)
                l = jnp.sum(p, axis=0, keepdims=True)
                a = dot_tn(v, p.astype(jnp.bfloat16))
                if not first:
                    l = l + st_ref[0, half, 8 + h : 9 + h, :] * decay
                    a = a + acc_ref[cols, :] * decay
                st_ref[0, half, h : h + 1, :] = m
                st_ref[0, half, 8 + h : 9 + h, :] = l
                acc_ref[cols, :] = a

        @pl.when(n == 0)
        def _():
            o_ref[0, half] = jnp.zeros_like(o_ref[0, half])
            st_ref[0, half, 0:8, :] = jnp.full_like(st_ref[0, half, 0:8, :], NEG)
            st_ref[0, half, 8:16, :] = jnp.zeros_like(st_ref[0, half, 8:16, :])

        @pl.when(n > 0)
        def _():
            pair(0, True)

            @pl.loop(1, (n + 1) // 2)
            def _(j):
                pair(j, False)

            for h in range(heads):
                cols = slice(h * HDIM, (h + 1) * HDIM)
                o_ref[0, half, cols, :] = (
                    acc_ref[cols, :] / st_ref[0, half, 8 + h : 9 + h, :]
                ).astype(jnp.bfloat16)


def owner_attention(rows, n, q_all, cache_keys, cache_values, heads, cap):
    devices, tokens, width = q_all.shape
    span_count = n.shape[0] // devices
    span = (tokens - EXTRA) // span_count
    whole = pl.BlockSpec(cache_keys.shape, lambda s, *_: (0, 0, 0), pipeline_mode=pl.Buffered(1))
    return pl.pallas_call(
        functools.partial(owner_kernel, heads, cap),
        grid_spec=pltpu.PrefetchScalarGridSpec(
            num_scalar_prefetch=2,
            grid=(devices,),
            in_specs=[
                pl.BlockSpec((1, tokens, width), lambda s, *_: (s, 0, 0)),
                whole,
                whole,
            ],
            out_specs=[
                pl.BlockSpec((1, span_count, width, span), lambda s, *_: (s, 0, 0, 0)),
                pl.BlockSpec((1, span_count, 16, span), lambda s, *_: (s, 0, 0, 0)),
            ],
            scratch_shapes=[pltpu.VMEM((width, span), jnp.float32)],
        ),
        out_shape=[
            jax.ShapeDtypeStruct((devices, span_count, width, span), jnp.bfloat16),
            jax.ShapeDtypeStruct((devices, span_count, 16, span), jnp.float32),
        ],
    )(rows, n, q_all, cache_keys, cache_values)


def local_kernel(heads, first_ref, q_ref, pk_ref, pv_ref, k_ref, v_ref, o_ref, st_ref, out_ref):
    half = pl.program_id(0)
    span = q_ref.shape[0]
    bias = jnp.where((first_ref[0] + half) > 0, 0.0, NEG)
    key = lax.broadcasted_iota(jnp.int32, (span, span), 0)
    row = lax.broadcasted_iota(jnp.int32, (span, span), 1)
    for h in range(heads):
        cols = slice(h * HDIM, (h + 1) * HDIM)
        q = q_ref[:, cols]
        s0 = dot_nt(pk_ref[0, :, cols], q) * SCALE + bias
        s1 = jnp.where(key <= row, dot_nt(k_ref[:, cols], q) * SCALE, NEG)
        far_m = st_ref[:, 0, h, :]
        far_l = st_ref[:, 0, 8 + h, :]
        m = jnp.maximum(
            jnp.maximum(jnp.max(s0, axis=0, keepdims=True), jnp.max(s1, axis=0, keepdims=True)),
            jnp.max(far_m, axis=0, keepdims=True),
        )
        p0 = jnp.exp2(s0 - m)
        p1 = jnp.exp2(s1 - m)
        w = far_l * jnp.exp2(far_m - m)
        total = (
            jnp.sum(p0, axis=0, keepdims=True)
            + jnp.sum(p1, axis=0, keepdims=True)
            + jnp.sum(w, axis=0, keepdims=True)
        )
        a = dot_tn(pv_ref[0, :, cols], p0.astype(jnp.bfloat16))
        a = a + dot_tn(v_ref[:, cols], p1.astype(jnp.bfloat16))
        for i in range(o_ref.shape[0]):
            a = a + o_ref[i, 0, cols, :].astype(jnp.float32) * w[i : i + 1, :]
        out_ref[:, cols] = jnp.transpose(a / total).astype(out_ref.dtype)


def local_attention(first, q, prior_k, prior_v, k, v, o, st, heads):
    devices, span_count, width, span = o.shape
    rows = pl.BlockSpec((span, width), lambda c, *_: (c, 0))
    before = pl.BlockSpec((1, span, width), lambda c, *_: (c, 0, 0))
    return pl.pallas_call(
        functools.partial(local_kernel, heads),
        grid_spec=pltpu.PrefetchScalarGridSpec(
            num_scalar_prefetch=1,
            grid=(span_count,),
            in_specs=[
                rows,
                before,
                before,
                rows,
                rows,
                pl.BlockSpec((devices, 1, width, span), lambda c, *_: (0, c, 0, 0)),
                pl.BlockSpec((devices, 1, 16, span), lambda c, *_: (0, c, 0, 0)),
            ],
            out_specs=rows,
        ),
        out_shape=jax.ShapeDtypeStruct(q.shape, jnp.bfloat16),
    )(first, q, prior_k, prior_v, k, v, o, st)


def from_behind(block, axis, distance):
    devices = range(lax.axis_size(axis))
    route = [(i - distance, i) for i in devices if i - distance in devices]
    return lax.ppermute(block, axis, route)


def chosen_slots(selected, counts, block_slot, stored, width):
    span_count, select_count = selected.shape
    live = jnp.arange(select_count)[None, :] < counts[:, None]
    hit = selected[:, :, None] == jnp.arange(block_slot.shape[0])[None, None, :]
    slot = jnp.sum(jnp.where(hit, block_slot[None, None, :], 0), axis=2)
    owner = jnp.where(live, slot // stored, -1)
    both = jnp.concatenate([owner, slot % stored], 0).astype(jnp.bfloat16)
    return jnp.pad(both, ((0, EXTRA - 2 * span_count), (0, width - select_count)))


def owner_table(extra, span_count, select_count, cap):
    owner = extra[:, :span_count, :select_count].reshape(-1, select_count).astype(jnp.int32)
    row = extra[:, span_count : 2 * span_count, :select_count]
    row = row.reshape(-1, select_count).astype(jnp.int32)
    mine = owner == lax.axis_index("context")
    position = jnp.arange(select_count)
    earlier = position[None, :] < position[:, None]
    rank = jnp.sum(jnp.where(mine[:, None, :] & earlier[None], 1, 0), axis=2)
    place = mine[:, :, None] & (rank[:, :, None] == jnp.arange(cap)[None, None, :])
    rows = jnp.sum(jnp.where(place, row[:, :, None], 0), axis=1)
    return rows.reshape(-1).astype(jnp.int32), jnp.sum(mine, axis=1).astype(jnp.int32)


def shards(
    tokens,
    query_weight,
    key_weight,
    value_weight,
    cache_keys,
    cache_values,
    selected,
    counts,
    block_slot,
):
    token_count = tokens.shape[0]
    width = query_weight.shape[1]
    heads = width // HDIM
    span_count, select_count = selected.shape
    devices = lax.axis_size("context")
    cap = max(2, 2 * span_count * select_count // devices)
    span = token_count // span_count

    extra = chosen_slots(selected, counts, block_slot, cache_keys.shape[0], width)
    q_all, k, v = gather_project(tokens, query_weight, key_weight, value_weight, extra)
    rows, n = owner_table(q_all[:, token_count:], span_count, select_count, cap)
    o, st = owner_attention(rows, n, q_all, cache_keys, cache_values, heads, cap)
    o = lax.all_to_all(o, "context", split_axis=0, concat_axis=0, tiled=True)
    st = lax.all_to_all(st, "context", split_axis=0, concat_axis=0, tiled=True)
    last = token_count - span
    before_k, before_v = from_behind((k[last:], v[last:]), "context", 1)

    def prior(before, own):
        return jnp.concatenate([before, own[:last]], 0).reshape(span_count, span, width)

    me = lax.axis_index("context")
    q = lax.dynamic_slice(q_all, (me, 0, 0), (1, token_count, width))[0]
    first = (me * span_count).astype(jnp.int32).reshape(1)
    return local_attention(first, q, prior(before_k, k), prior(before_v, v), k, v, o, st, heads)


def solution(mesh):
    placed = (
        P("context", "tensor"),
        P("context", "tensor"),
        P("context", "tensor"),
        P("context", "tensor"),
        P("context", None, "tensor"),
        P("context", None, "tensor"),
        P("context", None),
        P("context"),
        P(),
    )
    return jax.shard_map(
        shards, mesh=mesh, in_specs=placed, out_specs=P("context", "tensor"), check_vma=False
    )
```

```python
import functools

import jax
import jax.numpy as jnp
from jax import lax
from jax.experimental import pallas as pl
from jax.experimental.pallas import tpu as pltpu
from jax.sharding import PartitionSpec as P

HDIM = 128
NEG = -1e30
MESH = pl.DeviceIdType.MESH
EXTRA = 16
SCALE = HDIM ** (-0.5) * 1.4426950408889634


def dot_nt(a, b):
    return lax.dot_general(a, b, (((1,), (1,)), ((), ())), preferred_element_type=jnp.float32)


def dot_tn(a, b):
    return lax.dot_general(a, b, (((0,), (0,)), ((), ())), preferred_element_type=jnp.float32)


RING = 4
OFFSETS = (0, -1, 1, 2)


def halves(total, extra):
    half = (total - extra) // 2
    part = half // 2
    first = ((0, half), (0, part), (part, half - part))
    second = ((half, half + extra), (half, part), (half + part, half - part + extra))
    return (first, second)


class ContextGather:
    def __init__(self, buf, ranges, send, recv, zpos, xpos):
        self.buf, self.ranges, self.send, self.recv = buf, ranges, send, recv
        self.zpos, self.xpos = zpos, xpos
        self.waited, self.sent = set(), []

    def on_x(self, half, phase):
        return (half == 0) == (phase == 0)

    def chunk(self, half, phase, step):
        first = 0 if phase == 0 else OFFSETS[phase - 1]
        if self.on_x(half, phase):
            dz, dx = (0, step) if phase == 0 else (first, step)
        else:
            dz, dx = (step, 0) if phase == 0 else (step, first)
        return context_of(self.zpos + dz, self.xpos + dx)

    def copy(self, half, phase, index, step):
        start, size = self.ranges[half][max(0, index - 1)]
        ref = self.buf.at[self.chunk(half, phase, step), pl.ds(start, size), :]
        way = 1 if index % 2 == 0 else -1
        if self.on_x(half, phase):
            to = context_of(self.zpos, self.xpos + way)
        else:
            to = context_of(self.zpos + way, self.xpos)
        slot = half * 20 + phase * 4 + index
        return pltpu.make_async_remote_copy(
            src_ref=ref,
            dst_ref=ref,
            send_sem=self.send.at[slot],
            recv_sem=self.recv.at[slot],
            device_id={"context": to},
            device_id_type=MESH,
        )

    def start(self, half, phase, index):
        copy = self.copy(half, phase, index, (0, 0, -1, 1)[index])
        copy.start()
        self.sent.append(copy)

    def arrive(self, half, phase, index):
        if (half, phase, index) not in self.waited:
            self.waited.add((half, phase, index))
            self.copy(half, phase, index, (-1, 1, 2, 2)[index]).wait_recv()

    def whole(self, half, phase):
        self.start(half, phase, 0)
        self.start(half, phase, 1)

    def onward(self, half, phase):
        self.arrive(half, phase, 0)
        self.start(half, phase, 2)
        self.arrive(half, phase, 1)
        self.start(half, phase, 3)

    def opposite(self, half, phase):
        self.arrive(half, phase, 2)
        self.arrive(half, phase, 3)

    def stages(self):
        def own():
            for half in (0, 1):
                self.whole(half, 0)
                self.whole(half, 1)

        def neighbours():
            for half in (0, 1):
                self.onward(half, 0)
                self.whole(half, 2)
                self.whole(half, 3)
            for half in (0, 1):
                self.onward(half, 1)

        def far():
            for half in (0, 1):
                self.opposite(half, 0)
                self.whole(half, 4)

        def corners():
            for half in (0, 1):
                self.onward(half, 2)
                self.onward(half, 3)

        def last():
            for half in (0, 1):
                self.onward(half, 4)

        def rest():
            for half in (0, 1):
                for phase in (1, 2, 3, 4):
                    self.opposite(half, phase)

        return [own, neighbours, far, corners, last, rest]

    def drain(self):
        for copy in self.sent:
            copy.wait_send()


def context_of(zpos, xpos):
    return lax.rem(zpos + RING, RING) * RING + lax.rem(xpos + RING, RING)


def project_kernel(
    tok_ref, wq_ref, wk_ref, wv_ref, ex_ref,
    q_ref, k_ref, v_ref,
    tok, wq, wk, wv, acc,
    wsend, wrecv, tsend, trecv, local_sem,
):
    me = lax.axis_index("context")
    zpos, xpos = me // RING, lax.rem(me, RING)
    col = lax.axis_index("tensor")
    ypos, core = col // 2, lax.rem(col, 2)
    mate = ypos * 2 + 1 - core
    up = lax.rem(ypos + 1, RING) * 2 + core
    down = lax.rem(ypos + RING - 1, RING) * 2 + core
    token_count = tok.shape[1]

    loads = [
        pltpu.make_async_copy(tok_ref, tok.at[col], local_sem.at[0]),
        pltpu.make_async_copy(wq_ref, wq.at[me], local_sem.at[1]),
        pltpu.make_async_copy(wk_ref, wk.at[me], local_sem.at[2]),
        pltpu.make_async_copy(wv_ref, wv.at[me], local_sem.at[3]),
        pltpu.make_async_copy(
            ex_ref, q_ref.at[me, pl.ds(token_count, EXTRA), :], local_sem.at[4]
        ),
    ]
    for load in loads:
        load.start()

    barrier = pltpu.get_barrier_semaphore()
    for dz, dx in ((1, 0), (-1, 0), (0, 1), (0, -1)):
        pl.semaphore_signal(
            barrier,
            inc=1,
            device_id={"context": context_of(zpos + dz, xpos + dx)},
            device_id_type=MESH,
        )
    for other in (up, down, mate):
        pl.semaphore_signal(barrier, inc=1, device_id={"tensor": other}, device_id_type=MESH)
    pl.semaphore_wait(barrier, 7)

    tsent = []
    part = token_count // 2

    def tcopy(index, block, rows, to):
        ref = tok.at[block, rows, :]
        return pltpu.make_async_remote_copy(
            src_ref=ref, dst_ref=ref, send_sem=tsend.at[index], recv_sem=trecv.at[index],
            device_id={"tensor": to}, device_id_type=MESH,
        )

    def tstart(index, block, rows, to):
        copy = tcopy(index, block, rows, to)
        copy.start()
        tsent.append(copy)

    every = pl.ds(0, token_count)
    low, high = pl.ds(0, part), pl.ds(part, part)
    across = lax.rem(ypos + 2, RING) * 2 + core

    gathers = [
        ContextGather(buf, halves(buf.shape[1], extra), wsend.at[i], wrecv.at[i], zpos, xpos)
        for i, (buf, extra) in enumerate(((wq, 0), (q_ref, EXTRA), (wk, 0), (wv, 0)))
    ]
    for_q, for_all, for_k, for_v = [g.stages() for g in gathers]

    loads[0].wait()
    loads[1].wait()
    tstart(0, col, every, up)
    tstart(1, col, every, down)
    tstart(4, col, every, mate)
    for_q[0]()
    tcopy(0, down, every, up).wait_recv()
    tstart(2, down, low, up)
    tcopy(1, up, every, down).wait_recv()
    tstart(3, up, high, down)
    tstart(5, down, every, mate)
    tstart(6, up, every, mate)
    for_q[1]()
    tcopy(2, across, low, up).wait_recv()
    tcopy(3, across, high, down).wait_recv()
    tstart(7, across, every, mate)
    for stage in for_q[2:5]:
        stage()
    loads[2].wait()
    for_k[0]()
    for index, block in ((4, mate), (5, down), (6, up), (7, across)):
        other = lax.rem(block, 2) * 0 + block // 2 * 2 + 1 - core
        tcopy(index, other, every, mate).wait_recv()
    for_q[5]()

    def project(w):
        @pl.loop(0, tok.shape[0])
        def _(t):
            base = pl.multiple_of(t * 2, 2)
            piece = w[pl.ds(base, 2)].reshape(tok.shape[2], w.shape[2])
            new = jnp.dot(tok[t], piece, preferred_element_type=jnp.float32)

            @pl.when(t == 0)
            def _():
                acc[...] = new

            @pl.when(t > 0)
            def _():
                acc[...] += new

    project(wq)
    q_ref[me, 0:token_count, :] = acc[...].astype(jnp.bfloat16)
    loads[4].wait()
    for_all[0]()
    for step in range(1, 6):
        for_all[step]()
        for_k[step]()
        if step == 3:
            loads[3].wait()
            for_v[0]()
    project(wk)
    k_ref[...] = acc[...].astype(jnp.bfloat16)
    for step in range(1, 6):
        for_v[step]()
    project(wv)
    v_ref[...] = acc[...].astype(jnp.bfloat16)
    for copy in tsent:
        copy.wait_send()
    for gather in gathers:
        gather.drain()


def gather_project(tokens, wq, wk, wv, extra):
    token_count, depth = tokens.shape
    rows, width = wq.shape
    devices = lax.axis_size("context")
    columns = lax.axis_size("tensor")
    hbm = pl.BlockSpec(memory_space=pl.ANY)
    vmem = pl.BlockSpec(memory_space=pltpu.VMEM)
    weight = pltpu.VMEM((devices, rows, width), jnp.bfloat16)
    return pl.pallas_call(
        project_kernel,
        in_specs=[hbm] * 5,
        out_specs=[vmem] * 3,
        out_shape=[
            jax.ShapeDtypeStruct((devices, token_count + EXTRA, width), jnp.bfloat16),
            jax.ShapeDtypeStruct((token_count, width), jnp.bfloat16),
            jax.ShapeDtypeStruct((token_count, width), jnp.bfloat16),
        ],
        scratch_shapes=[
            pltpu.VMEM((columns, token_count, depth), jnp.bfloat16),
            weight,
            weight,
            weight,
            pltpu.VMEM((token_count, width), jnp.float32),
            pltpu.SemaphoreType.DMA((4, 40)),
            pltpu.SemaphoreType.DMA((4, 40)),
            pltpu.SemaphoreType.DMA((8,)),
            pltpu.SemaphoreType.DMA((8,)),
            pltpu.SemaphoreType.DMA((5,)),
        ],
        compiler_params=pltpu.CompilerParams(
            collective_id=0, has_side_effects=True, vmem_limit_bytes=60 << 20
        ),
        name="gather_project",
    )(tokens, wq, wk, wv, extra)


def owner_kernel(heads, cap, rows_ref, n_ref, q_ref, k_ref, v_ref, o_ref, st_ref, acc_ref):
    src = pl.program_id(0)
    span_count = o_ref.shape[1]
    span = o_ref.shape[3]
    block = k_ref.shape[1]
    columns = [slice(h * HDIM, (h + 1) * HDIM) for h in range(heads)]

    def scores(half, j):
        c = src * span_count + half
        n = n_ref[c]
        r0 = rows_ref[c * cap + 2 * j]
        r1 = rows_ref[c * cap + 2 * j + 1]
        bias0 = jnp.where(2 * j < n, 0.0, NEG)
        bias1 = jnp.where(2 * j + 1 < n, 0.0, NEG)
        out = []
        for cols in columns:
            q = q_ref[0, half * span : (half + 1) * span, cols]
            k = jnp.concatenate([k_ref[r0, :, cols], k_ref[r1, :, cols]], 0)
            v = jnp.concatenate([v_ref[r0, :, cols], v_ref[r1, :, cols]], 0)
            s = dot_nt(k, q) * SCALE
            out.append((jnp.concatenate([s[:block] + bias0, s[block:] + bias1], 0), v))
        return out

    for half in range(span_count):
        results = []
        for s, v in scores(half, 0):
            m = jnp.max(s, axis=0, keepdims=True)
            p = jnp.exp2(s - m)
            l = jnp.sum(p, axis=0, keepdims=True)
            results.append((m, l, dot_tn(v, p.astype(jnp.bfloat16))))
        for h, (m, l, a) in enumerate(results):
            st_ref[0, half, h : h + 1, :] = m
            st_ref[0, half, 8 + h : 9 + h, :] = l
            acc_ref[half, columns[h], :] = a
            o_ref[0, half, columns[h], :] = (a * (1.0 / l)).astype(jnp.bfloat16)

    for half in range(span_count):
        n = n_ref[src * span_count + half]

        @pl.when(n > 2)
        def _():
            @pl.loop(1, (n + 1) // 2)
            def _(j):
                results = []
                for h, (s, v) in enumerate(scores(half, j)):
                    old = st_ref[0, half, h : h + 1, :]
                    m = jnp.maximum(jnp.max(s, axis=0, keepdims=True), old)
                    decay = jnp.exp2(old - m)
                    p = jnp.exp2(s - m)
                    l = jnp.sum(p, axis=0, keepdims=True)
                    l = l + st_ref[0, half, 8 + h : 9 + h, :] * decay
                    a = dot_tn(v, p.astype(jnp.bfloat16)) + acc_ref[half, columns[h], :] * decay
                    results.append((m, l, a))
                for h, (m, l, a) in enumerate(results):
                    st_ref[0, half, h : h + 1, :] = m
                    st_ref[0, half, 8 + h : 9 + h, :] = l
                    acc_ref[half, columns[h], :] = a

            for h in range(heads):
                l = st_ref[0, half, 8 + h : 9 + h, :]
                o_ref[0, half, columns[h], :] = (
                    acc_ref[half, columns[h], :] * (1.0 / l)
                ).astype(jnp.bfloat16)


def owner_attention(rows, n, q_all, cache_keys, cache_values, heads, cap):
    devices, tokens, width = q_all.shape
    span_count = n.shape[0] // devices
    span = (tokens - EXTRA) // span_count
    whole = pl.BlockSpec(cache_keys.shape, lambda s, *_: (0, 0, 0), pipeline_mode=pl.Buffered(1))
    return pl.pallas_call(
        functools.partial(owner_kernel, heads, cap),
        grid_spec=pltpu.PrefetchScalarGridSpec(
            num_scalar_prefetch=2,
            grid=(devices,),
            in_specs=[
                pl.BlockSpec((1, tokens, width), lambda s, *_: (s, 0, 0)),
                whole,
                whole,
            ],
            out_specs=[
                pl.BlockSpec((1, span_count, width, span), lambda s, *_: (s, 0, 0, 0)),
                pl.BlockSpec((1, span_count, 16, span), lambda s, *_: (s, 0, 0, 0)),
            ],
            scratch_shapes=[pltpu.VMEM((span_count, width, span), jnp.float32)],
        ),
        out_shape=[
            jax.ShapeDtypeStruct((devices, span_count, width, span), jnp.bfloat16),
            jax.ShapeDtypeStruct((devices, span_count, 16, span), jnp.float32),
        ],
    )(rows, n, q_all, cache_keys, cache_values)


def combine_kernel(
    heads,
    o_ref, st_ref, q_ref, k_ref, v_ref,
    out_ref,
    before, relay, relay_st, got, got_st, mid, mid_st,
    relay2, relay2_st, got2, got2_st, acc, acc_st,
    send, recv, send_st, recv_st, psend, precv,
):
    me = lax.axis_index("context")
    zpos, xpos = me // RING, lax.rem(me, RING)
    devices = RING * RING
    behind, ahead = lax.rem(me + devices - 1, devices), lax.rem(me + 1, devices)
    span = o_ref.shape[-1]
    cut = (heads + 1) // 2 * HDIM
    parts = ((0, cut), (cut, heads * HDIM - cut))

    barrier = pltpu.get_barrier_semaphore()
    for other in (
        context_of(zpos + 1, xpos),
        context_of(zpos - 1, xpos),
        context_of(zpos, xpos + 1),
        context_of(zpos, xpos - 1),
        behind,
        ahead,
    ):
        pl.semaphore_signal(barrier, inc=1, device_id={"context": other}, device_id_type=MESH)
    pl.semaphore_wait(barrier, 6)

    started = []

    def near(half, first, way):
        if (half == 0) == first:
            return context_of(zpos, xpos + way)
        return context_of(zpos + way, xpos)

    def copies(half, index, src, src_st, dst, dst_st):
        slot = half * 12 + index
        to = near(half, index < 6, 1 if index % 2 == 0 else -1)
        make = pltpu.make_async_remote_copy
        where = dict(device_id={"context": to}, device_id_type=MESH)
        return (
            make(src, dst, send.at[slot], recv.at[slot], **where),
            make(src_st, dst_st, send_st.at[slot], recv_st.at[slot], **where),
        )

    def start(*args):
        for copy in copies(*args):
            copy.start()
            started.append(copy)

    def arrive(half, index, dst, dst_st):
        for copy in copies(half, index, dst, dst_st, dst, dst_st):
            copy.wait_recv()

    def first_at(half):
        return xpos if half == 0 else zpos

    def second_at(half):
        return zpos if half == 0 else xpos

    def wrap(position):
        return lax.rem(position + RING, RING)

    def held(ref, half, step, low):
        to = wrap(first_at(half) + step)
        if half == 0:
            return ref.at[pl.ds(low, 2), to, 0]
        return ref.at[to, pl.ds(low, 2), 1]

    def merge(out, out_st, sources, head_range):
        @pl.loop(*head_range)
        def _(h):
            rows = pl.ds(pl.multiple_of(h * HDIM, HDIM), HDIM)
            ms = [st[pl.ds(h, 1), :] for _, st in sources]
            m = functools.reduce(jnp.maximum, ms)
            ws = [st[pl.ds(8 + h, 1), :] * jnp.exp2(x - m) for (_, st), x in zip(sources, ms)]
            total = functools.reduce(jnp.add, ws)
            inverse = 1.0 / total
            terms = [
                part[rows, :].astype(jnp.float32) * (w * inverse)
                for (part, _), w in zip(sources, ws)
            ]
            out[rows, :] = functools.reduce(jnp.add, terms).astype(jnp.bfloat16)
            out_st[pl.ds(h, 1), :] = m
            out_st[pl.ds(8 + h, 1), :] = total

    for half in (0, 1):
        for index, low in ((0, 0), (1, 2)):
            start(
                half, index, held(o_ref, half, 2, low), held(st_ref, half, 2, low),
                relay.at[half, index], relay_st.at[half, index],
            )
    for half in (0, 1):
        for index, low, way in ((2, 2, 1), (3, 0, -1)):
            start(
                half, index, held(o_ref, half, way, low), held(st_ref, half, way, low),
                got.at[half, index - 2, pl.ds(low, 2)], got_st.at[half, index - 2, pl.ds(low, 2)],
            )
    prior = []
    for i, ref in enumerate((k_ref, v_ref)):
        prior.append(
            pltpu.make_async_remote_copy(
                ref.at[pl.ds(ref.shape[0] - span, span), :], before.at[i],
                psend.at[i], precv.at[i],
                device_id={"context": ahead}, device_id_type=MESH,
            )
        )
        prior[-1].start()

    key = lax.broadcasted_iota(jnp.int32, (span, span), 0)
    row = lax.broadcasted_iota(jnp.int32, (span, span), 1)

    def local(half, h, keys, values, bias, first):
        cols = slice(h * HDIM, (h + 1) * HDIM)
        q = q_ref[0, half * span : (half + 1) * span, cols]
        s = dot_nt(keys, q) * SCALE
        s = jnp.where(key <= row, s, NEG) if bias is None else s + bias
        m = jnp.max(s, axis=0, keepdims=True)
        if not first:
            old = acc_st[half, h : h + 1, :]
            m = jnp.maximum(m, old)
            decay = jnp.exp2(old - m)
        p = jnp.exp2(s - m)
        l = jnp.sum(p, axis=0, keepdims=True)
        a = dot_tn(values, p.astype(jnp.bfloat16))
        if not first:
            l = l + acc_st[half, 8 + h : 9 + h, :] * decay
            a = a + acc[half, cols, :] * decay
        acc_st[half, h : h + 1, :] = m
        acc_st[half, 8 + h : 9 + h, :] = l
        acc[half, cols, :] = a

    for half in (0, 1):
        rows = slice(half * span, (half + 1) * span)
        for h in range(heads):
            cols = slice(h * HDIM, (h + 1) * HDIM)
            local(half, h, k_ref[rows, cols], v_ref[rows, cols], None, True)
    for h in range(heads):
        cols = slice(h * HDIM, (h + 1) * HDIM)
        local(1, h, k_ref[0:span, cols], v_ref[0:span, cols], 0.0, False)

    for half in (0, 1):
        for index, low, way in ((0, 0, 1), (1, 2, -1)):
            arrive(half, index, relay.at[half, index], relay_st.at[half, index])
            to = wrap(first_at(half) + way)
            for i in (0, 1):
                part, st = relay.at[half, index, i], relay_st.at[half, index, i]
                at = (low + i, to, 0) if half == 0 else (to, low + i, 1)
                merge(part, st, [(part, st), (o_ref.at[at], st_ref.at[at])], (0, heads))
            start(
                half, 4 + index, relay.at[half, index], relay_st.at[half, index],
                got.at[half, index, pl.ds(low, 2)], got_st.at[half, index, pl.ds(low, 2)],
            )

    for copy in prior:
        copy.wait_recv()
    bias = jnp.where(me > 0, 0.0, NEG)
    for h in range(heads):
        cols = slice(h * HDIM, (h + 1) * HDIM)
        local(0, h, before[0, :, cols], before[1, :, cols], bias, False)

    for half in (0, 1):
        for index, low in ((2, 2), (3, 0), (4, 0), (5, 2)):
            side = index % 2
            arrive(
                half, index,
                got.at[half, side, pl.ds(low, 2)], got_st.at[half, side, pl.ds(low, 2)],
            )
        for step in (2, 1, -1, 0):
            to = wrap(second_at(half) + step)
            at = (to, xpos, 0) if half == 0 else (zpos, to, 1)
            merge(
                mid.at[half, to], mid_st.at[half, to],
                [(o_ref.at[at], st_ref.at[at])]
                + [(got.at[half, i, to], got_st.at[half, i, to]) for i in (0, 1)],
                (0, heads),
            )
            for side in (0, 1):
                rows = pl.ds(*parts[side])
                if step == 2:
                    start(
                        half, 6 + side, mid.at[half, to, rows], mid_st.at[half, to],
                        relay2.at[half, rows], relay2_st.at[half, side],
                    )
            if step in (1, -1):
                side = 0 if step == 1 else 1
                other = pl.ds(*parts[1 - side])
                start(
                    half, 8 + side, mid.at[half, to, other], mid_st.at[half, to],
                    got2.at[half, side, other], got2_st.at[half, side, 1 - side],
                )

    for half in (0, 1):
        for side, way in ((0, 1), (1, -1)):
            rows = pl.ds(*parts[side])
            arrive(half, 6 + side, relay2.at[half, rows], relay2_st.at[half, side])
            to = wrap(second_at(half) + way)
            merge(
                relay2.at[half], relay2_st.at[half, side],
                [
                    (relay2.at[half], relay2_st.at[half, side]),
                    (mid.at[half, to], mid_st.at[half, to]),
                ],
                (parts[side][0] // HDIM, sum(parts[side]) // HDIM),
            )
            start(
                half, 10 + side, relay2.at[half, rows], relay2_st.at[half, side],
                got2.at[half, side, rows], got2_st.at[half, side, side],
            )

    for half in (0, 1):
        for side in (0, 1):
            for index, which in ((8 + side, 1 - side), (10 + side, side)):
                arrive(
                    half, index,
                    got2.at[half, side, pl.ds(*parts[which])], got2_st.at[half, side, which],
                )
        at = second_at(half)
        for h in range(heads):
            cols = slice(h * HDIM, (h + 1) * HDIM)
            which = 0 if h * HDIM < cut else 1
            sources = [(mid.at[half, at], mid_st.at[half, at])]
            sources += [(got2.at[half, i], got2_st.at[half, i, which]) for i in (0, 1)]
            old = acc_st[half, h : h + 1, :]
            ms = [st[h : h + 1, :] for _, st in sources]
            m = functools.reduce(jnp.maximum, ms, old)
            decay = jnp.exp2(old - m)
            total = acc_st[half, 8 + h : 9 + h, :] * decay
            a = acc[half, cols, :] * decay
            for (part, st), x in zip(sources, ms):
                w = st[8 + h : 9 + h, :] * jnp.exp2(x - m)
                total = total + w
                a = a + part[cols, :].astype(jnp.float32) * w
            out_ref[half * span : (half + 1) * span, cols] = jnp.transpose(a / total).astype(
                out_ref.dtype
            )

    for copy in started + prior:
        copy.wait_send()


def combine(o, st, q, k, v, heads):
    span_count, width, span = o.shape[1:]
    rows = st.shape[2]
    o = o.reshape(RING, RING, span_count, width, span)
    st = st.reshape(RING, RING, span_count, rows, span)
    vmem = pl.BlockSpec(memory_space=pltpu.VMEM)

    def pair(*lead):
        return [
            pltpu.VMEM(lead + (width, span), jnp.bfloat16),
            pltpu.VMEM(lead + (rows, span), jnp.float32),
        ]

    return pl.pallas_call(
        functools.partial(combine_kernel, heads),
        in_specs=[vmem] * 5,
        out_specs=vmem,
        out_shape=jax.ShapeDtypeStruct(k.shape, jnp.bfloat16),
        scratch_shapes=[pltpu.VMEM((2, span, width), jnp.bfloat16)]
        + pair(2, 2, 2)
        + pair(2, 2, RING)
        + pair(2, RING)
        + [pltpu.VMEM((2, width, span), jnp.bfloat16), pltpu.VMEM((2, 2, rows, span), jnp.float32)]
        + [
            pltpu.VMEM((2, 2, width, span), jnp.bfloat16),
            pltpu.VMEM((2, 2, 2, rows, span), jnp.float32),
        ]
        + [pltpu.VMEM((2, width, span), jnp.float32), pltpu.VMEM((2, rows, span), jnp.float32)]
        + [pltpu.SemaphoreType.DMA((24,))] * 4
        + [pltpu.SemaphoreType.DMA((2,))] * 2,
        compiler_params=pltpu.CompilerParams(
            collective_id=1, has_side_effects=True, vmem_limit_bytes=60 << 20
        ),
        name="combine",
    )(o, st, q, k, v)


def chosen_slots(selected, counts, block_slot, stored, width):
    span_count, select_count = selected.shape
    live = jnp.arange(select_count)[None, :] < counts[:, None]
    hit = selected[:, :, None] == jnp.arange(block_slot.shape[0])[None, None, :]
    slot = jnp.sum(jnp.where(hit, block_slot[None, None, :], 0), axis=2)
    owner = jnp.where(live, slot // stored, -1)
    both = jnp.concatenate([owner, slot % stored], 0).astype(jnp.bfloat16)
    return jnp.pad(both, ((0, EXTRA - 2 * span_count), (0, width - select_count)))


def owner_table(extra, span_count, select_count, cap):
    owner = extra[:, :span_count, :select_count].reshape(-1, select_count).astype(jnp.int32)
    row = extra[:, span_count : 2 * span_count, :select_count]
    row = row.reshape(-1, select_count).astype(jnp.int32)
    mine = owner == lax.axis_index("context")
    position = jnp.arange(select_count)
    earlier = position[None, :] < position[:, None]
    rank = jnp.sum(jnp.where(mine[:, None, :] & earlier[None], 1, 0), axis=2)
    place = mine[:, :, None] & (rank[:, :, None] == jnp.arange(cap)[None, None, :])
    rows = jnp.sum(jnp.where(place, row[:, :, None], 0), axis=1)
    return rows.reshape(-1).astype(jnp.int32), jnp.sum(mine, axis=1).astype(jnp.int32)


def shards(
    tokens,
    query_weight,
    key_weight,
    value_weight,
    cache_keys,
    cache_values,
    selected,
    counts,
    block_slot,
):
    token_count = tokens.shape[0]
    width = query_weight.shape[1]
    heads = width // HDIM
    span_count, select_count = selected.shape
    devices = lax.axis_size("context")
    cap = max(2, 2 * span_count * select_count // devices)

    extra = chosen_slots(selected, counts, block_slot, cache_keys.shape[0], width)
    q_all, k, v = gather_project(tokens, query_weight, key_weight, value_weight, extra)
    rows, n = owner_table(q_all[:, token_count:], span_count, select_count, cap)
    o, st = owner_attention(rows, n, q_all, cache_keys, cache_values, heads, cap)
    me = lax.axis_index("context")
    q = lax.dynamic_slice(q_all, (me, 0, 0), (1, token_count, width))
    return combine(o, st, q, k, v, heads)


def solution(mesh):
    placed = (
        P("context", "tensor"),
        P("context", "tensor"),
        P("context", "tensor"),
        P("context", "tensor"),
        P("context", None, "tensor"),
        P("context", None, "tensor"),
        P("context", None),
        P("context"),
        P(),
    )
    return jax.shard_map(
        shards, mesh=mesh, in_specs=placed, out_specs=P("context", "tensor"), check_vma=False
    )
```

```python
import functools

import jax
import jax.numpy as jnp
from jax import lax
from jax.experimental import pallas as pl
from jax.experimental.pallas import tpu as pltpu
from jax.sharding import PartitionSpec as P

HDIM = 128
NEG = -1e30
MESH = pl.DeviceIdType.MESH
EXTRA = 16
SCALE = HDIM ** (-0.5) * 1.4426950408889634


def dot_nt(a, b):
    return lax.dot_general(a, b, (((1,), (1,)), ((), ())), preferred_element_type=jnp.float32)


def dot_tn(a, b):
    return lax.dot_general(a, b, (((0,), (0,)), ((), ())), preferred_element_type=jnp.float32)


RING = 4
OFFSETS = (0, -1, 1, 2)


def wrap(position):
    return lax.rem(position + RING, RING)


def context_of(zpos, xpos):
    return wrap(zpos) * RING + wrap(xpos)


class Ring:
    def __init__(self, view, to, sems, sent):
        self.view, self.to, self.sems, self.sent = view, to, sems, sent
        self.waited = set()

    def copy(self, index, step):
        ref = self.view(step, max(0, index - 1))
        return remote(ref, ref, self.sems, index, self.to(1 if index % 2 == 0 else -1))

    def start(self, index):
        copy = self.copy(index, (0, 0, -1, 1)[index])
        copy.start()
        self.sent.append(copy)

    def arrive(self, index):
        if index not in self.waited:
            self.waited.add(index)
            self.copy(index, (-1, 1, 2, 2)[index]).wait_recv()

    def whole(self):
        self.start(0)
        self.start(1)

    def onward(self):
        self.arrive(0)
        self.start(2)
        self.arrive(1)
        self.start(3)

    def opposite(self):
        self.arrive(2)
        self.arrive(3)


def remote(src, dst, sems, index, to):
    send, recv, base = sems
    return pltpu.make_async_remote_copy(
        src_ref=src,
        dst_ref=dst,
        send_sem=send.at[base + index],
        recv_sem=recv.at[base + index],
        device_id=to,
        device_id_type=MESH,
    )


def context_gather(buf, extra, send, recv, zpos, xpos, sent):
    half_rows = (buf.shape[1] - extra) // 2
    part_rows = half_rows // 2
    spans = (
        ((0, half_rows), (0, part_rows), (part_rows, half_rows - part_rows)),
        (
            (half_rows, half_rows + extra),
            (half_rows, part_rows),
            (half_rows + part_rows, half_rows - part_rows + extra),
        ),
    )
    rings = {}

    def make(half, phase):
        along_x = (half == 0) == (phase == 0)
        first = 0 if phase == 0 else OFFSETS[phase - 1]

        def view(step, part):
            start, size = spans[half][part]
            dz, dx = (first, step) if along_x else (step, first)
            return buf.at[context_of(zpos + dz, xpos + dx), pl.ds(start, size), :]

        def to(way):
            dz, dx = (0, way) if along_x else (way, 0)
            return {"context": context_of(zpos + dz, xpos + dx)}

        return Ring(view, to, (send, recv, half * 20 + phase * 4), sent)

    for half in (0, 1):
        for phase in range(5):
            rings[half, phase] = make(half, phase)

    def own():
        for half in (0, 1):
            rings[half, 0].whole()
            rings[half, 1].whole()

    def neighbours():
        for half in (0, 1):
            rings[half, 0].onward()
            rings[half, 2].whole()
            rings[half, 3].whole()
        for half in (0, 1):
            rings[half, 1].onward()

    def far():
        for half in (0, 1):
            rings[half, 0].opposite()
            rings[half, 4].whole()

    def corners():
        for half in (0, 1):
            rings[half, 2].onward()
            rings[half, 3].onward()

    def last():
        for half in (0, 1):
            rings[half, 4].onward()

    def rest():
        for half in (0, 1):
            for phase in (1, 2, 3, 4):
                rings[half, phase].opposite()

    return [own, neighbours, far, corners, last, rest]


def project_kernel(
    span_count, select_count, cap,
    tok_ref, wq_ref, wk_ref, wv_ref, ex_ref,
    q_ref, own_ref, k_ref, v_ref, tab_ref,
    tok, stage, w, acc, done, back,
    load_sem, tsend, trecv, wsend, wrecv, bsend, brecv, qsend, qrecv,
):
    me = lax.axis_index("context")
    zpos, xpos = me // RING, lax.rem(me, RING)
    col = lax.axis_index("tensor")
    ypos, core = col // 2, lax.rem(col, 2)
    token_count, depth = tok.shape[2], tok.shape[3]
    rows = w.shape[3]
    sent = []

    token_load = pltpu.make_async_copy(tok_ref, tok.at[col, zpos], load_sem.at[0])
    token_load.start()
    extra_load = pltpu.make_async_copy(
        ex_ref, q_ref.at[me, pl.ds(token_count, EXTRA), :], load_sem.at[1]
    )
    extra_load.start()
    loads = ([], [])
    for part in (0, 1):
        for to in range(RING):
            left = (wq_ref, wk_ref, wv_ref, wq_ref)[to]
            pair = ((wq_ref, to), (left, RING)) if part == 0 else ((wk_ref, to), (wv_ref, to))
            for i, (ref, head) in enumerate(pair):
                load = pltpu.make_async_copy(
                    ref.at[:, pl.ds(head * HDIM, HDIM)],
                    stage.at[part, to, :, pl.ds(i * HDIM, HDIM)],
                    load_sem.at[2 + part * 8 + to * 2 + i],
                )
                load.start()
                loads[part].append(load)

    def at_x(way):
        return {"context": context_of(zpos, xpos + way)}

    def at_z(way):
        return {"context": context_of(zpos + way, xpos)}

    def at_y(way):
        return {"tensor": wrap(ypos + way) * 2 + core}

    mate = {"tensor": ypos * 2 + 1 - core}
    barrier = pltpu.get_barrier_semaphore()
    partners = [at_x(1), at_x(-1), at_z(1), at_z(-1), at_z(2), at_y(1), at_y(-1), mate]
    for other in partners:
        pl.semaphore_signal(barrier, inc=1, device_id=other, device_id_type=MESH)
    pl.semaphore_wait(barrier, len(partners))

    def cut(size):
        return (pl.ds(0, size), pl.ds(0, size // 2), pl.ds(size // 2, size // 2))

    ztok = Ring(
        lambda step, part: tok.at[col, wrap(zpos + step), cut(token_count)[part]],
        at_z, (tsend, trecv, 0), sent,
    )
    ytok = {
        o: Ring(
            lambda step, part, o=o: tok.at[
                wrap(ypos + step) * 2 + core, wrap(zpos + o), cut(token_count)[part]
            ],
            at_y, (tsend, trecv, 4 + 4 * i), sent,
        )
        for i, o in enumerate(OFFSETS)
    }

    def share(step, o, receive=False):
        side = 1 - core if receive else core
        ref = tok.at[wrap(ypos + step) * 2 + side, wrap(zpos + o)]
        index = 20 + OFFSETS.index(step) * 4 + OFFSETS.index(o)
        copy = remote(ref, ref, (tsend, trecv, 0), index, mate)
        if receive:
            copy.wait_recv()
        else:
            copy.start()
            sent.append(copy)

    def exchange(part, step, receive=False):
        index = part * 3 + OFFSETS.index(step) - 1
        src = stage.at[part, wrap(zpos + step)]
        if receive:
            dst = w.at[part, wrap(zpos - step), xpos]
            remote(src, dst, (wsend, wrecv, 0), index, at_z(step)).wait_recv()
        else:
            copy = remote(src, w.at[part, zpos, xpos], (wsend, wrecv, 0), index, at_z(step))
            copy.start()
            sent.append(copy)

    xw = {
        (part, o): Ring(
            lambda step, piece, part=part, o=o: w.at[
                part, wrap(zpos + o), wrap(xpos + step), cut(rows)[piece]
            ],
            at_x, (wsend, wrecv, 6 + part * 16 + 4 * i), sent,
        )
        for part in (0, 1)
        for i, o in enumerate(OFFSETS)
    }

    def keep(part):
        for load in loads[part]:
            load.wait()
        copy = pltpu.make_async_copy(
            stage.at[part, zpos], w.at[part, zpos, xpos], load_sem.at[18 + part]
        )
        copy.start()
        copy.wait()

    token_load.wait()
    ztok.whole()
    ytok[0].whole()
    share(0, 0)
    keep(0)
    xw[0, 0].whole()
    exchange(0, 1)
    exchange(0, -1)
    keep(1)
    xw[1, 0].whole()
    xw[0, 0].onward()
    ztok.onward()
    for o in (-1, 1):
        ytok[o].whole()
        share(0, o)
    ytok[0].onward()
    exchange(0, 2)
    exchange(1, 1)
    exchange(1, -1)
    exchange(1, 2)
    share(-1, 0)
    share(1, 0)
    for step in (1, -1):
        exchange(0, step, receive=True)
        xw[0, -step].whole()
    xw[1, 0].onward()
    ztok.opposite()
    ytok[2].whole()
    share(0, 2)
    exchange(0, 2, receive=True)
    xw[0, 2].whole()
    for o in (-1, 1):
        ytok[o].onward()
        share(-1, o)
        share(1, o)
    xw[0, -1].onward()
    xw[0, 1].onward()
    for step in (1, -1):
        exchange(1, step, receive=True)
        xw[1, -step].whole()
    ytok[0].opposite()
    share(2, 0)
    xw[0, 2].onward()
    exchange(1, 2, receive=True)
    xw[1, 2].whole()
    ytok[2].onward()
    share(-1, 2)
    share(1, 2)
    for o in (-1, 1, 2):
        xw[1, o].onward()
    for o in (-1, 1):
        ytok[o].opposite()
        share(2, o)

    def compute(part, step):
        for side in (0, 1):
            t = wrap(ypos + step) * 2 + side
            piece = w[part, wrap(ypos + step), 2 * side : 2 * side + 2].reshape(depth, w.shape[4])

            @pl.loop(0, RING)
            def _(z):
                new = jnp.dot(tok[t, z], piece, preferred_element_type=jnp.float32)
                if step == 0 and side == 0:
                    acc[z] = new
                else:
                    acc[z] += new

    def give_back(part):
        @pl.loop(0, RING)
        def _(z):
            done[part, z] = acc[z].astype(jnp.bfloat16)

        back[part, zpos] = acc[zpos].astype(jnp.bfloat16)
        for i, step in enumerate(OFFSETS[1:]):
            copy = remote(
                done.at[part, wrap(zpos + step)], back.at[part, zpos],
                (bsend, brecv, 0), part * 3 + i, at_z(step),
            )
            copy.start()
            sent.append(copy)

    def take_back(part):
        for i, step in enumerate(OFFSETS[1:]):
            ref = back.at[part, wrap(zpos - step)]
            remote(ref, ref, (bsend, brecv, 0), part * 3 + i, at_z(step)).wait_recv()

    for o in OFFSETS:
        xw[0, o].opposite()
    for step in OFFSETS[:3]:
        for o in OFFSETS:
            share(step, o, receive=True)
        compute(0, step)
    ytok[2].opposite()
    share(2, 2)
    for o in OFFSETS:
        share(2, o, receive=True)
    compute(0, 2)
    give_back(0)
    gather = context_gather(q_ref, EXTRA, qsend, qrecv, zpos, xpos, sent)
    extra_load.wait()
    take_back(0)
    for head in range(RING + 1):
        cols = slice(head * HDIM, (head + 1) * HDIM)
        if head < RING:
            piece = back[0, head, :, 0:HDIM]
        else:
            piece = back[0, 0, :, HDIM : 2 * HDIM]
        q_ref[me, 0:token_count, cols] = piece
        own_ref[:, cols] = piece
    gather[0]()
    for o in OFFSETS:
        xw[1, o].opposite()
    compute(1, 0)
    gather[1]()
    compute(1, -1)
    gather[2]()
    compute(1, 1)
    gather[3]()
    compute(1, 2)
    give_back(1)
    gather[4]()
    take_back(1)
    for head in range(RING):
        cols = slice(head * HDIM, (head + 1) * HDIM)
        k_ref[:, cols] = back[1, head, :, 0:HDIM]
        v_ref[:, cols] = back[1, head, :, HDIM : 2 * HDIM]
    k_ref[:, RING * HDIM :] = back[0, 1, :, HDIM : 2 * HDIM]
    v_ref[:, RING * HDIM :] = back[0, 2, :, HDIM : 2 * HDIM]
    gather[5]()

    devices = q_ref.shape[0]
    lane = lax.broadcasted_iota(jnp.int32, (devices, HDIM), 1)
    before = lax.broadcasted_iota(jnp.int32, (HDIM, HDIM), 0)
    after = lax.broadcasted_iota(jnp.int32, (HDIM, HDIM), 1)
    earlier = jnp.where(before < after, 1.0, 0.0).astype(jnp.bfloat16)
    told = q_ref[:, token_count:, 0:HDIM].astype(jnp.float32)
    for half in range(span_count):
        owner = told[:, half, :]
        row = told[:, span_count + half, :]
        mine = jnp.where((owner == me.astype(jnp.float32)) & (lane < select_count), 1.0, 0.0)
        rank = jnp.dot(mine.astype(jnp.bfloat16), earlier, preferred_element_type=jnp.float32)
        table = jnp.where(lane == cap, jnp.sum(mine, axis=1, keepdims=True), 0.0)
        for r in range(cap):
            value = jnp.sum(jnp.where(rank == r, mine * row, 0.0), axis=1, keepdims=True)
            table = jnp.where(lane == r, value, table)
        tab_ref[half] = table.astype(jnp.int32)

    for copy in sent:
        copy.wait_send()


def gather_project(tokens, wq, wk, wv, extra, span_count, select_count, cap):
    token_count, depth = tokens.shape
    rows, width = wq.shape
    devices = lax.axis_size("context")
    columns = lax.axis_size("tensor")
    hbm = pl.BlockSpec(memory_space=pl.ANY)
    vmem = pl.BlockSpec(memory_space=pltpu.VMEM)
    own = jax.ShapeDtypeStruct((token_count, width), jnp.bfloat16)
    two = 2 * HDIM

    def dma(count):
        return [pltpu.SemaphoreType.DMA((count,))] * 2

    return pl.pallas_call(
        functools.partial(project_kernel, span_count, select_count, cap),
        in_specs=[hbm] * 5,
        out_specs=[vmem] * 5,
        out_shape=[
            jax.ShapeDtypeStruct((devices, token_count + EXTRA, width), jnp.bfloat16),
            own,
            own,
            own,
            jax.ShapeDtypeStruct((span_count, devices, HDIM), jnp.int32),
        ],
        scratch_shapes=[
            pltpu.VMEM((columns, RING, token_count, depth), jnp.bfloat16),
            pltpu.VMEM((2, RING, rows, two), jnp.bfloat16),
            pltpu.VMEM((2, RING, RING, rows, two), jnp.bfloat16),
            pltpu.VMEM((RING, token_count, two), jnp.float32),
            pltpu.VMEM((2, RING, token_count, two), jnp.bfloat16),
            pltpu.VMEM((2, RING, token_count, two), jnp.bfloat16),
            pltpu.SemaphoreType.DMA((20,)),
        ]
        + dma(36)
        + dma(38)
        + dma(6)
        + dma(40),
        compiler_params=pltpu.CompilerParams(
            collective_id=0, has_side_effects=True, vmem_limit_bytes=60 << 20
        ),
        name="gather_project",
    )(tokens, wq, wk, wv, extra)


def owner_kernel(heads, cap, tab_ref, q_ref, k_ref, v_ref, o_ref, st_ref, acc_ref):
    src = pl.program_id(0)
    span_count = o_ref.shape[1]
    span = o_ref.shape[3]
    block = k_ref.shape[1]
    columns = [slice(h * HDIM, (h + 1) * HDIM) for h in range(heads)]

    def scores(half, j):
        n = tab_ref[half, src, cap]
        r0 = tab_ref[half, src, 2 * j]
        r1 = tab_ref[half, src, 2 * j + 1]
        bias0 = jnp.where(2 * j < n, 0.0, NEG)
        bias1 = jnp.where(2 * j + 1 < n, 0.0, NEG)
        out = []
        for cols in columns:
            q = q_ref[0, half * span : (half + 1) * span, cols]
            k = jnp.concatenate([k_ref[r0, :, cols], k_ref[r1, :, cols]], 0)
            v = jnp.concatenate([v_ref[r0, :, cols], v_ref[r1, :, cols]], 0)
            s = dot_nt(k, q) * SCALE
            out.append((jnp.concatenate([s[:block] + bias0, s[block:] + bias1], 0), v))
        return out

    for half in range(span_count):
        results = []
        for s, v in scores(half, 0):
            m = jnp.max(s, axis=0, keepdims=True)
            p = jnp.exp2(s - m)
            l = jnp.sum(p, axis=0, keepdims=True)
            results.append((m, l, dot_tn(v, p.astype(jnp.bfloat16))))
        for h, (m, l, a) in enumerate(results):
            st_ref[0, half, h : h + 1, :] = m
            st_ref[0, half, 8 + h : 9 + h, :] = l
            acc_ref[half, columns[h], :] = a
            o_ref[0, half, columns[h], :] = (a * (1.0 / l)).astype(jnp.bfloat16)

    for half in range(span_count):
        n = tab_ref[half, src, cap]

        @pl.when(n > 2)
        def _():
            @pl.loop(1, (n + 1) // 2)
            def _(j):
                results = []
                for h, (s, v) in enumerate(scores(half, j)):
                    old = st_ref[0, half, h : h + 1, :]
                    m = jnp.maximum(jnp.max(s, axis=0, keepdims=True), old)
                    decay = jnp.exp2(old - m)
                    p = jnp.exp2(s - m)
                    l = jnp.sum(p, axis=0, keepdims=True)
                    l = l + st_ref[0, half, 8 + h : 9 + h, :] * decay
                    a = dot_tn(v, p.astype(jnp.bfloat16)) + acc_ref[half, columns[h], :] * decay
                    results.append((m, l, a))
                for h, (m, l, a) in enumerate(results):
                    st_ref[0, half, h : h + 1, :] = m
                    st_ref[0, half, 8 + h : 9 + h, :] = l
                    acc_ref[half, columns[h], :] = a

            for h in range(heads):
                l = st_ref[0, half, 8 + h : 9 + h, :]
                o_ref[0, half, columns[h], :] = (
                    acc_ref[half, columns[h], :] * (1.0 / l)
                ).astype(jnp.bfloat16)


def owner_attention(table, q_all, cache_keys, cache_values, heads, cap):
    devices, tokens, width = q_all.shape
    span_count = table.shape[0]
    span = (tokens - EXTRA) // span_count
    whole = pl.BlockSpec(cache_keys.shape, lambda s, *_: (0, 0, 0), pipeline_mode=pl.Buffered(1))
    return pl.pallas_call(
        functools.partial(owner_kernel, heads, cap),
        grid_spec=pltpu.PrefetchScalarGridSpec(
            num_scalar_prefetch=1,
            grid=(devices,),
            in_specs=[
                pl.BlockSpec((1, tokens, width), lambda s, *_: (s, 0, 0)),
                whole,
                whole,
            ],
            out_specs=[
                pl.BlockSpec((1, span_count, width, span), lambda s, *_: (s, 0, 0, 0)),
                pl.BlockSpec((1, span_count, 16, span), lambda s, *_: (s, 0, 0, 0)),
            ],
            scratch_shapes=[pltpu.VMEM((span_count, width, span), jnp.float32)],
        ),
        out_shape=[
            jax.ShapeDtypeStruct((devices, span_count, width, span), jnp.bfloat16),
            jax.ShapeDtypeStruct((devices, span_count, 16, span), jnp.float32),
        ],
    )(table, q_all, cache_keys, cache_values)


def combine_kernel(
    heads,
    o_ref, st_ref, q_ref, k_ref, v_ref,
    out_ref,
    before, relay, relay_st, got, got_st, mid, mid_st,
    relay2, relay2_st, got2, got2_st, acc, acc_st,
    send, recv, send_st, recv_st, psend, precv,
):
    me = lax.axis_index("context")
    zpos, xpos = me // RING, lax.rem(me, RING)
    devices = RING * RING
    behind, ahead = lax.rem(me + devices - 1, devices), lax.rem(me + 1, devices)
    span = o_ref.shape[-1]
    cut = (heads + 1) // 2 * HDIM
    parts = ((0, cut), (cut, heads * HDIM - cut))

    barrier = pltpu.get_barrier_semaphore()
    for other in (
        context_of(zpos + 1, xpos),
        context_of(zpos - 1, xpos),
        context_of(zpos, xpos + 1),
        context_of(zpos, xpos - 1),
        behind,
        ahead,
    ):
        pl.semaphore_signal(barrier, inc=1, device_id={"context": other}, device_id_type=MESH)
    pl.semaphore_wait(barrier, 6)

    started = []

    def near(half, first, way):
        if (half == 0) == first:
            return context_of(zpos, xpos + way)
        return context_of(zpos + way, xpos)

    def copies(half, index, src, src_st, dst, dst_st):
        slot = half * 12 + index
        to = near(half, index < 6, 1 if index % 2 == 0 else -1)
        make = pltpu.make_async_remote_copy
        where = dict(device_id={"context": to}, device_id_type=MESH)
        return (
            make(src, dst, send.at[slot], recv.at[slot], **where),
            make(src_st, dst_st, send_st.at[slot], recv_st.at[slot], **where),
        )

    def start(*args):
        for copy in copies(*args):
            copy.start()
            started.append(copy)

    def arrive(half, index, dst, dst_st):
        for copy in copies(half, index, dst, dst_st, dst, dst_st):
            copy.wait_recv()

    def first_at(half):
        return xpos if half == 0 else zpos

    def second_at(half):
        return zpos if half == 0 else xpos

    def held(ref, half, step, low):
        to = wrap(first_at(half) + step)
        if half == 0:
            return ref.at[pl.ds(low, 2), to, 0]
        return ref.at[to, pl.ds(low, 2), 1]

    def merge(out, out_st, sources, head_range):
        @pl.loop(*head_range)
        def _(h):
            rows = pl.ds(pl.multiple_of(h * HDIM, HDIM), HDIM)
            ms = [st[pl.ds(h, 1), :] for _, st in sources]
            m = functools.reduce(jnp.maximum, ms)
            ws = [st[pl.ds(8 + h, 1), :] * jnp.exp2(x - m) for (_, st), x in zip(sources, ms)]
            total = functools.reduce(jnp.add, ws)
            inverse = 1.0 / total
            terms = [
                part[rows, :].astype(jnp.float32) * (w * inverse)
                for (part, _), w in zip(sources, ws)
            ]
            out[rows, :] = functools.reduce(jnp.add, terms).astype(jnp.bfloat16)
            out_st[pl.ds(h, 1), :] = m
            out_st[pl.ds(8 + h, 1), :] = total

    for half in (0, 1):
        for index, low in ((0, 0), (1, 2)):
            start(
                half, index, held(o_ref, half, 2, low), held(st_ref, half, 2, low),
                relay.at[half, index], relay_st.at[half, index],
            )
    for half in (0, 1):
        for index, low, way in ((2, 2, 1), (3, 0, -1)):
            start(
                half, index, held(o_ref, half, way, low), held(st_ref, half, way, low),
                got.at[half, index - 2, pl.ds(low, 2)], got_st.at[half, index - 2, pl.ds(low, 2)],
            )
    prior = []
    for i, ref in enumerate((k_ref, v_ref)):
        prior.append(
            pltpu.make_async_remote_copy(
                ref.at[pl.ds(ref.shape[0] - span, span), :], before.at[i],
                psend.at[i], precv.at[i],
                device_id={"context": ahead}, device_id_type=MESH,
            )
        )
        prior[-1].start()

    key = lax.broadcasted_iota(jnp.int32, (span, span), 0)
    row = lax.broadcasted_iota(jnp.int32, (span, span), 1)

    def local(half, h, keys, values, bias, first):
        cols = slice(h * HDIM, (h + 1) * HDIM)
        q = q_ref[half * span : (half + 1) * span, cols]
        s = dot_nt(keys, q) * SCALE
        s = jnp.where(key <= row, s, NEG) if bias is None else s + bias
        m = jnp.max(s, axis=0, keepdims=True)
        if not first:
            old = acc_st[half, h : h + 1, :]
            m = jnp.maximum(m, old)
            decay = jnp.exp2(old - m)
        p = jnp.exp2(s - m)
        l = jnp.sum(p, axis=0, keepdims=True)
        a = dot_tn(values, p.astype(jnp.bfloat16))
        if not first:
            l = l + acc_st[half, 8 + h : 9 + h, :] * decay
            a = a + acc[half, cols, :] * decay
        acc_st[half, h : h + 1, :] = m
        acc_st[half, 8 + h : 9 + h, :] = l
        acc[half, cols, :] = a

    for half in (0, 1):
        rows = slice(half * span, (half + 1) * span)
        for h in range(heads):
            cols = slice(h * HDIM, (h + 1) * HDIM)
            local(half, h, k_ref[rows, cols], v_ref[rows, cols], None, True)
    for h in range(heads):
        cols = slice(h * HDIM, (h + 1) * HDIM)
        local(1, h, k_ref[0:span, cols], v_ref[0:span, cols], 0.0, False)

    for half in (0, 1):
        for index, low, way in ((0, 0, 1), (1, 2, -1)):
            arrive(half, index, relay.at[half, index], relay_st.at[half, index])
            to = wrap(first_at(half) + way)
            for i in (0, 1):
                part, st = relay.at[half, index, i], relay_st.at[half, index, i]
                at = (low + i, to, 0) if half == 0 else (to, low + i, 1)
                merge(part, st, [(part, st), (o_ref.at[at], st_ref.at[at])], (0, heads))
            start(
                half, 4 + index, relay.at[half, index], relay_st.at[half, index],
                got.at[half, index, pl.ds(low, 2)], got_st.at[half, index, pl.ds(low, 2)],
            )

    for copy in prior:
        copy.wait_recv()
    bias = jnp.where(me > 0, 0.0, NEG)
    for h in range(heads):
        cols = slice(h * HDIM, (h + 1) * HDIM)
        local(0, h, before[0, :, cols], before[1, :, cols], bias, False)

    for half in (0, 1):
        for index, low in ((2, 2), (3, 0), (4, 0), (5, 2)):
            side = index % 2
            arrive(
                half, index,
                got.at[half, side, pl.ds(low, 2)], got_st.at[half, side, pl.ds(low, 2)],
            )
        for step in (2, 1, -1, 0):
            to = wrap(second_at(half) + step)
            at = (to, xpos, 0) if half == 0 else (zpos, to, 1)
            merge(
                mid.at[half, to], mid_st.at[half, to],
                [(o_ref.at[at], st_ref.at[at])]
                + [(got.at[half, i, to], got_st.at[half, i, to]) for i in (0, 1)],
                (0, heads),
            )
            for side in (0, 1):
                rows = pl.ds(*parts[side])
                if step == 2:
                    start(
                        half, 6 + side, mid.at[half, to, rows], mid_st.at[half, to],
                        relay2.at[half, rows], relay2_st.at[half, side],
                    )
            if step in (1, -1):
                side = 0 if step == 1 else 1
                other = pl.ds(*parts[1 - side])
                start(
                    half, 8 + side, mid.at[half, to, other], mid_st.at[half, to],
                    got2.at[half, side, other], got2_st.at[half, side, 1 - side],
                )

    for half in (0, 1):
        for side, way in ((0, 1), (1, -1)):
            rows = pl.ds(*parts[side])
            arrive(half, 6 + side, relay2.at[half, rows], relay2_st.at[half, side])
            to = wrap(second_at(half) + way)
            merge(
                relay2.at[half], relay2_st.at[half, side],
                [
                    (relay2.at[half], relay2_st.at[half, side]),
                    (mid.at[half, to], mid_st.at[half, to]),
                ],
                (parts[side][0] // HDIM, sum(parts[side]) // HDIM),
            )
            start(
                half, 10 + side, relay2.at[half, rows], relay2_st.at[half, side],
                got2.at[half, side, rows], got2_st.at[half, side, side],
            )

    for half in (0, 1):
        for side in (0, 1):
            for index, which in ((8 + side, 1 - side), (10 + side, side)):
                arrive(
                    half, index,
                    got2.at[half, side, pl.ds(*parts[which])], got2_st.at[half, side, which],
                )
        at = second_at(half)
        for h in range(heads):
            cols = slice(h * HDIM, (h + 1) * HDIM)
            which = 0 if h * HDIM < cut else 1
            sources = [(mid.at[half, at], mid_st.at[half, at])]
            sources += [(got2.at[half, i], got2_st.at[half, i, which]) for i in (0, 1)]
            old = acc_st[half, h : h + 1, :]
            ms = [st[h : h + 1, :] for _, st in sources]
            m = functools.reduce(jnp.maximum, ms, old)
            decay = jnp.exp2(old - m)
            total = acc_st[half, 8 + h : 9 + h, :] * decay
            a = acc[half, cols, :] * decay
            for (part, st), x in zip(sources, ms):
                w = st[8 + h : 9 + h, :] * jnp.exp2(x - m)
                total = total + w
                a = a + part[cols, :].astype(jnp.float32) * w
            out_ref[half * span : (half + 1) * span, cols] = jnp.transpose(a / total).astype(
                out_ref.dtype
            )

    for copy in started + prior:
        copy.wait_send()


def combine(o, st, q, k, v, heads):
    span_count, width, span = o.shape[1:]
    rows = st.shape[2]
    o = o.reshape(RING, RING, span_count, width, span)
    st = st.reshape(RING, RING, span_count, rows, span)
    vmem = pl.BlockSpec(memory_space=pltpu.VMEM)

    def pair(*lead):
        return [
            pltpu.VMEM(lead + (width, span), jnp.bfloat16),
            pltpu.VMEM(lead + (rows, span), jnp.float32),
        ]

    return pl.pallas_call(
        functools.partial(combine_kernel, heads),
        in_specs=[vmem] * 5,
        out_specs=vmem,
        out_shape=jax.ShapeDtypeStruct(k.shape, jnp.bfloat16),
        scratch_shapes=[pltpu.VMEM((2, span, width), jnp.bfloat16)]
        + pair(2, 2, 2)
        + pair(2, 2, RING)
        + pair(2, RING)
        + [pltpu.VMEM((2, width, span), jnp.bfloat16), pltpu.VMEM((2, 2, rows, span), jnp.float32)]
        + [
            pltpu.VMEM((2, 2, width, span), jnp.bfloat16),
            pltpu.VMEM((2, 2, 2, rows, span), jnp.float32),
        ]
        + [pltpu.VMEM((2, width, span), jnp.float32), pltpu.VMEM((2, rows, span), jnp.float32)]
        + [pltpu.SemaphoreType.DMA((24,))] * 4
        + [pltpu.SemaphoreType.DMA((2,))] * 2,
        compiler_params=pltpu.CompilerParams(
            collective_id=1, has_side_effects=True, vmem_limit_bytes=60 << 20
        ),
        name="combine",
    )(o, st, q, k, v)


def chosen_slots(selected, counts, block_slot, stored, width):
    span_count, select_count = selected.shape
    live = jnp.arange(select_count)[None, :] < counts[:, None]
    hit = selected[:, :, None] == jnp.arange(block_slot.shape[0])[None, None, :]
    slot = jnp.sum(jnp.where(hit, block_slot[None, None, :], 0), axis=2)
    owner = jnp.where(live, slot // stored, -1)
    both = jnp.concatenate([owner, slot % stored], 0).astype(jnp.bfloat16)
    return jnp.pad(both, ((0, EXTRA - 2 * span_count), (0, width - select_count)))


def shards(
    tokens,
    query_weight,
    key_weight,
    value_weight,
    cache_keys,
    cache_values,
    selected,
    counts,
    block_slot,
):
    token_count = tokens.shape[0]
    width = query_weight.shape[1]
    heads = width // HDIM
    span_count, select_count = selected.shape
    devices = lax.axis_size("context")
    cap = max(2, 2 * span_count * select_count // devices)

    extra = chosen_slots(selected, counts, block_slot, cache_keys.shape[0], width)
    q_all, q, k, v, table = gather_project(
        tokens, query_weight, key_weight, value_weight, extra, span_count, select_count, cap
    )
    o, st = owner_attention(table, q_all, cache_keys, cache_values, heads, cap)
    return combine(o, st, q, k, v, heads)


def solution(mesh):
    placed = (
        P("context", "tensor"),
        P("context", "tensor"),
        P("context", "tensor"),
        P("context", "tensor"),
        P("context", None, "tensor"),
        P("context", None, "tensor"),
        P("context", None),
        P("context"),
        P(),
    )
    return jax.shard_map(
        shards, mesh=mesh, in_specs=placed, out_specs=P("context", "tensor"), check_vma=False
    )
```

```python
import functools

import jax
import jax.numpy as jnp
from jax import lax
from jax.experimental import pallas as pl
from jax.experimental.pallas import tpu as pltpu
from jax.sharding import PartitionSpec as P

HDIM = 128
NEG = -1e30
MESH = pl.DeviceIdType.MESH
EXTRA = 16
SCALE = HDIM ** (-0.5) * 1.4426950408889634


def dot_nt(a, b):
    return lax.dot_general(a, b, (((1,), (1,)), ((), ())), preferred_element_type=jnp.float32)


def dot_tn(a, b):
    return lax.dot_general(a, b, (((0,), (0,)), ((), ())), preferred_element_type=jnp.float32)


RING = 4
OFFSETS = (0, -1, 1, 2)


def wrap(position):
    return lax.rem(position + RING, RING)


def context_of(zpos, xpos):
    return wrap(zpos) * RING + wrap(xpos)


class Ring:
    def __init__(self, view, to, sems, sent, own=None):
        self.view, self.to, self.sems, self.sent, self.own = view, to, sems, sent, own
        self.waited = set()

    def copy(self, index, step):
        ref = self.view(step, max(0, index - 1))
        src = self.own if step == 0 and self.own is not None else ref
        return remote(src, ref, self.sems, index, self.to(1 if index % 2 == 0 else -1))

    def start(self, index):
        copy = self.copy(index, (0, 0, -1, 1)[index])
        copy.start()
        self.sent.append(copy)

    def arrive(self, index):
        if index not in self.waited:
            self.waited.add(index)
            self.copy(index, (-1, 1, 2, 2)[index]).wait_recv()

    def whole(self):
        self.start(0)
        self.start(1)

    def onward(self):
        self.arrive(0)
        self.start(2)
        self.arrive(1)
        self.start(3)

    def opposite(self):
        self.arrive(2)
        self.arrive(3)


def remote(src, dst, sems, index, to):
    send, recv, base = sems
    return pltpu.make_async_remote_copy(
        src_ref=src,
        dst_ref=dst,
        send_sem=send.at[base + index],
        recv_sem=recv.at[base + index],
        device_id=to,
        device_id_type=MESH,
    )


def context_gather(view, own, sems, zpos, xpos, sent):
    rings = {}

    def make(half, phase):
        along_x = (half == 0) == (phase == 0)
        first = 0 if phase == 0 else OFFSETS[phase - 1]

        def piece(step, part):
            dz, dx = (first, step) if along_x else (step, first)
            return view(wrap(zpos + dz), wrap(xpos + dx), half, part)

        def to(way):
            dz, dx = (0, way) if along_x else (way, 0)
            return {"context": context_of(zpos + dz, xpos + dx)}

        send, recv, base = sems
        source = own(half) if first == 0 else None
        return Ring(piece, to, (send, recv, base + half * 20 + phase * 4), sent, source)

    for half in (0, 1):
        for phase in range(5):
            rings[half, phase] = make(half, phase)

    def own():
        for half in (0, 1):
            rings[half, 0].whole()
            rings[half, 1].whole()

    def neighbours():
        for half in (0, 1):
            rings[half, 0].onward()
            rings[half, 2].whole()
            rings[half, 3].whole()
        for half in (0, 1):
            rings[half, 1].onward()

    def far():
        for half in (0, 1):
            rings[half, 0].opposite()
            rings[half, 4].whole()

    def corners():
        for half in (0, 1):
            rings[half, 2].onward()
            rings[half, 3].onward()

    def last():
        for half in (0, 1):
            rings[half, 4].onward()

    def rest():
        for half in (0, 1):
            for phase in (1, 2, 3, 4):
                rings[half, phase].opposite()

    return [own, neighbours, far, corners, last, rest]


def project_kernel(
    span_count, select_count, cap, stored,
    tok_ref, wq_ref, wk_ref, wv_ref, sel_ref, count_ref, slot_ref,
    q_ref, k_ref, v_ref, tab_ref,
    tok, stage, w, acc, done, back, fifth, small, told,
    load_sem, tsend, trecv, wsend, wrecv, bsend, brecv, qsend, qrecv,
):
    me = lax.axis_index("context")
    zpos, xpos = me // RING, lax.rem(me, RING)
    col = lax.axis_index("tensor")
    ypos, core = col // 2, lax.rem(col, 2)
    token_count, depth = tok.shape[2], tok.shape[3]
    rows = w.shape[3]
    sent = []

    token_load = pltpu.make_async_copy(tok_ref, tok.at[col, zpos], load_sem.at[0])
    token_load.start()
    loads = ([], [])
    for part in (0, 1):
        for to in range(RING):
            left = (wq_ref, wk_ref, wv_ref, wq_ref)[to]
            pair = ((wq_ref, to), (left, RING)) if part == 0 else ((wk_ref, to), (wv_ref, to))
            for i, (ref, head) in enumerate(pair):
                load = pltpu.make_async_copy(
                    ref.at[:, pl.ds(head * HDIM, HDIM)],
                    stage.at[part, to, :, pl.ds(i * HDIM, HDIM)],
                    load_sem.at[2 + part * 8 + to * 2 + i],
                )
                load.start()
                loads[part].append(load)

    def at_x(way):
        return {"context": context_of(zpos, xpos + way)}

    def at_z(way):
        return {"context": context_of(zpos + way, xpos)}

    def at_y(way):
        return {"tensor": wrap(ypos + way) * 2 + core}

    mate = {"tensor": ypos * 2 + 1 - core}
    barrier = pltpu.get_barrier_semaphore()
    partners = [at_x(1), at_x(-1), at_z(1), at_z(-1), at_z(2), at_y(1), at_y(-1), mate]
    for other in partners:
        pl.semaphore_signal(barrier, inc=1, device_id=other, device_id_type=MESH)
    pl.semaphore_wait(barrier, len(partners))

    def cut(size):
        return (pl.ds(0, size), pl.ds(0, size // 2), pl.ds(size // 2, size // 2))

    ztok = Ring(
        lambda step, part: tok.at[col, wrap(zpos + step), cut(token_count)[part]],
        at_z, (tsend, trecv, 0), sent,
    )
    ytok = {
        o: Ring(
            lambda step, part, o=o: tok.at[
                wrap(ypos + step) * 2 + core, wrap(zpos + o), cut(token_count)[part]
            ],
            at_y, (tsend, trecv, 4 + 4 * i), sent,
        )
        for i, o in enumerate(OFFSETS)
    }

    def share(step, o, receive=False):
        side = 1 - core if receive else core
        ref = tok.at[wrap(ypos + step) * 2 + side, wrap(zpos + o)]
        index = 20 + OFFSETS.index(step) * 4 + OFFSETS.index(o)
        copy = remote(ref, ref, (tsend, trecv, 0), index, mate)
        if receive:
            copy.wait_recv()
        else:
            copy.start()
            sent.append(copy)

    def exchange(part, step, receive=False):
        index = part * 3 + OFFSETS.index(step) - 1
        src = stage.at[part, wrap(zpos + step)]
        if receive:
            dst = w.at[part, wrap(zpos - step), xpos]
            remote(src, dst, (wsend, wrecv, 0), index, at_z(step)).wait_recv()
        else:
            copy = remote(src, w.at[part, zpos, xpos], (wsend, wrecv, 0), index, at_z(step))
            copy.start()
            sent.append(copy)

    xw = {
        (part, o): Ring(
            lambda step, piece, part=part, o=o: w.at[
                part, wrap(zpos + o), wrap(xpos + step), cut(rows)[piece]
            ],
            at_x, (wsend, wrecv, 6 + part * 16 + 4 * i), sent,
        )
        for part in (0, 1)
        for i, o in enumerate(OFFSETS)
    }

    def keep(part):
        for load in loads[part]:
            load.wait()
        copy = pltpu.make_async_copy(
            stage.at[part, zpos], w.at[part, zpos, xpos], load_sem.at[18 + part]
        )
        copy.start()
        copy.wait()

    token_load.wait()
    ztok.whole()
    ytok[0].whole()
    share(0, 0)
    keep(0)
    xw[0, 0].whole()
    exchange(0, 1)
    exchange(0, -1)
    keep(1)
    xw[1, 0].whole()
    xw[0, 0].onward()
    ztok.onward()
    for o in (-1, 1):
        ytok[o].whole()
        share(0, o)
    ytok[0].onward()
    exchange(0, 2)
    exchange(1, 1)
    exchange(1, -1)
    exchange(1, 2)
    share(-1, 0)
    share(1, 0)
    for step in (1, -1):
        exchange(0, step, receive=True)
        xw[0, -step].whole()
    xw[1, 0].onward()
    ztok.opposite()
    ytok[2].whole()
    share(0, 2)
    exchange(0, 2, receive=True)
    xw[0, 2].whole()
    for o in (-1, 1):
        ytok[o].onward()
        share(-1, o)
        share(1, o)
    xw[0, -1].onward()
    xw[0, 1].onward()
    for step in (1, -1):
        exchange(1, step, receive=True)
        xw[1, -step].whole()
    ytok[0].opposite()
    share(2, 0)
    xw[0, 2].onward()
    exchange(1, 2, receive=True)
    xw[1, 2].whole()
    ytok[2].onward()
    share(-1, 2)
    share(1, 2)
    for o in (-1, 1, 2):
        xw[1, o].onward()
    for o in (-1, 1):
        ytok[o].opposite()
        share(2, o)

    def compute(part, step):
        for side in (0, 1):
            t = wrap(ypos + step) * 2 + side
            piece = w[part, wrap(ypos + step), 2 * side : 2 * side + 2].reshape(depth, w.shape[4])

            @pl.loop(0, RING)
            def _(z):
                new = jnp.dot(tok[t, z], piece, preferred_element_type=jnp.float32)
                if step == 0 and side == 0:
                    acc[z] = new
                else:
                    acc[z] += new

    def give_back(part, buf, columns, base):
        buf[zpos] = acc[zpos, :, columns].astype(jnp.bfloat16)
        for i, step in enumerate(OFFSETS[1:]):
            copy = remote(
                done.at[part, wrap(zpos + step), :, columns], buf.at[zpos],
                (bsend, brecv, base), i, at_z(step),
            )
            copy.start()
            sent.append(copy)

    def take_back(buf, base):
        for i, step in enumerate(OFFSETS[1:]):
            ref = buf.at[wrap(zpos - step)]
            remote(ref, ref, (bsend, brecv, base), i, at_z(step)).wait_recv()

    def finish(part):
        @pl.loop(0, RING)
        def _(z):
            done[part, z] = acc[z].astype(jnp.bfloat16)

    lane = lax.broadcasted_iota(jnp.int32, (EXTRA, HDIM), 1)
    line = lax.broadcasted_iota(jnp.int32, (EXTRA, HDIM), 0)
    chosen = jnp.zeros((EXTRA, HDIM), jnp.int32)
    for half in range(span_count):

        def note(j, chosen, half=half):
            slot = slot_ref[jnp.maximum(sel_ref[half, j], 0)]
            owner = jnp.where(j < count_ref[half], slot // stored, -1)
            value = jnp.where(line == half, owner, slot % stored)
            here = (lane == j) & ((line == half) | (line == span_count + half))
            return jnp.where(here, value, chosen)

        chosen = lax.fori_loop(0, select_count, note, chosen)
    small[token_count:, :] = chosen.astype(jnp.float32).astype(jnp.bfloat16)

    for o in OFFSETS:
        xw[0, o].opposite()
    for step in OFFSETS[:3]:
        for o in OFFSETS:
            share(step, o, receive=True)
        compute(0, step)
    ytok[2].opposite()
    share(2, 2)
    for o in OFFSETS:
        share(2, o, receive=True)
    compute(0, 2)
    finish(0)

    groups = RING // 2

    def head_view(z, x, half, part):
        low, size = ((0, groups), (0, groups // 2), (groups // 2, groups // 2))[part]
        head = pl.ds(pl.multiple_of(z * HDIM, HDIM), HDIM)
        return q_ref.at[pl.ds(half * groups + low, size), x, pl.ds(0, token_count), head]

    def head_own(half):
        return done.at[0, pl.ds(half * groups, groups), :, pl.ds(0, HDIM)]

    heads = context_gather(head_view, head_own, (qsend, qrecv, 0), zpos, xpos, sent)

    half_rows = token_count // 2
    quarter = half_rows // 2
    ranges = (
        ((0, half_rows), (0, quarter), (quarter, quarter)),
        (
            (half_rows, half_rows + EXTRA),
            (half_rows, quarter),
            (half_rows + quarter, quarter + EXTRA),
        ),
    )

    def last_view(z, x, half, part):
        return q_ref.at[z, x, pl.ds(*ranges[half][part]), pl.ds(RING * HDIM, HDIM)]

    def last_own(half):
        return small.at[pl.ds(*ranges[half][0]), :]

    last = context_gather(last_view, last_own, (qsend, qrecv, 40), zpos, xpos, sent)

    heads[0]()
    give_back(0, fifth, slice(HDIM, 2 * HDIM), 0)
    keeps = [
        pltpu.make_async_copy(
            done.at[0, :, :, pl.ds(0, HDIM)],
            q_ref.at[
                :, xpos, pl.ds(0, token_count), pl.ds(pl.multiple_of(zpos * HDIM, HDIM), HDIM)
            ],
            load_sem.at[1],
        )
    ]
    keeps[0].start()
    for o in OFFSETS:
        xw[1, o].opposite()
    compute(1, 0)
    take_back(fifth, 0)
    small[0:token_count, :] = fifth[0]
    last[0]()
    keeps.append(
        pltpu.make_async_copy(
            small, q_ref.at[zpos, xpos, :, pl.ds(RING * HDIM, HDIM)], load_sem.at[20]
        )
    )
    keeps[1].start()
    heads[1]()
    compute(1, -1)
    heads[2]()
    last[1]()
    compute(1, 1)
    heads[3]()
    last[2]()
    compute(1, 2)
    finish(1)
    give_back(1, back, slice(0, 2 * HDIM), 3)
    heads[4]()
    last[3]()
    last[4]()
    for keep_copy in keeps:
        keep_copy.wait()
    heads[5]()
    last[5]()
    look = pltpu.make_async_copy(
        q_ref.at[:, :, pl.ds(token_count, EXTRA), pl.ds(RING * HDIM, HDIM)],
        told,
        load_sem.at[21],
    )
    look.start()
    take_back(back, 3)
    for head in range(RING):
        cols = slice(head * HDIM, (head + 1) * HDIM)
        k_ref[:, cols] = back[head, :, 0:HDIM]
        v_ref[:, cols] = back[head, :, HDIM : 2 * HDIM]
    k_ref[:, RING * HDIM :] = fifth[1]
    v_ref[:, RING * HDIM :] = fifth[2]
    look.wait()

    devices = RING * RING
    lane = lax.broadcasted_iota(jnp.int32, (devices, HDIM), 1)
    before = lax.broadcasted_iota(jnp.int32, (HDIM, HDIM), 0)
    after = lax.broadcasted_iota(jnp.int32, (HDIM, HDIM), 1)
    earlier = jnp.where(before < after, 1.0, 0.0).astype(jnp.bfloat16)
    listed = told[...].reshape(devices, EXTRA, HDIM).astype(jnp.float32)
    for half in range(span_count):
        owner = listed[:, half, :]
        row = listed[:, span_count + half, :]
        mine = jnp.where((owner == me.astype(jnp.float32)) & (lane < select_count), 1.0, 0.0)
        rank = jnp.dot(mine.astype(jnp.bfloat16), earlier, preferred_element_type=jnp.float32)
        table = jnp.where(lane == cap, jnp.sum(mine, axis=1, keepdims=True), 0.0)
        for r in range(cap):
            value = jnp.sum(jnp.where(rank == r, mine * row, 0.0), axis=1, keepdims=True)
            table = jnp.where(lane == r, value, table)
        tab_ref[half] = table.astype(jnp.int32)

    for copy in sent:
        copy.wait_send()


def gather_project(tokens, wq, wk, wv, selected, counts, block_slot, cap, stored):
    token_count, depth = tokens.shape
    rows, width = wq.shape
    span_count, select_count = selected.shape
    devices = lax.axis_size("context")
    columns = lax.axis_size("tensor")
    hbm = pl.BlockSpec(memory_space=pl.ANY)
    vmem = pl.BlockSpec(memory_space=pltpu.VMEM)
    smem = pl.BlockSpec(memory_space=pltpu.SMEM)
    own = jax.ShapeDtypeStruct((token_count, width), jnp.bfloat16)
    two = 2 * HDIM

    def dma(count):
        return [pltpu.SemaphoreType.DMA((count,))] * 2

    return pl.pallas_call(
        functools.partial(project_kernel, span_count, select_count, cap, stored),
        in_specs=[hbm] * 4 + [smem] * 3,
        out_specs=[hbm] + [vmem] * 3,
        out_shape=[
            jax.ShapeDtypeStruct((RING, RING, token_count + EXTRA, width), jnp.bfloat16),
            own,
            own,
            jax.ShapeDtypeStruct((span_count, devices, HDIM), jnp.int32),
        ],
        scratch_shapes=[
            pltpu.VMEM((columns, RING, token_count, depth), jnp.bfloat16),
            pltpu.VMEM((2, RING, rows, two), jnp.bfloat16),
            pltpu.VMEM((2, RING, RING, rows, two), jnp.bfloat16),
            pltpu.VMEM((RING, token_count, two), jnp.float32),
            pltpu.VMEM((2, RING, token_count, two), jnp.bfloat16),
            pltpu.VMEM((RING, token_count, two), jnp.bfloat16),
            pltpu.VMEM((RING, token_count, HDIM), jnp.bfloat16),
            pltpu.VMEM((token_count + EXTRA, HDIM), jnp.bfloat16),
            pltpu.VMEM((RING, RING, EXTRA, HDIM), jnp.bfloat16),
            pltpu.SemaphoreType.DMA((22,)),
        ]
        + dma(36)
        + dma(38)
        + dma(6)
        + dma(80),
        compiler_params=pltpu.CompilerParams(
            collective_id=0, has_side_effects=True, vmem_limit_bytes=40 << 20
        ),
        name="gather_project",
    )(tokens, wq, wk, wv, selected, counts, block_slot)


def owner_kernel(heads, cap, tab_ref, q_ref, k_ref, v_ref, o_ref, st_ref, acc_ref):
    src = pl.program_id(0)
    span_count = o_ref.shape[1]
    span = o_ref.shape[3]
    block = k_ref.shape[1]
    columns = [slice(h * HDIM, (h + 1) * HDIM) for h in range(heads)]

    def scores(half, j):
        n = tab_ref[half, src, cap]
        r0 = tab_ref[half, src, 2 * j]
        r1 = tab_ref[half, src, 2 * j + 1]
        bias1 = jnp.where(2 * j + 1 < n, 0.0, NEG)
        out = []
        for cols in columns:
            q = q_ref[0, half * span : (half + 1) * span, cols]
            k = jnp.concatenate([k_ref[r0, :, cols], k_ref[r1, :, cols]], 0)
            v = jnp.concatenate([v_ref[r0, :, cols], v_ref[r1, :, cols]], 0)
            s = dot_nt(k, q) * SCALE
            out.append((jnp.concatenate([s[:block], s[block:] + bias1], 0), v))
        return out

    for half in range(span_count):
        results = []
        for s, v in scores(half, 0):
            m = jnp.max(s, axis=0, keepdims=True)
            p = jnp.exp2(s - m)
            l = jnp.sum(p, axis=0, keepdims=True)
            results.append((m, l, dot_tn(v, p.astype(jnp.bfloat16))))
        some = tab_ref[half, src, cap] > 0
        for h, (m, l, a) in enumerate(results):
            st_ref[0, half, h : h + 1, :] = jnp.where(some, m, NEG)
            st_ref[0, half, 8 + h : 9 + h, :] = l
            acc_ref[half, columns[h], :] = a
            o_ref[0, half, columns[h], :] = a.astype(jnp.bfloat16)

    for half in range(span_count):
        n = tab_ref[half, src, cap]

        @pl.when(n > 2)
        def _():
            @pl.loop(1, (n + 1) // 2)
            def _(j):
                results = []
                for h, (s, v) in enumerate(scores(half, j)):
                    old = st_ref[0, half, h : h + 1, :]
                    m = jnp.maximum(jnp.max(s, axis=0, keepdims=True), old)
                    decay = jnp.exp2(old - m)
                    p = jnp.exp2(s - m)
                    l = jnp.sum(p, axis=0, keepdims=True)
                    l = l + st_ref[0, half, 8 + h : 9 + h, :] * decay
                    a = dot_tn(v, p.astype(jnp.bfloat16)) + acc_ref[half, columns[h], :] * decay
                    results.append((m, l, a))
                for h, (m, l, a) in enumerate(results):
                    st_ref[0, half, h : h + 1, :] = m
                    st_ref[0, half, 8 + h : 9 + h, :] = l
                    acc_ref[half, columns[h], :] = a

            for h in range(heads):
                o_ref[0, half, columns[h], :] = acc_ref[half, columns[h], :].astype(jnp.bfloat16)


def owner_attention(table, q_all, cache_keys, cache_values, heads, cap):
    tokens, width = q_all.shape[2] - EXTRA, q_all.shape[3]
    span_count, devices = table.shape[:2]
    span = tokens // span_count
    q_all = q_all.reshape(devices, tokens + EXTRA, width)
    whole = pl.BlockSpec(cache_keys.shape, lambda s, *_: (0, 0, 0), pipeline_mode=pl.Buffered(1))
    return pl.pallas_call(
        functools.partial(owner_kernel, heads, cap),
        grid_spec=pltpu.PrefetchScalarGridSpec(
            num_scalar_prefetch=1,
            grid=(devices,),
            in_specs=[
                pl.BlockSpec((1, tokens, width), lambda s, *_: (s, 0, 0)),
                whole,
                whole,
            ],
            out_specs=[
                pl.BlockSpec((1, span_count, width, span), lambda s, *_: (s, 0, 0, 0)),
                pl.BlockSpec((1, span_count, 16, span), lambda s, *_: (s, 0, 0, 0)),
            ],
            scratch_shapes=[pltpu.VMEM((span_count, width, span), jnp.float32)],
        ),
        out_shape=[
            jax.ShapeDtypeStruct((devices, span_count, width, span), jnp.bfloat16),
            jax.ShapeDtypeStruct((devices, span_count, 16, span), jnp.float32),
        ],
    )(table, q_all, cache_keys, cache_values)


def combine_kernel(
    heads,
    o_ref, st_ref, q_ref, k_ref, v_ref,
    out_ref,
    own, query, before, relay, relay_st, got, got_st, mid, mid_st,
    relay2, relay2_st, got2, got2_st, acc, acc_st,
    load_sem, send, recv, send_st, recv_st, psend, precv,
):
    me = lax.axis_index("context")
    zpos, xpos = me // RING, lax.rem(me, RING)
    devices = RING * RING
    behind, ahead = lax.rem(me + devices - 1, devices), lax.rem(me + 1, devices)
    span = o_ref.shape[-1]
    token_count = k_ref.shape[0]
    cut = (heads + 1) // 2 * HDIM
    parts = ((0, cut), (cut, heads * HDIM - cut))
    order = (2, -1, 1, 0)

    def first_at(half, step):
        return wrap((xpos if half == 0 else zpos) + step)

    def second_at(half, step):
        return wrap((zpos if half == 0 else xpos) + step)

    def place(half, step, further):
        a, b = first_at(half, step), second_at(half, further)
        return (b, a, half) if half == 0 else (a, b, half)

    loads = {}
    count = 0
    for kind in (0, 1):
        for further in order:
            step = (1 if further in (2, 1) else -1) if kind == 0 else 0
            for half in (0, 1):
                slot = (half, kind, order.index(further))
                loads[slot] = pltpu.make_async_copy(
                    o_ref.at[place(half, step, further)], own.at[slot], load_sem.at[count]
                )
                loads[slot].start()
                count += 1
    query_load = pltpu.make_async_copy(
        q_ref.at[zpos, xpos, pl.ds(0, token_count)], query, load_sem.at[count]
    )
    query_load.start()

    barrier = pltpu.get_barrier_semaphore()
    for other in (
        context_of(zpos + 1, xpos),
        context_of(zpos - 1, xpos),
        context_of(zpos, xpos + 1),
        context_of(zpos, xpos - 1),
        behind,
        ahead,
    ):
        pl.semaphore_signal(barrier, inc=1, device_id={"context": other}, device_id_type=MESH)
    pl.semaphore_wait(barrier, 6)

    started = []

    def copies(half, index, way, first, src, src_st, dst, dst_st):
        if (half == 0) == first:
            to = {"context": context_of(zpos, xpos + way)}
        else:
            to = {"context": context_of(zpos + way, xpos)}
        base = half * 18
        return (
            remote(src, dst, (send, recv, base), index, to),
            remote(src_st, dst_st, (send_st, recv_st, base), index, to),
        )

    def start(*args):
        for copy in copies(*args):
            copy.start()
            started.append(copy)

    def arrive(half, index, dst, dst_st):
        for copy in copies(half, index, 1, True, dst, dst_st, dst, dst_st):
            copy.wait_recv()

    def merge(out, out_st, sources, head_range):
        results = []
        for h in head_range:
            rows = slice(h * HDIM, (h + 1) * HDIM)
            ms = [st[h : h + 1, :] for _, st in sources]
            m = functools.reduce(jnp.maximum, ms)
            ws = [jnp.exp2(x - m) for x in ms]
            ls = [st[8 + h : 9 + h, :] * w for (_, st), w in zip(sources, ws)]
            terms = [part[rows, :].astype(jnp.float32) * w for (part, _), w in zip(sources, ws)]
            total = functools.reduce(jnp.add, terms).astype(jnp.bfloat16)
            results.append((h, rows, m, functools.reduce(jnp.add, ls), total))
        for h, rows, m, l, total in results:
            out[rows, :] = total
            out_st[h : h + 1, :] = m
            out_st[8 + h : 9 + h, :] = l

    every = range(heads)

    def way_of(further):
        return 1 if further in (2, 1) else -1

    def forward(half, further):
        i, at = order.index(further), place(half, 2, further)
        start(
            half, i, way_of(further), True, o_ref.at[at], st_ref.at[at],
            relay.at[half, i], relay_st.at[half, i],
        )

    def direct(half, further):
        way = -way_of(further)
        i, at, side = order.index(further), place(half, way, further), 0 if way == 1 else 1
        start(
            half, 4 + i, way, True, o_ref.at[at], st_ref.at[at],
            got.at[half, side, i], got_st.at[half, side, i],
        )

    def merged(half, further):
        way = way_of(further)
        i, at, side = order.index(further), place(half, way, further), 0 if way == 1 else 1
        part, st = relay.at[half, i], relay_st.at[half, i]
        arrive(half, i, part, st)
        loads[half, 0, i].wait()
        merge(part, st, [(part, st), (own.at[half, 0, i], st_ref.at[at])], every)
        start(
            half, 8 + i, way, True, part, st, got.at[half, side, i], got_st.at[half, side, i]
        )

    def collect(half, further):
        i = order.index(further)
        side = 0 if way_of(further) == 1 else 1
        arrive(half, 4 + i, got.at[half, 1 - side, i], got_st.at[half, 1 - side, i])
        arrive(half, 8 + i, got.at[half, side, i], got_st.at[half, side, i])
        loads[half, 1, i].wait()
        merge(
            mid.at[half, i], mid_st.at[half, i],
            [(own.at[half, 1, i], st_ref.at[place(half, 0, further)])]
            + [(got.at[half, n, i], got_st.at[half, n, i]) for n in (0, 1)],
            every,
        )

    halves = (0, 1)
    for further in order:
        for half in halves:
            forward(half, further)
    for further in (2, -1):
        for half in halves:
            direct(half, further)

    key = lax.broadcasted_iota(jnp.int32, (span, span), 0)
    row = lax.broadcasted_iota(jnp.int32, (span, span), 1)

    def local(half, keys_of, values_of, bias, first):
        results = []
        for h in every:
            cols = slice(h * HDIM, (h + 1) * HDIM)
            s = dot_nt(keys_of(cols), query[half * span : (half + 1) * span, cols]) * SCALE
            s = jnp.where(key <= row, s, NEG) if bias is None else s + bias
            m = jnp.max(s, axis=0, keepdims=True)
            if not first:
                old = acc_st[half, h : h + 1, :]
                m = jnp.maximum(m, old)
                decay = jnp.exp2(old - m)
            p = jnp.exp2(s - m)
            l = jnp.sum(p, axis=0, keepdims=True)
            a = dot_tn(values_of(cols), p.astype(jnp.bfloat16))
            if not first:
                l = l + acc_st[half, 8 + h : 9 + h, :] * decay
                a = a + acc[half, cols, :] * decay
            results.append((h, cols, m, l, a))
        for h, cols, m, l, a in results:
            acc_st[half, h : h + 1, :] = m
            acc_st[half, 8 + h : 9 + h, :] = l
            acc[half, cols, :] = a

    query_load.wait()
    for half in halves:
        rows = slice(half * span, (half + 1) * span)
        local(half, lambda c, r=rows: k_ref[r, c], lambda c, r=rows: v_ref[r, c], None, True)

    for further in (2, -1):
        for half in halves:
            merged(half, further)
    for further in (1, 0):
        for half in halves:
            direct(half, further)
    prior = []
    for i, ref in enumerate((k_ref, v_ref)):
        prior.append(
            remote(
                ref.at[pl.ds(token_count - span, span), :], before.at[i], (psend, precv, 0), i,
                {"context": ahead},
            )
        )
        prior[-1].start()
    for further in (1, 0):
        for half in halves:
            merged(half, further)
    local(1, lambda c: k_ref[0:span, c], lambda c: v_ref[0:span, c], 0.0, False)

    for half in halves:
        collect(half, 2)
        for side, way in ((0, 1), (1, -1)):
            rows = pl.ds(*parts[side])
            start(
                half, 12 + side, way, False, mid.at[half, 0, rows], mid_st.at[half, 0],
                relay2.at[half, rows], relay2_st.at[half, side],
            )
    for side, way in ((1, -1), (0, 1)):
        for half in halves:
            i = order.index(way)
            collect(half, way)
            other = pl.ds(*parts[1 - side])
            start(
                half, 14 + side, way, False, mid.at[half, i, other], mid_st.at[half, i],
                got2.at[half, side, other], got2_st.at[half, side, 1 - side],
            )
    for half in halves:
        for side, way in ((0, 1), (1, -1)):
            i = order.index(way)
            rows = pl.ds(*parts[side])
            part, st = relay2.at[half], relay2_st.at[half, side]
            arrive(half, 12 + side, relay2.at[half, rows], st)
            merge(
                part, st, [(part, st), (mid.at[half, i], mid_st.at[half, i])],
                range(parts[side][0] // HDIM, sum(parts[side]) // HDIM),
            )
            start(
                half, 16 + side, way, False, relay2.at[half, rows], st,
                got2.at[half, side, rows], got2_st.at[half, side, side],
            )

    for copy in prior:
        copy.wait_recv()
    local(
        0, lambda c: before[0, :, c], lambda c: before[1, :, c], jnp.where(me > 0, 0.0, NEG), False
    )
    last = order.index(0)
    for half in halves:
        collect(half, 0)
    for half in halves:
        for side in (0, 1):
            for index, which in ((14 + side, 1 - side), (16 + side, side)):
                arrive(
                    half, index,
                    got2.at[half, side, pl.ds(*parts[which])], got2_st.at[half, side, which],
                )
        for h in every:
            cols = slice(h * HDIM, (h + 1) * HDIM)
            which = 0 if h * HDIM < cut else 1
            sources = [(mid.at[half, last], mid_st.at[half, last])]
            sources += [(got2.at[half, i], got2_st.at[half, i, which]) for i in (0, 1)]
            old = acc_st[half, h : h + 1, :]
            ms = [st[h : h + 1, :] for _, st in sources]
            m = functools.reduce(jnp.maximum, ms, old)
            decay = jnp.exp2(old - m)
            total = acc_st[half, 8 + h : 9 + h, :] * decay
            a = acc[half, cols, :] * decay
            for (part, st), x in zip(sources, ms):
                w = jnp.exp2(x - m)
                total = total + st[8 + h : 9 + h, :] * w
                a = a + part[cols, :].astype(jnp.float32) * w
            out_ref[half * span : (half + 1) * span, cols] = jnp.transpose(a / total).astype(
                out_ref.dtype
            )

    for copy in started + prior:
        copy.wait_send()


def combine(o, st, q_all, k, v, heads):
    span_count, width, span = o.shape[1:]
    rows = st.shape[2]
    o = o.reshape(RING, RING, span_count, width, span)
    st = st.reshape(RING, RING, span_count, rows, span)
    vmem = pl.BlockSpec(memory_space=pltpu.VMEM)
    hbm = pl.BlockSpec(memory_space=pl.ANY)

    def part(*lead):
        return pltpu.VMEM(lead + (width, span), jnp.bfloat16)

    def stats(*lead):
        return pltpu.VMEM(lead + (rows, span), jnp.float32)

    return pl.pallas_call(
        functools.partial(combine_kernel, heads),
        in_specs=[hbm, vmem, hbm, vmem, vmem],
        out_specs=vmem,
        out_shape=jax.ShapeDtypeStruct(k.shape, jnp.bfloat16),
        scratch_shapes=[
            part(2, 2, RING),
            pltpu.VMEM(k.shape, jnp.bfloat16),
            pltpu.VMEM((2, span, width), jnp.bfloat16),
            part(2, RING),
            stats(2, RING),
            part(2, 2, RING),
            stats(2, 2, RING),
            part(2, RING),
            stats(2, RING),
            part(2),
            stats(2, 2),
            part(2, 2),
            stats(2, 2, 2),
            pltpu.VMEM((2, width, span), jnp.float32),
            stats(2),
            pltpu.SemaphoreType.DMA((17,)),
        ]
        + [pltpu.SemaphoreType.DMA((36,))] * 4
        + [pltpu.SemaphoreType.DMA((2,))] * 2,
        compiler_params=pltpu.CompilerParams(
            collective_id=1, has_side_effects=True, vmem_limit_bytes=40 << 20
        ),
        name="combine",
    )(o, st, q_all, k, v)


def shards(
    tokens,
    query_weight,
    key_weight,
    value_weight,
    cache_keys,
    cache_values,
    selected,
    counts,
    block_slot,
):
    heads = query_weight.shape[1] // HDIM
    span_count, select_count = selected.shape
    devices = lax.axis_size("context")
    cap = max(2, 2 * span_count * select_count // devices)

    stored = cache_keys.shape[0]
    q_all, k, v, table = gather_project(
        tokens, query_weight, key_weight, value_weight, selected, counts, block_slot, cap, stored
    )
    o, st = owner_attention(table, q_all, cache_keys, cache_values, heads, cap)
    return combine(o, st, q_all, k, v, heads)


def solution(mesh):
    placed = (
        P("context", "tensor"),
        P("context", "tensor"),
        P("context", "tensor"),
        P("context", "tensor"),
        P("context", None, "tensor"),
        P("context", None, "tensor"),
        P("context", None),
        P("context"),
        P(),
    )
    return jax.shard_map(
        shards, mesh=mesh, in_specs=placed, out_specs=P("context", "tensor"), check_vma=False
    )
```

```python
import functools

import jax
import jax.numpy as jnp
from jax import lax
from jax.experimental import pallas as pl
from jax.experimental.pallas import tpu as pltpu
from jax.sharding import PartitionSpec as P

HDIM = 128
NEG = -1e30
MESH = pl.DeviceIdType.MESH
EXTRA = 16
SCALE = HDIM ** (-0.5) * 1.4426950408889634


def dot_nt(a, b):
    return lax.dot_general(a, b, (((1,), (1,)), ((), ())), preferred_element_type=jnp.float32)


def dot_tn(a, b):
    return lax.dot_general(a, b, (((0,), (0,)), ((), ())), preferred_element_type=jnp.float32)


RING = 4
OFFSETS = (0, -1, 1, 2)


def wrap(position):
    return lax.rem(position + RING, RING)


def context_of(zpos, xpos):
    return wrap(zpos) * RING + wrap(xpos)


class Ring:
    def __init__(self, view, to, sems, sent, own=None):
        self.view, self.to, self.sems, self.sent, self.own = view, to, sems, sent, own
        self.waited = set()

    def copy(self, index, step):
        ref = self.view(step, max(0, index - 1))
        src = self.own if step == 0 and self.own is not None else ref
        return remote(src, ref, self.sems, index, self.to(1 if index % 2 == 0 else -1))

    def start(self, index):
        copy = self.copy(index, (0, 0, -1, 1)[index])
        copy.start()
        self.sent.append(copy)

    def arrive(self, index):
        if index not in self.waited:
            self.waited.add(index)
            self.copy(index, (-1, 1, 2, 2)[index]).wait_recv()

    def whole(self):
        self.start(0)
        self.start(1)

    def onward(self):
        self.arrive(0)
        self.start(2)
        self.arrive(1)
        self.start(3)

    def opposite(self):
        self.arrive(2)
        self.arrive(3)


def remote(src, dst, sems, index, to):
    send, recv, base = sems
    return pltpu.make_async_remote_copy(
        src_ref=src,
        dst_ref=dst,
        send_sem=send.at[base + index],
        recv_sem=recv.at[base + index],
        device_id=to,
        device_id_type=MESH,
    )


def context_gather(view, own, sems, zpos, xpos, sent):
    rings = {}

    def make(half, phase):
        along_x = (half == 0) == (phase == 0)
        first = 0 if phase == 0 else OFFSETS[phase - 1]

        def piece(step, part):
            dz, dx = (first, step) if along_x else (step, first)
            return view(wrap(zpos + dz), wrap(xpos + dx), half, part)

        def to(way):
            dz, dx = (0, way) if along_x else (way, 0)
            return {"context": context_of(zpos + dz, xpos + dx)}

        send, recv, base = sems
        source = own(half) if first == 0 else None
        return Ring(piece, to, (send, recv, base + half * 20 + phase * 4), sent, source)

    for half in (0, 1):
        for phase in range(5):
            rings[half, phase] = make(half, phase)

    def own():
        for half in (0, 1):
            rings[half, 0].whole()
            rings[half, 1].whole()

    def neighbours():
        for half in (0, 1):
            rings[half, 0].onward()
            rings[half, 2].whole()
            rings[half, 3].whole()
        for half in (0, 1):
            rings[half, 1].onward()

    def far():
        for half in (0, 1):
            rings[half, 0].opposite()
            rings[half, 4].whole()

    def corners():
        for half in (0, 1):
            rings[half, 2].onward()
            rings[half, 3].onward()

    def last():
        for half in (0, 1):
            rings[half, 4].onward()

    def rest():
        for half in (0, 1):
            for phase in (1, 2, 3, 4):
                rings[half, phase].opposite()

    return [own, neighbours, far, corners, last, rest]


def project_kernel(
    span_count, select_count, cap, stored,
    tok_ref, wq_ref, wk_ref, wv_ref, sel_ref, count_ref, slot_ref,
    q_ref, k_ref, v_ref, tab_ref,
    tok, stage, w, acc, done, back, fifth, small, told,
    load_sem, tsend, trecv, wsend, wrecv, bsend, brecv, qsend, qrecv,
):
    me = lax.axis_index("context")
    zpos, xpos = me // RING, lax.rem(me, RING)
    col = lax.axis_index("tensor")
    ypos, core = col // 2, lax.rem(col, 2)
    token_count, depth = tok.shape[2], tok.shape[3]
    rows = w.shape[3]
    sent = []

    token_load = pltpu.make_async_copy(tok_ref, tok.at[col, zpos], load_sem.at[0])
    token_load.start()
    loads = ([], [])
    for part in (0, 1):
        for to in range(RING):
            left = (wq_ref, wk_ref, wv_ref, wq_ref)[to]
            pair = ((wq_ref, to), (left, RING)) if part == 0 else ((wk_ref, to), (wv_ref, to))
            for i, (ref, head) in enumerate(pair):
                load = pltpu.make_async_copy(
                    ref.at[:, pl.ds(head * HDIM, HDIM)],
                    stage.at[part, to, :, pl.ds(i * HDIM, HDIM)],
                    load_sem.at[2 + part * 8 + to * 2 + i],
                )
                load.start()
                loads[part].append(load)

    def at_x(way):
        return {"context": context_of(zpos, xpos + way)}

    def at_z(way):
        return {"context": context_of(zpos + way, xpos)}

    def at_y(way):
        return {"tensor": wrap(ypos + way) * 2 + core}

    mate = {"tensor": ypos * 2 + 1 - core}
    barrier = pltpu.get_barrier_semaphore()
    partners = [at_x(1), at_x(-1), at_z(1), at_z(-1), at_z(2), at_y(1), at_y(-1), mate]
    for other in partners:
        pl.semaphore_signal(barrier, inc=1, device_id=other, device_id_type=MESH)
    pl.semaphore_wait(barrier, len(partners))

    def cut(size):
        return (pl.ds(0, size), pl.ds(0, size // 2), pl.ds(size // 2, size // 2))

    ztok = Ring(
        lambda step, part: tok.at[col, wrap(zpos + step), cut(token_count)[part]],
        at_z, (tsend, trecv, 0), sent,
    )
    ytok = {
        o: Ring(
            lambda step, part, o=o: tok.at[
                wrap(ypos + step) * 2 + core, wrap(zpos + o), cut(token_count)[part]
            ],
            at_y, (tsend, trecv, 4 + 4 * i), sent,
        )
        for i, o in enumerate(OFFSETS)
    }

    def share(step, o, receive=False):
        side = 1 - core if receive else core
        ref = tok.at[wrap(ypos + step) * 2 + side, wrap(zpos + o)]
        index = 20 + OFFSETS.index(step) * 4 + OFFSETS.index(o)
        copy = remote(ref, ref, (tsend, trecv, 0), index, mate)
        if receive:
            copy.wait_recv()
        else:
            copy.start()
            sent.append(copy)

    def exchange(part, step, receive=False):
        index = part * 3 + OFFSETS.index(step) - 1
        src = stage.at[part, wrap(zpos + step)]
        if receive:
            dst = w.at[part, wrap(zpos - step), xpos]
            remote(src, dst, (wsend, wrecv, 0), index, at_z(step)).wait_recv()
        else:
            copy = remote(src, w.at[part, zpos, xpos], (wsend, wrecv, 0), index, at_z(step))
            copy.start()
            sent.append(copy)

    xw = {
        (part, o): Ring(
            lambda step, piece, part=part, o=o: w.at[
                part, wrap(zpos + o), wrap(xpos + step), cut(rows)[piece]
            ],
            at_x, (wsend, wrecv, 6 + part * 16 + 4 * i), sent,
        )
        for part in (0, 1)
        for i, o in enumerate(OFFSETS)
    }

    def keep(part):
        for load in loads[part]:
            load.wait()
        copy = pltpu.make_async_copy(
            stage.at[part, zpos], w.at[part, zpos, xpos], load_sem.at[18 + part]
        )
        copy.start()
        copy.wait()

    def compute(part, step):
        for side in (0, 1):
            t = wrap(ypos + step) * 2 + side
            piece = w[part, wrap(ypos + step), 2 * side : 2 * side + 2].reshape(depth, w.shape[4])

            @pl.loop(0, RING)
            def _(z):
                new = jnp.dot(tok[t, z], piece, preferred_element_type=jnp.float32)
                if step == 0 and side == 0:
                    acc[z] = new
                else:
                    acc[z] += new

    def give_back(part, buf, columns, base):
        buf[zpos] = acc[zpos, :, columns].astype(jnp.bfloat16)
        for i, step in enumerate(OFFSETS[1:]):
            copy = remote(
                done.at[part, wrap(zpos + step), :, columns], buf.at[zpos],
                (bsend, brecv, base), i, at_z(step),
            )
            copy.start()
            sent.append(copy)

    def take_back(buf, base):
        for i, step in enumerate(OFFSETS[1:]):
            ref = buf.at[wrap(zpos - step)]
            remote(ref, ref, (bsend, brecv, base), i, at_z(step)).wait_recv()

    def finish(part):
        @pl.loop(0, RING)
        def _(z):
            done[part, z] = acc[z].astype(jnp.bfloat16)

    token_load.wait()
    ztok.whole()
    ytok[0].whole()
    share(0, 0)
    keep(0)
    xw[0, 0].whole()
    exchange(0, 1)
    exchange(0, -1)
    keep(1)
    xw[1, 0].whole()

    lane = lax.broadcasted_iota(jnp.int32, (EXTRA, HDIM), 1)
    line = lax.broadcasted_iota(jnp.int32, (EXTRA, HDIM), 0)
    chosen = jnp.zeros((EXTRA, HDIM), jnp.int32)
    for half in range(span_count):

        def note(j, chosen, half=half):
            slot = slot_ref[jnp.maximum(sel_ref[half, j], 0)]
            owner = jnp.where(j < count_ref[half], slot // stored, -1)
            value = jnp.where(line == half, owner, slot % stored)
            here = (lane == j) & ((line == half) | (line == span_count + half))
            return jnp.where(here, value, chosen)

        chosen = lax.fori_loop(0, select_count, note, chosen)
    small[token_count:, :] = chosen.astype(jnp.float32).astype(jnp.bfloat16)

    xw[0, 0].onward()
    ztok.onward()
    for o in (-1, 1):
        ytok[o].whole()
        share(0, o)
    ytok[0].onward()
    exchange(0, 2)
    exchange(1, 1)
    exchange(1, -1)
    exchange(1, 2)
    share(-1, 0)
    share(1, 0)
    for step in (1, -1):
        exchange(0, step, receive=True)
        xw[0, -step].whole()
    xw[1, 0].onward()
    ztok.opposite()
    ytok[2].whole()
    share(0, 2)
    exchange(0, 2, receive=True)
    xw[0, 2].whole()
    for o in (-1, 1):
        ytok[o].onward()
        share(-1, o)
        share(1, o)
    xw[0, -1].onward()
    xw[0, 1].onward()
    for step in (1, -1):
        exchange(1, step, receive=True)
        xw[1, -step].whole()
    xw[0, 2].onward()
    exchange(1, 2, receive=True)
    xw[1, 2].whole()
    for o in (-1, 1):
        xw[1, o].onward()
    ytok[0].opposite()
    share(2, 0)

    def shared(step):
        for o in OFFSETS:
            share(step, o, receive=True)

    for o in OFFSETS:
        xw[0, o].opposite()
    shared(0)
    compute(0, 0)
    ytok[2].onward()
    share(-1, 2)
    share(1, 2)
    xw[1, 2].onward()
    shared(-1)
    compute(0, -1)
    ytok[-1].opposite()
    share(2, -1)
    shared(1)
    compute(0, 1)
    ytok[1].opposite()
    share(2, 1)
    ytok[2].opposite()
    share(2, 2)
    shared(2)
    compute(0, 2)
    finish(0)

    groups = (pl.ds(0, 1), pl.ds(1, RING - 1))

    def head_view(z, x, half, part):
        head = pl.ds(pl.multiple_of(z * HDIM, HDIM), HDIM)
        return q_ref.at[groups[half], x, cut(token_count)[part], head]

    def head_own(half):
        return done.at[0, groups[half], :, pl.ds(0, HDIM)]

    heads = context_gather(head_view, head_own, (qsend, qrecv, 0), zpos, xpos, sent)

    half_rows = token_count // 2
    quarter = half_rows // 2
    ranges = (
        ((0, half_rows), (0, quarter), (quarter, quarter)),
        (
            (half_rows, half_rows + EXTRA),
            (half_rows, quarter),
            (half_rows + quarter, quarter + EXTRA),
        ),
    )

    def last_view(z, x, half, part):
        return q_ref.at[z, x, pl.ds(*ranges[half][part]), pl.ds(RING * HDIM, HDIM)]

    def last_own(half):
        return small.at[pl.ds(*ranges[half][0]), :]

    last = context_gather(last_view, last_own, (qsend, qrecv, 40), zpos, xpos, sent)

    give_back(0, fifth, slice(HDIM, 2 * HDIM), 0)
    heads[0]()
    keeps = [
        pltpu.make_async_copy(
            done.at[0, :, :, pl.ds(0, HDIM)],
            q_ref.at[
                :, xpos, pl.ds(0, token_count), pl.ds(pl.multiple_of(zpos * HDIM, HDIM), HDIM)
            ],
            load_sem.at[1],
        )
    ]
    keeps[0].start()
    for o in OFFSETS:
        xw[1, o].opposite()
    compute(1, 0)
    take_back(fifth, 0)
    small[0:token_count, :] = fifth[0]
    last[0]()
    keeps.append(
        pltpu.make_async_copy(
            small, q_ref.at[zpos, xpos, :, pl.ds(RING * HDIM, HDIM)], load_sem.at[20]
        )
    )
    keeps[1].start()
    heads[1]()
    compute(1, -1)
    compute(1, 1)
    heads[2]()
    last[1]()
    compute(1, 2)
    finish(1)
    give_back(1, back, slice(0, 2 * HDIM), 3)
    heads[3]()
    last[2]()
    heads[4]()
    last[3]()
    last[4]()
    for keep_copy in keeps:
        keep_copy.wait()
    heads[5]()
    last[5]()
    look = pltpu.make_async_copy(
        q_ref.at[:, :, pl.ds(token_count, EXTRA), pl.ds(RING * HDIM, HDIM)],
        told,
        load_sem.at[21],
    )
    look.start()
    take_back(back, 3)
    for head in range(RING):
        cols = slice(head * HDIM, (head + 1) * HDIM)
        k_ref[:, cols] = back[head, :, 0:HDIM]
        v_ref[:, cols] = back[head, :, HDIM : 2 * HDIM]
    k_ref[:, RING * HDIM :] = fifth[1]
    v_ref[:, RING * HDIM :] = fifth[2]
    look.wait()

    devices = RING * RING
    lane = lax.broadcasted_iota(jnp.int32, (devices, HDIM), 1)
    before = lax.broadcasted_iota(jnp.int32, (HDIM, HDIM), 0)
    after = lax.broadcasted_iota(jnp.int32, (HDIM, HDIM), 1)
    earlier = jnp.where(before < after, 1.0, 0.0).astype(jnp.bfloat16)
    listed = told[...].reshape(devices, EXTRA, HDIM).astype(jnp.float32)
    for half in range(span_count):
        owner = listed[:, half, :]
        row = listed[:, span_count + half, :]
        mine = jnp.where((owner == me.astype(jnp.float32)) & (lane < select_count), 1.0, 0.0)
        rank = jnp.dot(mine.astype(jnp.bfloat16), earlier, preferred_element_type=jnp.float32)
        table = jnp.where(lane == cap, jnp.sum(mine, axis=1, keepdims=True), 0.0)
        for r in range(cap):
            value = jnp.sum(jnp.where(rank == r, mine * row, 0.0), axis=1, keepdims=True)
            table = jnp.where(lane == r, value, table)
        tab_ref[half] = table.astype(jnp.int32)

    for copy in sent:
        copy.wait_send()


def gather_project(tokens, wq, wk, wv, selected, counts, block_slot, cap, stored):
    token_count, depth = tokens.shape
    rows, width = wq.shape
    span_count, select_count = selected.shape
    devices = lax.axis_size("context")
    columns = lax.axis_size("tensor")
    hbm = pl.BlockSpec(memory_space=pl.ANY)
    vmem = pl.BlockSpec(memory_space=pltpu.VMEM)
    smem = pl.BlockSpec(memory_space=pltpu.SMEM)
    own = jax.ShapeDtypeStruct((token_count, width), jnp.bfloat16)
    two = 2 * HDIM

    def dma(count):
        return [pltpu.SemaphoreType.DMA((count,))] * 2

    return pl.pallas_call(
        functools.partial(project_kernel, span_count, select_count, cap, stored),
        in_specs=[hbm] * 4 + [smem] * 3,
        out_specs=[hbm] + [vmem] * 3,
        out_shape=[
            jax.ShapeDtypeStruct((RING, RING, token_count + EXTRA, width), jnp.bfloat16),
            own,
            own,
            jax.ShapeDtypeStruct((span_count, devices, HDIM), jnp.int32),
        ],
        scratch_shapes=[
            pltpu.VMEM((columns, RING, token_count, depth), jnp.bfloat16),
            pltpu.VMEM((2, RING, rows, two), jnp.bfloat16),
            pltpu.VMEM((2, RING, RING, rows, two), jnp.bfloat16),
            pltpu.VMEM((RING, token_count, two), jnp.float32),
            pltpu.VMEM((2, RING, token_count, two), jnp.bfloat16),
            pltpu.VMEM((RING, token_count, two), jnp.bfloat16),
            pltpu.VMEM((RING, token_count, HDIM), jnp.bfloat16),
            pltpu.VMEM((token_count + EXTRA, HDIM), jnp.bfloat16),
            pltpu.VMEM((RING, RING, EXTRA, HDIM), jnp.bfloat16),
            pltpu.SemaphoreType.DMA((22,)),
        ]
        + dma(36)
        + dma(38)
        + dma(6)
        + dma(80),
        compiler_params=pltpu.CompilerParams(
            collective_id=0, has_side_effects=True, vmem_limit_bytes=60 << 20
        ),
        name="gather_project",
    )(tokens, wq, wk, wv, selected, counts, block_slot)


def owner_kernel(heads, cap, tab_ref, q_ref, k_ref, v_ref, o_ref, st_ref, acc_ref):
    src = pl.program_id(0)
    span_count = o_ref.shape[1]
    span = o_ref.shape[3]
    block = k_ref.shape[1]
    columns = [slice(h * HDIM, (h + 1) * HDIM) for h in range(heads)]

    def scores(half, j):
        n = tab_ref[half, src, cap]
        r0 = tab_ref[half, src, 2 * j]
        r1 = tab_ref[half, src, 2 * j + 1]
        bias1 = jnp.where(2 * j + 1 < n, 0.0, NEG)
        out = []
        for cols in columns:
            q = q_ref[0, half * span : (half + 1) * span, cols]
            k = jnp.concatenate([k_ref[r0, :, cols], k_ref[r1, :, cols]], 0)
            v = jnp.concatenate([v_ref[r0, :, cols], v_ref[r1, :, cols]], 0)
            s = dot_nt(k, q) * SCALE
            out.append((jnp.concatenate([s[:block], s[block:] + bias1], 0), v))
        return out

    for half in range(span_count):
        results = []
        for s, v in scores(half, 0):
            m = jnp.max(s, axis=0, keepdims=True)
            p = jnp.exp2(s - m)
            l = jnp.sum(p, axis=0, keepdims=True)
            results.append((m, l, dot_tn(v, p.astype(jnp.bfloat16))))
        some = tab_ref[half, src, cap] > 0
        for h, (m, l, a) in enumerate(results):
            st_ref[0, half, h : h + 1, :] = jnp.where(some, m, NEG)
            st_ref[0, half, 8 + h : 9 + h, :] = l
            acc_ref[half, columns[h], :] = a
            o_ref[0, half, columns[h], :] = a.astype(jnp.bfloat16)

    for half in range(span_count):
        n = tab_ref[half, src, cap]

        @pl.when(n > 2)
        def _():
            @pl.loop(1, (n + 1) // 2)
            def _(j):
                results = []
                for h, (s, v) in enumerate(scores(half, j)):
                    old = st_ref[0, half, h : h + 1, :]
                    m = jnp.maximum(jnp.max(s, axis=0, keepdims=True), old)
                    decay = jnp.exp2(old - m)
                    p = jnp.exp2(s - m)
                    l = jnp.sum(p, axis=0, keepdims=True)
                    l = l + st_ref[0, half, 8 + h : 9 + h, :] * decay
                    a = dot_tn(v, p.astype(jnp.bfloat16)) + acc_ref[half, columns[h], :] * decay
                    results.append((m, l, a))
                for h, (m, l, a) in enumerate(results):
                    st_ref[0, half, h : h + 1, :] = m
                    st_ref[0, half, 8 + h : 9 + h, :] = l
                    acc_ref[half, columns[h], :] = a

            for h in range(heads):
                o_ref[0, half, columns[h], :] = acc_ref[half, columns[h], :].astype(jnp.bfloat16)


def owner_attention(table, q_all, cache_keys, cache_values, heads, cap):
    tokens, width = q_all.shape[2] - EXTRA, q_all.shape[3]
    span_count, devices = table.shape[:2]
    span = tokens // span_count
    q_all = q_all.reshape(devices, tokens + EXTRA, width)
    whole = pl.BlockSpec(cache_keys.shape, lambda s, *_: (0, 0, 0), pipeline_mode=pl.Buffered(1))
    return pl.pallas_call(
        functools.partial(owner_kernel, heads, cap),
        grid_spec=pltpu.PrefetchScalarGridSpec(
            num_scalar_prefetch=1,
            grid=(devices,),
            in_specs=[
                pl.BlockSpec((1, tokens, width), lambda s, *_: (s, 0, 0)),
                whole,
                whole,
            ],
            out_specs=[
                pl.BlockSpec((1, span_count, width, span), lambda s, *_: (s, 0, 0, 0)),
                pl.BlockSpec((1, span_count, 16, span), lambda s, *_: (s, 0, 0, 0)),
            ],
            scratch_shapes=[pltpu.VMEM((span_count, width, span), jnp.float32)],
        ),
        out_shape=[
            jax.ShapeDtypeStruct((devices, span_count, width, span), jnp.bfloat16),
            jax.ShapeDtypeStruct((devices, span_count, 16, span), jnp.float32),
        ],
    )(table, q_all, cache_keys, cache_values)


def combine_kernel(
    heads,
    o_ref, st_ref, q_ref, k_ref, v_ref,
    out_ref,
    own, query, before, relay, relay_st, got, got_st, mid, mid_st,
    relay2, relay2_st, got2, got2_st, acc, acc_st,
    load_sem, send, recv, send_st, recv_st, psend, precv,
):
    me = lax.axis_index("context")
    zpos, xpos = me // RING, lax.rem(me, RING)
    devices = RING * RING
    behind, ahead = lax.rem(me + devices - 1, devices), lax.rem(me + 1, devices)
    span = o_ref.shape[-1]
    token_count = k_ref.shape[0]
    cut = (heads + 1) // 2 * HDIM
    parts = ((0, cut), (cut, heads * HDIM - cut))
    order = (2, -1, 1, 0)

    def first_at(half, step):
        return wrap((xpos if half == 0 else zpos) + step)

    def second_at(half, step):
        return wrap((zpos if half == 0 else xpos) + step)

    def place(half, step, further):
        a, b = first_at(half, step), second_at(half, further)
        return (b, a, half) if half == 0 else (a, b, half)

    def way_of(half, further):
        return 1 if further == 2 or (further == 1 and half == 1) else -1

    loads = {}
    count = 0
    for kind in (0, 1):
        for further in order:
            for half in (0, 1):
                step = way_of(half, further) if kind == 0 else 0
                slot = (half, kind, order.index(further))
                loads[slot] = pltpu.make_async_copy(
                    o_ref.at[place(half, step, further)], own.at[slot], load_sem.at[count]
                )
                loads[slot].start()
                count += 1
    query_load = pltpu.make_async_copy(
        q_ref.at[zpos, xpos, pl.ds(0, token_count)], query, load_sem.at[count]
    )
    query_load.start()

    barrier = pltpu.get_barrier_semaphore()
    for other in (
        context_of(zpos + 1, xpos),
        context_of(zpos - 1, xpos),
        context_of(zpos, xpos + 1),
        context_of(zpos, xpos - 1),
        behind,
        ahead,
    ):
        pl.semaphore_signal(barrier, inc=1, device_id={"context": other}, device_id_type=MESH)
    pl.semaphore_wait(barrier, 6)

    started = []

    def copies(half, index, way, first, src, src_st, dst, dst_st):
        if (half == 0) == first:
            to = {"context": context_of(zpos, xpos + way)}
        else:
            to = {"context": context_of(zpos + way, xpos)}
        base = half * 18
        return (
            remote(src, dst, (send, recv, base), index, to),
            remote(src_st, dst_st, (send_st, recv_st, base), index, to),
        )

    def start(*args):
        for copy in copies(*args):
            copy.start()
            started.append(copy)

    def arrive(half, index, dst, dst_st):
        for copy in copies(half, index, 1, True, dst, dst_st, dst, dst_st):
            copy.wait_recv()

    def merge(out, out_st, sources, head_range):
        results = []
        for h in head_range:
            rows = slice(h * HDIM, (h + 1) * HDIM)
            ms = [st[h : h + 1, :] for _, st in sources]
            m = functools.reduce(jnp.maximum, ms)
            ws = [jnp.exp2(x - m) for x in ms]
            ls = [st[8 + h : 9 + h, :] * w for (_, st), w in zip(sources, ws)]
            terms = [part[rows, :].astype(jnp.float32) * w for (part, _), w in zip(sources, ws)]
            total = functools.reduce(jnp.add, terms).astype(jnp.bfloat16)
            results.append((h, rows, m, functools.reduce(jnp.add, ls), total))
        for h, rows, m, l, total in results:
            out[rows, :] = total
            out_st[h : h + 1, :] = m
            out_st[8 + h : 9 + h, :] = l

    every = range(heads)

    def forward(half, further):
        i, at = order.index(further), place(half, 2, further)
        start(
            half, i, way_of(half, further), True, o_ref.at[at], st_ref.at[at],
            relay.at[half, i], relay_st.at[half, i],
        )

    def direct(half, further):
        way = -way_of(half, further)
        i, at, side = order.index(further), place(half, way, further), 0 if way == 1 else 1
        start(
            half, 4 + i, way, True, o_ref.at[at], st_ref.at[at],
            got.at[half, side, i], got_st.at[half, side, i],
        )

    def merged(half, further):
        way = way_of(half, further)
        i, at, side = order.index(further), place(half, way, further), 0 if way == 1 else 1
        part, st = relay.at[half, i], relay_st.at[half, i]
        arrive(half, i, part, st)
        loads[half, 0, i].wait()
        merge(part, st, [(part, st), (own.at[half, 0, i], st_ref.at[at])], every)
        start(
            half, 8 + i, way, True, part, st, got.at[half, side, i], got_st.at[half, side, i]
        )

    def collect(half, further):
        i = order.index(further)
        side = 0 if way_of(half, further) == 1 else 1
        arrive(half, 4 + i, got.at[half, 1 - side, i], got_st.at[half, 1 - side, i])
        arrive(half, 8 + i, got.at[half, side, i], got_st.at[half, side, i])
        loads[half, 1, i].wait()
        merge(
            mid.at[half, i], mid_st.at[half, i],
            [(own.at[half, 1, i], st_ref.at[place(half, 0, further)])]
            + [(got.at[half, n, i], got_st.at[half, n, i]) for n in (0, 1)],
            every,
        )

    halves = (0, 1)
    for further in order:
        for half in halves:
            forward(half, further)
    for further in (2, -1):
        for half in halves:
            direct(half, further)

    key = lax.broadcasted_iota(jnp.int32, (span, span), 0)
    row = lax.broadcasted_iota(jnp.int32, (span, span), 1)

    def local(half, keys_of, values_of, bias, first):
        results = []
        for h in every:
            cols = slice(h * HDIM, (h + 1) * HDIM)
            s = dot_nt(keys_of(cols), query[half * span : (half + 1) * span, cols]) * SCALE
            s = jnp.where(key <= row, s, NEG) if bias is None else s + bias
            m = jnp.max(s, axis=0, keepdims=True)
            if not first:
                old = acc_st[half, h : h + 1, :]
                m = jnp.maximum(m, old)
                decay = jnp.exp2(old - m)
            p = jnp.exp2(s - m)
            l = jnp.sum(p, axis=0, keepdims=True)
            a = dot_tn(values_of(cols), p.astype(jnp.bfloat16))
            if not first:
                l = l + acc_st[half, 8 + h : 9 + h, :] * decay
                a = a + acc[half, cols, :] * decay
            results.append((h, cols, m, l, a))
        for h, cols, m, l, a in results:
            acc_st[half, h : h + 1, :] = m
            acc_st[half, 8 + h : 9 + h, :] = l
            acc[half, cols, :] = a

    query_load.wait()
    for half in halves:
        rows = slice(half * span, (half + 1) * span)
        local(half, lambda c, r=rows: k_ref[r, c], lambda c, r=rows: v_ref[r, c], None, True)

    for further in (2, -1):
        for half in halves:
            merged(half, further)
    for further in (1, 0):
        for half in halves:
            direct(half, further)
    prior = []
    for i, ref in enumerate((k_ref, v_ref)):
        prior.append(
            remote(
                ref.at[pl.ds(token_count - span, span), :], before.at[i], (psend, precv, 0), i,
                {"context": ahead},
            )
        )
        prior[-1].start()
    for further in (1, 0):
        for half in halves:
            merged(half, further)
    local(1, lambda c: k_ref[0:span, c], lambda c: v_ref[0:span, c], 0.0, False)

    for half in halves:
        collect(half, 2)
        for side, way in ((0, 1), (1, -1)):
            rows = pl.ds(*parts[side])
            start(
                half, 12 + side, way, False, mid.at[half, 0, rows], mid_st.at[half, 0],
                relay2.at[half, rows], relay2_st.at[half, side],
            )
    for side, way in ((1, -1), (0, 1)):
        for half in halves:
            i = order.index(way)
            collect(half, way)
            other = pl.ds(*parts[1 - side])
            start(
                half, 14 + side, way, False, mid.at[half, i, other], mid_st.at[half, i],
                got2.at[half, side, other], got2_st.at[half, side, 1 - side],
            )
    for half in halves:
        for side, way in ((0, 1), (1, -1)):
            i = order.index(way)
            rows = pl.ds(*parts[side])
            part, st = relay2.at[half], relay2_st.at[half, side]
            arrive(half, 12 + side, relay2.at[half, rows], st)
            merge(
                part, st, [(part, st), (mid.at[half, i], mid_st.at[half, i])],
                range(parts[side][0] // HDIM, sum(parts[side]) // HDIM),
            )
            start(
                half, 16 + side, way, False, relay2.at[half, rows], st,
                got2.at[half, side, rows], got2_st.at[half, side, side],
            )

    for copy in prior:
        copy.wait_recv()
    local(
        0, lambda c: before[0, :, c], lambda c: before[1, :, c], jnp.where(me > 0, 0.0, NEG), False
    )
    last = order.index(0)
    for half in halves:
        collect(half, 0)
    for half in halves:
        for side in (0, 1):
            for index, which in ((14 + side, 1 - side), (16 + side, side)):
                arrive(
                    half, index,
                    got2.at[half, side, pl.ds(*parts[which])], got2_st.at[half, side, which],
                )
        for h in every:
            cols = slice(h * HDIM, (h + 1) * HDIM)
            which = 0 if h * HDIM < cut else 1
            sources = [(mid.at[half, last], mid_st.at[half, last])]
            sources += [(got2.at[half, i], got2_st.at[half, i, which]) for i in (0, 1)]
            old = acc_st[half, h : h + 1, :]
            ms = [st[h : h + 1, :] for _, st in sources]
            m = functools.reduce(jnp.maximum, ms, old)
            decay = jnp.exp2(old - m)
            total = acc_st[half, 8 + h : 9 + h, :] * decay
            a = acc[half, cols, :] * decay
            for (part, st), x in zip(sources, ms):
                w = jnp.exp2(x - m)
                total = total + st[8 + h : 9 + h, :] * w
                a = a + part[cols, :].astype(jnp.float32) * w
            out_ref[half * span : (half + 1) * span, cols] = jnp.transpose(a / total).astype(
                out_ref.dtype
            )

    for copy in started + prior:
        copy.wait_send()


def combine(o, st, q_all, k, v, heads):
    span_count, width, span = o.shape[1:]
    rows = st.shape[2]
    o = o.reshape(RING, RING, span_count, width, span)
    st = st.reshape(RING, RING, span_count, rows, span)
    vmem = pl.BlockSpec(memory_space=pltpu.VMEM)
    hbm = pl.BlockSpec(memory_space=pl.ANY)

    def part(*lead):
        return pltpu.VMEM(lead + (width, span), jnp.bfloat16)

    def stats(*lead):
        return pltpu.VMEM(lead + (rows, span), jnp.float32)

    return pl.pallas_call(
        functools.partial(combine_kernel, heads),
        in_specs=[hbm, vmem, hbm, vmem, vmem],
        out_specs=vmem,
        out_shape=jax.ShapeDtypeStruct(k.shape, jnp.bfloat16),
        scratch_shapes=[
            part(2, 2, RING),
            pltpu.VMEM(k.shape, jnp.bfloat16),
            pltpu.VMEM((2, span, width), jnp.bfloat16),
            part(2, RING),
            stats(2, RING),
            part(2, 2, RING),
            stats(2, 2, RING),
            part(2, RING),
            stats(2, RING),
            part(2),
            stats(2, 2),
            part(2, 2),
            stats(2, 2, 2),
            pltpu.VMEM((2, width, span), jnp.float32),
            stats(2),
            pltpu.SemaphoreType.DMA((17,)),
        ]
        + [pltpu.SemaphoreType.DMA((36,))] * 4
        + [pltpu.SemaphoreType.DMA((2,))] * 2,
        compiler_params=pltpu.CompilerParams(
            collective_id=1, has_side_effects=True, vmem_limit_bytes=60 << 20
        ),
        name="combine",
    )(o, st, q_all, k, v)


def shards(
    tokens,
    query_weight,
    key_weight,
    value_weight,
    cache_keys,
    cache_values,
    selected,
    counts,
    block_slot,
):
    heads = query_weight.shape[1] // HDIM
    span_count, select_count = selected.shape
    devices = lax.axis_size("context")
    cap = max(2, 2 * span_count * select_count // devices)

    stored = cache_keys.shape[0]
    q_all, k, v, table = gather_project(
        tokens, query_weight, key_weight, value_weight, selected, counts, block_slot, cap, stored
    )
    o, st = owner_attention(table, q_all, cache_keys, cache_values, heads, cap)
    return combine(o, st, q_all, k, v, heads)


def solution(mesh):
    placed = (
        P("context", "tensor"),
        P("context", "tensor"),
        P("context", "tensor"),
        P("context", "tensor"),
        P("context", None, "tensor"),
        P("context", None, "tensor"),
        P("context", None),
        P("context"),
        P(),
    )
    return jax.shard_map(
        shards, mesh=mesh, in_specs=placed, out_specs=P("context", "tensor"), check_vma=False
    )
```

```python
import functools

import jax
import jax.numpy as jnp
from jax import lax
from jax.experimental import pallas as pl
from jax.experimental.pallas import tpu as pltpu
from jax.sharding import PartitionSpec as P

HDIM = 128
NEG = -1e30
MESH = pl.DeviceIdType.MESH
EXTRA = 16
GROUP = 2
SCALE = HDIM ** (-0.5) * 1.4426950408889634


def dot_nt(a, b):
    return lax.dot_general(a, b, (((1,), (1,)), ((), ())), preferred_element_type=jnp.float32)


def dot_tn(a, b):
    return lax.dot_general(a, b, (((0,), (0,)), ((), ())), preferred_element_type=jnp.float32)


RING = 4
OFFSETS = (0, -1, 1, 2)


def wrap(position):
    return lax.rem(position + RING, RING)


def context_of(zpos, xpos):
    return wrap(zpos) * RING + wrap(xpos)


class Ring:
    def __init__(self, view, to, sems, sent, own=None):
        self.view, self.to, self.sems, self.sent, self.own = view, to, sems, sent, own
        self.waited = set()

    def copy(self, index, step):
        ref = self.view(step, max(0, index - 1))
        src = self.own if step == 0 and self.own is not None else ref
        return remote(src, ref, self.sems, index, self.to(1 if index % 2 == 0 else -1))

    def start(self, index):
        copy = self.copy(index, (0, 0, -1, 1)[index])
        copy.start()
        self.sent.append(copy)

    def arrive(self, index):
        if index not in self.waited:
            self.waited.add(index)
            self.copy(index, (-1, 1, 2, 2)[index]).wait_recv()

    def whole(self):
        self.start(0)
        self.start(1)

    def onward(self):
        self.arrive(0)
        self.start(2)
        self.arrive(1)
        self.start(3)

    def opposite(self):
        self.arrive(2)
        self.arrive(3)


def remote(src, dst, sems, index, to):
    send, recv, base = sems
    return pltpu.make_async_remote_copy(
        src_ref=src,
        dst_ref=dst,
        send_sem=send.at[base + index],
        recv_sem=recv.at[base + index],
        device_id=to,
        device_id_type=MESH,
    )


def context_gather(view, own, sems, zpos, xpos, sent):
    rings = {}

    def make(half, phase):
        along_x = (half == 0) == (phase == 0)
        first = 0 if phase == 0 else OFFSETS[phase - 1]

        def piece(step, part):
            dz, dx = (first, step) if along_x else (step, first)
            return view(wrap(zpos + dz), wrap(xpos + dx), half, part)

        def to(way):
            dz, dx = (0, way) if along_x else (way, 0)
            return {"context": context_of(zpos + dz, xpos + dx)}

        send, recv, base = sems
        source = own(half) if first == 0 else None
        return Ring(piece, to, (send, recv, base + half * 20 + phase * 4), sent, source)

    for half in (0, 1):
        for phase in range(5):
            rings[half, phase] = make(half, phase)

    def own():
        for half in (0, 1):
            rings[half, 0].whole()
            rings[half, 1].whole()

    def neighbours():
        for half in (0, 1):
            rings[half, 0].onward()
            rings[half, 2].whole()
            rings[half, 3].whole()
        for half in (0, 1):
            rings[half, 1].onward()

    def far():
        for half in (0, 1):
            rings[half, 0].opposite()
            rings[half, 4].whole()

    def corners():
        for half in (0, 1):
            rings[half, 2].onward()
            rings[half, 3].onward()

    def last():
        for half in (0, 1):
            rings[half, 4].onward()

    def rest():
        for half in (0, 1):
            for phase in (1, 2, 3, 4):
                rings[half, phase].opposite()

    return [own, neighbours, far, corners, last, rest]


def project_kernel(
    span_count, select_count, cap, stored,
    tok_ref, wq_ref, wk_ref, wv_ref, sel_ref, count_ref, slot_ref,
    q_ref, k_ref, v_ref, tab_ref,
    tok, stage, w, acc, done, back, fifth, small, told,
    load_sem, tsend, trecv, wsend, wrecv, bsend, brecv, qsend, qrecv,
):
    me = lax.axis_index("context")
    zpos, xpos = me // RING, lax.rem(me, RING)
    col = lax.axis_index("tensor")
    ypos, core = col // 2, lax.rem(col, 2)
    token_count, depth = tok.shape[2], tok.shape[3]
    rows = w.shape[3]
    sent = []

    token_load = pltpu.make_async_copy(tok_ref, tok.at[col, zpos], load_sem.at[0])
    token_load.start()
    loads = ([], [])
    for part in (0, 1):
        for to in range(RING):
            left = (wq_ref, wk_ref, wv_ref, wq_ref)[to]
            pair = ((wq_ref, to), (left, RING)) if part == 0 else ((wk_ref, to), (wv_ref, to))
            for i, (ref, head) in enumerate(pair):
                load = pltpu.make_async_copy(
                    ref.at[:, pl.ds(head * HDIM, HDIM)],
                    stage.at[part, to, :, pl.ds(i * HDIM, HDIM)],
                    load_sem.at[2 + part * 8 + to * 2 + i],
                )
                load.start()
                loads[part].append(load)

    def at_x(way):
        return {"context": context_of(zpos, xpos + way)}

    def at_z(way):
        return {"context": context_of(zpos + way, xpos)}

    def at_y(way):
        return {"tensor": wrap(ypos + way) * 2 + core}

    mate = {"tensor": ypos * 2 + 1 - core}
    barrier = pltpu.get_barrier_semaphore()
    partners = [at_x(1), at_x(-1), at_z(1), at_z(-1), at_z(2), at_y(1), at_y(-1), mate]
    for other in partners:
        pl.semaphore_signal(barrier, inc=1, device_id=other, device_id_type=MESH)
    pl.semaphore_wait(barrier, len(partners))

    def cut(size):
        return (pl.ds(0, size), pl.ds(0, size // 2), pl.ds(size // 2, size // 2))

    ztok = Ring(
        lambda step, part: tok.at[col, wrap(zpos + step), cut(token_count)[part]],
        at_z, (tsend, trecv, 0), sent,
    )
    ytok = {
        o: Ring(
            lambda step, part, o=o: tok.at[
                wrap(ypos + step) * 2 + core, wrap(zpos + o), cut(token_count)[part]
            ],
            at_y, (tsend, trecv, 4 + 4 * i), sent,
        )
        for i, o in enumerate(OFFSETS)
    }

    def share(step, o, receive=False):
        side = 1 - core if receive else core
        ref = tok.at[wrap(ypos + step) * 2 + side, wrap(zpos + o)]
        index = 20 + OFFSETS.index(step) * 4 + OFFSETS.index(o)
        copy = remote(ref, ref, (tsend, trecv, 0), index, mate)
        if receive:
            copy.wait_recv()
        else:
            copy.start()
            sent.append(copy)

    def exchange(part, step, receive=False):
        index = part * 3 + OFFSETS.index(step) - 1
        src = stage.at[part, wrap(zpos + step)]
        if receive:
            dst = w.at[part, wrap(zpos - step), xpos]
            remote(src, dst, (wsend, wrecv, 0), index, at_z(step)).wait_recv()
        else:
            copy = remote(src, w.at[part, zpos, xpos], (wsend, wrecv, 0), index, at_z(step))
            copy.start()
            sent.append(copy)

    xw = {
        (part, o): Ring(
            lambda step, piece, part=part, o=o: w.at[
                part, wrap(zpos + o), wrap(xpos + step), cut(rows)[piece]
            ],
            at_x, (wsend, wrecv, 6 + part * 16 + 4 * i), sent,
        )
        for part in (0, 1)
        for i, o in enumerate(OFFSETS)
    }

    def keep(part):
        for load in loads[part]:
            load.wait()
        copy = pltpu.make_async_copy(
            stage.at[part, zpos], w.at[part, zpos, xpos], load_sem.at[18 + part]
        )
        copy.start()
        copy.wait()

    def compute(part, step):
        for side in (0, 1):
            t = wrap(ypos + step) * 2 + side
            piece = w[part, wrap(ypos + step), 2 * side : 2 * side + 2].reshape(depth, w.shape[4])

            @pl.loop(0, RING)
            def _(z):
                new = jnp.dot(tok[t, z], piece, preferred_element_type=jnp.float32)
                if step == 0 and side == 0:
                    acc[z] = new
                else:
                    acc[z] += new

    def give_back(part, buf, columns, base):
        buf[zpos] = acc[zpos, :, columns].astype(jnp.bfloat16)
        for i, step in enumerate(OFFSETS[1:]):
            copy = remote(
                done.at[part, wrap(zpos + step), :, columns], buf.at[zpos],
                (bsend, brecv, base), i, at_z(step),
            )
            copy.start()
            sent.append(copy)

    def take_back(buf, base):
        for i, step in enumerate(OFFSETS[1:]):
            ref = buf.at[wrap(zpos - step)]
            remote(ref, ref, (bsend, brecv, base), i, at_z(step)).wait_recv()

    def finish(part):
        @pl.loop(0, RING)
        def _(z):
            done[part, z] = acc[z].astype(jnp.bfloat16)

    token_load.wait()
    ztok.whole()
    ytok[0].whole()
    share(0, 0)
    keep(0)
    xw[0, 0].whole()
    exchange(0, 1)
    exchange(0, -1)
    keep(1)
    xw[1, 0].whole()

    lane = lax.broadcasted_iota(jnp.int32, (EXTRA, HDIM), 1)
    line = lax.broadcasted_iota(jnp.int32, (EXTRA, HDIM), 0)
    chosen = jnp.zeros((EXTRA, HDIM), jnp.int32)
    for half in range(span_count):

        def note(j, chosen, half=half):
            slot = slot_ref[jnp.maximum(sel_ref[half, j], 0)]
            owner = jnp.where(j < count_ref[half], slot // stored, -1)
            value = jnp.where(line == half, owner, slot % stored)
            here = (lane == j) & ((line == half) | (line == span_count + half))
            return jnp.where(here, value, chosen)

        chosen = lax.fori_loop(0, select_count, note, chosen)
    small[token_count:, :] = chosen.astype(jnp.float32).astype(jnp.bfloat16)

    xw[0, 0].onward()
    ztok.onward()
    for o in (-1, 1):
        ytok[o].whole()
        share(0, o)
    ytok[0].onward()
    exchange(0, 2)
    exchange(1, 1)
    exchange(1, -1)
    exchange(1, 2)
    share(-1, 0)
    share(1, 0)
    for step in (1, -1):
        exchange(0, step, receive=True)
        xw[0, -step].whole()
    xw[1, 0].onward()
    ztok.opposite()
    ytok[2].whole()
    share(0, 2)
    exchange(0, 2, receive=True)
    xw[0, 2].whole()
    for o in (-1, 1):
        ytok[o].onward()
        share(-1, o)
        share(1, o)
    xw[0, -1].onward()
    xw[0, 1].onward()
    for step in (1, -1):
        exchange(1, step, receive=True)
        xw[1, -step].whole()
    xw[0, 2].onward()
    exchange(1, 2, receive=True)
    xw[1, 2].whole()
    for o in (-1, 1):
        xw[1, o].onward()
    ytok[0].opposite()
    share(2, 0)

    def shared(step):
        for o in OFFSETS:
            share(step, o, receive=True)

    for o in OFFSETS:
        xw[0, o].opposite()
    shared(0)
    compute(0, 0)
    ytok[2].onward()
    share(-1, 2)
    share(1, 2)
    xw[1, 2].onward()
    shared(-1)
    compute(0, -1)
    ytok[-1].opposite()
    share(2, -1)
    shared(1)
    compute(0, 1)
    ytok[1].opposite()
    share(2, 1)
    ytok[2].opposite()
    share(2, 2)
    shared(2)
    compute(0, 2)
    finish(0)

    groups = (pl.ds(0, 1), pl.ds(1, RING - 1))

    def head_view(z, x, half, part):
        head = pl.ds(pl.multiple_of(z * HDIM, HDIM), HDIM)
        return q_ref.at[groups[half], x, cut(token_count)[part], head]

    def head_own(half):
        return done.at[0, groups[half], :, pl.ds(0, HDIM)]

    heads = context_gather(head_view, head_own, (qsend, qrecv, 0), zpos, xpos, sent)

    half_rows = token_count // 2
    quarter = half_rows // 2
    ranges = (
        ((0, half_rows), (0, quarter), (quarter, quarter)),
        (
            (half_rows, half_rows + EXTRA),
            (half_rows, quarter),
            (half_rows + quarter, quarter + EXTRA),
        ),
    )

    def last_view(z, x, half, part):
        return q_ref.at[z, x, pl.ds(*ranges[half][part]), pl.ds(RING * HDIM, HDIM)]

    def last_own(half):
        return small.at[pl.ds(*ranges[half][0]), :]

    last = context_gather(last_view, last_own, (qsend, qrecv, 40), zpos, xpos, sent)

    give_back(0, fifth, slice(HDIM, 2 * HDIM), 0)
    heads[0]()
    keeps = [
        pltpu.make_async_copy(
            done.at[0, :, :, pl.ds(0, HDIM)],
            q_ref.at[
                :, xpos, pl.ds(0, token_count), pl.ds(pl.multiple_of(zpos * HDIM, HDIM), HDIM)
            ],
            load_sem.at[1],
        )
    ]
    keeps[0].start()
    for o in OFFSETS:
        xw[1, o].opposite()
    compute(1, 0)
    take_back(fifth, 0)
    small[0:token_count, :] = fifth[0]
    last[0]()
    keeps.append(
        pltpu.make_async_copy(
            small, q_ref.at[zpos, xpos, :, pl.ds(RING * HDIM, HDIM)], load_sem.at[20]
        )
    )
    keeps[1].start()
    heads[1]()
    compute(1, -1)
    compute(1, 1)
    heads[2]()
    last[1]()
    compute(1, 2)
    finish(1)
    give_back(1, back, slice(0, 2 * HDIM), 3)
    heads[3]()
    last[2]()
    heads[4]()
    last[3]()
    last[4]()
    for keep_copy in keeps:
        keep_copy.wait()
    heads[5]()
    last[5]()
    look = pltpu.make_async_copy(
        q_ref.at[:, :, pl.ds(token_count, EXTRA), pl.ds(RING * HDIM, HDIM)],
        told,
        load_sem.at[21],
    )
    look.start()
    take_back(back, 3)
    for head in range(RING):
        cols = slice(head * HDIM, (head + 1) * HDIM)
        k_ref[:, cols] = back[head, :, 0:HDIM]
        v_ref[:, cols] = back[head, :, HDIM : 2 * HDIM]
    k_ref[:, RING * HDIM :] = fifth[1]
    v_ref[:, RING * HDIM :] = fifth[2]
    look.wait()

    devices = RING * RING
    lane = lax.broadcasted_iota(jnp.int32, (devices, HDIM), 1)
    before = lax.broadcasted_iota(jnp.int32, (HDIM, HDIM), 0)
    after = lax.broadcasted_iota(jnp.int32, (HDIM, HDIM), 1)
    earlier = jnp.where(before < after, 1.0, 0.0).astype(jnp.bfloat16)
    listed = told[...].reshape(devices, EXTRA, HDIM).astype(jnp.float32)
    for half in range(span_count):
        owner = listed[:, half, :]
        row = listed[:, span_count + half, :]
        mine = jnp.where((owner == me.astype(jnp.float32)) & (lane < select_count), 1.0, 0.0)
        rank = jnp.dot(mine.astype(jnp.bfloat16), earlier, preferred_element_type=jnp.float32)
        table = jnp.where(lane == cap, jnp.sum(mine, axis=1, keepdims=True), 0.0)
        for r in range(cap):
            value = jnp.sum(jnp.where(rank == r, mine * row, 0.0), axis=1, keepdims=True)
            table = jnp.where(lane == r, value, table)
        tab_ref[half] = table.astype(jnp.int32)

    for copy in sent:
        copy.wait_send()


def gather_project(tokens, wq, wk, wv, selected, counts, block_slot, cap, stored):
    token_count, depth = tokens.shape
    rows, width = wq.shape
    span_count, select_count = selected.shape
    devices = lax.axis_size("context")
    columns = lax.axis_size("tensor")
    hbm = pl.BlockSpec(memory_space=pl.ANY)
    vmem = pl.BlockSpec(memory_space=pltpu.VMEM)
    smem = pl.BlockSpec(memory_space=pltpu.SMEM)
    own = jax.ShapeDtypeStruct((token_count, width), jnp.bfloat16)
    two = 2 * HDIM

    def dma(count):
        return [pltpu.SemaphoreType.DMA((count,))] * 2

    return pl.pallas_call(
        functools.partial(project_kernel, span_count, select_count, cap, stored),
        in_specs=[hbm] * 4 + [smem] * 3,
        out_specs=[hbm] + [vmem] * 3,
        out_shape=[
            jax.ShapeDtypeStruct((RING, RING, token_count + EXTRA, width), jnp.bfloat16),
            own,
            own,
            jax.ShapeDtypeStruct((span_count, devices, HDIM), jnp.int32),
        ],
        scratch_shapes=[
            pltpu.VMEM((columns, RING, token_count, depth), jnp.bfloat16),
            pltpu.VMEM((2, RING, rows, two), jnp.bfloat16),
            pltpu.VMEM((2, RING, RING, rows, two), jnp.bfloat16),
            pltpu.VMEM((RING, token_count, two), jnp.float32),
            pltpu.VMEM((2, RING, token_count, two), jnp.bfloat16),
            pltpu.VMEM((RING, token_count, two), jnp.bfloat16),
            pltpu.VMEM((RING, token_count, HDIM), jnp.bfloat16),
            pltpu.VMEM((token_count + EXTRA, HDIM), jnp.bfloat16),
            pltpu.VMEM((RING, RING, EXTRA, HDIM), jnp.bfloat16),
            pltpu.SemaphoreType.DMA((22,)),
        ]
        + dma(36)
        + dma(38)
        + dma(6)
        + dma(80),
        compiler_params=pltpu.CompilerParams(
            collective_id=0, has_side_effects=True, vmem_limit_bytes=60 << 20
        ),
        name="gather_project",
    )(tokens, wq, wk, wv, selected, counts, block_slot)


def owner_kernel(heads, cap, tab_ref, q_ref, k_ref, v_ref, o_ref, st_ref, acc_ref):
    group, span_count, span = o_ref.shape[0], o_ref.shape[1], o_ref.shape[3]
    first = pl.program_id(0) * group
    block = k_ref.shape[1]
    columns = [slice(h * HDIM, (h + 1) * HDIM) for h in range(heads)]

    def score(i, half, h, j):
        r0 = tab_ref[half, first + i, 2 * j]
        r1 = tab_ref[half, first + i, 2 * j + 1]
        bias = jnp.where(2 * j + 1 < tab_ref[half, first + i, cap], 0.0, NEG)
        cols = columns[h]
        q = q_ref[i, half * span : (half + 1) * span, cols]
        k = jnp.concatenate([k_ref[r0, :, cols], k_ref[r1, :, cols]], 0)
        v = jnp.concatenate([v_ref[r0, :, cols], v_ref[r1, :, cols]], 0)
        s = dot_nt(k, q) * SCALE
        return jnp.concatenate([s[:block], s[block:] + bias], 0), v

    def put(i, half, h, m, l, a):
        st_ref[i, half, h : h + 1, :] = m
        st_ref[i, half, 8 + h : 9 + h, :] = l
        acc_ref[i, half, columns[h], :] = a
        o_ref[i, half, columns[h], :] = a.astype(jnp.bfloat16)

    places = [(i, half) for i in range(group) for half in range(span_count)]
    def soften(i, half, h, s, v):
        m = jnp.max(s, axis=0, keepdims=True)
        p = jnp.exp2(s - m)
        l = jnp.sum(p, axis=0, keepdims=True)
        m = jnp.where(tab_ref[half, first + i, cap] > 0, m, NEG)
        return i, half, h, m, l, p.astype(jnp.bfloat16), v

    def weigh(i, half, h, m, l, p, v):
        return i, half, h, m, l, dot_tn(v, p)

    made = [[(i, half, h, *score(i, half, h, 0)) for h in range(heads)] for i, half in places]
    results = []
    for tiles in made:
        soft = [soften(*tile) for tile in tiles]
        results += [weigh(*tile) for tile in soft]
    for result in results:
        put(*result)

    for i, half in places:
        n = tab_ref[half, first + i, cap]

        @pl.when(n > 2)
        def _(i=i, half=half, n=n):
            @pl.loop(1, (n + 1) // 2)
            def _(j):
                results = []
                for h, (s, v) in enumerate([score(i, half, h, j) for h in range(heads)]):
                    old = st_ref[i, half, h : h + 1, :]
                    m = jnp.maximum(jnp.max(s, axis=0, keepdims=True), old)
                    decay = jnp.exp2(old - m)
                    p = jnp.exp2(s - m)
                    l = jnp.sum(p, axis=0, keepdims=True)
                    l = l + st_ref[i, half, 8 + h : 9 + h, :] * decay
                    a = dot_tn(v, p.astype(jnp.bfloat16))
                    a = a + acc_ref[i, half, columns[h], :] * decay
                    results.append((i, half, h, m, l, a))
                for result in results:
                    put(*result)


def owner_attention(table, q_all, cache_keys, cache_values, heads, cap):
    tokens, width = q_all.shape[2] - EXTRA, q_all.shape[3]
    span_count, devices = table.shape[:2]
    span = tokens // span_count
    q_all = q_all.reshape(devices, tokens + EXTRA, width)
    whole = pl.BlockSpec(cache_keys.shape, lambda s, *_: (0, 0, 0), pipeline_mode=pl.Buffered(1))
    return pl.pallas_call(
        functools.partial(owner_kernel, heads, cap),
        grid_spec=pltpu.PrefetchScalarGridSpec(
            num_scalar_prefetch=1,
            grid=(devices // GROUP,),
            in_specs=[
                pl.BlockSpec((GROUP, tokens, width), lambda s, *_: (s, 0, 0)),
                whole,
                whole,
            ],
            out_specs=[
                pl.BlockSpec((GROUP, span_count, width, span), lambda s, *_: (s, 0, 0, 0)),
                pl.BlockSpec((GROUP, span_count, 16, span), lambda s, *_: (s, 0, 0, 0)),
            ],
            scratch_shapes=[pltpu.VMEM((GROUP, span_count, width, span), jnp.float32)],
        ),
        out_shape=[
            jax.ShapeDtypeStruct((devices, span_count, width, span), jnp.bfloat16),
            jax.ShapeDtypeStruct((devices, span_count, 16, span), jnp.float32),
        ],
        name="owner_attention",
    )(table, q_all, cache_keys, cache_values)


def combine_kernel(
    heads,
    o_ref, st_ref, q_ref, k_ref, v_ref,
    out_ref,
    own, query, before, relay, relay_st, got, got_st, mid, mid_st,
    relay2, relay2_st, got2, got2_st, acc, acc_st,
    load_sem, send, recv, send_st, recv_st, psend, precv,
):
    me = lax.axis_index("context")
    zpos, xpos = me // RING, lax.rem(me, RING)
    devices = RING * RING
    behind, ahead = lax.rem(me + devices - 1, devices), lax.rem(me + 1, devices)
    span = o_ref.shape[-1]
    token_count = k_ref.shape[0]
    cut = (heads + 1) // 2 * HDIM
    parts = ((0, cut), (cut, heads * HDIM - cut))
    order = (2, -1, 1, 0)

    def first_at(half, step):
        return wrap((xpos if half == 0 else zpos) + step)

    def second_at(half, step):
        return wrap((zpos if half == 0 else xpos) + step)

    def place(half, step, further):
        a, b = first_at(half, step), second_at(half, further)
        return (b, a, half) if half == 0 else (a, b, half)

    def way_of(half, further):
        return 1 if further == 2 or (further == 1 and half == 1) else -1

    loads = {}
    count = 0
    for kind in (0, 1):
        for further in order:
            for half in (0, 1):
                step = way_of(half, further) if kind == 0 else 0
                slot = (half, kind, order.index(further))
                loads[slot] = pltpu.make_async_copy(
                    o_ref.at[place(half, step, further)], own.at[slot], load_sem.at[count]
                )
                loads[slot].start()
                count += 1
    query_load = pltpu.make_async_copy(
        q_ref.at[zpos, xpos, pl.ds(0, token_count)], query, load_sem.at[count]
    )
    query_load.start()

    barrier = pltpu.get_barrier_semaphore()
    for other in (
        context_of(zpos + 1, xpos),
        context_of(zpos - 1, xpos),
        context_of(zpos, xpos + 1),
        context_of(zpos, xpos - 1),
        behind,
        ahead,
    ):
        pl.semaphore_signal(barrier, inc=1, device_id={"context": other}, device_id_type=MESH)
    pl.semaphore_wait(barrier, 6)

    started = []

    def copies(half, index, way, first, src, src_st, dst, dst_st):
        if (half == 0) == first:
            to = {"context": context_of(zpos, xpos + way)}
        else:
            to = {"context": context_of(zpos + way, xpos)}
        base = half * 18
        return (
            remote(src, dst, (send, recv, base), index, to),
            remote(src_st, dst_st, (send_st, recv_st, base), index, to),
        )

    def start(*args):
        for copy in copies(*args):
            copy.start()
            started.append(copy)

    def arrive(half, index, dst, dst_st):
        for copy in copies(half, index, 1, True, dst, dst_st, dst, dst_st):
            copy.wait_recv()

    def merge(out, out_st, sources, head_range):
        results = []
        for h in head_range:
            rows = slice(h * HDIM, (h + 1) * HDIM)
            ms = [st[h : h + 1, :] for _, st in sources]
            m = functools.reduce(jnp.maximum, ms)
            ws = [jnp.exp2(x - m) for x in ms]
            ls = [st[8 + h : 9 + h, :] * w for (_, st), w in zip(sources, ws)]
            terms = [part[rows, :].astype(jnp.float32) * w for (part, _), w in zip(sources, ws)]
            total = functools.reduce(jnp.add, terms).astype(jnp.bfloat16)
            results.append((h, rows, m, functools.reduce(jnp.add, ls), total))
        for h, rows, m, l, total in results:
            out[rows, :] = total
            out_st[h : h + 1, :] = m
            out_st[8 + h : 9 + h, :] = l

    every = range(heads)

    def forward(half, further):
        i, at = order.index(further), place(half, 2, further)
        start(
            half, i, way_of(half, further), True, o_ref.at[at], st_ref.at[at],
            relay.at[half, i], relay_st.at[half, i],
        )

    def direct(half, further):
        way = -way_of(half, further)
        i, at, side = order.index(further), place(half, way, further), 0 if way == 1 else 1
        start(
            half, 4 + i, way, True, o_ref.at[at], st_ref.at[at],
            got.at[half, side, i], got_st.at[half, side, i],
        )

    def merged(half, further):
        way = way_of(half, further)
        i, at, side = order.index(further), place(half, way, further), 0 if way == 1 else 1
        part, st = relay.at[half, i], relay_st.at[half, i]
        arrive(half, i, part, st)
        loads[half, 0, i].wait()
        merge(part, st, [(part, st), (own.at[half, 0, i], st_ref.at[at])], every)
        start(
            half, 8 + i, way, True, part, st, got.at[half, side, i], got_st.at[half, side, i]
        )

    def collect(half, further):
        i = order.index(further)
        side = 0 if way_of(half, further) == 1 else 1
        arrive(half, 4 + i, got.at[half, 1 - side, i], got_st.at[half, 1 - side, i])
        arrive(half, 8 + i, got.at[half, side, i], got_st.at[half, side, i])
        loads[half, 1, i].wait()
        merge(
            mid.at[half, i], mid_st.at[half, i],
            [(own.at[half, 1, i], st_ref.at[place(half, 0, further)])]
            + [(got.at[half, n, i], got_st.at[half, n, i]) for n in (0, 1)],
            every,
        )

    halves = (0, 1)
    for further in order:
        for half in halves:
            forward(half, further)
    for further in (2, -1):
        for half in halves:
            direct(half, further)

    key = lax.broadcasted_iota(jnp.int32, (span, span), 0)
    row = lax.broadcasted_iota(jnp.int32, (span, span), 1)

    def local(half, keys_of, values_of, bias, first):
        results = []
        for h in every:
            cols = slice(h * HDIM, (h + 1) * HDIM)
            s = dot_nt(keys_of(cols), query[half * span : (half + 1) * span, cols]) * SCALE
            s = jnp.where(key <= row, s, NEG) if bias is None else s + bias
            m = jnp.max(s, axis=0, keepdims=True)
            if not first:
                old = acc_st[half, h : h + 1, :]
                m = jnp.maximum(m, old)
                decay = jnp.exp2(old - m)
            p = jnp.exp2(s - m)
            l = jnp.sum(p, axis=0, keepdims=True)
            a = dot_tn(values_of(cols), p.astype(jnp.bfloat16))
            if not first:
                l = l + acc_st[half, 8 + h : 9 + h, :] * decay
                a = a + acc[half, cols, :] * decay
            results.append((h, cols, m, l, a))
        for h, cols, m, l, a in results:
            acc_st[half, h : h + 1, :] = m
            acc_st[half, 8 + h : 9 + h, :] = l
            acc[half, cols, :] = a

    query_load.wait()
    for half in halves:
        rows = slice(half * span, (half + 1) * span)
        local(half, lambda c, r=rows: k_ref[r, c], lambda c, r=rows: v_ref[r, c], None, True)

    for further in (2, -1):
        for half in halves:
            merged(half, further)
    for further in (1, 0):
        for half in halves:
            direct(half, further)
    prior = []
    for i, ref in enumerate((k_ref, v_ref)):
        prior.append(
            remote(
                ref.at[pl.ds(token_count - span, span), :], before.at[i], (psend, precv, 0), i,
                {"context": ahead},
            )
        )
        prior[-1].start()
    for further in (1, 0):
        for half in halves:
            merged(half, further)
    local(1, lambda c: k_ref[0:span, c], lambda c: v_ref[0:span, c], 0.0, False)

    for half in halves:
        collect(half, 2)
        for side, way in ((0, 1), (1, -1)):
            rows = pl.ds(*parts[side])
            start(
                half, 12 + side, way, False, mid.at[half, 0, rows], mid_st.at[half, 0],
                relay2.at[half, rows], relay2_st.at[half, side],
            )
    for side, way in ((1, -1), (0, 1)):
        for half in halves:
            i = order.index(way)
            collect(half, way)
            other = pl.ds(*parts[1 - side])
            start(
                half, 14 + side, way, False, mid.at[half, i, other], mid_st.at[half, i],
                got2.at[half, side, other], got2_st.at[half, side, 1 - side],
            )
    for half in halves:
        for side, way in ((0, 1), (1, -1)):
            i = order.index(way)
            rows = pl.ds(*parts[side])
            part, st = relay2.at[half], relay2_st.at[half, side]
            arrive(half, 12 + side, relay2.at[half, rows], st)
            merge(
                part, st, [(part, st), (mid.at[half, i], mid_st.at[half, i])],
                range(parts[side][0] // HDIM, sum(parts[side]) // HDIM),
            )
            start(
                half, 16 + side, way, False, relay2.at[half, rows], st,
                got2.at[half, side, rows], got2_st.at[half, side, side],
            )

    for copy in prior:
        copy.wait_recv()
    local(
        0, lambda c: before[0, :, c], lambda c: before[1, :, c], jnp.where(me > 0, 0.0, NEG), False
    )
    last = order.index(0)
    for half in halves:
        collect(half, 0)
    for half in halves:
        for side in (0, 1):
            for index, which in ((14 + side, 1 - side), (16 + side, side)):
                arrive(
                    half, index,
                    got2.at[half, side, pl.ds(*parts[which])], got2_st.at[half, side, which],
                )
        for h in every:
            cols = slice(h * HDIM, (h + 1) * HDIM)
            which = 0 if h * HDIM < cut else 1
            sources = [(mid.at[half, last], mid_st.at[half, last])]
            sources += [(got2.at[half, i], got2_st.at[half, i, which]) for i in (0, 1)]
            old = acc_st[half, h : h + 1, :]
            ms = [st[h : h + 1, :] for _, st in sources]
            m = functools.reduce(jnp.maximum, ms, old)
            decay = jnp.exp2(old - m)
            total = acc_st[half, 8 + h : 9 + h, :] * decay
            a = acc[half, cols, :] * decay
            for (part, st), x in zip(sources, ms):
                w = jnp.exp2(x - m)
                total = total + st[8 + h : 9 + h, :] * w
                a = a + part[cols, :].astype(jnp.float32) * w
            out_ref[half * span : (half + 1) * span, cols] = jnp.transpose(a / total).astype(
                out_ref.dtype
            )

    for copy in started + prior:
        copy.wait_send()


def combine(o, st, q_all, k, v, heads):
    span_count, width, span = o.shape[1:]
    rows = st.shape[2]
    o = o.reshape(RING, RING, span_count, width, span)
    st = st.reshape(RING, RING, span_count, rows, span)
    vmem = pl.BlockSpec(memory_space=pltpu.VMEM)
    hbm = pl.BlockSpec(memory_space=pl.ANY)

    def part(*lead):
        return pltpu.VMEM(lead + (width, span), jnp.bfloat16)

    def stats(*lead):
        return pltpu.VMEM(lead + (rows, span), jnp.float32)

    return pl.pallas_call(
        functools.partial(combine_kernel, heads),
        in_specs=[hbm, vmem, hbm, vmem, vmem],
        out_specs=vmem,
        out_shape=jax.ShapeDtypeStruct(k.shape, jnp.bfloat16),
        scratch_shapes=[
            part(2, 2, RING),
            pltpu.VMEM(k.shape, jnp.bfloat16),
            pltpu.VMEM((2, span, width), jnp.bfloat16),
            part(2, RING),
            stats(2, RING),
            part(2, 2, RING),
            stats(2, 2, RING),
            part(2, RING),
            stats(2, RING),
            part(2),
            stats(2, 2),
            part(2, 2),
            stats(2, 2, 2),
            pltpu.VMEM((2, width, span), jnp.float32),
            stats(2),
            pltpu.SemaphoreType.DMA((17,)),
        ]
        + [pltpu.SemaphoreType.DMA((36,))] * 4
        + [pltpu.SemaphoreType.DMA((2,))] * 2,
        compiler_params=pltpu.CompilerParams(
            collective_id=1, has_side_effects=True, vmem_limit_bytes=60 << 20
        ),
        name="combine",
    )(o, st, q_all, k, v)


def shards(
    tokens,
    query_weight,
    key_weight,
    value_weight,
    cache_keys,
    cache_values,
    selected,
    counts,
    block_slot,
):
    heads = query_weight.shape[1] // HDIM
    span_count, select_count = selected.shape
    devices = lax.axis_size("context")
    cap = max(2, 2 * span_count * select_count // devices)

    stored = cache_keys.shape[0]
    q_all, k, v, table = gather_project(
        tokens, query_weight, key_weight, value_weight, selected, counts, block_slot, cap, stored
    )
    o, st = owner_attention(table, q_all, cache_keys, cache_values, heads, cap)
    return combine(o, st, q_all, k, v, heads)


def solution(mesh):
    placed = (
        P("context", "tensor"),
        P("context", "tensor"),
        P("context", "tensor"),
        P("context", "tensor"),
        P("context", None, "tensor"),
        P("context", None, "tensor"),
        P("context", None),
        P("context"),
        P(),
    )
    return jax.shard_map(
        shards, mesh=mesh, in_specs=placed, out_specs=P("context", "tensor"), check_vma=False
    )
```

```python
import functools

import jax
import jax.numpy as jnp
from jax import lax
from jax.experimental import pallas as pl
from jax.experimental.pallas import tpu as pltpu
from jax.sharding import PartitionSpec as P

HDIM = 128
NEG = -1e30
MESH = pl.DeviceIdType.MESH
EXTRA = 16
GROUP = 2
SCALE = HDIM ** (-0.5) * 1.4426950408889634


def dot_nt(a, b):
    return lax.dot_general(a, b, (((1,), (1,)), ((), ())), preferred_element_type=jnp.float32)


def dot_tn(a, b):
    return lax.dot_general(a, b, (((0,), (0,)), ((), ())), preferred_element_type=jnp.float32)


RING = 4
OFFSETS = (0, -1, 1, 2)


def wrap(position):
    return lax.rem(position + RING, RING)


def context_of(zpos, xpos):
    return wrap(zpos) * RING + wrap(xpos)


class Ring:
    def __init__(self, view, to, sems, own=None):
        self.view, self.to, self.sems, self.own = view, to, sems, own

    def copy(self, index, step):
        ref = self.view(step, max(0, index - 1))
        src = self.own if step == 0 and self.own is not None else ref
        return remote(src, ref, self.sems, min(index, 2), self.to(1 if index % 2 == 0 else -1))

    def start(self, index):
        self.copy(index, (0, 0, -1, 1)[index]).start()

    def whole(self):
        self.start(0)
        self.start(1)

    def onward(self):
        self.copy(0, -1).wait_recv()
        self.start(2)
        self.copy(1, 1).wait_recv()
        self.start(3)

    def opposite(self):
        ref = self.view(2, 0)
        remote(ref, ref, self.sems, 2, self.to(1)).wait_recv()


def remote(src, dst, sems, index, to):
    send, recv, base = sems
    return pltpu.make_async_remote_copy(
        src_ref=src,
        dst_ref=dst,
        send_sem=send,
        recv_sem=recv.at[base + index],
        device_id=to,
        device_id_type=MESH,
    )


def context_gather(view, own, sems, zpos, xpos, halves=(0, 1)):
    rings = {}

    def make(half, phase):
        along_x = (half == 0) == (phase == 0)
        first = 0 if phase == 0 else OFFSETS[phase - 1]

        def piece(step, part):
            dz, dx = (first, step) if along_x else (step, first)
            return view(wrap(zpos + dz), wrap(xpos + dx), half, part)

        def to(way):
            dz, dx = (0, way) if along_x else (way, 0)
            return {"context": context_of(zpos + dz, xpos + dx)}

        send, recv, base = sems
        source = own(half) if first == 0 else None
        return Ring(piece, to, (send, recv, base + halves.index(half) * 15 + phase * 3), source)

    for half in halves:
        for phase in range(5):
            rings[half, phase] = make(half, phase)

    def own():
        for half in halves:
            rings[half, 0].whole()
            rings[half, 1].whole()

    def neighbours():
        for half in halves:
            rings[half, 0].onward()
            rings[half, 2].whole()
            rings[half, 3].whole()
        for half in halves:
            rings[half, 1].onward()

    def far():
        for half in halves:
            rings[half, 0].opposite()
            rings[half, 4].whole()

    def corners():
        for half in halves:
            rings[half, 2].onward()
            rings[half, 3].onward()

    def last():
        for half in halves:
            rings[half, 4].onward()

    def rest():
        for half in halves:
            for phase in (1, 2, 3, 4):
                rings[half, phase].opposite()

    return [own, neighbours, far, corners, last, rest]


def project_kernel(
    span_count, select_count, cap, stored,
    tok_ref, wq_ref, wk_ref, wv_ref, sel_ref, count_ref, slot_ref,
    q_ref, k_ref, v_ref, tab_ref,
    tok, stage, w, acc, done, back, fifth, small, told,
    load_sem, send, trecv, wrecv, brecv, qrecv,
):
    me = lax.axis_index("context")
    zpos, xpos = me // RING, lax.rem(me, RING)
    col = lax.axis_index("tensor")
    ypos, core = col // 2, lax.rem(col, 2)
    token_count, depth = tok.shape[2], tok.shape[3]
    rows = w.shape[3]

    token_load = pltpu.make_async_copy(tok_ref, tok.at[col, zpos], load_sem.at[0])
    token_load.start()
    for part in (0, 1):
        for to in range(RING):
            left = (wq_ref, wk_ref, wv_ref, wq_ref)[to]
            pair = ((wq_ref, to), (left, RING)) if part == 0 else ((wk_ref, to), (wv_ref, to))
            for i, (ref, head) in enumerate(pair):
                load = pltpu.make_async_copy(
                    ref.at[:, pl.ds(head * HDIM, HDIM)],
                    stage.at[part, to, :, pl.ds(i * HDIM, HDIM)],
                    load_sem.at[2 + part],
                )
                load.start()

    def at_x(way):
        return {"context": context_of(zpos, xpos + way)}

    def at_z(way):
        return {"context": context_of(zpos + way, xpos)}

    def at_y(way):
        return {"tensor": wrap(ypos + way) * 2 + core}

    mate = {"tensor": ypos * 2 + 1 - core}
    barrier = pltpu.get_barrier_semaphore()
    partners = [at_x(1), at_x(-1), at_z(1), at_z(-1), at_z(2), at_y(1), at_y(-1), mate]
    for other in partners:
        pl.semaphore_signal(barrier, inc=1, device_id=other, device_id_type=MESH)
    pl.semaphore_wait(barrier, len(partners))

    def cut(size):
        return (pl.ds(0, size), pl.ds(0, size // 2), pl.ds(size // 2, size // 2))

    ztok = Ring(
        lambda step, part: tok.at[col, wrap(zpos + step), cut(token_count)[part]],
        at_z, (send.at[0], trecv, 0),
    )
    ytok = {
        o: Ring(
            lambda step, part, o=o: tok.at[
                wrap(ypos + step) * 2 + core, wrap(zpos + o), cut(token_count)[part]
            ],
            at_y, (send.at[0], trecv, 3 + 3 * i),
        )
        for i, o in enumerate(OFFSETS)
    }

    def share(step, o):
        ref = tok.at[wrap(ypos + step) * 2 + core, wrap(zpos + o)]
        remote(ref, ref, (send.at[1], trecv, 15), OFFSETS.index(o), mate).start()

    def shared(o):
        ref = tok.at[pl.ds(0, RING), 0]
        remote(ref, ref, (send.at[1], trecv, 15), OFFSETS.index(o), mate).wait_recv()

    def exchange(part, step, receive=False):
        index = part * 3 + OFFSETS.index(step) - 1
        src = stage.at[part, wrap(zpos + step)]
        if receive:
            dst = w.at[part, wrap(zpos - step), xpos]
            remote(src, dst, (send.at[2], wrecv, 0), index, at_z(step)).wait_recv()
        else:
            dst = w.at[part, zpos, xpos]
            remote(src, dst, (send.at[2], wrecv, 0), index, at_z(step)).start()

    xw = {
        (part, o): Ring(
            lambda step, piece, part=part, o=o: w.at[
                part, wrap(zpos + o), wrap(xpos + step), cut(rows)[piece]
            ],
            at_x, (send.at[3], wrecv, 6 + part * 12 + 3 * i),
        )
        for part in (0, 1)
        for i, o in enumerate(OFFSETS)
    }

    def keep(part):
        whole = stage.at[part]
        pltpu.make_async_copy(whole, whole, load_sem.at[2 + part]).wait()
        copy = pltpu.make_async_copy(
            stage.at[part, zpos], w.at[part, zpos, xpos], load_sem.at[4 + part]
        )
        copy.start()
        copy.wait()

    def queries(o):
        z = wrap(zpos + o)

        @pl.loop(0, tok.shape[0])
        def _(t):
            piece = w[0, t // 2, pl.ds(lax.rem(t, 2) * 2, 2)].reshape(depth, w.shape[4])
            new = jnp.dot(tok[t, z], piece, preferred_element_type=jnp.float32)

            @pl.when(t == 0)
            def _():
                acc[z] = new

            @pl.when(t > 0)
            def _():
                acc[z] += new

        done[0, z] = acc[z].astype(jnp.bfloat16)
        last_head = slice(HDIM, 2 * HDIM)
        if o == 0:
            fifth[zpos] = acc[z, :, last_head].astype(jnp.bfloat16)
        else:
            src = done.at[0, z, :, last_head]
            remote(src, fifth.at[zpos], (send.at[4], brecv, 0), 0, at_z(o)).start()

    def compute(step):
        for side in (0, 1):
            t = wrap(ypos + step) * 2 + side
            piece = w[1, wrap(ypos + step), 2 * side : 2 * side + 2].reshape(depth, w.shape[4])

            @pl.loop(0, RING)
            def _(z):
                new = jnp.dot(tok[t, z], piece, preferred_element_type=jnp.float32)
                if step == 0 and side == 0:
                    acc[z] = new
                else:
                    acc[z] += new

    def give_back():
        @pl.loop(0, RING)
        def _(z):
            done[1, z] = acc[z].astype(jnp.bfloat16)

        back[zpos] = acc[zpos].astype(jnp.bfloat16)
        for step in OFFSETS[1:]:
            src = done.at[1, wrap(zpos + step)]
            remote(src, back.at[zpos], (send.at[5], brecv, 1), 0, at_z(step)).start()

    def take_back(buf, index):
        ref = buf.at[pl.ds(0, RING - 1)]
        remote(ref, ref, (send.at[4], brecv, index), 0, at_z(1)).wait_recv()

    def heads_of(o):
        def view(z, x, half, part):
            head = pl.ds(pl.multiple_of(z * HDIM, HDIM), HDIM)
            return q_ref.at[wrap(z + o), x, cut(token_count)[part], head]

        def own(half):
            return done.at[0, wrap(zpos + o), :, pl.ds(0, HDIM)]

        i = OFFSETS.index(o)
        return context_gather(
            view, own, (send.at[6], qrecv, 30 + 15 * i), zpos, xpos, ((0,), (1,))[i % 2]
        )

    heads = {o: heads_of(o) for o in OFFSETS}

    half_rows = token_count // 2
    quarter = half_rows // 2
    ranges = (
        ((0, half_rows), (0, quarter), (quarter, quarter)),
        (
            (half_rows, half_rows + EXTRA),
            (half_rows, quarter),
            (half_rows + quarter, quarter + EXTRA),
        ),
    )

    def last_view(z, x, half, part):
        return q_ref.at[z, x, pl.ds(*ranges[half][part]), pl.ds(RING * HDIM, HDIM)]

    def last_own(half):
        return small.at[pl.ds(*ranges[half][0]), :]

    last = context_gather(last_view, last_own, (send.at[7], qrecv, 0), zpos, xpos)

    token_load.wait()
    ztok.whole()
    ytok[0].whole()
    share(0, 0)
    keep(0)
    xw[0, 0].whole()
    exchange(0, 1)
    exchange(0, -1)
    keep(1)

    lane = lax.broadcasted_iota(jnp.int32, (EXTRA, HDIM), 1)
    line = lax.broadcasted_iota(jnp.int32, (EXTRA, HDIM), 0)
    chosen = jnp.zeros((EXTRA, HDIM), jnp.int32)
    for half in range(span_count):

        def note(j, chosen, half=half):
            slot = slot_ref[jnp.maximum(sel_ref[half, j], 0)]
            owner = jnp.where(j < count_ref[half], slot // stored, -1)
            value = jnp.where(line == half, owner, slot % stored)
            here = (lane == j) & ((line == half) | (line == span_count + half))
            return jnp.where(here, value, chosen)

        chosen = lax.fori_loop(0, select_count, note, chosen)
    small[token_count:, :] = chosen.astype(jnp.float32).astype(jnp.bfloat16)

    xw[0, 0].onward()
    ztok.onward()
    ytok[0].onward()
    for o in (-1, 1):
        ytok[o].whole()
        share(0, o)
    exchange(0, 2)
    xw[1, 0].whole()
    exchange(1, 1)
    exchange(1, -1)
    exchange(1, 2)
    share(-1, 0)
    share(1, 0)
    for step in (1, -1):
        exchange(0, step, receive=True)
        xw[0, -step].whole()
    ztok.opposite()
    ytok[2].whole()
    share(0, 2)
    exchange(0, 2, receive=True)
    xw[0, 2].whole()
    ytok[-1].onward()
    share(-1, -1)
    share(1, -1)
    ytok[0].opposite()
    share(2, 0)
    xw[0, -1].onward()
    xw[0, 1].onward()
    xw[1, 0].onward()
    ytok[1].onward()
    share(-1, 1)
    share(1, 1)
    xw[0, 2].onward()
    for step in (1, -1):
        exchange(1, step, receive=True)
        xw[1, -step].whole()
    exchange(1, 2, receive=True)
    xw[1, 2].whole()
    for o in OFFSETS:
        xw[0, o].opposite()
    shared(0)
    queries(0)
    heads[0][0]()
    ytok[-1].opposite()
    share(2, -1)
    xw[1, -1].onward()
    xw[1, 1].onward()
    ytok[2].onward()
    share(-1, 2)
    share(1, 2)
    shared(-1)
    queries(-1)
    heads[-1][0]()
    ytok[1].opposite()
    share(2, 1)
    xw[1, 2].onward()
    heads[0][1]()
    shared(1)
    queries(1)
    heads[1][0]()
    ytok[2].opposite()
    share(2, 2)
    heads[-1][1]()
    shared(2)
    queries(2)
    heads[2][0]()
    keeps = [
        pltpu.make_async_copy(
            done.at[0, :, :, pl.ds(0, HDIM)],
            q_ref.at[
                :, xpos, pl.ds(0, token_count), pl.ds(pl.multiple_of(zpos * HDIM, HDIM), HDIM)
            ],
            load_sem.at[1],
        )
    ]
    keeps[0].start()
    heads[0][2]()
    heads[1][1]()
    take_back(fifth, 0)
    small[0:token_count, :] = fifth[0]
    last[0]()
    keeps.append(
        pltpu.make_async_copy(
            small, q_ref.at[zpos, xpos, :, pl.ds(RING * HDIM, HDIM)], load_sem.at[6]
        )
    )
    keeps[1].start()
    for o in OFFSETS:
        xw[1, o].opposite()
    compute(0)
    heads[-1][2]()
    heads[0][3]()
    heads[2][1]()
    compute(-1)
    last[1]()
    heads[1][2]()
    heads[-1][3]()
    heads[0][4]()
    compute(1)
    heads[2][2]()
    heads[1][3]()
    last[2]()
    compute(2)
    give_back()
    heads[-1][4]()
    heads[2][3]()
    last[3]()
    heads[1][4]()
    heads[2][4]()
    last[4]()
    for keep_copy in keeps:
        keep_copy.wait()
    for o in OFFSETS:
        heads[o][5]()
    last[5]()
    look = pltpu.make_async_copy(
        q_ref.at[:, :, pl.ds(token_count, EXTRA), pl.ds(RING * HDIM, HDIM)],
        told,
        load_sem.at[7],
    )
    look.start()
    take_back(back, 1)
    for head in range(RING):
        cols = slice(head * HDIM, (head + 1) * HDIM)
        k_ref[:, cols] = back[head, :, 0:HDIM]
        v_ref[:, cols] = back[head, :, HDIM : 2 * HDIM]
    k_ref[:, RING * HDIM :] = fifth[1]
    v_ref[:, RING * HDIM :] = fifth[2]
    look.wait()

    devices = RING * RING
    lane = lax.broadcasted_iota(jnp.int32, (devices, HDIM), 1)
    before = lax.broadcasted_iota(jnp.int32, (HDIM, HDIM), 0)
    after = lax.broadcasted_iota(jnp.int32, (HDIM, HDIM), 1)
    earlier = jnp.where(before < after, 1.0, 0.0).astype(jnp.bfloat16)
    listed = told[...].reshape(devices, EXTRA, HDIM).astype(jnp.float32)
    for half in range(span_count):
        owner = listed[:, half, :]
        row = listed[:, span_count + half, :]
        mine = jnp.where((owner == me.astype(jnp.float32)) & (lane < select_count), 1.0, 0.0)
        rank = jnp.dot(mine.astype(jnp.bfloat16), earlier, preferred_element_type=jnp.float32)
        table = jnp.where(lane == cap, jnp.sum(mine, axis=1, keepdims=True), 0.0)
        for r in range(cap):
            value = jnp.sum(jnp.where(rank == r, mine * row, 0.0), axis=1, keepdims=True)
            table = jnp.where(lane == r, value, table)
        tab_ref[half] = table.astype(jnp.int32)

    for index, ref in enumerate(
        (
            tok.at[pl.ds(0, 5), pl.ds(0, 3)],
            tok.at[pl.ds(0, 4)],
            w.at[pl.ds(0, 2), pl.ds(0, 3), 0],
            w.at[pl.ds(0, 2), pl.ds(0, 3)],
            fifth.at[pl.ds(0, 3)],
            back.at[pl.ds(0, 3)],
            q_ref.at[:, pl.ds(0, 3), pl.ds(0, token_count), :],
            q_ref.at[0, pl.ds(0, 3)],
        )
    ):
        remote(ref, ref, (send.at[index], brecv, 0), 0, at_z(1)).wait_send()


def gather_project(tokens, wq, wk, wv, selected, counts, block_slot, cap, stored):
    token_count, depth = tokens.shape
    rows, width = wq.shape
    span_count, select_count = selected.shape
    devices = lax.axis_size("context")
    columns = lax.axis_size("tensor")
    hbm = pl.BlockSpec(memory_space=pl.ANY)
    vmem = pl.BlockSpec(memory_space=pltpu.VMEM)
    smem = pl.BlockSpec(memory_space=pltpu.SMEM)
    own = jax.ShapeDtypeStruct((token_count, width), jnp.bfloat16)
    two = 2 * HDIM

    return pl.pallas_call(
        functools.partial(project_kernel, span_count, select_count, cap, stored),
        in_specs=[hbm] * 4 + [smem] * 3,
        out_specs=[hbm] + [vmem] * 3,
        out_shape=[
            jax.ShapeDtypeStruct((RING, RING, token_count + EXTRA, width), jnp.bfloat16),
            own,
            own,
            jax.ShapeDtypeStruct((span_count, devices, HDIM), jnp.int32),
        ],
        scratch_shapes=[
            pltpu.VMEM((columns, RING, token_count, depth), jnp.bfloat16),
            pltpu.VMEM((2, RING, rows, two), jnp.bfloat16),
            pltpu.VMEM((2, RING, RING, rows, two), jnp.bfloat16),
            pltpu.VMEM((RING, token_count, two), jnp.float32),
            pltpu.VMEM((2, RING, token_count, two), jnp.bfloat16),
            pltpu.VMEM((RING, token_count, two), jnp.bfloat16),
            pltpu.VMEM((RING, token_count, HDIM), jnp.bfloat16),
            pltpu.VMEM((token_count + EXTRA, HDIM), jnp.bfloat16),
            pltpu.VMEM((RING, RING, EXTRA, HDIM), jnp.bfloat16),
        ]
        + [pltpu.SemaphoreType.DMA((count,)) for count in (8, 8, 19, 30, 2, 90)],
        compiler_params=pltpu.CompilerParams(
            collective_id=0, has_side_effects=True, vmem_limit_bytes=60 << 20
        ),
        name="gather_project",
    )(tokens, wq, wk, wv, selected, counts, block_slot)


def owner_kernel(heads, cap, tab_ref, q_ref, k_ref, v_ref, o_ref, st_ref, acc_ref):
    group, span_count, span = o_ref.shape[0], o_ref.shape[1], o_ref.shape[3]
    first = pl.program_id(0) * group
    block = k_ref.shape[1]
    columns = [slice(h * HDIM, (h + 1) * HDIM) for h in range(heads)]

    def score(i, half, h, j):
        r0 = tab_ref[half, first + i, 2 * j]
        r1 = tab_ref[half, first + i, 2 * j + 1]
        bias = jnp.where(2 * j + 1 < tab_ref[half, first + i, cap], 0.0, NEG)
        cols = columns[h]
        q = q_ref[i, half * span : (half + 1) * span, cols]
        k = jnp.concatenate([k_ref[r0, :, cols], k_ref[r1, :, cols]], 0)
        v = jnp.concatenate([v_ref[r0, :, cols], v_ref[r1, :, cols]], 0)
        s = dot_nt(k, q) * SCALE
        return jnp.concatenate([s[:block], s[block:] + bias], 0), v

    def put(i, half, h, m, l, a):
        st_ref[i, half, h : h + 1, :] = m
        st_ref[i, half, 8 + h : 9 + h, :] = l
        acc_ref[i, half, columns[h], :] = a
        o_ref[i, half, columns[h], :] = a.astype(jnp.bfloat16)

    places = [(i, half) for i in range(group) for half in range(span_count)]
    def soften(i, half, h, s, v):
        m = jnp.max(s, axis=0, keepdims=True)
        p = jnp.exp2(s - m)
        l = jnp.sum(p, axis=0, keepdims=True)
        m = jnp.where(tab_ref[half, first + i, cap] > 0, m, NEG)
        return i, half, h, m, l, p.astype(jnp.bfloat16), v

    def weigh(i, half, h, m, l, p, v):
        return i, half, h, m, l, dot_tn(v, p)

    made = [[(i, half, h, *score(i, half, h, 0)) for h in range(heads)] for i, half in places]
    results = []
    for tiles in made:
        soft = [soften(*tile) for tile in tiles]
        results += [weigh(*tile) for tile in soft]
    for result in results:
        put(*result)

    for i, half in places:
        n = tab_ref[half, first + i, cap]

        @pl.when(n > 2)
        def _(i=i, half=half, n=n):
            @pl.loop(1, (n + 1) // 2)
            def _(j):
                results = []
                for h, (s, v) in enumerate([score(i, half, h, j) for h in range(heads)]):
                    old = st_ref[i, half, h : h + 1, :]
                    m = jnp.maximum(jnp.max(s, axis=0, keepdims=True), old)
                    decay = jnp.exp2(old - m)
                    p = jnp.exp2(s - m)
                    l = jnp.sum(p, axis=0, keepdims=True)
                    l = l + st_ref[i, half, 8 + h : 9 + h, :] * decay
                    a = dot_tn(v, p.astype(jnp.bfloat16))
                    a = a + acc_ref[i, half, columns[h], :] * decay
                    results.append((i, half, h, m, l, a))
                for result in results:
                    put(*result)


def owner_attention(table, q_all, cache_keys, cache_values, heads, cap):
    tokens, width = q_all.shape[2] - EXTRA, q_all.shape[3]
    span_count, devices = table.shape[:2]
    span = tokens // span_count
    q_all = q_all.reshape(devices, tokens + EXTRA, width)
    whole = pl.BlockSpec(cache_keys.shape, lambda s, *_: (0, 0, 0), pipeline_mode=pl.Buffered(1))
    return pl.pallas_call(
        functools.partial(owner_kernel, heads, cap),
        grid_spec=pltpu.PrefetchScalarGridSpec(
            num_scalar_prefetch=1,
            grid=(devices // GROUP,),
            in_specs=[
                pl.BlockSpec((GROUP, tokens, width), lambda s, *_: (s, 0, 0)),
                whole,
                whole,
            ],
            out_specs=[
                pl.BlockSpec((GROUP, span_count, width, span), lambda s, *_: (s, 0, 0, 0)),
                pl.BlockSpec((GROUP, span_count, 16, span), lambda s, *_: (s, 0, 0, 0)),
            ],
            scratch_shapes=[pltpu.VMEM((GROUP, span_count, width, span), jnp.float32)],
        ),
        out_shape=[
            jax.ShapeDtypeStruct((devices, span_count, width, span), jnp.bfloat16),
            jax.ShapeDtypeStruct((devices, span_count, 16, span), jnp.float32),
        ],
        name="owner_attention",
    )(table, q_all, cache_keys, cache_values)


def combine_kernel(
    heads,
    o_ref, st_ref, q_ref, k_ref, v_ref,
    out_ref,
    own, query, before, relay, relay_st, got, got_st, mid, mid_st,
    relay2, relay2_st, got2, got2_st, acc, acc_st,
    load_sem, send, recv, recv_st, precv,
):
    me = lax.axis_index("context")
    zpos, xpos = me // RING, lax.rem(me, RING)
    devices = RING * RING
    behind, ahead = lax.rem(me + devices - 1, devices), lax.rem(me + 1, devices)
    span = o_ref.shape[-1]
    token_count = k_ref.shape[0]
    cut = (heads + 1) // 2 * HDIM
    parts = ((0, cut), (cut, heads * HDIM - cut))
    order = (2, -1, 1, 0)

    def first_at(half, step):
        return wrap((xpos if half == 0 else zpos) + step)

    def second_at(half, step):
        return wrap((zpos if half == 0 else xpos) + step)

    def place(half, step, further):
        a, b = first_at(half, step), second_at(half, further)
        return (b, a, half) if half == 0 else (a, b, half)

    def way_of(half, further):
        return 1 if further == 2 or (further == 1 and half == 1) else -1

    def load(ref, dst, index):
        return pltpu.make_async_copy(ref, dst, load_sem.at[index])

    for kind in (0, 1):
        for further in order:
            for half in (0, 1):
                step = way_of(half, further) if kind == 0 else 0
                slot = (half, kind, order.index(further))
                load(o_ref.at[place(half, step, further)], own.at[slot], 0).start()
    query_load = load(q_ref.at[zpos, xpos, pl.ds(0, token_count)], query, 1)
    query_load.start()

    barrier = pltpu.get_barrier_semaphore()
    for other in (
        context_of(zpos + 1, xpos),
        context_of(zpos - 1, xpos),
        context_of(zpos, xpos + 1),
        context_of(zpos, xpos - 1),
        behind,
        ahead,
    ):
        pl.semaphore_signal(barrier, inc=1, device_id={"context": other}, device_id_type=MESH)
    pl.semaphore_wait(barrier, 6)

    def copies(half, index, way, src, src_st, dst, dst_st):
        first = index < 8
        if (half == 0) == first:
            to = {"context": context_of(zpos, xpos + way)}
        else:
            to = {"context": context_of(zpos + way, xpos)}
        kind = 0 if first else 2
        return (
            remote(src, dst, (send.at[kind], recv, half * 11), index, to),
            remote(src_st, dst_st, (send.at[kind + 1], recv_st, half * 11), index, to),
        )

    def start(*args):
        for copy in copies(*args):
            copy.start()

    def arrive(half, index, dst, dst_st):
        for copy in copies(half, index, 1, dst, dst_st, dst, dst_st):
            copy.wait_recv()

    def merge(out, out_st, sources, head_range):
        results = []
        for h in head_range:
            rows = slice(h * HDIM, (h + 1) * HDIM)
            ms = [st[h : h + 1, :] for _, st in sources]
            m = functools.reduce(jnp.maximum, ms)
            ws = [jnp.exp2(x - m) for x in ms]
            ls = [st[8 + h : 9 + h, :] * w for (_, st), w in zip(sources, ws)]
            terms = [part[rows, :].astype(jnp.float32) * w for (part, _), w in zip(sources, ws)]
            total = functools.reduce(jnp.add, terms).astype(jnp.bfloat16)
            results.append((h, rows, m, functools.reduce(jnp.add, ls), total))
        for h, rows, m, l, total in results:
            out[rows, :] = total
            out_st[h : h + 1, :] = m
            out_st[8 + h : 9 + h, :] = l

    every = range(heads)

    def forward(half, further):
        i, at = order.index(further), place(half, 2, further)
        start(
            half, i, way_of(half, further), o_ref.at[at], st_ref.at[at],
            relay.at[half, i], relay_st.at[half, i],
        )

    def direct(half, further):
        way = -way_of(half, further)
        i, at, side = order.index(further), place(half, way, further), 0 if way == 1 else 1
        start(
            half, 4 + i, way, o_ref.at[at], st_ref.at[at],
            got.at[half, side, i], got_st.at[half, side, i],
        )

    def merged(half, further):
        way = way_of(half, further)
        i, at, side = order.index(further), place(half, way, further), 0 if way == 1 else 1
        part, st = relay.at[half, i], relay_st.at[half, i]
        arrive(half, i, part, st)
        merge(part, st, [(part, st), (own.at[half, 0, i], st_ref.at[at])], every)
        start(
            half, 4 + i, way, part, st, got.at[half, side, i], got_st.at[half, side, i]
        )

    def collect(half, further):
        i = order.index(further)
        both = pl.ds(0, 2)
        arrive(half, 4 + i, got.at[half, both, i], got_st.at[half, both, i])
        merge(
            mid.at[half, i], mid_st.at[half, i],
            [(own.at[half, 1, i], st_ref.at[place(half, 0, further)])]
            + [(got.at[half, n, i], got_st.at[half, n, i]) for n in (0, 1)],
            every,
        )

    halves = (0, 1)
    for further in order:
        for half in halves:
            forward(half, further)
    for further in (2, -1):
        for half in halves:
            direct(half, further)

    key = lax.broadcasted_iota(jnp.int32, (span, span), 0)
    row = lax.broadcasted_iota(jnp.int32, (span, span), 1)

    def local(half, keys_of, values_of, bias, first):
        results = []
        for h in every:
            cols = slice(h * HDIM, (h + 1) * HDIM)
            s = dot_nt(keys_of(cols), query[half * span : (half + 1) * span, cols]) * SCALE
            s = jnp.where(key <= row, s, NEG) if bias is None else s + bias
            m = jnp.max(s, axis=0, keepdims=True)
            if not first:
                old = acc_st[half, h : h + 1, :]
                m = jnp.maximum(m, old)
                decay = jnp.exp2(old - m)
            p = jnp.exp2(s - m)
            l = jnp.sum(p, axis=0, keepdims=True)
            a = dot_tn(values_of(cols), p.astype(jnp.bfloat16))
            if not first:
                l = l + acc_st[half, 8 + h : 9 + h, :] * decay
                a = a + acc[half, cols, :] * decay
            results.append((h, cols, m, l, a))
        for h, cols, m, l, a in results:
            acc_st[half, h : h + 1, :] = m
            acc_st[half, 8 + h : 9 + h, :] = l
            acc[half, cols, :] = a

    query_load.wait()
    load(own, own, 0).wait()
    for half in halves:
        rows = slice(half * span, (half + 1) * span)
        local(half, lambda c, r=rows: k_ref[r, c], lambda c, r=rows: v_ref[r, c], None, True)

    for further in (2, -1):
        for half in halves:
            merged(half, further)
    for further in (1, 0):
        for half in halves:
            direct(half, further)
    for i, ref in enumerate((k_ref, v_ref)):
        last_rows = ref.at[pl.ds(token_count - span, span), :]
        remote(last_rows, before.at[i], (send.at[4], precv, 0), 0, {"context": ahead}).start()
    for further in (1, 0):
        for half in halves:
            merged(half, further)
    local(1, lambda c: k_ref[0:span, c], lambda c: v_ref[0:span, c], 0.0, False)

    for half in halves:
        collect(half, 2)
        for side, way in ((0, 1), (1, -1)):
            rows = pl.ds(*parts[side])
            start(
                half, 8 + side, way, mid.at[half, 0, rows], mid_st.at[half, 0],
                relay2.at[half, rows], relay2_st.at[half, side],
            )
    for side, way in ((1, -1), (0, 1)):
        for half in halves:
            i = order.index(way)
            collect(half, way)
            other = pl.ds(*parts[1 - side])
            start(
                half, 10, way, mid.at[half, i, other], mid_st.at[half, i],
                got2.at[half, side, other], got2_st.at[half, side, 1 - side],
            )
    for half in halves:
        for side, way in ((0, 1), (1, -1)):
            i = order.index(way)
            rows = pl.ds(*parts[side])
            part, st = relay2.at[half], relay2_st.at[half, side]
            arrive(half, 8 + side, relay2.at[half, rows], st)
            merge(
                part, st, [(part, st), (mid.at[half, i], mid_st.at[half, i])],
                range(parts[side][0] // HDIM, sum(parts[side]) // HDIM),
            )
            start(
                half, 10, way, relay2.at[half, rows], st,
                got2.at[half, side, rows], got2_st.at[half, side, side],
            )

    remote(before, before, (send.at[4], precv, 0), 0, {"context": ahead}).wait_recv()
    local(
        0, lambda c: before[0, :, c], lambda c: before[1, :, c], jnp.where(me > 0, 0.0, NEG), False
    )
    last = order.index(0)
    for half in halves:
        collect(half, 0)
    for half in halves:
        arrive(half, 10, got2.at[half], got2_st.at[half])
        for h in every:
            cols = slice(h * HDIM, (h + 1) * HDIM)
            which = 0 if h * HDIM < cut else 1
            sources = [(mid.at[half, last], mid_st.at[half, last])]
            sources += [(got2.at[half, i], got2_st.at[half, i, which]) for i in (0, 1)]
            old = acc_st[half, h : h + 1, :]
            ms = [st[h : h + 1, :] for _, st in sources]
            m = functools.reduce(jnp.maximum, ms, old)
            decay = jnp.exp2(old - m)
            total = acc_st[half, 8 + h : 9 + h, :] * decay
            a = acc[half, cols, :] * decay
            for (part, st), x in zip(sources, ms):
                w = jnp.exp2(x - m)
                total = total + st[8 + h : 9 + h, :] * w
                a = a + part[cols, :].astype(jnp.float32) * w
            out_ref[half * span : (half + 1) * span, cols] = jnp.transpose(a / total).astype(
                out_ref.dtype
            )

    for index, ref in enumerate(
        (
            o_ref.at[pl.ds(0, 3)],
            st_ref.at[pl.ds(0, 3)],
            o_ref.at[pl.ds(0, 3), 0],
            st_ref.at[pl.ds(0, 3), pl.ds(0, 2)],
            before,
        )
    ):
        remote(ref, ref, (send.at[index], precv, 0), 0, {"context": ahead}).wait_send()


def combine(o, st, q_all, k, v, heads):
    span_count, width, span = o.shape[1:]
    rows = st.shape[2]
    o = o.reshape(RING, RING, span_count, width, span)
    st = st.reshape(RING, RING, span_count, rows, span)
    vmem = pl.BlockSpec(memory_space=pltpu.VMEM)
    hbm = pl.BlockSpec(memory_space=pl.ANY)

    def part(*lead):
        return pltpu.VMEM(lead + (width, span), jnp.bfloat16)

    def stats(*lead):
        return pltpu.VMEM(lead + (rows, span), jnp.float32)

    return pl.pallas_call(
        functools.partial(combine_kernel, heads),
        in_specs=[hbm, vmem, hbm, vmem, vmem],
        out_specs=vmem,
        out_shape=jax.ShapeDtypeStruct(k.shape, jnp.bfloat16),
        scratch_shapes=[
            part(2, 2, RING),
            pltpu.VMEM(k.shape, jnp.bfloat16),
            pltpu.VMEM((2, span, width), jnp.bfloat16),
            part(2, RING),
            stats(2, RING),
            part(2, 2, RING),
            stats(2, 2, RING),
            part(2, RING),
            stats(2, RING),
            part(2),
            stats(2, 2),
            part(2, 2),
            stats(2, 2, 2),
            pltpu.VMEM((2, width, span), jnp.float32),
            stats(2),
        ]
        + [pltpu.SemaphoreType.DMA((count,)) for count in (2, 5, 22, 22, 1)],
        compiler_params=pltpu.CompilerParams(
            collective_id=1, has_side_effects=True, vmem_limit_bytes=60 << 20
        ),
        name="combine",
    )(o, st, q_all, k, v)


def shards(
    tokens,
    query_weight,
    key_weight,
    value_weight,
    cache_keys,
    cache_values,
    selected,
    counts,
    block_slot,
):
    heads = query_weight.shape[1] // HDIM
    span_count, select_count = selected.shape
    devices = lax.axis_size("context")
    cap = max(2, 2 * span_count * select_count // devices)

    stored = cache_keys.shape[0]
    q_all, k, v, table = gather_project(
        tokens, query_weight, key_weight, value_weight, selected, counts, block_slot, cap, stored
    )
    o, st = owner_attention(table, q_all, cache_keys, cache_values, heads, cap)
    return combine(o, st, q_all, k, v, heads)


def solution(mesh):
    placed = (
        P("context", "tensor"),
        P("context", "tensor"),
        P("context", "tensor"),
        P("context", "tensor"),
        P("context", None, "tensor"),
        P("context", None, "tensor"),
        P("context", None),
        P("context"),
        P(),
    )
    return jax.shard_map(
        shards, mesh=mesh, in_specs=placed, out_specs=P("context", "tensor"), check_vma=False
    )
```

```python
import functools

import jax
import jax.numpy as jnp
from jax import lax
from jax.experimental import pallas as pl
from jax.experimental.pallas import tpu as pltpu
from jax.sharding import PartitionSpec as P

HDIM = 128
NEG = -1e30
MESH = pl.DeviceIdType.MESH
EXTRA = 16
GROUP = 2
SCALE = HDIM ** (-0.5) * 1.4426950408889634


def dot_nt(a, b):
    return lax.dot_general(a, b, (((1,), (1,)), ((), ())), preferred_element_type=jnp.float32)


def dot_tn(a, b):
    return lax.dot_general(a, b, (((0,), (0,)), ((), ())), preferred_element_type=jnp.float32)


RING = 4
OFFSETS = (0, -1, 1, 2)


def wrap(position):
    return lax.rem(position + RING, RING)


def context_of(zpos, xpos):
    return wrap(zpos) * RING + wrap(xpos)


class Ring:
    def __init__(self, view, to, sems, own=None):
        self.view, self.to, self.sems, self.own = view, to, sems, own

    def copy(self, index, step):
        ref = self.view(step, max(0, index - 1))
        src = self.own if step == 0 and self.own is not None else ref
        return remote(src, ref, self.sems, min(index, 2), self.to(1 if index % 2 == 0 else -1))

    def start(self, index):
        self.copy(index, (0, 0, -1, 1)[index]).start()

    def whole(self):
        self.start(0)
        self.start(1)

    def onward(self):
        self.copy(0, -1).wait_recv()
        self.start(2)
        self.copy(1, 1).wait_recv()
        self.start(3)

    def opposite(self):
        ref = self.view(2, 0)
        remote(ref, ref, self.sems, 2, self.to(1)).wait_recv()


def remote(src, dst, sems, index, to):
    send, recv, base = sems
    return pltpu.make_async_remote_copy(
        src_ref=src,
        dst_ref=dst,
        send_sem=send,
        recv_sem=recv.at[base + index],
        device_id=to,
        device_id_type=MESH,
    )


def context_gather(view, own, sems, zpos, xpos, halves=(0, 1)):
    rings = {}

    def make(half, phase):
        along_x = (half == 0) == (phase == 0)
        first = 0 if phase == 0 else OFFSETS[phase - 1]

        def piece(step, part):
            dz, dx = (first, step) if along_x else (step, first)
            return view(wrap(zpos + dz), wrap(xpos + dx), half, part)

        def to(way):
            dz, dx = (0, way) if along_x else (way, 0)
            return {"context": context_of(zpos + dz, xpos + dx)}

        send, recv, base = sems
        source = own(half) if first == 0 else None
        return Ring(piece, to, (send, recv, base + halves.index(half) * 15 + phase * 3), source)

    for half in halves:
        for phase in range(5):
            rings[half, phase] = make(half, phase)

    def own():
        for half in halves:
            rings[half, 0].whole()
            rings[half, 1].whole()

    def neighbours():
        for half in halves:
            rings[half, 0].onward()
            rings[half, 2].whole()
            rings[half, 3].whole()
        for half in halves:
            rings[half, 1].onward()

    def far():
        for half in halves:
            rings[half, 0].opposite()
            rings[half, 4].whole()

    def corners():
        for half in halves:
            rings[half, 2].onward()
            rings[half, 3].onward()

    def last():
        for half in halves:
            rings[half, 4].onward()

    def rest():
        for half in halves:
            for phase in (1, 2, 3, 4):
                rings[half, phase].opposite()

    return [own, neighbours, far, corners, last, rest]


def project_kernel(
    span_count, select_count, cap, stored,
    tok_ref, wq_ref, wk_ref, wv_ref, sel_ref, count_ref, slot_ref,
    q_ref, k_ref, v_ref, tab_ref,
    tok, stage, w, acc, done, back, fifth, small, told,
    load_sem, send, trecv, wrecv, brecv, qrecv,
):
    me = lax.axis_index("context")
    zpos, xpos = me // RING, lax.rem(me, RING)
    col = lax.axis_index("tensor")
    ypos, core = col // 2, lax.rem(col, 2)
    token_count, depth = tok.shape[2], tok.shape[3]
    rows = w.shape[3]

    token_load = pltpu.make_async_copy(tok_ref, tok.at[col, zpos], load_sem.at[0])
    token_load.start()
    for part in (0, 1):
        for to in range(RING):
            left = (wq_ref, wk_ref, wv_ref, wq_ref)[to]
            pair = ((wq_ref, to), (left, RING)) if part == 0 else ((wk_ref, to), (wv_ref, to))
            for i, (ref, head) in enumerate(pair):
                load = pltpu.make_async_copy(
                    ref.at[:, pl.ds(head * HDIM, HDIM)],
                    stage.at[part, to, :, pl.ds(i * HDIM, HDIM)],
                    load_sem.at[2 + part],
                )
                load.start()

    def at_x(way):
        return {"context": context_of(zpos, xpos + way)}

    def at_z(way):
        return {"context": context_of(zpos + way, xpos)}

    def at_y(way):
        return {"tensor": wrap(ypos + way) * 2 + core}

    mate = {"tensor": ypos * 2 + 1 - core}
    barrier = pltpu.get_barrier_semaphore()
    partners = [at_x(1), at_x(-1), at_z(1), at_z(-1), at_z(2), at_y(1), at_y(-1), mate]
    for other in partners:
        pl.semaphore_signal(barrier, inc=1, device_id=other, device_id_type=MESH)
    pl.semaphore_wait(barrier, len(partners))

    def cut(size):
        return (pl.ds(0, size), pl.ds(0, size // 2), pl.ds(size // 2, size // 2))

    ztok = Ring(
        lambda step, part: tok.at[col, wrap(zpos + step), cut(token_count)[part]],
        at_z, (send.at[0], trecv, 0),
    )
    ytok = {
        o: Ring(
            lambda step, part, o=o: tok.at[
                wrap(ypos + step) * 2 + core, wrap(zpos + o), cut(token_count)[part]
            ],
            at_y, (send.at[0], trecv, 3 + 3 * i),
        )
        for i, o in enumerate(OFFSETS)
    }

    def share(step, o):
        ref = tok.at[wrap(ypos + step) * 2 + core, wrap(zpos + o)]
        remote(ref, ref, (send.at[1], trecv, 15), OFFSETS.index(o), mate).start()

    def shared(o):
        ref = tok.at[pl.ds(0, RING), 0]
        remote(ref, ref, (send.at[1], trecv, 15), OFFSETS.index(o), mate).wait_recv()

    def exchange(part, step, receive=False):
        index = part * 3 + OFFSETS.index(step) - 1
        src = stage.at[part, wrap(zpos + step)]
        if receive:
            dst = w.at[part, wrap(zpos - step), xpos]
            remote(src, dst, (send.at[2], wrecv, 0), index, at_z(step)).wait_recv()
        else:
            dst = w.at[part, zpos, xpos]
            remote(src, dst, (send.at[2], wrecv, 0), index, at_z(step)).start()

    xw = {
        (part, o): Ring(
            lambda step, piece, part=part, o=o: w.at[
                part, wrap(zpos + o), wrap(xpos + step), cut(rows)[piece]
            ],
            at_x, (send.at[3], wrecv, 6 + part * 12 + 3 * i),
        )
        for part in (0, 1)
        for i, o in enumerate(OFFSETS)
    }

    def keep(part):
        whole = stage.at[part]
        pltpu.make_async_copy(whole, whole, load_sem.at[2 + part]).wait()
        copy = pltpu.make_async_copy(
            stage.at[part, zpos], w.at[part, zpos, xpos], load_sem.at[4 + part]
        )
        copy.start()
        copy.wait()

    def queries(o):
        z = wrap(zpos + o)

        @pl.loop(0, tok.shape[0])
        def _(t):
            piece = w[0, t // 2, pl.ds(lax.rem(t, 2) * 2, 2)].reshape(depth, w.shape[4])
            new = jnp.dot(tok[t, z], piece, preferred_element_type=jnp.float32)

            @pl.when(t == 0)
            def _():
                acc[z] = new

            @pl.when(t > 0)
            def _():
                acc[z] += new

        done[0, z] = acc[z].astype(jnp.bfloat16)
        last_head = slice(HDIM, 2 * HDIM)
        if o == 0:
            fifth[zpos] = acc[z, :, last_head].astype(jnp.bfloat16)
        else:
            src = done.at[0, z, :, last_head]
            remote(src, fifth.at[zpos], (send.at[4], brecv, 0), 0, at_z(o)).start()

    def compute(step):
        for side in (0, 1):
            t = wrap(ypos + step) * 2 + side
            piece = w[1, wrap(ypos + step), 2 * side : 2 * side + 2].reshape(depth, w.shape[4])

            @pl.loop(0, RING)
            def _(z):
                new = jnp.dot(tok[t, z], piece, preferred_element_type=jnp.float32)
                if step == 0 and side == 0:
                    acc[z] = new
                else:
                    acc[z] += new

    def give_back():
        @pl.loop(0, RING)
        def _(z):
            done[1, z] = acc[z].astype(jnp.bfloat16)

        back[zpos] = acc[zpos].astype(jnp.bfloat16)
        for step in OFFSETS[1:]:
            src = done.at[1, wrap(zpos + step)]
            remote(src, back.at[zpos], (send.at[5], brecv, 1), 0, at_z(step)).start()

    def take_back(buf, index):
        ref = buf.at[pl.ds(0, RING - 1)]
        remote(ref, ref, (send.at[4], brecv, index), 0, at_z(1)).wait_recv()

    def heads_of(o, base, halves):
        size = token_count // len(halves)

        def view(z, x, half, part):
            head = pl.ds(pl.multiple_of(z * HDIM, HDIM), HDIM)
            low = (half * size, half * size, half * size + size // 2)[part]
            rows = pl.ds(low, size if part == 0 else size // 2)
            return q_ref.at[wrap(z + o), x, rows, head]

        def own(half):
            return done.at[0, wrap(zpos + o), pl.ds(half * size, size), pl.ds(0, HDIM)]

        return context_gather(view, own, (send.at[6], qrecv, base), zpos, xpos, halves)

    heads = {
        o: heads_of(o, *rest)
        for o, *rest in ((0, 30, (0,)), (-1, 45, (0,)), (1, 60, (0, 1)), (2, 90, (0, 1)))
    }

    half_rows = token_count // 2
    quarter = half_rows // 2
    ranges = (
        ((0, half_rows), (0, quarter), (quarter, quarter)),
        (
            (half_rows, half_rows + EXTRA),
            (half_rows, quarter),
            (half_rows + quarter, quarter + EXTRA),
        ),
    )

    def last_view(z, x, half, part):
        return q_ref.at[z, x, pl.ds(*ranges[half][part]), pl.ds(RING * HDIM, HDIM)]

    def last_own(half):
        return small.at[pl.ds(*ranges[half][0]), :]

    last = context_gather(last_view, last_own, (send.at[7], qrecv, 0), zpos, xpos)

    token_load.wait()
    ztok.whole()
    ytok[0].whole()
    share(0, 0)
    keep(0)
    xw[0, 0].whole()
    exchange(0, 1)
    exchange(0, -1)
    keep(1)

    lane = lax.broadcasted_iota(jnp.int32, (EXTRA, HDIM), 1)
    line = lax.broadcasted_iota(jnp.int32, (EXTRA, HDIM), 0)
    chosen = jnp.zeros((EXTRA, HDIM), jnp.int32)
    for half in range(span_count):

        def note(j, chosen, half=half):
            slot = slot_ref[jnp.maximum(sel_ref[half, j], 0)]
            owner = jnp.where(j < count_ref[half], slot // stored, -1)
            value = jnp.where(line == half, owner, slot % stored)
            here = (lane == j) & ((line == half) | (line == span_count + half))
            return jnp.where(here, value, chosen)

        chosen = lax.fori_loop(0, select_count, note, chosen)
    small[token_count:, :] = chosen.astype(jnp.float32).astype(jnp.bfloat16)

    xw[0, 0].onward()
    ztok.onward()
    ytok[0].onward()
    for o in (-1, 1):
        ytok[o].whole()
        share(0, o)
    exchange(0, 2)
    xw[1, 0].whole()
    exchange(1, 1)
    exchange(1, -1)
    exchange(1, 2)
    share(-1, 0)
    share(1, 0)
    for step in (1, -1):
        exchange(0, step, receive=True)
        xw[0, -step].whole()
    ztok.opposite()
    ytok[2].whole()
    share(0, 2)
    exchange(0, 2, receive=True)
    xw[0, 2].whole()
    ytok[-1].onward()
    share(-1, -1)
    share(1, -1)
    ytok[0].opposite()
    share(2, 0)
    xw[0, -1].onward()
    xw[0, 1].onward()
    xw[1, 0].onward()
    ytok[1].onward()
    share(-1, 1)
    share(1, 1)
    xw[0, 2].onward()
    for step in (1, -1):
        exchange(1, step, receive=True)
        xw[1, -step].whole()
    exchange(1, 2, receive=True)
    xw[1, 2].whole()
    for o in OFFSETS:
        xw[0, o].opposite()
    shared(0)
    queries(0)
    heads[0][0]()
    ytok[-1].opposite()
    share(2, -1)
    xw[1, -1].onward()
    xw[1, 1].onward()
    ytok[2].onward()
    share(-1, 2)
    share(1, 2)
    shared(-1)
    queries(-1)
    heads[-1][0]()
    ytok[1].opposite()
    share(2, 1)
    xw[1, 2].onward()
    heads[0][1]()
    shared(1)
    queries(1)
    heads[1][0]()
    ytok[2].opposite()
    share(2, 2)
    heads[-1][1]()
    shared(2)
    queries(2)
    heads[2][0]()
    keeps = [
        pltpu.make_async_copy(
            done.at[0, :, :, pl.ds(0, HDIM)],
            q_ref.at[
                :, xpos, pl.ds(0, token_count), pl.ds(pl.multiple_of(zpos * HDIM, HDIM), HDIM)
            ],
            load_sem.at[1],
        )
    ]
    keeps[0].start()
    heads[0][2]()
    heads[1][1]()
    take_back(fifth, 0)
    small[0:token_count, :] = fifth[0]
    last[0]()
    keeps.append(
        pltpu.make_async_copy(
            small, q_ref.at[zpos, xpos, :, pl.ds(RING * HDIM, HDIM)], load_sem.at[6]
        )
    )
    keeps[1].start()
    for o in OFFSETS:
        xw[1, o].opposite()
    compute(0)
    heads[-1][2]()
    heads[0][3]()
    heads[2][1]()
    compute(-1)
    last[1]()
    heads[1][2]()
    heads[-1][3]()
    heads[0][4]()
    compute(1)
    heads[2][2]()
    heads[1][3]()
    last[2]()
    compute(2)
    give_back()
    heads[-1][4]()
    heads[2][3]()
    last[3]()
    heads[1][4]()
    heads[2][4]()
    last[4]()
    for keep_copy in keeps:
        keep_copy.wait()
    for o in OFFSETS:
        heads[o][5]()
    last[5]()
    look = pltpu.make_async_copy(
        q_ref.at[:, :, pl.ds(token_count, EXTRA), pl.ds(RING * HDIM, HDIM)],
        told,
        load_sem.at[7],
    )
    look.start()
    take_back(back, 1)
    for head in range(RING):
        cols = slice(head * HDIM, (head + 1) * HDIM)
        k_ref[:, cols] = back[head, :, 0:HDIM]
        v_ref[:, cols] = back[head, :, HDIM : 2 * HDIM]
    k_ref[:, RING * HDIM :] = fifth[1]
    v_ref[:, RING * HDIM :] = fifth[2]
    look.wait()

    devices = RING * RING
    lane = lax.broadcasted_iota(jnp.int32, (devices, HDIM), 1)
    source = lax.broadcasted_iota(jnp.int32, (devices, HDIM), 0)
    before = lax.broadcasted_iota(jnp.int32, (HDIM, HDIM), 0)
    after = lax.broadcasted_iota(jnp.int32, (HDIM, HDIM), 1)
    earlier = jnp.where(before < after, 1.0, 0.0).astype(jnp.bfloat16)
    listed = told[...].reshape(devices, EXTRA, HDIM).astype(jnp.float32)
    for half in range(span_count):
        owner = listed[:, half, :]
        row = listed[:, span_count + half, :]
        mine = jnp.where((owner == me.astype(jnp.float32)) & (lane < select_count), 1.0, 0.0)
        rank = jnp.dot(mine.astype(jnp.bfloat16), earlier, preferred_element_type=jnp.float32)
        table = jnp.where(lane == cap, jnp.sum(mine, axis=1, keepdims=True), 0.0)
        for r in range(cap):
            value = jnp.sum(jnp.where(rank == r, mine * row, 0.0), axis=1, keepdims=True)
            table = jnp.where(lane == r, value, table)
        if half == 0:
            table = jnp.where((lane == cap + 1) & (source == me + 1), 1.0, table)
        tab_ref[half] = table.astype(jnp.int32)

    for index, ref in enumerate(
        (
            tok.at[pl.ds(0, 5), pl.ds(0, 3)],
            tok.at[pl.ds(0, 4)],
            w.at[pl.ds(0, 2), pl.ds(0, 3), 0],
            w.at[pl.ds(0, 2), pl.ds(0, 3)],
            fifth.at[pl.ds(0, 3)],
            back.at[pl.ds(0, 3)],
            q_ref.at[:, pl.ds(0, 3), pl.ds(0, token_count), :],
            q_ref.at[0, pl.ds(0, 3)],
        )
    ):
        remote(ref, ref, (send.at[index], brecv, 0), 0, at_z(1)).wait_send()


def gather_project(tokens, wq, wk, wv, selected, counts, block_slot, cap, stored):
    token_count, depth = tokens.shape
    rows, width = wq.shape
    span_count, select_count = selected.shape
    devices = lax.axis_size("context")
    columns = lax.axis_size("tensor")
    hbm = pl.BlockSpec(memory_space=pl.ANY)
    vmem = pl.BlockSpec(memory_space=pltpu.VMEM)
    smem = pl.BlockSpec(memory_space=pltpu.SMEM)
    own = jax.ShapeDtypeStruct((token_count, width), jnp.bfloat16)
    two = 2 * HDIM

    return pl.pallas_call(
        functools.partial(project_kernel, span_count, select_count, cap, stored),
        in_specs=[hbm] * 4 + [smem] * 3,
        out_specs=[hbm] + [vmem] * 3,
        out_shape=[
            jax.ShapeDtypeStruct((RING, RING, token_count + EXTRA, width), jnp.bfloat16),
            own,
            own,
            jax.ShapeDtypeStruct((span_count, devices, HDIM), jnp.int32),
        ],
        scratch_shapes=[
            pltpu.VMEM((columns, RING, token_count, depth), jnp.bfloat16),
            pltpu.VMEM((2, RING, rows, two), jnp.bfloat16),
            pltpu.VMEM((2, RING, RING, rows, two), jnp.bfloat16),
            pltpu.VMEM((RING, token_count, two), jnp.float32),
            pltpu.VMEM((2, RING, token_count, two), jnp.bfloat16),
            pltpu.VMEM((RING, token_count, two), jnp.bfloat16),
            pltpu.VMEM((RING, token_count, HDIM), jnp.bfloat16),
            pltpu.VMEM((token_count + EXTRA, HDIM), jnp.bfloat16),
            pltpu.VMEM((RING, RING, EXTRA, HDIM), jnp.bfloat16),
        ]
        + [pltpu.SemaphoreType.DMA((count,)) for count in (8, 8, 19, 30, 2, 120)],
        compiler_params=pltpu.CompilerParams(
            collective_id=0, has_side_effects=True, vmem_limit_bytes=60 << 20
        ),
        name="gather_project",
    )(tokens, wq, wk, wv, selected, counts, block_slot)


def owner_kernel(
    heads, cap, tab_ref, q_ref, k_ref, v_ref, pk_ref, pv_ref, o_ref, st_ref, acc_ref
):
    group, span_count, span = o_ref.shape[0], o_ref.shape[1], o_ref.shape[3]
    first = pl.program_id(0) * group
    block = k_ref.shape[1]
    columns = [slice(h * HDIM, (h + 1) * HDIM) for h in range(heads)]

    def score(i, half, h, j):
        r0 = tab_ref[half, first + i, 2 * j]
        r1 = tab_ref[half, first + i, 2 * j + 1]
        bias = jnp.where(2 * j + 1 < tab_ref[half, first + i, cap], 0.0, NEG)
        cols = columns[h]
        q = q_ref[i, half * span : (half + 1) * span, cols]
        k = jnp.concatenate([k_ref[r0, :, cols], k_ref[r1, :, cols]], 0)
        v = jnp.concatenate([v_ref[r0, :, cols], v_ref[r1, :, cols]], 0)
        s = dot_nt(k, q) * SCALE
        return jnp.concatenate([s[:block], s[block:] + bias], 0), v

    def put(i, half, h, m, l, a):
        st_ref[i, half, h : h + 1, :] = m
        st_ref[i, half, 8 + h : 9 + h, :] = l
        acc_ref[i, half, columns[h], :] = a
        o_ref[i, half, columns[h], :] = a.astype(jnp.bfloat16)

    places = [(i, half) for i in range(group) for half in range(span_count)]
    def soften(i, half, h, s, v):
        m = jnp.max(s, axis=0, keepdims=True)
        p = jnp.exp2(s - m)
        l = jnp.sum(p, axis=0, keepdims=True)
        m = jnp.where(tab_ref[half, first + i, cap] > 0, m, NEG)
        return i, half, h, m, l, p.astype(jnp.bfloat16), v

    def weigh(i, half, h, m, l, p, v):
        return i, half, h, m, l, dot_tn(v, p)

    made = [[(i, half, h, *score(i, half, h, 0)) for h in range(heads)] for i, half in places]
    results = []
    for tiles in made:
        soft = [soften(*tile) for tile in tiles]
        results += [weigh(*tile) for tile in soft]
    for result in results:
        put(*result)

    def more(i, half, tiles):
        results = []
        for h, (s, v) in enumerate(tiles):
            old = st_ref[i, half, h : h + 1, :]
            m = jnp.maximum(jnp.max(s, axis=0, keepdims=True), old)
            decay = jnp.exp2(old - m)
            p = jnp.exp2(s - m)
            l = jnp.sum(p, axis=0, keepdims=True)
            l = l + st_ref[i, half, 8 + h : 9 + h, :] * decay
            a = dot_tn(v, p.astype(jnp.bfloat16))
            a = a + acc_ref[i, half, columns[h], :] * decay
            results.append((i, half, h, m, l, a))
        for result in results:
            put(*result)

    for i, half in places:
        n = tab_ref[half, first + i, cap]

        @pl.when(n > 2)
        def _(i=i, half=half, n=n):
            @pl.loop(1, (n + 1) // 2)
            def _(j):
                more(i, half, [score(i, half, h, j) for h in range(heads)])

    for i in range(group):

        @pl.when(tab_ref[0, first + i, cap + 1] > 0)
        def _(i=i):
            tiles = [
                (dot_nt(pk_ref[:, cols], q_ref[i, 0:span, cols]) * SCALE, pv_ref[:, cols])
                for cols in columns
            ]
            more(i, 0, tiles)


def owner_attention(table, q_all, cache_keys, cache_values, k, v, heads, cap):
    tokens, width = q_all.shape[2] - EXTRA, q_all.shape[3]
    span_count, devices = table.shape[:2]
    span = tokens // span_count
    q_all = q_all.reshape(devices, tokens + EXTRA, width)
    newest = pl.BlockSpec((span, width), lambda s, *_: (span_count - 1, 0))
    whole = pl.BlockSpec(cache_keys.shape, lambda s, *_: (0, 0, 0), pipeline_mode=pl.Buffered(1))
    return pl.pallas_call(
        functools.partial(owner_kernel, heads, cap),
        grid_spec=pltpu.PrefetchScalarGridSpec(
            num_scalar_prefetch=1,
            grid=(devices // GROUP,),
            in_specs=[
                pl.BlockSpec((GROUP, tokens, width), lambda s, *_: (s, 0, 0)),
                whole,
                whole,
                newest,
                newest,
            ],
            out_specs=[
                pl.BlockSpec((GROUP, span_count, width, span), lambda s, *_: (s, 0, 0, 0)),
                pl.BlockSpec((GROUP, span_count, 16, span), lambda s, *_: (s, 0, 0, 0)),
            ],
            scratch_shapes=[pltpu.VMEM((GROUP, span_count, width, span), jnp.float32)],
        ),
        out_shape=[
            jax.ShapeDtypeStruct((devices, span_count, width, span), jnp.bfloat16),
            jax.ShapeDtypeStruct((devices, span_count, 16, span), jnp.float32),
        ],
        name="owner_attention",
    )(table, q_all, cache_keys, cache_values, k, v)


def combine_kernel(
    heads,
    o_ref, st_ref, q_ref, k_ref, v_ref,
    out_ref,
    own, query, relay, relay_st, got, got_st, mid, mid_st,
    relay2, relay2_st, got2, got2_st, acc, acc_st,
    load_sem, send, recv, recv_st,
):
    me = lax.axis_index("context")
    zpos, xpos = me // RING, lax.rem(me, RING)
    span = o_ref.shape[-1]
    token_count = k_ref.shape[0]
    cut = (heads + 1) // 2 * HDIM
    parts = ((0, cut), (cut, heads * HDIM - cut))
    order = (2, -1, 1, 0)

    def first_at(half, step):
        return wrap((xpos if half == 0 else zpos) + step)

    def second_at(half, step):
        return wrap((zpos if half == 0 else xpos) + step)

    def place(half, step, further):
        a, b = first_at(half, step), second_at(half, further)
        return (b, a, half) if half == 0 else (a, b, half)

    def way_of(further):
        return 1 if further in (2, 1) else -1

    def load(ref, dst, index):
        return pltpu.make_async_copy(ref, dst, load_sem.at[index])

    for kind in (0, 1):
        for further in order:
            for half in (0, 1):
                step = way_of(further) if kind == 0 else 0
                slot = (half, kind, order.index(further))
                load(o_ref.at[place(half, step, further)], own.at[slot], 0).start()
    query_load = load(q_ref.at[zpos, xpos, pl.ds(0, token_count)], query, 1)
    query_load.start()

    barrier = pltpu.get_barrier_semaphore()
    for other in (
        context_of(zpos + 1, xpos),
        context_of(zpos - 1, xpos),
        context_of(zpos, xpos + 1),
        context_of(zpos, xpos - 1),
    ):
        pl.semaphore_signal(barrier, inc=1, device_id={"context": other}, device_id_type=MESH)
    pl.semaphore_wait(barrier, 4)

    def copies(half, index, way, src, src_st, dst, dst_st):
        first = index < 8
        if (half == 0) == first:
            to = {"context": context_of(zpos, xpos + way)}
        else:
            to = {"context": context_of(zpos + way, xpos)}
        kind = 0 if first else 2
        return (
            remote(src, dst, (send.at[kind], recv, half * 11), index, to),
            remote(src_st, dst_st, (send.at[kind + 1], recv_st, half * 11), index, to),
        )

    def start(*args):
        for copy in copies(*args):
            copy.start()

    def arrive(half, index, dst, dst_st):
        for copy in copies(half, index, 1, dst, dst_st, dst, dst_st):
            copy.wait_recv()

    def merge(out, out_st, sources, head_range):
        results = []
        for h in head_range:
            rows = slice(h * HDIM, (h + 1) * HDIM)
            ms = [st[h : h + 1, :] for _, st in sources]
            m = functools.reduce(jnp.maximum, ms)
            ws = [jnp.exp2(x - m) for x in ms]
            ls = [st[8 + h : 9 + h, :] * w for (_, st), w in zip(sources, ws)]
            terms = [part[rows, :].astype(jnp.float32) * w for (part, _), w in zip(sources, ws)]
            total = functools.reduce(jnp.add, terms).astype(jnp.bfloat16)
            results.append((h, rows, m, functools.reduce(jnp.add, ls), total))
        for h, rows, m, l, total in results:
            out[rows, :] = total
            out_st[h : h + 1, :] = m
            out_st[8 + h : 9 + h, :] = l

    every = range(heads)

    def forward(half, further):
        i, at = order.index(further), place(half, 2, further)
        start(
            half, i, way_of(further), o_ref.at[at], st_ref.at[at],
            relay.at[half, i], relay_st.at[half, i],
        )

    def direct(half, further):
        way = -way_of(further)
        i, at, side = order.index(further), place(half, way, further), 0 if way == 1 else 1
        start(
            half, 4 + i, way, o_ref.at[at], st_ref.at[at],
            got.at[half, side, i], got_st.at[half, side, i],
        )

    def merged(half, further):
        way = way_of(further)
        i, at, side = order.index(further), place(half, way, further), 0 if way == 1 else 1
        part, st = relay.at[half, i], relay_st.at[half, i]
        arrive(half, i, part, st)
        merge(part, st, [(part, st), (own.at[half, 0, i], st_ref.at[at])], every)
        start(
            half, 4 + i, way, part, st, got.at[half, side, i], got_st.at[half, side, i]
        )

    def collect(half, further):
        i = order.index(further)
        both = pl.ds(0, 2)
        arrive(half, 4 + i, got.at[half, both, i], got_st.at[half, both, i])
        merge(
            mid.at[half, i], mid_st.at[half, i],
            [(own.at[half, 1, i], st_ref.at[place(half, 0, further)])]
            + [(got.at[half, n, i], got_st.at[half, n, i]) for n in (0, 1)],
            every,
        )

    halves = (0, 1)
    for further in order:
        for half in halves:
            forward(half, further)
    for further in (2, -1):
        for half in halves:
            direct(half, further)

    key = lax.broadcasted_iota(jnp.int32, (span, span), 0)
    row = lax.broadcasted_iota(jnp.int32, (span, span), 1)

    def local(half, keys_of, values_of, bias, first):
        results = []
        for h in every:
            cols = slice(h * HDIM, (h + 1) * HDIM)
            s = dot_nt(keys_of(cols), query[half * span : (half + 1) * span, cols]) * SCALE
            s = jnp.where(key <= row, s, NEG) if bias is None else s + bias
            m = jnp.max(s, axis=0, keepdims=True)
            if not first:
                old = acc_st[half, h : h + 1, :]
                m = jnp.maximum(m, old)
                decay = jnp.exp2(old - m)
            p = jnp.exp2(s - m)
            l = jnp.sum(p, axis=0, keepdims=True)
            a = dot_tn(values_of(cols), p.astype(jnp.bfloat16))
            if not first:
                l = l + acc_st[half, 8 + h : 9 + h, :] * decay
                a = a + acc[half, cols, :] * decay
            results.append((h, cols, m, l, a))
        for h, cols, m, l, a in results:
            acc_st[half, h : h + 1, :] = m
            acc_st[half, 8 + h : 9 + h, :] = l
            acc[half, cols, :] = a

    query_load.wait()
    load(own, own, 0).wait()
    for half in halves:
        rows = slice(half * span, (half + 1) * span)
        local(half, lambda c, r=rows: k_ref[r, c], lambda c, r=rows: v_ref[r, c], None, True)

    for further in (2, -1):
        for half in halves:
            merged(half, further)
    for further in (1, 0):
        for half in halves:
            direct(half, further)
    for further in (1, 0):
        for half in halves:
            merged(half, further)
    local(1, lambda c: k_ref[0:span, c], lambda c: v_ref[0:span, c], 0.0, False)

    for half in halves:
        collect(half, 2)
        for side, way in ((0, 1), (1, -1)):
            rows = pl.ds(*parts[side])
            start(
                half, 8 + side, way, mid.at[half, 0, rows], mid_st.at[half, 0],
                relay2.at[half, rows], relay2_st.at[half, side],
            )
    for side, way in ((1, -1), (0, 1)):
        for half in halves:
            i = order.index(way)
            collect(half, way)
            other = pl.ds(*parts[1 - side])
            start(
                half, 10, way, mid.at[half, i, other], mid_st.at[half, i],
                got2.at[half, side, other], got2_st.at[half, side, 1 - side],
            )
    for half in halves:
        for side, way in ((0, 1), (1, -1)):
            i = order.index(way)
            rows = pl.ds(*parts[side])
            part, st = relay2.at[half], relay2_st.at[half, side]
            arrive(half, 8 + side, relay2.at[half, rows], st)
            merge(
                part, st, [(part, st), (mid.at[half, i], mid_st.at[half, i])],
                range(parts[side][0] // HDIM, sum(parts[side]) // HDIM),
            )
            start(
                half, 10, way, relay2.at[half, rows], st,
                got2.at[half, side, rows], got2_st.at[half, side, side],
            )

    last = order.index(0)
    for half in halves:
        collect(half, 0)
        part, st = mid.at[half, last], mid_st.at[half, last]
        results = []
        for h in every:
            cols = slice(h * HDIM, (h + 1) * HDIM)
            old, new = acc_st[half, h : h + 1, :], st[h : h + 1, :]
            m = jnp.maximum(old, new)
            decay, w = jnp.exp2(old - m), jnp.exp2(new - m)
            l = acc_st[half, 8 + h : 9 + h, :] * decay + st[8 + h : 9 + h, :] * w
            a = acc[half, cols, :] * decay + part[cols, :].astype(jnp.float32) * w
            results.append((h, cols, m, l, a))
        for h, cols, m, l, a in results:
            acc_st[half, h : h + 1, :] = m
            acc_st[half, 8 + h : 9 + h, :] = l
            acc[half, cols, :] = a
    for half in halves:
        arrive(half, 10, got2.at[half], got2_st.at[half])
        for h in every:
            cols = slice(h * HDIM, (h + 1) * HDIM)
            which = 0 if h * HDIM < cut else 1
            sources = [(got2.at[half, i], got2_st.at[half, i, which]) for i in (0, 1)]
            old = acc_st[half, h : h + 1, :]
            ms = [st[h : h + 1, :] for _, st in sources]
            m = functools.reduce(jnp.maximum, ms, old)
            decay = jnp.exp2(old - m)
            total = acc_st[half, 8 + h : 9 + h, :] * decay
            a = acc[half, cols, :] * decay
            for (part, st), x in zip(sources, ms):
                w = jnp.exp2(x - m)
                total = total + st[8 + h : 9 + h, :] * w
                a = a + part[cols, :].astype(jnp.float32) * w
            out_ref[half * span : (half + 1) * span, cols] = jnp.transpose(a / total).astype(
                out_ref.dtype
            )

    for index, ref in enumerate(
        (
            o_ref.at[pl.ds(0, 3)],
            st_ref.at[pl.ds(0, 3)],
            o_ref.at[pl.ds(0, 3), 0],
            st_ref.at[pl.ds(0, 3), pl.ds(0, 2)],
        )
    ):
        to = {"context": context_of(zpos, xpos + 1)}
        remote(ref, ref, (send.at[index], recv, 0), 0, to).wait_send()


def combine(o, st, q_all, k, v, heads):
    span_count, width, span = o.shape[1:]
    rows = st.shape[2]
    o = o.reshape(RING, RING, span_count, width, span)
    st = st.reshape(RING, RING, span_count, rows, span)
    vmem = pl.BlockSpec(memory_space=pltpu.VMEM)
    hbm = pl.BlockSpec(memory_space=pl.ANY)

    def part(*lead):
        return pltpu.VMEM(lead + (width, span), jnp.bfloat16)

    def stats(*lead):
        return pltpu.VMEM(lead + (rows, span), jnp.float32)

    return pl.pallas_call(
        functools.partial(combine_kernel, heads),
        in_specs=[hbm, vmem, hbm, vmem, vmem],
        out_specs=vmem,
        out_shape=jax.ShapeDtypeStruct(k.shape, jnp.bfloat16),
        scratch_shapes=[
            part(2, 2, RING),
            pltpu.VMEM(k.shape, jnp.bfloat16),
            part(2, RING),
            stats(2, RING),
            part(2, 2, RING),
            stats(2, 2, RING),
            part(2, RING),
            stats(2, RING),
            part(2),
            stats(2, 2),
            part(2, 2),
            stats(2, 2, 2),
            pltpu.VMEM((2, width, span), jnp.float32),
            stats(2),
        ]
        + [pltpu.SemaphoreType.DMA((count,)) for count in (2, 4, 22, 22)],
        compiler_params=pltpu.CompilerParams(
            collective_id=1, has_side_effects=True, vmem_limit_bytes=60 << 20
        ),
        name="combine",
    )(o, st, q_all, k, v)


def shards(
    tokens,
    query_weight,
    key_weight,
    value_weight,
    cache_keys,
    cache_values,
    selected,
    counts,
    block_slot,
):
    heads = query_weight.shape[1] // HDIM
    span_count, select_count = selected.shape
    devices = lax.axis_size("context")
    cap = max(2, 2 * span_count * select_count // devices)

    stored = cache_keys.shape[0]
    q_all, k, v, table = gather_project(
        tokens, query_weight, key_weight, value_weight, selected, counts, block_slot, cap, stored
    )
    o, st = owner_attention(table, q_all, cache_keys, cache_values, k, v, heads, cap)
    return combine(o, st, q_all, k, v, heads)


def solution(mesh):
    placed = (
        P("context", "tensor"),
        P("context", "tensor"),
        P("context", "tensor"),
        P("context", "tensor"),
        P("context", None, "tensor"),
        P("context", None, "tensor"),
        P("context", None),
        P("context"),
        P(),
    )
    return jax.shard_map(
        shards, mesh=mesh, in_specs=placed, out_specs=P("context", "tensor"), check_vma=False
    )
```

```python
import functools

import jax
import jax.numpy as jnp
from jax import lax
from jax.experimental import pallas as pl
from jax.experimental.pallas import tpu as pltpu
from jax.sharding import PartitionSpec as P

HDIM = 128
NEG = -1e30
MESH = pl.DeviceIdType.MESH
EXTRA = 16
GROUP = 2
SCALE = HDIM ** (-0.5) * 1.4426950408889634


def dot_nt(a, b):
    return lax.dot_general(a, b, (((1,), (1,)), ((), ())), preferred_element_type=jnp.float32)


def dot_tn(a, b):
    return lax.dot_general(a, b, (((0,), (0,)), ((), ())), preferred_element_type=jnp.float32)


RING = 4
OFFSETS = (0, -1, 1, 2)


def wrap(position):
    return lax.rem(position + RING, RING)


def context_of(zpos, xpos):
    return wrap(zpos) * RING + wrap(xpos)


class Ring:
    def __init__(self, view, to, sems, own=None):
        self.view, self.to, self.sems, self.own = view, to, sems, own

    def copy(self, index, step):
        ref = self.view(step, max(0, index - 1))
        src = self.own if step == 0 and self.own is not None else ref
        return remote(src, ref, self.sems, min(index, 2), self.to(1 if index % 2 == 0 else -1))

    def start(self, index):
        self.copy(index, (0, 0, -1, 1)[index]).start()

    def whole(self):
        self.start(0)
        self.start(1)

    def onward(self):
        self.copy(0, -1).wait_recv()
        self.start(2)
        self.copy(1, 1).wait_recv()
        self.start(3)

    def opposite(self):
        ref = self.view(2, 0)
        remote(ref, ref, self.sems, 2, self.to(1)).wait_recv()


def remote(src, dst, sems, index, to):
    send, recv, base = sems
    return pltpu.make_async_remote_copy(
        src_ref=src,
        dst_ref=dst,
        send_sem=send,
        recv_sem=recv.at[base + index],
        device_id=to,
        device_id_type=MESH,
    )


def context_gather(view, own, sems, zpos, xpos, halves=(0, 1)):
    rings = {}

    def make(half, phase):
        along_x = (half == 0) == (phase == 0)
        first = 0 if phase == 0 else OFFSETS[phase - 1]

        def piece(step, part):
            dz, dx = (first, step) if along_x else (step, first)
            return view(wrap(zpos + dz), wrap(xpos + dx), half, part)

        def to(way):
            dz, dx = (0, way) if along_x else (way, 0)
            return {"context": context_of(zpos + dz, xpos + dx)}

        send, recv, base = sems
        source = own(half) if first == 0 else None
        return Ring(piece, to, (send, recv, base + halves.index(half) * 15 + phase * 3), source)

    for half in halves:
        for phase in range(5):
            rings[half, phase] = make(half, phase)

    def own():
        for half in halves:
            rings[half, 0].whole()
            rings[half, 1].whole()

    def neighbours():
        for half in halves:
            rings[half, 0].onward()
            rings[half, 2].whole()
            rings[half, 3].whole()
        for half in halves:
            rings[half, 1].onward()

    def far():
        for half in halves:
            rings[half, 0].opposite()
            rings[half, 4].whole()

    def corners():
        for half in halves:
            rings[half, 2].onward()
            rings[half, 3].onward()

    def last():
        for half in halves:
            rings[half, 4].onward()

    def rest():
        for half in halves:
            for phase in (1, 2, 3, 4):
                rings[half, phase].opposite()

    return [own, neighbours, far, corners, last, rest]


def project_kernel(
    span_count, select_count, cap, stored,
    tok_ref, wq_ref, wk_ref, wv_ref, sel_ref, count_ref, slot_ref,
    q_ref, k_ref, v_ref, tab_ref,
    tok, stage, w, acc, done, back, fifth, small, told,
    load_sem, send, trecv, wrecv, brecv, qrecv,
):
    me = lax.axis_index("context")
    zpos, xpos = me // RING, lax.rem(me, RING)
    col = lax.axis_index("tensor")
    ypos, core = col // 2, lax.rem(col, 2)
    token_count, depth = tok.shape[2], tok.shape[3]
    rows = w.shape[3]

    token_load = pltpu.make_async_copy(tok_ref, tok.at[col, zpos], load_sem.at[0])
    token_load.start()
    for part in (0, 1):
        for to in range(RING):
            left = (wq_ref, wk_ref, wv_ref, wq_ref)[to]
            pair = ((wq_ref, to), (left, RING)) if part == 0 else ((wk_ref, to), (wv_ref, to))
            for i, (ref, head) in enumerate(pair):
                load = pltpu.make_async_copy(
                    ref.at[:, pl.ds(head * HDIM, HDIM)],
                    stage.at[part, to, :, pl.ds(i * HDIM, HDIM)],
                    load_sem.at[2 + part],
                )
                load.start()

    def at_x(way):
        return {"context": context_of(zpos, xpos + way)}

    def at_z(way):
        return {"context": context_of(zpos + way, xpos)}

    def at_y(way):
        return {"tensor": wrap(ypos + way) * 2 + core}

    mate = {"tensor": ypos * 2 + 1 - core}
    barrier = pltpu.get_barrier_semaphore()
    partners = [at_x(1), at_x(-1), at_z(1), at_z(-1), at_z(2), at_y(1), at_y(-1), mate]
    for other in partners:
        pl.semaphore_signal(barrier, inc=1, device_id=other, device_id_type=MESH)
    pl.semaphore_wait(barrier, len(partners))

    def cut(size):
        return (pl.ds(0, size), pl.ds(0, size // 2), pl.ds(size // 2, size // 2))

    ztok = Ring(
        lambda step, part: tok.at[col, wrap(zpos + step), cut(token_count)[part]],
        at_z, (send.at[0], trecv, 0),
    )
    ytok = {
        o: Ring(
            lambda step, part, o=o: tok.at[
                wrap(ypos + step) * 2 + core, wrap(zpos + o), cut(token_count)[part]
            ],
            at_y, (send.at[0], trecv, 3 + 3 * i),
        )
        for i, o in enumerate(OFFSETS)
    }

    def share(step, o):
        ref = tok.at[wrap(ypos + step) * 2 + core, wrap(zpos + o)]
        remote(ref, ref, (send.at[1], trecv, 15), OFFSETS.index(o), mate).start()

    def shared(o):
        ref = tok.at[pl.ds(0, RING), 0]
        remote(ref, ref, (send.at[1], trecv, 15), OFFSETS.index(o), mate).wait_recv()

    def exchange(part, step, receive=False):
        index = part * 3 + OFFSETS.index(step) - 1
        src = stage.at[part, wrap(zpos + step)]
        if receive:
            dst = w.at[part, wrap(zpos - step), xpos]
            remote(src, dst, (send.at[2], wrecv, 0), index, at_z(step)).wait_recv()
        else:
            dst = w.at[part, zpos, xpos]
            remote(src, dst, (send.at[2], wrecv, 0), index, at_z(step)).start()

    xw = {
        (part, o): Ring(
            lambda step, piece, part=part, o=o: w.at[
                part, wrap(zpos + o), wrap(xpos + step), cut(rows)[piece]
            ],
            at_x, (send.at[3], wrecv, 6 + part * 12 + 3 * i),
        )
        for part in (0, 1)
        for i, o in enumerate(OFFSETS)
    }

    def keep(part):
        whole = stage.at[part]
        pltpu.make_async_copy(whole, whole, load_sem.at[2 + part]).wait()
        copy = pltpu.make_async_copy(
            stage.at[part, zpos], w.at[part, zpos, xpos], load_sem.at[4 + part]
        )
        copy.start()
        copy.wait()

    def queries(o):
        z = wrap(zpos + o)

        @pl.loop(0, tok.shape[0])
        def _(t):
            piece = w[0, t // 2, pl.ds(lax.rem(t, 2) * 2, 2)].reshape(depth, w.shape[4])
            new = jnp.dot(tok[t, z], piece, preferred_element_type=jnp.float32)

            @pl.when(t == 0)
            def _():
                acc[z] = new

            @pl.when(t > 0)
            def _():
                acc[z] += new

        done[0, z] = acc[z].astype(jnp.bfloat16)
        last_head = slice(HDIM, 2 * HDIM)
        if o == 0:
            fifth[zpos] = acc[z, :, last_head].astype(jnp.bfloat16)
        else:
            src = done.at[0, z, :, last_head]
            remote(src, fifth.at[zpos], (send.at[4], brecv, 0), 0, at_z(o)).start()

    def compute(step):
        for side in (0, 1):
            t = wrap(ypos + step) * 2 + side
            piece = w[1, wrap(ypos + step), 2 * side : 2 * side + 2].reshape(depth, w.shape[4])

            @pl.loop(0, RING)
            def _(z):
                new = jnp.dot(tok[t, z], piece, preferred_element_type=jnp.float32)
                if step == 0 and side == 0:
                    acc[z] = new
                else:
                    acc[z] += new

    def give_back():
        @pl.loop(0, RING)
        def _(z):
            done[1, z] = acc[z].astype(jnp.bfloat16)

        back[zpos] = acc[zpos].astype(jnp.bfloat16)
        for step in OFFSETS[1:]:
            src = done.at[1, wrap(zpos + step)]
            remote(src, back.at[zpos], (send.at[5], brecv, 1), 0, at_z(step)).start()

    def take_back(buf, index):
        ref = buf.at[pl.ds(0, RING - 1)]
        remote(ref, ref, (send.at[4], brecv, index), 0, at_z(1)).wait_recv()

    def heads_of(o, base, halves):
        size = token_count // len(halves)

        def view(z, x, half, part):
            head = pl.ds(pl.multiple_of(z * HDIM, HDIM), HDIM)
            low = halves.index(half) * size + (size // 2 if part == 2 else 0)
            rows = pl.ds(low, size if part == 0 else size // 2)
            return q_ref.at[wrap(z + o), x, rows, head]

        def own(half):
            return done.at[0, wrap(zpos + o), pl.ds(halves.index(half) * size, size), pl.ds(0, HDIM)]

        return context_gather(view, own, (send.at[6], qrecv, base), zpos, xpos, halves)

    heads = {
        o: heads_of(o, *rest)
        for o, *rest in ((0, 30, (0,)), (-1, 45, (0,)), (1, 60, (1,)), (2, 75, (1,)))
    }

    half_rows = token_count // 2
    quarter = half_rows // 2
    ranges = (
        ((0, half_rows), (0, quarter), (quarter, quarter)),
        (
            (half_rows, half_rows + EXTRA),
            (half_rows, quarter),
            (half_rows + quarter, quarter + EXTRA),
        ),
    )

    def last_view(z, x, half, part):
        return q_ref.at[z, x, pl.ds(*ranges[half][part]), pl.ds(RING * HDIM, HDIM)]

    def last_own(half):
        return small.at[pl.ds(*ranges[half][0]), :]

    last = context_gather(last_view, last_own, (send.at[7], qrecv, 0), zpos, xpos)

    token_load.wait()
    ytok[0].whole()
    keep(0)
    xw[0, 0].whole()
    exchange(0, 1)
    exchange(0, -1)
    ztok.whole()
    share(0, 0)
    keep(1)
    xw[1, 0].whole()

    lane = lax.broadcasted_iota(jnp.int32, (EXTRA, HDIM), 1)
    line = lax.broadcasted_iota(jnp.int32, (EXTRA, HDIM), 0)
    chosen = jnp.zeros((EXTRA, HDIM), jnp.int32)
    for half in range(span_count):

        def note(j, chosen, half=half):
            slot = slot_ref[jnp.maximum(sel_ref[half, j], 0)]
            owner = jnp.where(j < count_ref[half], slot // stored, -1)
            value = jnp.where(line == half, owner, slot % stored)
            here = (lane == j) & ((line == half) | (line == span_count + half))
            return jnp.where(here, value, chosen)

        chosen = lax.fori_loop(0, select_count, note, chosen)
    small[token_count:, :] = chosen.astype(jnp.float32).astype(jnp.bfloat16)

    xw[0, 0].onward()
    ytok[0].onward()
    ztok.onward()
    for o in (-1, 1):
        ytok[o].whole()
        share(0, o)
    exchange(0, 2)
    exchange(1, 1)
    exchange(1, -1)
    exchange(1, 2)
    share(-1, 0)
    share(1, 0)
    for step in (1, -1):
        exchange(0, step, receive=True)
        xw[0, -step].whole()
    ztok.opposite()
    ytok[2].whole()
    share(0, 2)
    exchange(0, 2, receive=True)
    xw[0, 2].whole()
    ytok[-1].onward()
    share(-1, -1)
    share(1, -1)
    ytok[0].opposite()
    share(2, 0)
    xw[0, -1].onward()
    xw[0, 1].onward()
    xw[1, 0].onward()
    ytok[1].onward()
    share(-1, 1)
    share(1, 1)
    xw[0, 2].onward()
    for step in (1, -1):
        exchange(1, step, receive=True)
        xw[1, -step].whole()
    exchange(1, 2, receive=True)
    xw[1, 2].whole()
    for o in OFFSETS:
        xw[0, o].opposite()
    shared(0)
    queries(0)
    heads[0][0]()
    ytok[-1].opposite()
    share(2, -1)
    xw[1, -1].onward()
    xw[1, 1].onward()
    ytok[2].onward()
    share(-1, 2)
    share(1, 2)
    shared(-1)
    queries(-1)
    heads[-1][0]()
    ytok[1].opposite()
    share(2, 1)
    xw[1, 2].onward()
    heads[0][1]()
    shared(1)
    queries(1)
    heads[1][0]()
    ytok[2].opposite()
    share(2, 2)
    heads[-1][1]()
    shared(2)
    queries(2)
    heads[2][0]()
    keeps = [
        pltpu.make_async_copy(
            done.at[0, :, :, pl.ds(0, HDIM)],
            q_ref.at[
                :, xpos, pl.ds(0, token_count), pl.ds(pl.multiple_of(zpos * HDIM, HDIM), HDIM)
            ],
            load_sem.at[1],
        )
    ]
    keeps[0].start()
    heads[0][2]()
    heads[1][1]()
    take_back(fifth, 0)
    small[0:token_count, :] = fifth[0]
    last[0]()
    keeps.append(
        pltpu.make_async_copy(
            small, q_ref.at[zpos, xpos, :, pl.ds(RING * HDIM, HDIM)], load_sem.at[6]
        )
    )
    keeps[1].start()
    for o in OFFSETS:
        xw[1, o].opposite()
    compute(0)
    heads[-1][2]()
    heads[0][3]()
    heads[2][1]()
    compute(-1)
    last[1]()
    heads[1][2]()
    heads[-1][3]()
    heads[0][4]()
    compute(1)
    heads[2][2]()
    heads[1][3]()
    last[2]()
    compute(2)
    give_back()
    heads[-1][4]()
    heads[2][3]()
    last[3]()
    heads[1][4]()
    heads[2][4]()
    last[4]()
    for keep_copy in keeps:
        keep_copy.wait()
    for o in OFFSETS:
        heads[o][5]()
    last[5]()
    look = pltpu.make_async_copy(
        q_ref.at[:, :, pl.ds(token_count, EXTRA), pl.ds(RING * HDIM, HDIM)],
        told,
        load_sem.at[7],
    )
    look.start()
    take_back(back, 1)
    for head in range(RING):
        cols = slice(head * HDIM, (head + 1) * HDIM)
        k_ref[:, cols] = back[head, :, 0:HDIM]
        v_ref[:, cols] = back[head, :, HDIM : 2 * HDIM]
    k_ref[:, RING * HDIM :] = fifth[1]
    v_ref[:, RING * HDIM :] = fifth[2]
    look.wait()

    devices = RING * RING
    lane = lax.broadcasted_iota(jnp.int32, (devices, HDIM), 1)
    source = lax.broadcasted_iota(jnp.int32, (devices, HDIM), 0)
    before = lax.broadcasted_iota(jnp.int32, (HDIM, HDIM), 0)
    after = lax.broadcasted_iota(jnp.int32, (HDIM, HDIM), 1)
    earlier = jnp.where(before < after, 1.0, 0.0).astype(jnp.bfloat16)
    listed = told[...].reshape(devices, EXTRA, HDIM).astype(jnp.float32)
    for half in range(span_count):
        owner = listed[:, half, :]
        row = listed[:, span_count + half, :]
        mine = jnp.where((owner == me.astype(jnp.float32)) & (lane < select_count), 1.0, 0.0)
        rank = jnp.dot(mine.astype(jnp.bfloat16), earlier, preferred_element_type=jnp.float32)
        table = jnp.where(lane == cap, jnp.sum(mine, axis=1, keepdims=True), 0.0)
        for r in range(cap):
            value = jnp.sum(jnp.where(rank == r, mine * row, 0.0), axis=1, keepdims=True)
            table = jnp.where(lane == r, value, table)
        if half == 0:
            table = jnp.where((lane == cap + 1) & (source == me + 1), 1.0, table)
        tab_ref[half] = table.astype(jnp.int32)

    for index, ref in enumerate(
        (
            tok.at[pl.ds(0, 5), pl.ds(0, 3)],
            tok.at[pl.ds(0, 4)],
            w.at[pl.ds(0, 2), pl.ds(0, 3), 0],
            w.at[pl.ds(0, 2), pl.ds(0, 3)],
            fifth.at[pl.ds(0, 3)],
            back.at[pl.ds(0, 3)],
            q_ref.at[:, pl.ds(0, 3), pl.ds(0, token_count), :],
            q_ref.at[0, pl.ds(0, 3)],
        )
    ):
        remote(ref, ref, (send.at[index], brecv, 0), 0, at_z(1)).wait_send()


def gather_project(tokens, wq, wk, wv, selected, counts, block_slot, cap, stored):
    token_count, depth = tokens.shape
    rows, width = wq.shape
    span_count, select_count = selected.shape
    devices = lax.axis_size("context")
    columns = lax.axis_size("tensor")
    hbm = pl.BlockSpec(memory_space=pl.ANY)
    vmem = pl.BlockSpec(memory_space=pltpu.VMEM)
    smem = pl.BlockSpec(memory_space=pltpu.SMEM)
    own = jax.ShapeDtypeStruct((token_count, width), jnp.bfloat16)
    two = 2 * HDIM

    return pl.pallas_call(
        functools.partial(project_kernel, span_count, select_count, cap, stored),
        in_specs=[hbm] * 4 + [smem] * 3,
        out_specs=[hbm] + [vmem] * 3,
        out_shape=[
            jax.ShapeDtypeStruct((RING, RING, token_count + EXTRA, width), jnp.bfloat16),
            own,
            own,
            jax.ShapeDtypeStruct((span_count, devices, HDIM), jnp.int32),
        ],
        scratch_shapes=[
            pltpu.VMEM((columns, RING, token_count, depth), jnp.bfloat16),
            pltpu.VMEM((2, RING, rows, two), jnp.bfloat16),
            pltpu.VMEM((2, RING, RING, rows, two), jnp.bfloat16),
            pltpu.VMEM((RING, token_count, two), jnp.float32),
            pltpu.VMEM((2, RING, token_count, two), jnp.bfloat16),
            pltpu.VMEM((RING, token_count, two), jnp.bfloat16),
            pltpu.VMEM((RING, token_count, HDIM), jnp.bfloat16),
            pltpu.VMEM((token_count + EXTRA, HDIM), jnp.bfloat16),
            pltpu.VMEM((RING, RING, EXTRA, HDIM), jnp.bfloat16),
        ]
        + [pltpu.SemaphoreType.DMA((count,)) for count in (8, 8, 19, 30, 2, 90)],
        compiler_params=pltpu.CompilerParams(
            collective_id=0, has_side_effects=True, vmem_limit_bytes=60 << 20
        ),
        name="gather_project",
    )(tokens, wq, wk, wv, selected, counts, block_slot)


def owner_kernel(
    heads, cap, tab_ref, q_ref, k_ref, v_ref, pk_ref, pv_ref, o_ref, st_ref, acc_ref
):
    group, span_count, span = o_ref.shape[0], o_ref.shape[1], o_ref.shape[3]
    first = pl.program_id(0) * group
    block = k_ref.shape[1]
    columns = [slice(h * HDIM, (h + 1) * HDIM) for h in range(heads)]

    def score(i, half, h, j):
        r0 = tab_ref[half, first + i, 2 * j]
        r1 = tab_ref[half, first + i, 2 * j + 1]
        bias = jnp.where(2 * j + 1 < tab_ref[half, first + i, cap], 0.0, NEG)
        cols = columns[h]
        q = q_ref[i, half * span : (half + 1) * span, cols]
        k = jnp.concatenate([k_ref[r0, :, cols], k_ref[r1, :, cols]], 0)
        v = jnp.concatenate([v_ref[r0, :, cols], v_ref[r1, :, cols]], 0)
        s = dot_nt(k, q) * SCALE
        return jnp.concatenate([s[:block], s[block:] + bias], 0), v

    def put(i, half, h, m, l, a):
        st_ref[i, half, h : h + 1, :] = m
        st_ref[i, half, 8 + h : 9 + h, :] = l
        acc_ref[i, half, columns[h], :] = a
        o_ref[i, half, columns[h], :] = a.astype(jnp.bfloat16)

    places = [(i, half) for i in range(group) for half in range(span_count)]
    def soften(i, half, h, s, v):
        m = jnp.max(s, axis=0, keepdims=True)
        p = jnp.exp2(s - m)
        l = jnp.sum(p, axis=0, keepdims=True)
        m = jnp.where(tab_ref[half, first + i, cap] > 0, m, NEG)
        return i, half, h, m, l, p.astype(jnp.bfloat16), v

    def weigh(i, half, h, m, l, p, v):
        return i, half, h, m, l, dot_tn(v, p)

    made = [[(i, half, h, *score(i, half, h, 0)) for h in range(heads)] for i, half in places]
    results = []
    for tiles in made:
        soft = [soften(*tile) for tile in tiles]
        results += [weigh(*tile) for tile in soft]
    for result in results:
        put(*result)

    def more(i, half, tiles):
        results = []
        for h, (s, v) in enumerate(tiles):
            old = st_ref[i, half, h : h + 1, :]
            m = jnp.maximum(jnp.max(s, axis=0, keepdims=True), old)
            decay = jnp.exp2(old - m)
            p = jnp.exp2(s - m)
            l = jnp.sum(p, axis=0, keepdims=True)
            l = l + st_ref[i, half, 8 + h : 9 + h, :] * decay
            a = dot_tn(v, p.astype(jnp.bfloat16))
            a = a + acc_ref[i, half, columns[h], :] * decay
            results.append((i, half, h, m, l, a))
        for result in results:
            put(*result)

    for i, half in places:
        n = tab_ref[half, first + i, cap]

        @pl.when(n > 2)
        def _(i=i, half=half, n=n):
            @pl.loop(1, (n + 1) // 2)
            def _(j):
                more(i, half, [score(i, half, h, j) for h in range(heads)])

    for i in range(group):

        @pl.when(tab_ref[0, first + i, cap + 1] > 0)
        def _(i=i):
            tiles = [
                (dot_nt(pk_ref[:, cols], q_ref[i, 0:span, cols]) * SCALE, pv_ref[:, cols])
                for cols in columns
            ]
            more(i, 0, tiles)


def owner_attention(table, q_all, cache_keys, cache_values, k, v, heads, cap):
    tokens, width = q_all.shape[2] - EXTRA, q_all.shape[3]
    span_count, devices = table.shape[:2]
    span = tokens // span_count
    q_all = q_all.reshape(devices, tokens + EXTRA, width)
    newest = pl.BlockSpec((span, width), lambda s, *_: (span_count - 1, 0))
    whole = pl.BlockSpec(cache_keys.shape, lambda s, *_: (0, 0, 0), pipeline_mode=pl.Buffered(1))
    return pl.pallas_call(
        functools.partial(owner_kernel, heads, cap),
        grid_spec=pltpu.PrefetchScalarGridSpec(
            num_scalar_prefetch=1,
            grid=(devices // GROUP,),
            in_specs=[
                pl.BlockSpec((GROUP, tokens, width), lambda s, *_: (s, 0, 0)),
                whole,
                whole,
                newest,
                newest,
            ],
            out_specs=[
                pl.BlockSpec((GROUP, span_count, width, span), lambda s, *_: (s, 0, 0, 0)),
                pl.BlockSpec((GROUP, span_count, 16, span), lambda s, *_: (s, 0, 0, 0)),
            ],
            scratch_shapes=[pltpu.VMEM((GROUP, span_count, width, span), jnp.float32)],
        ),
        out_shape=[
            jax.ShapeDtypeStruct((devices, span_count, width, span), jnp.bfloat16),
            jax.ShapeDtypeStruct((devices, span_count, 16, span), jnp.float32),
        ],
        name="owner_attention",
    )(table, q_all, cache_keys, cache_values, k, v)


def combine_kernel(
    heads,
    o_ref, st_ref, q_ref, k_ref, v_ref,
    out_ref,
    own, query, relay, relay_st, got, got_st, mid, mid_st,
    relay2, relay2_st, got2, got2_st, acc, acc_st,
    load_sem, send, recv, recv_st,
):
    me = lax.axis_index("context")
    zpos, xpos = me // RING, lax.rem(me, RING)
    span = o_ref.shape[-1]
    token_count = k_ref.shape[0]
    cut = (heads + 1) // 2 * HDIM
    parts = ((0, cut), (cut, heads * HDIM - cut))
    order = (2, -1, 1, 0)

    def first_at(half, step):
        return wrap((xpos if half == 0 else zpos) + step)

    def second_at(half, step):
        return wrap((zpos if half == 0 else xpos) + step)

    def place(half, step, further):
        a, b = first_at(half, step), second_at(half, further)
        return (b, a, half) if half == 0 else (a, b, half)

    def way_of(further):
        return 1 if further in (2, 1) else -1

    def load(ref, dst, index):
        return pltpu.make_async_copy(ref, dst, load_sem.at[index])

    for kind in (0, 1):
        for further in order:
            for half in (0, 1):
                step = way_of(further) if kind == 0 else 0
                slot = (half, kind, order.index(further))
                load(o_ref.at[place(half, step, further)], own.at[slot], 0).start()
    query_load = load(q_ref.at[zpos, xpos, pl.ds(0, token_count)], query, 1)
    query_load.start()

    barrier = pltpu.get_barrier_semaphore()
    for other in (
        context_of(zpos + 1, xpos),
        context_of(zpos - 1, xpos),
        context_of(zpos, xpos + 1),
        context_of(zpos, xpos - 1),
    ):
        pl.semaphore_signal(barrier, inc=1, device_id={"context": other}, device_id_type=MESH)
    pl.semaphore_wait(barrier, 4)

    def copies(half, index, way, src, src_st, dst, dst_st):
        first = index < 8
        if (half == 0) == first:
            to = {"context": context_of(zpos, xpos + way)}
        else:
            to = {"context": context_of(zpos + way, xpos)}
        kind = 0 if first else 2
        return (
            remote(src, dst, (send.at[kind], recv, half * 11), index, to),
            remote(src_st, dst_st, (send.at[kind + 1], recv_st, half * 11), index, to),
        )

    def start(*args):
        for copy in copies(*args):
            copy.start()

    def arrive(half, index, dst, dst_st):
        for copy in copies(half, index, 1, dst, dst_st, dst, dst_st):
            copy.wait_recv()

    def merge(out, out_st, sources, head_range):
        results = []
        for h in head_range:
            rows = slice(h * HDIM, (h + 1) * HDIM)
            ms = [st[h : h + 1, :] for _, st in sources]
            m = functools.reduce(jnp.maximum, ms)
            ws = [jnp.exp2(x - m) for x in ms]
            ls = [st[8 + h : 9 + h, :] * w for (_, st), w in zip(sources, ws)]
            terms = [part[rows, :].astype(jnp.float32) * w for (part, _), w in zip(sources, ws)]
            total = functools.reduce(jnp.add, terms).astype(jnp.bfloat16)
            results.append((h, rows, m, functools.reduce(jnp.add, ls), total))
        for h, rows, m, l, total in results:
            out[rows, :] = total
            out_st[h : h + 1, :] = m
            out_st[8 + h : 9 + h, :] = l

    every = range(heads)

    def forward(half, further):
        i, at = order.index(further), place(half, 2, further)
        start(
            half, i, way_of(further), o_ref.at[at], st_ref.at[at],
            relay.at[half, i], relay_st.at[half, i],
        )

    def direct(half, further):
        way = -way_of(further)
        i, at, side = order.index(further), place(half, way, further), 0 if way == 1 else 1
        start(
            half, 4 + i, way, o_ref.at[at], st_ref.at[at],
            got.at[half, side, i], got_st.at[half, side, i],
        )

    def merged(half, further):
        way = way_of(further)
        i, at, side = order.index(further), place(half, way, further), 0 if way == 1 else 1
        part, st = relay.at[half, i], relay_st.at[half, i]
        arrive(half, i, part, st)
        merge(part, st, [(part, st), (own.at[half, 0, i], st_ref.at[at])], every)
        start(
            half, 4 + i, way, part, st, got.at[half, side, i], got_st.at[half, side, i]
        )

    def collect(half, further):
        i = order.index(further)
        both = pl.ds(0, 2)
        arrive(half, 4 + i, got.at[half, both, i], got_st.at[half, both, i])
        merge(
            mid.at[half, i], mid_st.at[half, i],
            [(own.at[half, 1, i], st_ref.at[place(half, 0, further)])]
            + [(got.at[half, n, i], got_st.at[half, n, i]) for n in (0, 1)],
            every,
        )

    halves = (0, 1)
    for further in order:
        for half in halves:
            forward(half, further)
    for further in (2, -1):
        for half in halves:
            direct(half, further)

    key = lax.broadcasted_iota(jnp.int32, (span, span), 0)
    row = lax.broadcasted_iota(jnp.int32, (span, span), 1)

    def local(half, keys_of, values_of, bias, first):
        results = []
        for h in every:
            cols = slice(h * HDIM, (h + 1) * HDIM)
            s = dot_nt(keys_of(cols), query[half * span : (half + 1) * span, cols]) * SCALE
            s = jnp.where(key <= row, s, NEG) if bias is None else s + bias
            m = jnp.max(s, axis=0, keepdims=True)
            if not first:
                old = acc_st[half, h : h + 1, :]
                m = jnp.maximum(m, old)
                decay = jnp.exp2(old - m)
            p = jnp.exp2(s - m)
            l = jnp.sum(p, axis=0, keepdims=True)
            a = dot_tn(values_of(cols), p.astype(jnp.bfloat16))
            if not first:
                l = l + acc_st[half, 8 + h : 9 + h, :] * decay
                a = a + acc[half, cols, :] * decay
            results.append((h, cols, m, l, a))
        for h, cols, m, l, a in results:
            acc_st[half, h : h + 1, :] = m
            acc_st[half, 8 + h : 9 + h, :] = l
            acc[half, cols, :] = a

    query_load.wait()
    load(own, own, 0).wait()
    for half in halves:
        rows = slice(half * span, (half + 1) * span)
        local(half, lambda c, r=rows: k_ref[r, c], lambda c, r=rows: v_ref[r, c], None, True)

    for further in (2, -1):
        for half in halves:
            merged(half, further)
    for further in (1, 0):
        for half in halves:
            direct(half, further)
    for further in (1, 0):
        for half in halves:
            merged(half, further)
    local(1, lambda c: k_ref[0:span, c], lambda c: v_ref[0:span, c], 0.0, False)

    for half in halves:
        collect(half, 2)
        for side, way in ((0, 1), (1, -1)):
            rows = pl.ds(*parts[side])
            start(
                half, 8 + side, way, mid.at[half, 0, rows], mid_st.at[half, 0],
                relay2.at[half, rows], relay2_st.at[half, side],
            )
    for side, way in ((1, -1), (0, 1)):
        for half in halves:
            i = order.index(way)
            collect(half, way)
            other = pl.ds(*parts[1 - side])
            start(
                half, 10, way, mid.at[half, i, other], mid_st.at[half, i],
                got2.at[half, side, other], got2_st.at[half, side, 1 - side],
            )
    for half in halves:
        for side, way in ((0, 1), (1, -1)):
            i = order.index(way)
            rows = pl.ds(*parts[side])
            part, st = relay2.at[half], relay2_st.at[half, side]
            arrive(half, 8 + side, relay2.at[half, rows], st)
            merge(
                part, st, [(part, st), (mid.at[half, i], mid_st.at[half, i])],
                range(parts[side][0] // HDIM, sum(parts[side]) // HDIM),
            )
            start(
                half, 10, way, relay2.at[half, rows], st,
                got2.at[half, side, rows], got2_st.at[half, side, side],
            )

    last = order.index(0)
    for half in halves:
        collect(half, 0)
        part, st = mid.at[half, last], mid_st.at[half, last]
        results = []
        for h in every:
            cols = slice(h * HDIM, (h + 1) * HDIM)
            old, new = acc_st[half, h : h + 1, :], st[h : h + 1, :]
            m = jnp.maximum(old, new)
            decay, w = jnp.exp2(old - m), jnp.exp2(new - m)
            l = acc_st[half, 8 + h : 9 + h, :] * decay + st[8 + h : 9 + h, :] * w
            a = acc[half, cols, :] * decay + part[cols, :].astype(jnp.float32) * w
            results.append((h, cols, m, l, a))
        for h, cols, m, l, a in results:
            acc_st[half, h : h + 1, :] = m
            acc_st[half, 8 + h : 9 + h, :] = l
            acc[half, cols, :] = a
    for half in halves:
        arrive(half, 10, got2.at[half], got2_st.at[half])
        for h in every:
            cols = slice(h * HDIM, (h + 1) * HDIM)
            which = 0 if h * HDIM < cut else 1
            sources = [(got2.at[half, i], got2_st.at[half, i, which]) for i in (0, 1)]
            old = acc_st[half, h : h + 1, :]
            ms = [st[h : h + 1, :] for _, st in sources]
            m = functools.reduce(jnp.maximum, ms, old)
            decay = jnp.exp2(old - m)
            total = acc_st[half, 8 + h : 9 + h, :] * decay
            a = acc[half, cols, :] * decay
            for (part, st), x in zip(sources, ms):
                w = jnp.exp2(x - m)
                total = total + st[8 + h : 9 + h, :] * w
                a = a + part[cols, :].astype(jnp.float32) * w
            out_ref[half * span : (half + 1) * span, cols] = jnp.transpose(a / total).astype(
                out_ref.dtype
            )

    for index, ref in enumerate(
        (
            o_ref.at[pl.ds(0, 3)],
            st_ref.at[pl.ds(0, 3)],
            o_ref.at[pl.ds(0, 3), 0],
            st_ref.at[pl.ds(0, 3), pl.ds(0, 2)],
        )
    ):
        to = {"context": context_of(zpos, xpos + 1)}
        remote(ref, ref, (send.at[index], recv, 0), 0, to).wait_send()


def combine(o, st, q_all, k, v, heads):
    span_count, width, span = o.shape[1:]
    rows = st.shape[2]
    o = o.reshape(RING, RING, span_count, width, span)
    st = st.reshape(RING, RING, span_count, rows, span)
    vmem = pl.BlockSpec(memory_space=pltpu.VMEM)
    hbm = pl.BlockSpec(memory_space=pl.ANY)

    def part(*lead):
        return pltpu.VMEM(lead + (width, span), jnp.bfloat16)

    def stats(*lead):
        return pltpu.VMEM(lead + (rows, span), jnp.float32)

    return pl.pallas_call(
        functools.partial(combine_kernel, heads),
        in_specs=[hbm, vmem, hbm, vmem, vmem],
        out_specs=vmem,
        out_shape=jax.ShapeDtypeStruct(k.shape, jnp.bfloat16),
        scratch_shapes=[
            part(2, 2, RING),
            pltpu.VMEM(k.shape, jnp.bfloat16),
            part(2, RING),
            stats(2, RING),
            part(2, 2, RING),
            stats(2, 2, RING),
            part(2, RING),
            stats(2, RING),
            part(2),
            stats(2, 2),
            part(2, 2),
            stats(2, 2, 2),
            pltpu.VMEM((2, width, span), jnp.float32),
            stats(2),
        ]
        + [pltpu.SemaphoreType.DMA((count,)) for count in (2, 4, 22, 22)],
        compiler_params=pltpu.CompilerParams(
            collective_id=1, has_side_effects=True, vmem_limit_bytes=60 << 20
        ),
        name="combine",
    )(o, st, q_all, k, v)


def shards(
    tokens,
    query_weight,
    key_weight,
    value_weight,
    cache_keys,
    cache_values,
    selected,
    counts,
    block_slot,
):
    heads = query_weight.shape[1] // HDIM
    span_count, select_count = selected.shape
    devices = lax.axis_size("context")
    cap = max(2, 2 * span_count * select_count // devices)

    stored = cache_keys.shape[0]
    q_all, k, v, table = gather_project(
        tokens, query_weight, key_weight, value_weight, selected, counts, block_slot, cap, stored
    )
    o, st = owner_attention(table, q_all, cache_keys, cache_values, k, v, heads, cap)
    return combine(o, st, q_all, k, v, heads)


def solution(mesh):
    placed = (
        P("context", "tensor"),
        P("context", "tensor"),
        P("context", "tensor"),
        P("context", "tensor"),
        P("context", None, "tensor"),
        P("context", None, "tensor"),
        P("context", None),
        P("context"),
        P(),
    )
    return jax.shard_map(
        shards, mesh=mesh, in_specs=placed, out_specs=P("context", "tensor"), check_vma=False
    )
```

```python
import functools

import jax
import jax.numpy as jnp
from jax import lax
from jax.experimental import pallas as pl
from jax.experimental.pallas import tpu as pltpu
from jax.sharding import PartitionSpec as P

HDIM = 128
NEG = -1e30
MESH = pl.DeviceIdType.MESH
EXTRA = 16
GROUP = 2
SCALE = HDIM ** (-0.5) * 1.4426950408889634


def dot_nt(a, b):
    return lax.dot_general(a, b, (((1,), (1,)), ((), ())), preferred_element_type=jnp.float32)


def dot_tn(a, b):
    return lax.dot_general(a, b, (((0,), (0,)), ((), ())), preferred_element_type=jnp.float32)


RING = 4
OFFSETS = (0, -1, 1, 2)


def wrap(position):
    return lax.rem(position + RING, RING)


def context_of(zpos, xpos):
    return wrap(zpos) * RING + wrap(xpos)


class Ring:
    def __init__(self, view, to, sems, own=None):
        self.view, self.to, self.sems, self.own = view, to, sems, own

    def copy(self, index, step):
        ref = self.view(step, max(0, index - 1))
        src = self.own if step == 0 and self.own is not None else ref
        return remote(src, ref, self.sems, min(index, 2), self.to(1 if index % 2 == 0 else -1))

    def start(self, index):
        self.copy(index, (0, 0, -1, 1)[index]).start()

    def whole(self):
        self.start(0)
        self.start(1)

    def onward(self):
        self.copy(0, -1).wait_recv()
        self.start(2)
        self.copy(1, 1).wait_recv()
        self.start(3)

    def opposite(self):
        ref = self.view(2, 0)
        remote(ref, ref, self.sems, 2, self.to(1)).wait_recv()


def remote(src, dst, sems, index, to):
    send, recv, base = sems
    return pltpu.make_async_remote_copy(
        src_ref=src,
        dst_ref=dst,
        send_sem=send,
        recv_sem=recv.at[base + index],
        device_id=to,
        device_id_type=MESH,
    )


def context_gather(view, own, sems, zpos, xpos, halves=(0, 1)):
    rings = {}

    def make(half, phase):
        along_x = (half == 0) == (phase == 0)
        first = 0 if phase == 0 else OFFSETS[phase - 1]

        def piece(step, part):
            dz, dx = (first, step) if along_x else (step, first)
            return view(wrap(zpos + dz), wrap(xpos + dx), half, part)

        def to(way):
            dz, dx = (0, way) if along_x else (way, 0)
            return {"context": context_of(zpos + dz, xpos + dx)}

        send, recv, base = sems
        source = own(half) if first == 0 else None
        return Ring(piece, to, (send, recv, base + halves.index(half) * 15 + phase * 3), source)

    for half in halves:
        for phase in range(5):
            rings[half, phase] = make(half, phase)

    def own():
        for half in halves:
            rings[half, 0].whole()
            rings[half, 1].whole()

    def neighbours():
        for half in halves:
            rings[half, 0].onward()
            rings[half, 2].whole()
            rings[half, 3].whole()
        for half in halves:
            rings[half, 1].onward()

    def far():
        for half in halves:
            rings[half, 0].opposite()
            rings[half, 4].whole()

    def corners():
        for half in halves:
            rings[half, 2].onward()
            rings[half, 3].onward()

    def last():
        for half in halves:
            rings[half, 4].onward()

    def rest():
        for half in halves:
            for phase in (1, 2, 3, 4):
                rings[half, phase].opposite()

    return [own, neighbours, far, corners, last, rest]


def project_kernel(
    span_count, select_count, cap, stored,
    tok_ref, wq_ref, wk_ref, wv_ref, sel_hbm, count_hbm, slot_hbm,
    q_ref, k_out, v_out, tab_out,
    tok, stage, w, acc, done, back, fifth, small, told, sel_ref, count_ref, slot_ref,
    k_ref, v_ref, tab_ref,
    load_sem, send, trecv, wrecv, brecv, qrecv,
):
    me = lax.axis_index("context")
    zpos, xpos = me // RING, lax.rem(me, RING)
    col = lax.axis_index("tensor")
    ypos, core = col // 2, lax.rem(col, 2)
    token_count, depth = tok.shape[2], tok.shape[3]
    rows = w.shape[3]

    token_load = pltpu.make_async_copy(tok_ref, tok.at[col, zpos], load_sem.at[0])
    token_load.start()
    lists = [
        pltpu.make_async_copy(src, dst, load_sem.at[8 + i])
        for i, (src, dst) in enumerate(
            ((sel_hbm, sel_ref), (count_hbm, count_ref), (slot_hbm, slot_ref))
        )
    ]
    for load in lists:
        load.start()
    for part in (0, 1):
        for to in range(RING):
            left = (wq_ref, wk_ref, wv_ref, wq_ref)[to]
            pair = ((wq_ref, to), (left, RING)) if part == 0 else ((wk_ref, to), (wv_ref, to))
            for i, (ref, head) in enumerate(pair):
                load = pltpu.make_async_copy(
                    ref.at[:, pl.ds(head * HDIM, HDIM)],
                    stage.at[part, to, :, pl.ds(i * HDIM, HDIM)],
                    load_sem.at[2 + part],
                )
                load.start()

    def at_x(way):
        return {"context": context_of(zpos, xpos + way)}

    def at_z(way):
        return {"context": context_of(zpos + way, xpos)}

    def at_y(way):
        return {"tensor": wrap(ypos + way) * 2 + core}

    mate = {"tensor": ypos * 2 + 1 - core}
    barrier = pltpu.get_barrier_semaphore()
    partners = [at_x(1), at_x(-1), at_z(1), at_z(-1), at_z(2), at_y(1), at_y(-1), mate]
    for other in partners:
        pl.semaphore_signal(barrier, inc=1, device_id=other, device_id_type=MESH)
    pl.semaphore_wait(barrier, len(partners))

    def cut(size):
        return (pl.ds(0, size), pl.ds(0, size // 2), pl.ds(size // 2, size // 2))

    ztok = Ring(
        lambda step, part: tok.at[col, wrap(zpos + step), cut(token_count)[part]],
        at_z, (send.at[0], trecv, 0),
    )
    ytok = {
        o: Ring(
            lambda step, part, o=o: tok.at[
                wrap(ypos + step) * 2 + core, wrap(zpos + o), cut(token_count)[part]
            ],
            at_y, (send.at[0], trecv, 3 + 3 * i),
        )
        for i, o in enumerate(OFFSETS)
    }

    def share(step, o):
        ref = tok.at[wrap(ypos + step) * 2 + core, wrap(zpos + o)]
        remote(ref, ref, (send.at[1], trecv, 15), OFFSETS.index(o), mate).start()

    def shared(o):
        ref = tok.at[pl.ds(0, RING), 0]
        remote(ref, ref, (send.at[1], trecv, 15), OFFSETS.index(o), mate).wait_recv()

    def exchange(part, step, receive=False):
        index = part * 3 + OFFSETS.index(step) - 1
        src = stage.at[part, wrap(zpos + step)]
        if receive:
            dst = w.at[part, wrap(zpos - step), xpos]
            remote(src, dst, (send.at[2], wrecv, 0), index, at_z(step)).wait_recv()
        else:
            dst = w.at[part, zpos, xpos]
            remote(src, dst, (send.at[2], wrecv, 0), index, at_z(step)).start()

    xw = {
        (part, o): Ring(
            lambda step, piece, part=part, o=o: w.at[
                part, wrap(zpos + o), wrap(xpos + step), cut(rows)[piece]
            ],
            at_x, (send.at[3], wrecv, 6 + part * 12 + 3 * i),
        )
        for part in (0, 1)
        for i, o in enumerate(OFFSETS)
    }

    def keep(part):
        whole = stage.at[part]
        pltpu.make_async_copy(whole, whole, load_sem.at[2 + part]).wait()
        copy = pltpu.make_async_copy(
            stage.at[part, zpos], w.at[part, zpos, xpos], load_sem.at[4 + part]
        )
        copy.start()
        copy.wait()

    def queries(o):
        z = wrap(zpos + o)

        @pl.loop(0, tok.shape[0])
        def _(t):
            piece = w[0, t // 2, pl.ds(lax.rem(t, 2) * 2, 2)].reshape(depth, w.shape[4])
            new = jnp.dot(tok[t, z], piece, preferred_element_type=jnp.float32)

            @pl.when(t == 0)
            def _():
                acc[z] = new

            @pl.when(t > 0)
            def _():
                acc[z] += new

        done[0, z] = acc[z].astype(jnp.bfloat16)
        last_head = slice(HDIM, 2 * HDIM)
        if o == 0:
            fifth[zpos] = acc[z, :, last_head].astype(jnp.bfloat16)
        else:
            src = done.at[0, z, :, last_head]
            remote(src, fifth.at[zpos], (send.at[4], brecv, 0), 0, at_z(o)).start()

    def compute(step):
        for side in (0, 1):
            t = wrap(ypos + step) * 2 + side
            piece = w[1, wrap(ypos + step), 2 * side : 2 * side + 2].reshape(depth, w.shape[4])

            @pl.loop(0, RING)
            def _(z):
                new = jnp.dot(tok[t, z], piece, preferred_element_type=jnp.float32)
                if step == 0 and side == 0:
                    acc[z] = new
                else:
                    acc[z] += new

    def give_back():
        @pl.loop(0, RING)
        def _(z):
            done[1, z] = acc[z].astype(jnp.bfloat16)

        back[zpos] = acc[zpos].astype(jnp.bfloat16)
        for step in OFFSETS[1:]:
            src = done.at[1, wrap(zpos + step)]
            remote(src, back.at[zpos], (send.at[5], brecv, 1), 0, at_z(step)).start()

    def take_back(buf, index):
        ref = buf.at[pl.ds(0, RING - 1)]
        remote(ref, ref, (send.at[4], brecv, index), 0, at_z(1)).wait_recv()

    def heads_of(o, base, halves):
        size = token_count // len(halves)

        def view(z, x, half, part):
            head = pl.ds(pl.multiple_of(z * HDIM, HDIM), HDIM)
            low = halves.index(half) * size + (size // 2 if part == 2 else 0)
            rows = pl.ds(low, size if part == 0 else size // 2)
            return q_ref.at[wrap(z + o), x, rows, head]

        def own(half):
            return done.at[0, wrap(zpos + o), pl.ds(halves.index(half) * size, size), pl.ds(0, HDIM)]

        return context_gather(view, own, (send.at[6], qrecv, base), zpos, xpos, halves)

    heads = {
        o: heads_of(o, *rest)
        for o, *rest in ((0, 30, (0,)), (-1, 45, (0,)), (1, 60, (1,)), (2, 75, (1,)))
    }

    half_rows = token_count // 2
    quarter = half_rows // 2
    ranges = (
        ((0, half_rows), (0, quarter), (quarter, quarter)),
        (
            (half_rows, half_rows + EXTRA),
            (half_rows, quarter),
            (half_rows + quarter, quarter + EXTRA),
        ),
    )

    def last_view(z, x, half, part):
        return q_ref.at[z, x, pl.ds(*ranges[half][part]), pl.ds(RING * HDIM, HDIM)]

    def last_own(half):
        return small.at[pl.ds(*ranges[half][0]), :]

    last = context_gather(last_view, last_own, (send.at[7], qrecv, 0), zpos, xpos)

    token_load.wait()
    ytok[0].whole()
    keep(0)
    xw[0, 0].whole()
    exchange(0, 1)
    exchange(0, -1)
    ztok.whole()
    share(0, 0)
    keep(1)
    xw[1, 0].whole()

    lane = lax.broadcasted_iota(jnp.int32, (EXTRA, HDIM), 1)
    line = lax.broadcasted_iota(jnp.int32, (EXTRA, HDIM), 0)
    for load in lists:
        load.wait()
    chosen = jnp.zeros((EXTRA, HDIM), jnp.int32)
    for half in range(span_count):

        def note(j, chosen, half=half):
            slot = slot_ref[jnp.maximum(sel_ref[half, j], 0)]
            owner = jnp.where(j < count_ref[half], slot // stored, -1)
            value = jnp.where(line == half, owner, slot % stored)
            here = (lane == j) & ((line == half) | (line == span_count + half))
            return jnp.where(here, value, chosen)

        chosen = lax.fori_loop(0, select_count, note, chosen)
    small[token_count:, :] = chosen.astype(jnp.float32).astype(jnp.bfloat16)

    xw[0, 0].onward()
    ytok[0].onward()
    ztok.onward()
    for o in (-1, 1):
        ytok[o].whole()
        share(0, o)
    exchange(0, 2)
    exchange(1, 1)
    exchange(1, -1)
    exchange(1, 2)
    share(-1, 0)
    share(1, 0)
    for step in (1, -1):
        exchange(0, step, receive=True)
        xw[0, -step].whole()
    ztok.opposite()
    ytok[2].whole()
    share(0, 2)
    exchange(0, 2, receive=True)
    xw[0, 2].whole()
    ytok[-1].onward()
    share(-1, -1)
    share(1, -1)
    ytok[0].opposite()
    share(2, 0)
    xw[0, -1].onward()
    xw[0, 1].onward()
    xw[1, 0].onward()
    ytok[1].onward()
    share(-1, 1)
    share(1, 1)
    xw[0, 2].onward()
    for step in (1, -1):
        exchange(1, step, receive=True)
        xw[1, -step].whole()
    exchange(1, 2, receive=True)
    xw[1, 2].whole()
    for o in OFFSETS:
        xw[0, o].opposite()
    shared(0)
    queries(0)
    heads[0][0]()
    ytok[-1].opposite()
    share(2, -1)
    xw[1, -1].onward()
    xw[1, 1].onward()
    ytok[2].onward()
    share(-1, 2)
    share(1, 2)
    shared(-1)
    queries(-1)
    heads[-1][0]()
    ytok[1].opposite()
    share(2, 1)
    xw[1, 2].onward()
    heads[0][1]()
    shared(1)
    queries(1)
    heads[1][0]()
    ytok[2].opposite()
    share(2, 2)
    heads[-1][1]()
    shared(2)
    queries(2)
    heads[2][0]()
    keeps = [
        pltpu.make_async_copy(
            done.at[0, :, :, pl.ds(0, HDIM)],
            q_ref.at[
                :, xpos, pl.ds(0, token_count), pl.ds(pl.multiple_of(zpos * HDIM, HDIM), HDIM)
            ],
            load_sem.at[1],
        )
    ]
    keeps[0].start()
    heads[0][2]()
    heads[1][1]()
    take_back(fifth, 0)
    small[0:token_count, :] = fifth[0]
    last[0]()
    keeps.append(
        pltpu.make_async_copy(
            small, q_ref.at[zpos, xpos, :, pl.ds(RING * HDIM, HDIM)], load_sem.at[6]
        )
    )
    keeps[1].start()
    for o in OFFSETS:
        xw[1, o].opposite()
    compute(0)
    heads[-1][2]()
    heads[0][3]()
    heads[2][1]()
    compute(-1)
    last[1]()
    heads[1][2]()
    heads[-1][3]()
    heads[0][4]()
    compute(1)
    heads[2][2]()
    heads[1][3]()
    last[2]()
    compute(2)
    give_back()
    heads[-1][4]()
    heads[2][3]()
    last[3]()
    heads[1][4]()
    heads[2][4]()
    last[4]()
    for keep_copy in keeps:
        keep_copy.wait()
    for o in OFFSETS:
        heads[o][5]()
    last[5]()
    look = pltpu.make_async_copy(
        q_ref.at[:, :, pl.ds(token_count, EXTRA), pl.ds(RING * HDIM, HDIM)],
        told,
        load_sem.at[7],
    )
    look.start()
    take_back(back, 1)
    for head in range(RING):
        cols = slice(head * HDIM, (head + 1) * HDIM)
        k_ref[:, cols] = back[head, :, 0:HDIM]
        v_ref[:, cols] = back[head, :, HDIM : 2 * HDIM]
    k_ref[:, RING * HDIM :] = fifth[1]
    v_ref[:, RING * HDIM :] = fifth[2]
    puts = [
        pltpu.make_async_copy(k_ref, k_out, load_sem.at[11]),
        pltpu.make_async_copy(v_ref, v_out, load_sem.at[12]),
        pltpu.make_async_copy(tab_ref, tab_out, load_sem.at[13]),
    ]
    puts[0].start()
    puts[1].start()
    look.wait()

    devices = RING * RING
    lane = lax.broadcasted_iota(jnp.int32, (devices, HDIM), 1)
    source = lax.broadcasted_iota(jnp.int32, (devices, HDIM), 0)
    before = lax.broadcasted_iota(jnp.int32, (HDIM, HDIM), 0)
    after = lax.broadcasted_iota(jnp.int32, (HDIM, HDIM), 1)
    earlier = jnp.where(before < after, 1.0, 0.0).astype(jnp.bfloat16)
    listed = told[...].reshape(devices, EXTRA, HDIM).astype(jnp.float32)
    for half in range(span_count):
        owner = listed[:, half, :]
        row = listed[:, span_count + half, :]
        mine = jnp.where((owner == me.astype(jnp.float32)) & (lane < select_count), 1.0, 0.0)
        rank = jnp.dot(mine.astype(jnp.bfloat16), earlier, preferred_element_type=jnp.float32)
        table = jnp.where(lane == cap, jnp.sum(mine, axis=1, keepdims=True), 0.0)
        for r in range(cap):
            value = jnp.sum(jnp.where(rank == r, mine * row, 0.0), axis=1, keepdims=True)
            table = jnp.where(lane == r, value, table)
        if half == 0:
            table = jnp.where((lane == cap + 1) & (source == me + 1), 1.0, table)
        tab_ref[half] = table.astype(jnp.int32)
    puts[2].start()

    for put in puts:
        put.wait()
    for index, ref in enumerate(
        (
            tok.at[pl.ds(0, 5), pl.ds(0, 3)],
            tok.at[pl.ds(0, 4)],
            w.at[pl.ds(0, 2), pl.ds(0, 3), 0],
            w.at[pl.ds(0, 2), pl.ds(0, 3)],
            fifth.at[pl.ds(0, 3)],
            back.at[pl.ds(0, 3)],
            q_ref.at[:, pl.ds(0, 3), pl.ds(0, token_count), :],
            q_ref.at[0, pl.ds(0, 3)],
        )
    ):
        remote(ref, ref, (send.at[index], brecv, 0), 0, at_z(1)).wait_send()


def gather_project(tokens, wq, wk, wv, selected, counts, block_slot, cap, stored):
    token_count, depth = tokens.shape
    rows, width = wq.shape
    span_count, select_count = selected.shape
    devices = lax.axis_size("context")
    columns = lax.axis_size("tensor")
    hbm = pl.BlockSpec(memory_space=pl.ANY)
    own = jax.ShapeDtypeStruct((token_count, width), jnp.bfloat16)
    two = 2 * HDIM

    return pl.pallas_call(
        functools.partial(project_kernel, span_count, select_count, cap, stored),
        in_specs=[hbm] * 7,
        out_specs=[hbm] * 4,
        out_shape=[
            jax.ShapeDtypeStruct((RING, RING, token_count + EXTRA, width), jnp.bfloat16),
            own,
            own,
            jax.ShapeDtypeStruct((span_count, devices, HDIM), jnp.int32),
        ],
        scratch_shapes=[
            pltpu.VMEM((columns, RING, token_count, depth), jnp.bfloat16),
            pltpu.VMEM((2, RING, rows, two), jnp.bfloat16),
            pltpu.VMEM((2, RING, RING, rows, two), jnp.bfloat16),
            pltpu.VMEM((RING, token_count, two), jnp.float32),
            pltpu.VMEM((2, RING, token_count, two), jnp.bfloat16),
            pltpu.VMEM((RING, token_count, two), jnp.bfloat16),
            pltpu.VMEM((RING, token_count, HDIM), jnp.bfloat16),
            pltpu.VMEM((token_count + EXTRA, HDIM), jnp.bfloat16),
            pltpu.VMEM((RING, RING, EXTRA, HDIM), jnp.bfloat16),
            pltpu.SMEM(selected.shape, jnp.int32),
            pltpu.SMEM(counts.shape, jnp.int32),
            pltpu.SMEM(block_slot.shape, jnp.int32),
            pltpu.VMEM((token_count, width), jnp.bfloat16),
            pltpu.VMEM((token_count, width), jnp.bfloat16),
            pltpu.VMEM((span_count, devices, HDIM), jnp.int32),
        ]
        + [pltpu.SemaphoreType.DMA((count,)) for count in (14, 8, 19, 30, 2, 90)],
        compiler_params=pltpu.CompilerParams(
            collective_id=0, has_side_effects=True, vmem_limit_bytes=60 << 20
        ),
        name="gather_project",
    )(tokens, wq, wk, wv, selected, counts, block_slot)


def owner_kernel(
    heads, cap, tab_ref, q_ref, k_ref, v_ref, pk_ref, pv_ref, o_ref, st_ref, acc_ref
):
    group, span_count, span = o_ref.shape[0], o_ref.shape[1], o_ref.shape[3]
    first = pl.program_id(0) * group
    block = k_ref.shape[1]
    columns = [slice(h * HDIM, (h + 1) * HDIM) for h in range(heads)]

    def score(i, half, h, j):
        r0 = tab_ref[half, first + i, 2 * j]
        r1 = tab_ref[half, first + i, 2 * j + 1]
        bias = jnp.where(2 * j + 1 < tab_ref[half, first + i, cap], 0.0, NEG)
        cols = columns[h]
        q = q_ref[i, half * span : (half + 1) * span, cols]
        k = jnp.concatenate([k_ref[r0, :, cols], k_ref[r1, :, cols]], 0)
        v = jnp.concatenate([v_ref[r0, :, cols], v_ref[r1, :, cols]], 0)
        s = dot_nt(k, q) * SCALE
        return jnp.concatenate([s[:block], s[block:] + bias], 0), v

    def put(i, half, h, m, l, a):
        st_ref[i, half, h : h + 1, :] = m
        st_ref[i, half, 8 + h : 9 + h, :] = l
        acc_ref[i, half, columns[h], :] = a
        o_ref[i, half, columns[h], :] = a.astype(jnp.bfloat16)

    places = [(i, half) for i in range(group) for half in range(span_count)]
    def soften(i, half, h, s, v):
        m = jnp.max(s, axis=0, keepdims=True)
        p = jnp.exp2(s - m)
        l = jnp.sum(p, axis=0, keepdims=True)
        m = jnp.where(tab_ref[half, first + i, cap] > 0, m, NEG)
        return i, half, h, m, l, p.astype(jnp.bfloat16), v

    def weigh(i, half, h, m, l, p, v):
        return i, half, h, m, l, dot_tn(v, p)

    made = [[(i, half, h, *score(i, half, h, 0)) for h in range(heads)] for i, half in places]
    results = []
    for tiles in made:
        soft = [soften(*tile) for tile in tiles]
        results += [weigh(*tile) for tile in soft]
    for result in results:
        put(*result)

    def more(i, half, tiles):
        results = []
        for h, (s, v) in enumerate(tiles):
            old = st_ref[i, half, h : h + 1, :]
            m = jnp.maximum(jnp.max(s, axis=0, keepdims=True), old)
            decay = jnp.exp2(old - m)
            p = jnp.exp2(s - m)
            l = jnp.sum(p, axis=0, keepdims=True)
            l = l + st_ref[i, half, 8 + h : 9 + h, :] * decay
            a = dot_tn(v, p.astype(jnp.bfloat16))
            a = a + acc_ref[i, half, columns[h], :] * decay
            results.append((i, half, h, m, l, a))
        for result in results:
            put(*result)

    for i, half in places:
        n = tab_ref[half, first + i, cap]

        @pl.when(n > 2)
        def _(i=i, half=half, n=n):
            @pl.loop(1, (n + 1) // 2)
            def _(j):
                more(i, half, [score(i, half, h, j) for h in range(heads)])

    for i in range(group):

        @pl.when(tab_ref[0, first + i, cap + 1] > 0)
        def _(i=i):
            tiles = [
                (dot_nt(pk_ref[:, cols], q_ref[i, 0:span, cols]) * SCALE, pv_ref[:, cols])
                for cols in columns
            ]
            more(i, 0, tiles)


def owner_attention(table, q_all, cache_keys, cache_values, k, v, heads, cap):
    tokens, width = q_all.shape[2] - EXTRA, q_all.shape[3]
    span_count, devices = table.shape[:2]
    span = tokens // span_count
    q_all = q_all.reshape(devices, tokens + EXTRA, width)
    newest = pl.BlockSpec((span, width), lambda s, *_: (span_count - 1, 0))
    whole = pl.BlockSpec(cache_keys.shape, lambda s, *_: (0, 0, 0), pipeline_mode=pl.Buffered(1))
    return pl.pallas_call(
        functools.partial(owner_kernel, heads, cap),
        grid_spec=pltpu.PrefetchScalarGridSpec(
            num_scalar_prefetch=1,
            grid=(devices // GROUP,),
            in_specs=[
                pl.BlockSpec((GROUP, tokens, width), lambda s, *_: (s, 0, 0)),
                whole,
                whole,
                newest,
                newest,
            ],
            out_specs=[
                pl.BlockSpec((GROUP, span_count, width, span), lambda s, *_: (s, 0, 0, 0)),
                pl.BlockSpec((GROUP, span_count, 16, span), lambda s, *_: (s, 0, 0, 0)),
            ],
            scratch_shapes=[pltpu.VMEM((GROUP, span_count, width, span), jnp.float32)],
        ),
        out_shape=[
            jax.ShapeDtypeStruct((devices, span_count, width, span), jnp.bfloat16),
            jax.ShapeDtypeStruct((devices, span_count, 16, span), jnp.float32),
        ],
        name="owner_attention",
    )(table, q_all, cache_keys, cache_values, k, v)


def combine_kernel(
    heads,
    o_ref, st_ref, q_ref, k_ref, v_ref,
    out_ref,
    own, query, keys, values, st_own, relay, relay_st, got, got_st, mid, mid_st,
    relay2, relay2_st, got2, got2_st, acc, acc_st,
    load_sem, send, recv, recv_st,
):
    me = lax.axis_index("context")
    zpos, xpos = me // RING, lax.rem(me, RING)
    span = o_ref.shape[-1]
    token_count = k_ref.shape[0]
    cut = (heads + 1) // 2 * HDIM
    parts = ((0, cut), (cut, heads * HDIM - cut))
    order = (2, -1, 1, 0)

    def first_at(half, step):
        return wrap((xpos if half == 0 else zpos) + step)

    def second_at(half, step):
        return wrap((zpos if half == 0 else xpos) + step)

    def place(half, step, further):
        a, b = first_at(half, step), second_at(half, further)
        return (b, a, half) if half == 0 else (a, b, half)

    def way_of(further):
        return 1 if further in (2, 1) else -1

    def load(ref, dst, index):
        return pltpu.make_async_copy(ref, dst, load_sem.at[index])

    for kind in (0, 1):
        for further in order:
            for half in (0, 1):
                step = way_of(further) if kind == 0 else 0
                slot = (half, kind, order.index(further))
                load(o_ref.at[place(half, step, further)], own.at[slot], 0).start()
    query_load = load(q_ref.at[zpos, xpos, pl.ds(0, token_count)], query, 1)
    others = [load(k_ref, keys, 2), load(v_ref, values, 3), load(st_ref, st_own, 4)]
    for other in [query_load] + others:
        other.start()

    barrier = pltpu.get_barrier_semaphore()
    for other in (
        context_of(zpos + 1, xpos),
        context_of(zpos - 1, xpos),
        context_of(zpos, xpos + 1),
        context_of(zpos, xpos - 1),
    ):
        pl.semaphore_signal(barrier, inc=1, device_id={"context": other}, device_id_type=MESH)
    pl.semaphore_wait(barrier, 4)

    def copies(half, index, way, src, src_st, dst, dst_st):
        first = index < 8
        if (half == 0) == first:
            to = {"context": context_of(zpos, xpos + way)}
        else:
            to = {"context": context_of(zpos + way, xpos)}
        kind = 0 if first else 2
        return (
            remote(src, dst, (send.at[kind], recv, half * 11), index, to),
            remote(src_st, dst_st, (send.at[kind + 1], recv_st, half * 11), index, to),
        )

    def start(*args):
        for copy in copies(*args):
            copy.start()

    def arrive(half, index, dst, dst_st):
        for copy in copies(half, index, 1, dst, dst_st, dst, dst_st):
            copy.wait_recv()

    def merge(out, out_st, sources, head_range):
        results = []
        for h in head_range:
            rows = slice(h * HDIM, (h + 1) * HDIM)
            ms = [st[h : h + 1, :] for _, st in sources]
            m = functools.reduce(jnp.maximum, ms)
            ws = [jnp.exp2(x - m) for x in ms]
            ls = [st[8 + h : 9 + h, :] * w for (_, st), w in zip(sources, ws)]
            terms = [part[rows, :].astype(jnp.float32) * w for (part, _), w in zip(sources, ws)]
            total = functools.reduce(jnp.add, terms).astype(jnp.bfloat16)
            results.append((h, rows, m, functools.reduce(jnp.add, ls), total))
        for h, rows, m, l, total in results:
            out[rows, :] = total
            out_st[h : h + 1, :] = m
            out_st[8 + h : 9 + h, :] = l

    every = range(heads)

    def forward(half, further):
        i, at = order.index(further), place(half, 2, further)
        start(
            half, i, way_of(further), o_ref.at[at], st_ref.at[at],
            relay.at[half, i], relay_st.at[half, i],
        )

    def direct(half, further):
        way = -way_of(further)
        i, at, side = order.index(further), place(half, way, further), 0 if way == 1 else 1
        start(
            half, 4 + i, way, o_ref.at[at], st_ref.at[at],
            got.at[half, side, i], got_st.at[half, side, i],
        )

    def merged(half, further):
        way = way_of(further)
        i, at, side = order.index(further), place(half, way, further), 0 if way == 1 else 1
        part, st = relay.at[half, i], relay_st.at[half, i]
        arrive(half, i, part, st)
        merge(part, st, [(part, st), (own.at[half, 0, i], st_own.at[at])], every)
        start(
            half, 4 + i, way, part, st, got.at[half, side, i], got_st.at[half, side, i]
        )

    def collect(half, further):
        i = order.index(further)
        both = pl.ds(0, 2)
        arrive(half, 4 + i, got.at[half, both, i], got_st.at[half, both, i])
        merge(
            mid.at[half, i], mid_st.at[half, i],
            [(own.at[half, 1, i], st_own.at[place(half, 0, further)])]
            + [(got.at[half, n, i], got_st.at[half, n, i]) for n in (0, 1)],
            every,
        )

    halves = (0, 1)
    for further in order:
        for half in halves:
            forward(half, further)
    for further in (2, -1):
        for half in halves:
            direct(half, further)

    key = lax.broadcasted_iota(jnp.int32, (span, span), 0)
    row = lax.broadcasted_iota(jnp.int32, (span, span), 1)

    def local(half, keys_of, values_of, bias, first):
        results = []
        for h in every:
            cols = slice(h * HDIM, (h + 1) * HDIM)
            s = dot_nt(keys_of(cols), query[half * span : (half + 1) * span, cols]) * SCALE
            s = jnp.where(key <= row, s, NEG) if bias is None else s + bias
            m = jnp.max(s, axis=0, keepdims=True)
            if not first:
                old = acc_st[half, h : h + 1, :]
                m = jnp.maximum(m, old)
                decay = jnp.exp2(old - m)
            p = jnp.exp2(s - m)
            l = jnp.sum(p, axis=0, keepdims=True)
            a = dot_tn(values_of(cols), p.astype(jnp.bfloat16))
            if not first:
                l = l + acc_st[half, 8 + h : 9 + h, :] * decay
                a = a + acc[half, cols, :] * decay
            results.append((h, cols, m, l, a))
        for h, cols, m, l, a in results:
            acc_st[half, h : h + 1, :] = m
            acc_st[half, 8 + h : 9 + h, :] = l
            acc[half, cols, :] = a

    for other in [query_load] + others:
        other.wait()
    load(own, own, 0).wait()
    for half in halves:
        rows = slice(half * span, (half + 1) * span)
        local(half, lambda c, r=rows: keys[r, c], lambda c, r=rows: values[r, c], None, True)

    for further in (2, -1):
        for half in halves:
            merged(half, further)
    for further in (1, 0):
        for half in halves:
            direct(half, further)
    for further in (1, 0):
        for half in halves:
            merged(half, further)
    local(1, lambda c: keys[0:span, c], lambda c: values[0:span, c], 0.0, False)

    for half in halves:
        collect(half, 2)
        for side, way in ((0, 1), (1, -1)):
            rows = pl.ds(*parts[side])
            start(
                half, 8 + side, way, mid.at[half, 0, rows], mid_st.at[half, 0],
                relay2.at[half, rows], relay2_st.at[half, side],
            )
    for side, way in ((1, -1), (0, 1)):
        for half in halves:
            i = order.index(way)
            collect(half, way)
            other = pl.ds(*parts[1 - side])
            start(
                half, 10, way, mid.at[half, i, other], mid_st.at[half, i],
                got2.at[half, side, other], got2_st.at[half, side, 1 - side],
            )
    for half in halves:
        for side, way in ((0, 1), (1, -1)):
            i = order.index(way)
            rows = pl.ds(*parts[side])
            part, st = relay2.at[half], relay2_st.at[half, side]
            arrive(half, 8 + side, relay2.at[half, rows], st)
            merge(
                part, st, [(part, st), (mid.at[half, i], mid_st.at[half, i])],
                range(parts[side][0] // HDIM, sum(parts[side]) // HDIM),
            )
            start(
                half, 10, way, relay2.at[half, rows], st,
                got2.at[half, side, rows], got2_st.at[half, side, side],
            )

    last = order.index(0)
    for half in halves:
        collect(half, 0)
        part, st = mid.at[half, last], mid_st.at[half, last]
        results = []
        for h in every:
            cols = slice(h * HDIM, (h + 1) * HDIM)
            old, new = acc_st[half, h : h + 1, :], st[h : h + 1, :]
            m = jnp.maximum(old, new)
            decay, w = jnp.exp2(old - m), jnp.exp2(new - m)
            l = acc_st[half, 8 + h : 9 + h, :] * decay + st[8 + h : 9 + h, :] * w
            a = acc[half, cols, :] * decay + part[cols, :].astype(jnp.float32) * w
            results.append((h, cols, m, l, a))
        for h, cols, m, l, a in results:
            acc_st[half, h : h + 1, :] = m
            acc_st[half, 8 + h : 9 + h, :] = l
            acc[half, cols, :] = a
    for half in halves:
        arrive(half, 10, got2.at[half], got2_st.at[half])
        for h in every:
            cols = slice(h * HDIM, (h + 1) * HDIM)
            which = 0 if h * HDIM < cut else 1
            sources = [(got2.at[half, i], got2_st.at[half, i, which]) for i in (0, 1)]
            old = acc_st[half, h : h + 1, :]
            ms = [st[h : h + 1, :] for _, st in sources]
            m = functools.reduce(jnp.maximum, ms, old)
            decay = jnp.exp2(old - m)
            total = acc_st[half, 8 + h : 9 + h, :] * decay
            a = acc[half, cols, :] * decay
            for (part, st), x in zip(sources, ms):
                w = jnp.exp2(x - m)
                total = total + st[8 + h : 9 + h, :] * w
                a = a + part[cols, :].astype(jnp.float32) * w
            out_ref[half * span : (half + 1) * span, cols] = jnp.transpose(a / total).astype(
                out_ref.dtype
            )

    for index, ref in enumerate(
        (
            o_ref.at[pl.ds(0, 3)],
            st_ref.at[pl.ds(0, 3)],
            o_ref.at[pl.ds(0, 3), 0],
            st_ref.at[pl.ds(0, 3), pl.ds(0, 2)],
        )
    ):
        to = {"context": context_of(zpos, xpos + 1)}
        remote(ref, ref, (send.at[index], recv, 0), 0, to).wait_send()


def combine(o, st, q_all, k, v, heads):
    span_count, width, span = o.shape[1:]
    rows = st.shape[2]
    o = o.reshape(RING, RING, span_count, width, span)
    st = st.reshape(RING, RING, span_count, rows, span)
    vmem = pl.BlockSpec(memory_space=pltpu.VMEM)
    hbm = pl.BlockSpec(memory_space=pl.ANY)

    def part(*lead):
        return pltpu.VMEM(lead + (width, span), jnp.bfloat16)

    def stats(*lead):
        return pltpu.VMEM(lead + (rows, span), jnp.float32)

    return pl.pallas_call(
        functools.partial(combine_kernel, heads),
        in_specs=[hbm] * 5,
        out_specs=vmem,
        out_shape=jax.ShapeDtypeStruct(k.shape, jnp.bfloat16),
        scratch_shapes=[
            part(2, 2, RING),
            pltpu.VMEM(k.shape, jnp.bfloat16),
            pltpu.VMEM(k.shape, jnp.bfloat16),
            pltpu.VMEM(k.shape, jnp.bfloat16),
            stats(RING, RING, span_count),
            part(2, RING),
            stats(2, RING),
            part(2, 2, RING),
            stats(2, 2, RING),
            part(2, RING),
            stats(2, RING),
            part(2),
            stats(2, 2),
            part(2, 2),
            stats(2, 2, 2),
            pltpu.VMEM((2, width, span), jnp.float32),
            stats(2),
        ]
        + [pltpu.SemaphoreType.DMA((count,)) for count in (5, 4, 22, 22)],
        compiler_params=pltpu.CompilerParams(
            collective_id=1, has_side_effects=True, vmem_limit_bytes=60 << 20
        ),
        name="combine",
    )(o, st, q_all, k, v)


def shards(
    tokens,
    query_weight,
    key_weight,
    value_weight,
    cache_keys,
    cache_values,
    selected,
    counts,
    block_slot,
):
    heads = query_weight.shape[1] // HDIM
    span_count, select_count = selected.shape
    devices = lax.axis_size("context")
    cap = max(2, 2 * span_count * select_count // devices)

    stored = cache_keys.shape[0]
    q_all, k, v, table = gather_project(
        tokens, query_weight, key_weight, value_weight, selected, counts, block_slot, cap, stored
    )
    o, st = owner_attention(table, q_all, cache_keys, cache_values, k, v, heads, cap)
    return combine(o, st, q_all, k, v, heads)


def solution(mesh):
    placed = (
        P("context", "tensor"),
        P("context", "tensor"),
        P("context", "tensor"),
        P("context", "tensor"),
        P("context", None, "tensor"),
        P("context", None, "tensor"),
        P("context", None),
        P("context"),
        P(),
    )
    return jax.shard_map(
        shards, mesh=mesh, in_specs=placed, out_specs=P("context", "tensor"), check_vma=False
    )
```

```python
import functools

import jax
import jax.numpy as jnp
from jax import lax
from jax.experimental import pallas as pl
from jax.experimental.pallas import tpu as pltpu
from jax.sharding import PartitionSpec as P

HDIM = 128
NEG = -1e30
MESH = pl.DeviceIdType.MESH
EXTRA = 16
GROUP = 4
SCALE = HDIM ** (-0.5) * 1.4426950408889634


def dot_nt(a, b):
    return lax.dot_general(a, b, (((1,), (1,)), ((), ())), preferred_element_type=jnp.float32)


def dot_tn(a, b):
    return lax.dot_general(a, b, (((0,), (0,)), ((), ())), preferred_element_type=jnp.float32)


RING = 4
OFFSETS = (0, -1, 1, 2)


def wrap(position):
    return lax.rem(position + RING, RING)


def context_of(zpos, xpos):
    return wrap(zpos) * RING + wrap(xpos)


class Ring:
    def __init__(self, view, to, sems, own=None):
        self.view, self.to, self.sems, self.own = view, to, sems, own

    def copy(self, index, step):
        ref = self.view(step, max(0, index - 1))
        src = self.own if step == 0 and self.own is not None else ref
        return remote(src, ref, self.sems, min(index, 2), self.to(1 if index % 2 == 0 else -1))

    def start(self, index):
        self.copy(index, (0, 0, -1, 1)[index]).start()

    def whole(self):
        self.start(0)
        self.start(1)

    def onward(self):
        self.copy(0, -1).wait_recv()
        self.start(2)
        self.copy(1, 1).wait_recv()
        self.start(3)

    def opposite(self):
        ref = self.view(2, 0)
        remote(ref, ref, self.sems, 2, self.to(1)).wait_recv()


def remote(src, dst, sems, index, to):
    send, recv, base = sems
    return pltpu.make_async_remote_copy(
        src_ref=src,
        dst_ref=dst,
        send_sem=send,
        recv_sem=recv.at[base + index],
        device_id=to,
        device_id_type=MESH,
    )


def context_gather(view, own, sems, zpos, xpos, halves=(0, 1)):
    rings = {}

    def make(half, phase):
        along_x = (half == 0) == (phase == 0)
        first = 0 if phase == 0 else OFFSETS[phase - 1]

        def piece(step, part):
            dz, dx = (first, step) if along_x else (step, first)
            return view(wrap(zpos + dz), wrap(xpos + dx), half, part)

        def to(way):
            dz, dx = (0, way) if along_x else (way, 0)
            return {"context": context_of(zpos + dz, xpos + dx)}

        send, recv, base = sems
        source = own(half) if first == 0 else None
        return Ring(piece, to, (send, recv, base + halves.index(half) * 15 + phase * 3), source)

    for half in halves:
        for phase in range(5):
            rings[half, phase] = make(half, phase)

    def own():
        for half in halves:
            rings[half, 0].whole()
            rings[half, 1].whole()

    def neighbours():
        for half in halves:
            rings[half, 0].onward()
            rings[half, 2].whole()
            rings[half, 3].whole()
        for half in halves:
            rings[half, 1].onward()

    def far():
        for half in halves:
            rings[half, 0].opposite()
            rings[half, 4].whole()

    def corners():
        for half in halves:
            rings[half, 2].onward()
            rings[half, 3].onward()

    def last():
        for half in halves:
            rings[half, 4].onward()

    def rest():
        for half in halves:
            for phase in (1, 2, 3, 4):
                rings[half, phase].opposite()

    return [own, neighbours, far, corners, last, rest]


def project_kernel(
    span_count, select_count, cap, stored,
    tok_ref, wq_ref, wk_ref, wv_ref, sel_hbm, count_hbm, slot_hbm,
    q_ref, k_out, v_out, tab_out,
    tok, stage, w, acc, done, back, fifth, small, told, sel_ref, count_ref, slot_ref,
    k_ref, v_ref, tab_ref,
    load_sem, send, trecv, wrecv, brecv, qrecv,
):
    me = lax.axis_index("context")
    zpos, xpos = me // RING, lax.rem(me, RING)
    col = lax.axis_index("tensor")
    ypos, core = col // 2, lax.rem(col, 2)
    token_count, depth = tok.shape[2], tok.shape[3]
    rows = w.shape[3]

    token_load = pltpu.make_async_copy(tok_ref, tok.at[col, zpos], load_sem.at[0])
    token_load.start()
    lists = [
        pltpu.make_async_copy(src, dst, load_sem.at[8 + i])
        for i, (src, dst) in enumerate(
            ((sel_hbm, sel_ref), (count_hbm, count_ref), (slot_hbm, slot_ref))
        )
    ]
    for load in lists:
        load.start()
    for part in (0, 1):
        for to in range(RING):
            left = (wq_ref, wk_ref, wv_ref, wq_ref)[to]
            pair = ((wq_ref, to), (left, RING)) if part == 0 else ((wk_ref, to), (wv_ref, to))
            for i, (ref, head) in enumerate(pair):
                load = pltpu.make_async_copy(
                    ref.at[:, pl.ds(head * HDIM, HDIM)],
                    stage.at[part, to, :, pl.ds(i * HDIM, HDIM)],
                    load_sem.at[2 + part],
                )
                load.start()

    def at_x(way):
        return {"context": context_of(zpos, xpos + way)}

    def at_z(way):
        return {"context": context_of(zpos + way, xpos)}

    def at_y(way):
        return {"tensor": wrap(ypos + way) * 2 + core}

    mate = {"tensor": ypos * 2 + 1 - core}
    barrier = pltpu.get_barrier_semaphore()
    partners = [at_x(1), at_x(-1), at_z(1), at_z(-1), at_z(2), at_y(1), at_y(-1), mate]
    for other in partners:
        pl.semaphore_signal(barrier, inc=1, device_id=other, device_id_type=MESH)
    pl.semaphore_wait(barrier, len(partners))

    def cut(size):
        return (pl.ds(0, size), pl.ds(0, size // 2), pl.ds(size // 2, size // 2))

    ztok = Ring(
        lambda step, part: tok.at[col, wrap(zpos + step), cut(token_count)[part]],
        at_z, (send.at[0], trecv, 0),
    )
    ytok = {
        o: Ring(
            lambda step, part, o=o: tok.at[
                wrap(ypos + step) * 2 + core, wrap(zpos + o), cut(token_count)[part]
            ],
            at_y, (send.at[0], trecv, 3 + 3 * i),
        )
        for i, o in enumerate(OFFSETS)
    }

    def share(step, o):
        ref = tok.at[wrap(ypos + step) * 2 + core, wrap(zpos + o)]
        remote(ref, ref, (send.at[1], trecv, 15), OFFSETS.index(o), mate).start()

    def shared(o):
        ref = tok.at[pl.ds(0, RING), 0]
        remote(ref, ref, (send.at[1], trecv, 15), OFFSETS.index(o), mate).wait_recv()

    def exchange(part, step, receive=False):
        index = part * 3 + OFFSETS.index(step) - 1
        src = stage.at[part, wrap(zpos + step)]
        if receive:
            dst = w.at[part, wrap(zpos - step), xpos]
            remote(src, dst, (send.at[2], wrecv, 0), index, at_z(step)).wait_recv()
        else:
            dst = w.at[part, zpos, xpos]
            remote(src, dst, (send.at[2], wrecv, 0), index, at_z(step)).start()

    xw = {
        (part, o): Ring(
            lambda step, piece, part=part, o=o: w.at[
                part, wrap(zpos + o), wrap(xpos + step), cut(rows)[piece]
            ],
            at_x, (send.at[3], wrecv, 6 + part * 12 + 3 * i),
        )
        for part in (0, 1)
        for i, o in enumerate(OFFSETS)
    }

    def keep(part):
        whole = stage.at[part]
        pltpu.make_async_copy(whole, whole, load_sem.at[2 + part]).wait()
        copy = pltpu.make_async_copy(
            stage.at[part, zpos], w.at[part, zpos, xpos], load_sem.at[4 + part]
        )
        copy.start()
        copy.wait()

    def queries(o):
        z = wrap(zpos + o)

        @pl.loop(0, tok.shape[0])
        def _(t):
            piece = w[0, t // 2, pl.ds(lax.rem(t, 2) * 2, 2)].reshape(depth, w.shape[4])
            new = jnp.dot(tok[t, z], piece, preferred_element_type=jnp.float32)

            @pl.when(t == 0)
            def _():
                acc[z] = new

            @pl.when(t > 0)
            def _():
                acc[z] += new

        done[0, z] = acc[z].astype(jnp.bfloat16)
        last_head = slice(HDIM, 2 * HDIM)
        if o == 0:
            fifth[zpos] = acc[z, :, last_head].astype(jnp.bfloat16)
        else:
            src = done.at[0, z, :, last_head]
            remote(src, fifth.at[zpos], (send.at[4], brecv, 0), 0, at_z(o)).start()

    def compute(step):
        for side in (0, 1):
            t = wrap(ypos + step) * 2 + side
            piece = w[1, wrap(ypos + step), 2 * side : 2 * side + 2].reshape(depth, w.shape[4])

            @pl.loop(0, RING)
            def _(z):
                new = jnp.dot(tok[t, z], piece, preferred_element_type=jnp.float32)
                if step == 0 and side == 0:
                    acc[z] = new
                else:
                    acc[z] += new

    def give_back():
        @pl.loop(0, RING)
        def _(z):
            done[1, z] = acc[z].astype(jnp.bfloat16)

        back[zpos] = acc[zpos].astype(jnp.bfloat16)
        for step in OFFSETS[1:]:
            src = done.at[1, wrap(zpos + step)]
            remote(src, back.at[zpos], (send.at[5], brecv, 1), 0, at_z(step)).start()

    def take_back(buf, index):
        ref = buf.at[pl.ds(0, RING - 1)]
        remote(ref, ref, (send.at[4], brecv, index), 0, at_z(1)).wait_recv()

    def heads_of(o, base, halves):
        size = token_count // len(halves)

        def view(z, x, half, part):
            head = pl.ds(pl.multiple_of(z * HDIM, HDIM), HDIM)
            low = halves.index(half) * size + (size // 2 if part == 2 else 0)
            rows = pl.ds(low, size if part == 0 else size // 2)
            return q_ref.at[wrap(z + o), x, rows, head]

        def own(half):
            return done.at[0, wrap(zpos + o), pl.ds(halves.index(half) * size, size), pl.ds(0, HDIM)]

        return context_gather(view, own, (send.at[6], qrecv, base), zpos, xpos, halves)

    heads = {
        o: heads_of(o, *rest)
        for o, *rest in ((0, 30, (0,)), (-1, 45, (0,)), (1, 60, (1,)), (2, 75, (1,)))
    }

    half_rows = token_count // 2
    quarter = half_rows // 2
    ranges = (
        ((0, half_rows), (0, quarter), (quarter, quarter)),
        (
            (half_rows, half_rows + EXTRA),
            (half_rows, quarter),
            (half_rows + quarter, quarter + EXTRA),
        ),
    )

    def last_view(z, x, half, part):
        return q_ref.at[z, x, pl.ds(*ranges[half][part]), pl.ds(RING * HDIM, HDIM)]

    def last_own(half):
        return small.at[pl.ds(*ranges[half][0]), :]

    last = context_gather(last_view, last_own, (send.at[7], qrecv, 0), zpos, xpos)

    token_load.wait()
    ytok[0].whole()
    keep(0)
    xw[0, 0].whole()
    exchange(0, 1)
    exchange(0, -1)
    ztok.whole()
    share(0, 0)
    keep(1)
    xw[1, 0].whole()

    lane = lax.broadcasted_iota(jnp.int32, (EXTRA, HDIM), 1)
    line = lax.broadcasted_iota(jnp.int32, (EXTRA, HDIM), 0)
    for load in lists:
        load.wait()
    chosen = jnp.zeros((EXTRA, HDIM), jnp.int32)
    for half in range(span_count):

        def note(j, chosen, half=half):
            slot = slot_ref[jnp.maximum(sel_ref[half, j], 0)]
            owner = jnp.where(j < count_ref[half], slot // stored, -1)
            value = jnp.where(line == half, owner, slot % stored)
            here = (lane == j) & ((line == half) | (line == span_count + half))
            return jnp.where(here, value, chosen)

        chosen = lax.fori_loop(0, select_count, note, chosen)
    small[token_count:, :] = chosen.astype(jnp.float32).astype(jnp.bfloat16)

    xw[0, 0].onward()
    ytok[0].onward()
    ztok.onward()
    for o in (-1, 1):
        ytok[o].whole()
        share(0, o)
    exchange(0, 2)
    exchange(1, 1)
    exchange(1, -1)
    exchange(1, 2)
    share(-1, 0)
    share(1, 0)
    for step in (1, -1):
        exchange(0, step, receive=True)
        xw[0, -step].whole()
    ztok.opposite()
    ytok[2].whole()
    share(0, 2)
    exchange(0, 2, receive=True)
    xw[0, 2].whole()
    ytok[-1].onward()
    share(-1, -1)
    share(1, -1)
    ytok[0].opposite()
    share(2, 0)
    xw[0, -1].onward()
    xw[0, 1].onward()
    xw[1, 0].onward()
    ytok[1].onward()
    share(-1, 1)
    share(1, 1)
    xw[0, 2].onward()
    for step in (1, -1):
        exchange(1, step, receive=True)
        xw[1, -step].whole()
    exchange(1, 2, receive=True)
    xw[1, 2].whole()
    for o in OFFSETS:
        xw[0, o].opposite()
    shared(0)
    queries(0)
    heads[0][0]()
    ytok[-1].opposite()
    share(2, -1)
    xw[1, -1].onward()
    xw[1, 1].onward()
    ytok[2].onward()
    share(-1, 2)
    share(1, 2)
    shared(-1)
    queries(-1)
    heads[-1][0]()
    ytok[1].opposite()
    share(2, 1)
    xw[1, 2].onward()
    heads[0][1]()
    shared(1)
    queries(1)
    heads[1][0]()
    ytok[2].opposite()
    share(2, 2)
    heads[-1][1]()
    shared(2)
    queries(2)
    heads[2][0]()
    keeps = [
        pltpu.make_async_copy(
            done.at[0, :, :, pl.ds(0, HDIM)],
            q_ref.at[
                :, xpos, pl.ds(0, token_count), pl.ds(pl.multiple_of(zpos * HDIM, HDIM), HDIM)
            ],
            load_sem.at[1],
        )
    ]
    keeps[0].start()
    heads[0][2]()
    heads[1][1]()
    take_back(fifth, 0)
    small[0:token_count, :] = fifth[0]
    last[0]()
    keeps.append(
        pltpu.make_async_copy(
            small, q_ref.at[zpos, xpos, :, pl.ds(RING * HDIM, HDIM)], load_sem.at[6]
        )
    )
    keeps[1].start()
    for o in OFFSETS:
        xw[1, o].opposite()
    compute(0)
    heads[-1][2]()
    heads[0][3]()
    heads[2][1]()
    compute(-1)
    last[1]()
    heads[1][2]()
    heads[-1][3]()
    heads[0][4]()
    compute(1)
    heads[2][2]()
    heads[1][3]()
    last[2]()
    compute(2)
    give_back()
    heads[-1][4]()
    heads[2][3]()
    last[3]()
    heads[1][4]()
    heads[2][4]()
    last[4]()
    for keep_copy in keeps:
        keep_copy.wait()
    for o in OFFSETS:
        heads[o][5]()
    last[5]()
    look = pltpu.make_async_copy(
        q_ref.at[:, :, pl.ds(token_count, EXTRA), pl.ds(RING * HDIM, HDIM)],
        told,
        load_sem.at[7],
    )
    look.start()
    take_back(back, 1)
    for head in range(RING):
        cols = slice(head * HDIM, (head + 1) * HDIM)
        k_ref[:, cols] = back[head, :, 0:HDIM]
        v_ref[:, cols] = back[head, :, HDIM : 2 * HDIM]
    k_ref[:, RING * HDIM :] = fifth[1]
    v_ref[:, RING * HDIM :] = fifth[2]
    puts = [
        pltpu.make_async_copy(k_ref, k_out, load_sem.at[11]),
        pltpu.make_async_copy(v_ref, v_out, load_sem.at[12]),
        pltpu.make_async_copy(tab_ref, tab_out, load_sem.at[13]),
    ]
    puts[0].start()
    puts[1].start()
    look.wait()

    devices = RING * RING
    lane = lax.broadcasted_iota(jnp.int32, (devices, HDIM), 1)
    source = lax.broadcasted_iota(jnp.int32, (devices, HDIM), 0)
    before = lax.broadcasted_iota(jnp.int32, (HDIM, HDIM), 0)
    after = lax.broadcasted_iota(jnp.int32, (HDIM, HDIM), 1)
    earlier = jnp.where(before < after, 1.0, 0.0).astype(jnp.bfloat16)
    listed = told[...].reshape(devices, EXTRA, HDIM).astype(jnp.float32)
    for half in range(span_count):
        owner = listed[:, half, :]
        row = listed[:, span_count + half, :]
        mine = jnp.where((owner == me.astype(jnp.float32)) & (lane < select_count), 1.0, 0.0)
        rank = jnp.dot(mine.astype(jnp.bfloat16), earlier, preferred_element_type=jnp.float32)
        table = jnp.where(lane == cap, jnp.sum(mine, axis=1, keepdims=True), 0.0)
        for r in range(cap):
            value = jnp.sum(jnp.where(rank == r, mine * row, 0.0), axis=1, keepdims=True)
            table = jnp.where(lane == r, value, table)
        if half == 0:
            table = jnp.where((lane == cap + 1) & (source == me + 1), 1.0, table)
        tab_ref[half] = table.astype(jnp.int32)
    puts[2].start()

    for put in puts:
        put.wait()
    for index, ref in enumerate(
        (
            tok.at[pl.ds(0, 5), pl.ds(0, 3)],
            tok.at[pl.ds(0, 4)],
            w.at[pl.ds(0, 2), pl.ds(0, 3), 0],
            w.at[pl.ds(0, 2), pl.ds(0, 3)],
            fifth.at[pl.ds(0, 3)],
            back.at[pl.ds(0, 3)],
            q_ref.at[:, pl.ds(0, 3), pl.ds(0, token_count), :],
            q_ref.at[0, pl.ds(0, 3)],
        )
    ):
        remote(ref, ref, (send.at[index], brecv, 0), 0, at_z(1)).wait_send()


def gather_project(tokens, wq, wk, wv, selected, counts, block_slot, cap, stored):
    token_count, depth = tokens.shape
    rows, width = wq.shape
    span_count, select_count = selected.shape
    devices = lax.axis_size("context")
    columns = lax.axis_size("tensor")
    hbm = pl.BlockSpec(memory_space=pl.ANY)
    own = jax.ShapeDtypeStruct((token_count, width), jnp.bfloat16)
    two = 2 * HDIM

    return pl.pallas_call(
        functools.partial(project_kernel, span_count, select_count, cap, stored),
        in_specs=[hbm] * 7,
        out_specs=[hbm] * 4,
        out_shape=[
            jax.ShapeDtypeStruct((RING, RING, token_count + EXTRA, width), jnp.bfloat16),
            own,
            own,
            jax.ShapeDtypeStruct((span_count, devices, HDIM), jnp.int32),
        ],
        scratch_shapes=[
            pltpu.VMEM((columns, RING, token_count, depth), jnp.bfloat16),
            pltpu.VMEM((2, RING, rows, two), jnp.bfloat16),
            pltpu.VMEM((2, RING, RING, rows, two), jnp.bfloat16),
            pltpu.VMEM((RING, token_count, two), jnp.float32),
            pltpu.VMEM((2, RING, token_count, two), jnp.bfloat16),
            pltpu.VMEM((RING, token_count, two), jnp.bfloat16),
            pltpu.VMEM((RING, token_count, HDIM), jnp.bfloat16),
            pltpu.VMEM((token_count + EXTRA, HDIM), jnp.bfloat16),
            pltpu.VMEM((RING, RING, EXTRA, HDIM), jnp.bfloat16),
            pltpu.SMEM(selected.shape, jnp.int32),
            pltpu.SMEM(counts.shape, jnp.int32),
            pltpu.SMEM(block_slot.shape, jnp.int32),
            pltpu.VMEM((token_count, width), jnp.bfloat16),
            pltpu.VMEM((token_count, width), jnp.bfloat16),
            pltpu.VMEM((span_count, devices, HDIM), jnp.int32),
        ]
        + [pltpu.SemaphoreType.DMA((count,)) for count in (14, 8, 19, 30, 2, 90)],
        compiler_params=pltpu.CompilerParams(
            collective_id=0, has_side_effects=True, vmem_limit_bytes=60 << 20
        ),
        name="gather_project",
    )(tokens, wq, wk, wv, selected, counts, block_slot)


def owner_kernel(
    heads, cap, tab_ref, q_ref, k_ref, v_ref, pk_ref, pv_ref, o_ref, st_ref, acc_ref
):
    group, span_count, span = o_ref.shape[0], o_ref.shape[1], o_ref.shape[3]
    first = pl.program_id(0) * group
    block = k_ref.shape[1]
    columns = [slice(h * HDIM, (h + 1) * HDIM) for h in range(heads)]

    def score(i, half, h, j):
        r0 = tab_ref[half, first + i, 2 * j]
        r1 = tab_ref[half, first + i, 2 * j + 1]
        bias = jnp.where(2 * j + 1 < tab_ref[half, first + i, cap], 0.0, NEG)
        cols = columns[h]
        q = q_ref[i, half * span : (half + 1) * span, cols]
        k = jnp.concatenate([k_ref[r0, :, cols], k_ref[r1, :, cols]], 0)
        v = jnp.concatenate([v_ref[r0, :, cols], v_ref[r1, :, cols]], 0)
        s = dot_nt(k, q) * SCALE
        return jnp.concatenate([s[:block], s[block:] + bias], 0), v

    def put(i, half, h, m, l, a):
        st_ref[i, half, h : h + 1, :] = m
        st_ref[i, half, 8 + h : 9 + h, :] = l
        acc_ref[i, half, columns[h], :] = a
        o_ref[i, half, columns[h], :] = a.astype(jnp.bfloat16)

    places = [(i, half) for i in range(group) for half in range(span_count)]
    def soften(i, half, h, s, v):
        m = jnp.max(s, axis=0, keepdims=True)
        p = jnp.exp2(s - m)
        l = jnp.sum(p, axis=0, keepdims=True)
        m = jnp.where(tab_ref[half, first + i, cap] > 0, m, NEG)
        return i, half, h, m, l, p.astype(jnp.bfloat16), v

    def weigh(i, half, h, m, l, p, v):
        return i, half, h, m, l, dot_tn(v, p)

    made = [[(i, half, h, *score(i, half, h, 0)) for h in range(heads)] for i, half in places]
    results = []
    for tiles in made:
        soft = [soften(*tile) for tile in tiles]
        results += [weigh(*tile) for tile in soft]
    for result in results:
        put(*result)

    def more(i, half, tiles):
        results = []
        for h, (s, v) in enumerate(tiles):
            old = st_ref[i, half, h : h + 1, :]
            m = jnp.maximum(jnp.max(s, axis=0, keepdims=True), old)
            decay = jnp.exp2(old - m)
            p = jnp.exp2(s - m)
            l = jnp.sum(p, axis=0, keepdims=True)
            l = l + st_ref[i, half, 8 + h : 9 + h, :] * decay
            a = dot_tn(v, p.astype(jnp.bfloat16))
            a = a + acc_ref[i, half, columns[h], :] * decay
            results.append((i, half, h, m, l, a))
        for result in results:
            put(*result)

    for i, half in places:
        n = tab_ref[half, first + i, cap]

        @pl.when(n > 2)
        def _(i=i, half=half, n=n):
            @pl.loop(1, (n + 1) // 2)
            def _(j):
                more(i, half, [score(i, half, h, j) for h in range(heads)])

    for i in range(group):

        @pl.when(tab_ref[0, first + i, cap + 1] > 0)
        def _(i=i):
            tiles = [
                (dot_nt(pk_ref[:, cols], q_ref[i, 0:span, cols]) * SCALE, pv_ref[:, cols])
                for cols in columns
            ]
            more(i, 0, tiles)


def owner_attention(table, q_all, cache_keys, cache_values, k, v, heads, cap):
    tokens, width = q_all.shape[2] - EXTRA, q_all.shape[3]
    span_count, devices = table.shape[:2]
    span = tokens // span_count
    q_all = q_all.reshape(devices, tokens + EXTRA, width)
    newest = pl.BlockSpec((span, width), lambda s, *_: (span_count - 1, 0))
    whole = pl.BlockSpec(cache_keys.shape, lambda s, *_: (0, 0, 0), pipeline_mode=pl.Buffered(1))
    return pl.pallas_call(
        functools.partial(owner_kernel, heads, cap),
        grid_spec=pltpu.PrefetchScalarGridSpec(
            num_scalar_prefetch=1,
            grid=(devices // GROUP,),
            in_specs=[
                pl.BlockSpec((GROUP, tokens, width), lambda s, *_: (s, 0, 0)),
                whole,
                whole,
                newest,
                newest,
            ],
            out_specs=[
                pl.BlockSpec((GROUP, span_count, width, span), lambda s, *_: (s, 0, 0, 0)),
                pl.BlockSpec((GROUP, span_count, 16, span), lambda s, *_: (s, 0, 0, 0)),
            ],
            scratch_shapes=[pltpu.VMEM((GROUP, span_count, width, span), jnp.float32)],
        ),
        out_shape=[
            jax.ShapeDtypeStruct((devices, span_count, width, span), jnp.bfloat16),
            jax.ShapeDtypeStruct((devices, span_count, 16, span), jnp.float32),
        ],
        name="owner_attention",
    )(table, q_all, cache_keys, cache_values, k, v)


def combine_kernel(
    heads,
    o_ref, st_ref, q_ref, k_ref, v_ref,
    out_ref,
    own, query, keys, values, st_own, relay, relay_st, got, got_st, mid, mid_st,
    relay2, relay2_st, got2, got2_st, acc, acc_st,
    load_sem, send, recv, recv_st,
):
    me = lax.axis_index("context")
    zpos, xpos = me // RING, lax.rem(me, RING)
    span = o_ref.shape[-1]
    token_count = k_ref.shape[0]
    cut = (heads + 1) // 2 * HDIM
    parts = ((0, cut), (cut, heads * HDIM - cut))
    order = (2, -1, 1, 0)

    def first_at(half, step):
        return wrap((xpos if half == 0 else zpos) + step)

    def second_at(half, step):
        return wrap((zpos if half == 0 else xpos) + step)

    def place(half, step, further):
        a, b = first_at(half, step), second_at(half, further)
        return (b, a, half) if half == 0 else (a, b, half)

    def way_of(further):
        return 1 if further in (2, 1) else -1

    def load(ref, dst, index):
        return pltpu.make_async_copy(ref, dst, load_sem.at[index])

    for kind in (0, 1):
        for further in order:
            for half in (0, 1):
                step = way_of(further) if kind == 0 else 0
                slot = (half, kind, order.index(further))
                load(o_ref.at[place(half, step, further)], own.at[slot], 0).start()
    query_load = load(q_ref.at[zpos, xpos, pl.ds(0, token_count)], query, 1)
    others = [load(k_ref, keys, 2), load(v_ref, values, 3), load(st_ref, st_own, 4)]
    for other in [query_load] + others:
        other.start()

    barrier = pltpu.get_barrier_semaphore()
    for other in (
        context_of(zpos + 1, xpos),
        context_of(zpos - 1, xpos),
        context_of(zpos, xpos + 1),
        context_of(zpos, xpos - 1),
    ):
        pl.semaphore_signal(barrier, inc=1, device_id={"context": other}, device_id_type=MESH)
    pl.semaphore_wait(barrier, 4)

    def copies(half, index, way, src, src_st, dst, dst_st):
        first = index < 8
        if (half == 0) == first:
            to = {"context": context_of(zpos, xpos + way)}
        else:
            to = {"context": context_of(zpos + way, xpos)}
        kind = 0 if first else 2
        return (
            remote(src, dst, (send.at[kind], recv, half * 11), index, to),
            remote(src_st, dst_st, (send.at[kind + 1], recv_st, half * 11), index, to),
        )

    def start(*args):
        for copy in copies(*args):
            copy.start()

    def arrive(half, index, dst, dst_st):
        for copy in copies(half, index, 1, dst, dst_st, dst, dst_st):
            copy.wait_recv()

    def merge(out, out_st, sources, head_range):
        results = []
        for h in head_range:
            rows = slice(h * HDIM, (h + 1) * HDIM)
            ms = [st[h : h + 1, :] for _, st in sources]
            m = functools.reduce(jnp.maximum, ms)
            ws = [jnp.exp2(x - m) for x in ms]
            ls = [st[8 + h : 9 + h, :] * w for (_, st), w in zip(sources, ws)]
            terms = [part[rows, :].astype(jnp.float32) * w for (part, _), w in zip(sources, ws)]
            total = functools.reduce(jnp.add, terms).astype(jnp.bfloat16)
            results.append((h, rows, m, functools.reduce(jnp.add, ls), total))
        for h, rows, m, l, total in results:
            out[rows, :] = total
            out_st[h : h + 1, :] = m
            out_st[8 + h : 9 + h, :] = l

    every = range(heads)

    def forward(half, further):
        i, at = order.index(further), place(half, 2, further)
        start(
            half, i, way_of(further), o_ref.at[at], st_ref.at[at],
            relay.at[half, i], relay_st.at[half, i],
        )

    def direct(half, further):
        way = -way_of(further)
        i, at, side = order.index(further), place(half, way, further), 0 if way == 1 else 1
        start(
            half, 4 + i, way, o_ref.at[at], st_ref.at[at],
            got.at[half, side, i], got_st.at[half, side, i],
        )

    def merged(half, further):
        way = way_of(further)
        i, at, side = order.index(further), place(half, way, further), 0 if way == 1 else 1
        part, st = relay.at[half, i], relay_st.at[half, i]
        arrive(half, i, part, st)
        merge(part, st, [(part, st), (own.at[half, 0, i], st_own.at[at])], every)
        start(
            half, 4 + i, way, part, st, got.at[half, side, i], got_st.at[half, side, i]
        )

    def collect(half, further):
        i = order.index(further)
        both = pl.ds(0, 2)
        arrive(half, 4 + i, got.at[half, both, i], got_st.at[half, both, i])
        merge(
            mid.at[half, i], mid_st.at[half, i],
            [(own.at[half, 1, i], st_own.at[place(half, 0, further)])]
            + [(got.at[half, n, i], got_st.at[half, n, i]) for n in (0, 1)],
            every,
        )

    halves = (0, 1)
    for further in order:
        for half in halves:
            forward(half, further)
    for further in (2, -1):
        for half in halves:
            direct(half, further)

    key = lax.broadcasted_iota(jnp.int32, (span, span), 0)
    row = lax.broadcasted_iota(jnp.int32, (span, span), 1)

    def local(half, keys_of, values_of, bias, first):
        results = []
        for h in every:
            cols = slice(h * HDIM, (h + 1) * HDIM)
            s = dot_nt(keys_of(cols), query[half * span : (half + 1) * span, cols]) * SCALE
            s = jnp.where(key <= row, s, NEG) if bias is None else s + bias
            m = jnp.max(s, axis=0, keepdims=True)
            if not first:
                old = acc_st[half, h : h + 1, :]
                m = jnp.maximum(m, old)
                decay = jnp.exp2(old - m)
            p = jnp.exp2(s - m)
            l = jnp.sum(p, axis=0, keepdims=True)
            a = dot_tn(values_of(cols), p.astype(jnp.bfloat16))
            if not first:
                l = l + acc_st[half, 8 + h : 9 + h, :] * decay
                a = a + acc[half, cols, :] * decay
            results.append((h, cols, m, l, a))
        for h, cols, m, l, a in results:
            acc_st[half, h : h + 1, :] = m
            acc_st[half, 8 + h : 9 + h, :] = l
            acc[half, cols, :] = a

    for other in [query_load] + others:
        other.wait()
    load(own, own, 0).wait()
    for half in halves:
        rows = slice(half * span, (half + 1) * span)
        local(half, lambda c, r=rows: keys[r, c], lambda c, r=rows: values[r, c], None, True)

    for further in (2, -1):
        for half in halves:
            merged(half, further)
    for further in (1, 0):
        for half in halves:
            direct(half, further)
    for further in (1, 0):
        for half in halves:
            merged(half, further)
    local(1, lambda c: keys[0:span, c], lambda c: values[0:span, c], 0.0, False)

    for half in halves:
        collect(half, 2)
        for side, way in ((0, 1), (1, -1)):
            rows = pl.ds(*parts[side])
            start(
                half, 8 + side, way, mid.at[half, 0, rows], mid_st.at[half, 0],
                relay2.at[half, rows], relay2_st.at[half, side],
            )
    for side, way in ((1, -1), (0, 1)):
        for half in halves:
            i = order.index(way)
            collect(half, way)
            other = pl.ds(*parts[1 - side])
            start(
                half, 10, way, mid.at[half, i, other], mid_st.at[half, i],
                got2.at[half, side, other], got2_st.at[half, side, 1 - side],
            )
    for half in halves:
        for side, way in ((0, 1), (1, -1)):
            i = order.index(way)
            rows = pl.ds(*parts[side])
            part, st = relay2.at[half], relay2_st.at[half, side]
            arrive(half, 8 + side, relay2.at[half, rows], st)
            merge(
                part, st, [(part, st), (mid.at[half, i], mid_st.at[half, i])],
                range(parts[side][0] // HDIM, sum(parts[side]) // HDIM),
            )
            start(
                half, 10, way, relay2.at[half, rows], st,
                got2.at[half, side, rows], got2_st.at[half, side, side],
            )

    last = order.index(0)
    for half in halves:
        collect(half, 0)
        part, st = mid.at[half, last], mid_st.at[half, last]
        results = []
        for h in every:
            cols = slice(h * HDIM, (h + 1) * HDIM)
            old, new = acc_st[half, h : h + 1, :], st[h : h + 1, :]
            m = jnp.maximum(old, new)
            decay, w = jnp.exp2(old - m), jnp.exp2(new - m)
            l = acc_st[half, 8 + h : 9 + h, :] * decay + st[8 + h : 9 + h, :] * w
            a = acc[half, cols, :] * decay + part[cols, :].astype(jnp.float32) * w
            results.append((h, cols, m, l, a))
        for h, cols, m, l, a in results:
            acc_st[half, h : h + 1, :] = m
            acc_st[half, 8 + h : 9 + h, :] = l
            acc[half, cols, :] = a
    for half in halves:
        arrive(half, 10, got2.at[half], got2_st.at[half])
        for h in every:
            cols = slice(h * HDIM, (h + 1) * HDIM)
            which = 0 if h * HDIM < cut else 1
            sources = [(got2.at[half, i], got2_st.at[half, i, which]) for i in (0, 1)]
            old = acc_st[half, h : h + 1, :]
            ms = [st[h : h + 1, :] for _, st in sources]
            m = functools.reduce(jnp.maximum, ms, old)
            decay = jnp.exp2(old - m)
            total = acc_st[half, 8 + h : 9 + h, :] * decay
            a = acc[half, cols, :] * decay
            for (part, st), x in zip(sources, ms):
                w = jnp.exp2(x - m)
                total = total + st[8 + h : 9 + h, :] * w
                a = a + part[cols, :].astype(jnp.float32) * w
            out_ref[half * span : (half + 1) * span, cols] = jnp.transpose(a / total).astype(
                out_ref.dtype
            )

    for index, ref in enumerate(
        (
            o_ref.at[pl.ds(0, 3)],
            st_ref.at[pl.ds(0, 3)],
            o_ref.at[pl.ds(0, 3), 0],
            st_ref.at[pl.ds(0, 3), pl.ds(0, 2)],
        )
    ):
        to = {"context": context_of(zpos, xpos + 1)}
        remote(ref, ref, (send.at[index], recv, 0), 0, to).wait_send()


def combine(o, st, q_all, k, v, heads):
    span_count, width, span = o.shape[1:]
    rows = st.shape[2]
    o = o.reshape(RING, RING, span_count, width, span)
    st = st.reshape(RING, RING, span_count, rows, span)
    vmem = pl.BlockSpec(memory_space=pltpu.VMEM)
    hbm = pl.BlockSpec(memory_space=pl.ANY)

    def part(*lead):
        return pltpu.VMEM(lead + (width, span), jnp.bfloat16)

    def stats(*lead):
        return pltpu.VMEM(lead + (rows, span), jnp.float32)

    return pl.pallas_call(
        functools.partial(combine_kernel, heads),
        in_specs=[hbm] * 5,
        out_specs=vmem,
        out_shape=jax.ShapeDtypeStruct(k.shape, jnp.bfloat16),
        scratch_shapes=[
            part(2, 2, RING),
            pltpu.VMEM(k.shape, jnp.bfloat16),
            pltpu.VMEM(k.shape, jnp.bfloat16),
            pltpu.VMEM(k.shape, jnp.bfloat16),
            stats(RING, RING, span_count),
            part(2, RING),
            stats(2, RING),
            part(2, 2, RING),
            stats(2, 2, RING),
            part(2, RING),
            stats(2, RING),
            part(2),
            stats(2, 2),
            part(2, 2),
            stats(2, 2, 2),
            pltpu.VMEM((2, width, span), jnp.float32),
            stats(2),
        ]
        + [pltpu.SemaphoreType.DMA((count,)) for count in (5, 4, 22, 22)],
        compiler_params=pltpu.CompilerParams(
            collective_id=1, has_side_effects=True, vmem_limit_bytes=60 << 20
        ),
        name="combine",
    )(o, st, q_all, k, v)


def shards(
    tokens,
    query_weight,
    key_weight,
    value_weight,
    cache_keys,
    cache_values,
    selected,
    counts,
    block_slot,
):
    heads = query_weight.shape[1] // HDIM
    span_count, select_count = selected.shape
    devices = lax.axis_size("context")
    cap = max(2, 2 * span_count * select_count // devices)

    stored = cache_keys.shape[0]
    q_all, k, v, table = gather_project(
        tokens, query_weight, key_weight, value_weight, selected, counts, block_slot, cap, stored
    )
    o, st = owner_attention(table, q_all, cache_keys, cache_values, k, v, heads, cap)
    return combine(o, st, q_all, k, v, heads)


def solution(mesh):
    placed = (
        P("context", "tensor"),
        P("context", "tensor"),
        P("context", "tensor"),
        P("context", "tensor"),
        P("context", None, "tensor"),
        P("context", None, "tensor"),
        P("context", None),
        P("context"),
        P(),
    )
    return jax.shard_map(
        shards, mesh=mesh, in_specs=placed, out_specs=P("context", "tensor"), check_vma=False
    )
```

```python
import functools

import jax
import jax.numpy as jnp
from jax import lax
from jax.experimental import pallas as pl
from jax.experimental.pallas import tpu as pltpu
from jax.sharding import PartitionSpec as P

HDIM = 128
NEG = -1e30
MESH = pl.DeviceIdType.MESH
EXTRA = 16
GROUP = 2
SCALE = HDIM ** (-0.5) * 1.4426950408889634


def dot_nt(a, b):
    return lax.dot_general(a, b, (((1,), (1,)), ((), ())), preferred_element_type=jnp.float32)


def dot_tn(a, b):
    return lax.dot_general(a, b, (((0,), (0,)), ((), ())), preferred_element_type=jnp.float32)


RING = 4
OFFSETS = (0, -1, 1, 2)


def wrap(position):
    return lax.rem(position + RING, RING)


def context_of(zpos, xpos):
    return wrap(zpos) * RING + wrap(xpos)


class Ring:
    def __init__(self, view, to, sems, own=None):
        self.view, self.to, self.sems, self.own = view, to, sems, own

    def copy(self, index, step):
        ref = self.view(step, max(0, index - 1))
        src = self.own if step == 0 and self.own is not None else ref
        return remote(src, ref, self.sems, min(index, 2), self.to(1 if index % 2 == 0 else -1))

    def start(self, index):
        self.copy(index, (0, 0, -1, 1)[index]).start()

    def whole(self):
        self.start(0)
        self.start(1)

    def onward(self):
        self.copy(0, -1).wait_recv()
        self.start(2)
        self.copy(1, 1).wait_recv()
        self.start(3)

    def opposite(self):
        ref = self.view(2, 0)
        remote(ref, ref, self.sems, 2, self.to(1)).wait_recv()


def remote(src, dst, sems, index, to):
    send, recv, base = sems
    return pltpu.make_async_remote_copy(
        src_ref=src,
        dst_ref=dst,
        send_sem=send,
        recv_sem=recv.at[base + index],
        device_id=to,
        device_id_type=MESH,
    )


def context_gather(view, own, sems, zpos, xpos, halves=(0, 1)):
    rings = {}

    def make(half, phase):
        along_x = (half == 0) == (phase == 0)
        first = 0 if phase == 0 else OFFSETS[phase - 1]

        def piece(step, part):
            dz, dx = (first, step) if along_x else (step, first)
            return view(wrap(zpos + dz), wrap(xpos + dx), half, part)

        def to(way):
            dz, dx = (0, way) if along_x else (way, 0)
            return {"context": context_of(zpos + dz, xpos + dx)}

        send, recv, base = sems
        source = own(half) if first == 0 else None
        return Ring(piece, to, (send, recv, base + halves.index(half) * 15 + phase * 3), source)

    for half in halves:
        for phase in range(5):
            rings[half, phase] = make(half, phase)

    def own():
        for half in halves:
            rings[half, 0].whole()
            rings[half, 1].whole()

    def neighbours():
        for half in halves:
            rings[half, 0].onward()
            rings[half, 2].whole()
            rings[half, 3].whole()
        for half in halves:
            rings[half, 1].onward()

    def far():
        for half in halves:
            rings[half, 0].opposite()
            rings[half, 4].whole()

    def corners():
        for half in halves:
            rings[half, 2].onward()
            rings[half, 3].onward()

    def last():
        for half in halves:
            rings[half, 4].onward()

    def rest():
        for half in halves:
            for phase in (1, 2, 3, 4):
                rings[half, phase].opposite()

    return [own, neighbours, far, corners, last, rest]


def project_kernel(
    span_count, select_count, cap, stored,
    tok_ref, wq_ref, wk_ref, wv_ref, sel_hbm, count_hbm, slot_hbm,
    q_ref, k_out, v_out, tab_out,
    tok, stage, w, acc, done, back, fifth, small, told, sel_ref, count_ref, slot_ref,
    k_ref, v_ref, tab_ref,
    load_sem, send, trecv, wrecv, brecv, qrecv,
):
    me = lax.axis_index("context")
    zpos, xpos = me // RING, lax.rem(me, RING)
    col = lax.axis_index("tensor")
    ypos, core = col // 2, lax.rem(col, 2)
    token_count, depth = tok.shape[2], tok.shape[3]
    rows = w.shape[3]

    token_load = pltpu.make_async_copy(tok_ref, tok.at[col, zpos], load_sem.at[0])
    token_load.start()
    lists = [
        pltpu.make_async_copy(src, dst, load_sem.at[8 + i])
        for i, (src, dst) in enumerate(
            ((sel_hbm, sel_ref), (count_hbm, count_ref), (slot_hbm, slot_ref))
        )
    ]
    for load in lists:
        load.start()
    for part in (0, 1):
        for to in range(RING):
            left = (wq_ref, wk_ref, wv_ref, wq_ref)[to]
            pair = ((wq_ref, to), (left, RING)) if part == 0 else ((wk_ref, to), (wv_ref, to))
            for i, (ref, head) in enumerate(pair):
                load = pltpu.make_async_copy(
                    ref.at[:, pl.ds(head * HDIM, HDIM)],
                    stage.at[part, to, :, pl.ds(i * HDIM, HDIM)],
                    load_sem.at[2 + part],
                )
                load.start()

    def at_x(way):
        return {"context": context_of(zpos, xpos + way)}

    def at_z(way):
        return {"context": context_of(zpos + way, xpos)}

    def at_y(way):
        return {"tensor": wrap(ypos + way) * 2 + core}

    mate = {"tensor": ypos * 2 + 1 - core}
    barrier = pltpu.get_barrier_semaphore()
    partners = [at_x(1), at_x(-1), at_z(1), at_z(-1), at_z(2), at_y(1), at_y(-1), mate]
    for other in partners:
        pl.semaphore_signal(barrier, inc=1, device_id=other, device_id_type=MESH)
    pl.semaphore_wait(barrier, len(partners))

    def cut(size):
        return (pl.ds(0, size), pl.ds(0, size // 2), pl.ds(size // 2, size // 2))

    ztok = Ring(
        lambda step, part: tok.at[col, wrap(zpos + step), cut(token_count)[part]],
        at_z, (send.at[0], trecv, 0),
    )
    ytok = {
        o: Ring(
            lambda step, part, o=o: tok.at[
                wrap(ypos + step) * 2 + core, wrap(zpos + o), cut(token_count)[part]
            ],
            at_y, (send.at[0], trecv, 3 + 3 * i),
        )
        for i, o in enumerate(OFFSETS)
    }

    def share(step, o):
        ref = tok.at[wrap(ypos + step) * 2 + core, wrap(zpos + o)]
        remote(ref, ref, (send.at[1], trecv, 15), OFFSETS.index(o), mate).start()

    def shared(o):
        ref = tok.at[pl.ds(0, RING), 0]
        remote(ref, ref, (send.at[1], trecv, 15), OFFSETS.index(o), mate).wait_recv()

    def exchange(part, step, receive=False):
        index = part * 3 + OFFSETS.index(step) - 1
        src = stage.at[part, wrap(zpos + step)]
        if receive:
            dst = w.at[part, wrap(zpos - step), xpos]
            remote(src, dst, (send.at[2], wrecv, 0), index, at_z(step)).wait_recv()
        else:
            dst = w.at[part, zpos, xpos]
            remote(src, dst, (send.at[2], wrecv, 0), index, at_z(step)).start()

    xw = {
        (part, o): Ring(
            lambda step, piece, part=part, o=o: w.at[
                part, wrap(zpos + o), wrap(xpos + step), cut(rows)[piece]
            ],
            at_x, (send.at[3], wrecv, 6 + part * 12 + 3 * i),
        )
        for part in (0, 1)
        for i, o in enumerate(OFFSETS)
    }

    def keep(part):
        whole = stage.at[part]
        pltpu.make_async_copy(whole, whole, load_sem.at[2 + part]).wait()
        copy = pltpu.make_async_copy(
            stage.at[part, zpos], w.at[part, zpos, xpos], load_sem.at[4 + part]
        )
        copy.start()
        copy.wait()

    def queries(o):
        z = wrap(zpos + o)

        @pl.loop(0, tok.shape[0])
        def _(t):
            piece = w[0, t // 2, pl.ds(lax.rem(t, 2) * 2, 2)].reshape(depth, w.shape[4])
            new = jnp.dot(tok[t, z], piece, preferred_element_type=jnp.float32)

            @pl.when(t == 0)
            def _():
                acc[z] = new

            @pl.when(t > 0)
            def _():
                acc[z] += new

        done[0, z] = acc[z].astype(jnp.bfloat16)
        last_head = slice(HDIM, 2 * HDIM)
        if o == 0:
            fifth[zpos] = acc[z, :, last_head].astype(jnp.bfloat16)
        else:
            src = done.at[0, z, :, last_head]
            remote(src, fifth.at[zpos], (send.at[4], brecv, 0), 0, at_z(o)).start()

    def compute(step):
        for side in (0, 1):
            t = wrap(ypos + step) * 2 + side
            piece = w[1, wrap(ypos + step), 2 * side : 2 * side + 2].reshape(depth, w.shape[4])

            @pl.loop(0, RING)
            def _(z):
                new = jnp.dot(tok[t, z], piece, preferred_element_type=jnp.float32)
                if step == 0 and side == 0:
                    acc[z] = new
                else:
                    acc[z] += new

    def give_back():
        @pl.loop(0, RING)
        def _(z):
            done[1, z] = acc[z].astype(jnp.bfloat16)

        back[zpos] = acc[zpos].astype(jnp.bfloat16)
        for step in OFFSETS[1:]:
            src = done.at[1, wrap(zpos + step)]
            remote(src, back.at[zpos], (send.at[5], brecv, 1), 0, at_z(step)).start()

    def take_back(buf, index):
        ref = buf.at[pl.ds(0, RING - 1)]
        remote(ref, ref, (send.at[4], brecv, index), 0, at_z(1)).wait_recv()

    def heads_of(o, base, halves):
        size = token_count // len(halves)

        def view(z, x, half, part):
            head = pl.ds(pl.multiple_of(z * HDIM, HDIM), HDIM)
            low = halves.index(half) * size + (size // 2 if part == 2 else 0)
            rows = pl.ds(low, size if part == 0 else size // 2)
            return q_ref.at[wrap(z + o), x, rows, head]

        def own(half):
            return done.at[0, wrap(zpos + o), pl.ds(halves.index(half) * size, size), pl.ds(0, HDIM)]

        return context_gather(view, own, (send.at[6], qrecv, base), zpos, xpos, halves)

    heads = {
        o: heads_of(o, *rest)
        for o, *rest in ((0, 30, (0,)), (-1, 45, (1,)), (1, 60, (0,)), (2, 75, (1,)))
    }

    half_rows = token_count // 2
    quarter = half_rows // 2
    ranges = (
        ((0, half_rows), (0, quarter), (quarter, quarter)),
        (
            (half_rows, half_rows + EXTRA),
            (half_rows, quarter),
            (half_rows + quarter, quarter + EXTRA),
        ),
    )

    def last_view(z, x, half, part):
        return q_ref.at[z, x, pl.ds(*ranges[half][part]), pl.ds(RING * HDIM, HDIM)]

    def last_own(half):
        return small.at[pl.ds(*ranges[half][0]), :]

    last = context_gather(last_view, last_own, (send.at[7], qrecv, 0), zpos, xpos)

    token_load.wait()
    ytok[0].whole()
    keep(0)
    xw[0, 0].whole()
    exchange(0, 1)
    exchange(0, -1)
    ztok.whole()
    share(0, 0)
    keep(1)
    xw[1, 0].whole()

    lane = lax.broadcasted_iota(jnp.int32, (EXTRA, HDIM), 1)
    line = lax.broadcasted_iota(jnp.int32, (EXTRA, HDIM), 0)
    for load in lists:
        load.wait()
    chosen = jnp.zeros((EXTRA, HDIM), jnp.int32)
    for half in range(span_count):

        def note(j, chosen, half=half):
            slot = slot_ref[jnp.maximum(sel_ref[half, j], 0)]
            owner = jnp.where(j < count_ref[half], slot // stored, -1)
            value = jnp.where(line == half, owner, slot % stored)
            here = (lane == j) & ((line == half) | (line == span_count + half))
            return jnp.where(here, value, chosen)

        chosen = lax.fori_loop(0, select_count, note, chosen)
    small[token_count:, :] = chosen.astype(jnp.float32).astype(jnp.bfloat16)

    xw[0, 0].onward()
    ytok[0].onward()
    ztok.onward()
    for o in (-1, 1):
        ytok[o].whole()
        share(0, o)
    exchange(0, 2)
    exchange(1, 1)
    exchange(1, -1)
    exchange(1, 2)
    share(-1, 0)
    share(1, 0)
    for step in (1, -1):
        exchange(0, step, receive=True)
        xw[0, -step].whole()
    ztok.opposite()
    ytok[2].whole()
    share(0, 2)
    exchange(0, 2, receive=True)
    xw[0, 2].whole()
    ytok[-1].onward()
    share(-1, -1)
    share(1, -1)
    ytok[0].opposite()
    share(2, 0)
    xw[0, -1].onward()
    xw[0, 1].onward()
    xw[1, 0].onward()
    ytok[1].onward()
    share(-1, 1)
    share(1, 1)
    xw[0, 2].onward()
    for step in (1, -1):
        exchange(1, step, receive=True)
        xw[1, -step].whole()
    exchange(1, 2, receive=True)
    xw[1, 2].whole()
    for o in OFFSETS:
        xw[0, o].opposite()
    shared(0)
    queries(0)
    heads[0][0]()
    ytok[-1].opposite()
    share(2, -1)
    xw[1, -1].onward()
    xw[1, 1].onward()
    ytok[2].onward()
    share(-1, 2)
    share(1, 2)
    shared(-1)
    queries(-1)
    heads[-1][0]()
    ytok[1].opposite()
    share(2, 1)
    xw[1, 2].onward()
    heads[0][1]()
    shared(1)
    queries(1)
    heads[1][0]()
    ytok[2].opposite()
    share(2, 2)
    heads[-1][1]()
    shared(2)
    queries(2)
    heads[2][0]()
    keeps = [
        pltpu.make_async_copy(
            done.at[0, :, :, pl.ds(0, HDIM)],
            q_ref.at[
                :, xpos, pl.ds(0, token_count), pl.ds(pl.multiple_of(zpos * HDIM, HDIM), HDIM)
            ],
            load_sem.at[1],
        )
    ]
    keeps[0].start()
    heads[0][2]()
    heads[1][1]()
    take_back(fifth, 0)
    small[0:token_count, :] = fifth[0]
    last[0]()
    keeps.append(
        pltpu.make_async_copy(
            small, q_ref.at[zpos, xpos, :, pl.ds(RING * HDIM, HDIM)], load_sem.at[6]
        )
    )
    keeps[1].start()
    for o in OFFSETS:
        xw[1, o].opposite()
    compute(0)
    heads[-1][2]()
    heads[0][3]()
    heads[2][1]()
    compute(-1)
    last[1]()
    heads[1][2]()
    heads[-1][3]()
    heads[0][4]()
    compute(1)
    heads[2][2]()
    heads[1][3]()
    last[2]()
    compute(2)
    give_back()
    heads[-1][4]()
    heads[2][3]()
    last[3]()
    heads[1][4]()
    heads[2][4]()
    last[4]()
    for keep_copy in keeps:
        keep_copy.wait()
    for o in OFFSETS:
        heads[o][5]()
    last[5]()
    look = pltpu.make_async_copy(
        q_ref.at[:, :, pl.ds(token_count, EXTRA), pl.ds(RING * HDIM, HDIM)],
        told,
        load_sem.at[7],
    )
    look.start()
    take_back(back, 1)
    for head in range(RING):
        cols = slice(head * HDIM, (head + 1) * HDIM)
        k_ref[:, cols] = back[head, :, 0:HDIM]
        v_ref[:, cols] = back[head, :, HDIM : 2 * HDIM]
    k_ref[:, RING * HDIM :] = fifth[1]
    v_ref[:, RING * HDIM :] = fifth[2]
    puts = [
        pltpu.make_async_copy(k_ref, k_out, load_sem.at[11]),
        pltpu.make_async_copy(v_ref, v_out, load_sem.at[12]),
        pltpu.make_async_copy(tab_ref, tab_out, load_sem.at[13]),
    ]
    puts[0].start()
    puts[1].start()
    look.wait()

    devices = RING * RING
    lane = lax.broadcasted_iota(jnp.int32, (devices, HDIM), 1)
    source = lax.broadcasted_iota(jnp.int32, (devices, HDIM), 0)
    before = lax.broadcasted_iota(jnp.int32, (HDIM, HDIM), 0)
    after = lax.broadcasted_iota(jnp.int32, (HDIM, HDIM), 1)
    earlier = jnp.where(before < after, 1.0, 0.0).astype(jnp.bfloat16)
    listed = told[...].reshape(devices, EXTRA, HDIM).astype(jnp.float32)
    for half in range(span_count):
        owner = listed[:, half, :]
        row = listed[:, span_count + half, :]
        mine = jnp.where((owner == me.astype(jnp.float32)) & (lane < select_count), 1.0, 0.0)
        rank = jnp.dot(mine.astype(jnp.bfloat16), earlier, preferred_element_type=jnp.float32)
        table = jnp.where(lane == cap, jnp.sum(mine, axis=1, keepdims=True), 0.0)
        for r in range(cap):
            value = jnp.sum(jnp.where(rank == r, mine * row, 0.0), axis=1, keepdims=True)
            table = jnp.where(lane == r, value, table)
        if half == 0:
            table = jnp.where((lane == cap + 1) & (source == me + 1), 1.0, table)
        tab_ref[half] = table.astype(jnp.int32)
    puts[2].start()

    for put in puts:
        put.wait()
    for index, ref in enumerate(
        (
            tok.at[pl.ds(0, 5), pl.ds(0, 3)],
            tok.at[pl.ds(0, 4)],
            w.at[pl.ds(0, 2), pl.ds(0, 3), 0],
            w.at[pl.ds(0, 2), pl.ds(0, 3)],
            fifth.at[pl.ds(0, 3)],
            back.at[pl.ds(0, 3)],
            q_ref.at[:, pl.ds(0, 3), pl.ds(0, token_count), :],
            q_ref.at[0, pl.ds(0, 3)],
        )
    ):
        remote(ref, ref, (send.at[index], brecv, 0), 0, at_z(1)).wait_send()


def gather_project(tokens, wq, wk, wv, selected, counts, block_slot, cap, stored):
    token_count, depth = tokens.shape
    rows, width = wq.shape
    span_count, select_count = selected.shape
    devices = lax.axis_size("context")
    columns = lax.axis_size("tensor")
    hbm = pl.BlockSpec(memory_space=pl.ANY)
    own = jax.ShapeDtypeStruct((token_count, width), jnp.bfloat16)
    two = 2 * HDIM

    return pl.pallas_call(
        functools.partial(project_kernel, span_count, select_count, cap, stored),
        in_specs=[hbm] * 7,
        out_specs=[hbm] * 4,
        out_shape=[
            jax.ShapeDtypeStruct((RING, RING, token_count + EXTRA, width), jnp.bfloat16),
            own,
            own,
            jax.ShapeDtypeStruct((span_count, devices, HDIM), jnp.int32),
        ],
        scratch_shapes=[
            pltpu.VMEM((columns, RING, token_count, depth), jnp.bfloat16),
            pltpu.VMEM((2, RING, rows, two), jnp.bfloat16),
            pltpu.VMEM((2, RING, RING, rows, two), jnp.bfloat16),
            pltpu.VMEM((RING, token_count, two), jnp.float32),
            pltpu.VMEM((2, RING, token_count, two), jnp.bfloat16),
            pltpu.VMEM((RING, token_count, two), jnp.bfloat16),
            pltpu.VMEM((RING, token_count, HDIM), jnp.bfloat16),
            pltpu.VMEM((token_count + EXTRA, HDIM), jnp.bfloat16),
            pltpu.VMEM((RING, RING, EXTRA, HDIM), jnp.bfloat16),
            pltpu.SMEM(selected.shape, jnp.int32),
            pltpu.SMEM(counts.shape, jnp.int32),
            pltpu.SMEM(block_slot.shape, jnp.int32),
            pltpu.VMEM((token_count, width), jnp.bfloat16),
            pltpu.VMEM((token_count, width), jnp.bfloat16),
            pltpu.VMEM((span_count, devices, HDIM), jnp.int32),
        ]
        + [pltpu.SemaphoreType.DMA((count,)) for count in (14, 8, 19, 30, 2, 90)],
        compiler_params=pltpu.CompilerParams(
            collective_id=0, has_side_effects=True, vmem_limit_bytes=60 << 20
        ),
        name="gather_project",
    )(tokens, wq, wk, wv, selected, counts, block_slot)


def owner_kernel(
    heads, cap, tab_ref, q_ref, k_ref, v_ref, pk_ref, pv_ref, o_ref, st_ref, acc_ref
):
    group, span_count, span = o_ref.shape[0], o_ref.shape[1], o_ref.shape[3]
    first = pl.program_id(0) * group
    block = k_ref.shape[1]
    columns = [slice(h * HDIM, (h + 1) * HDIM) for h in range(heads)]

    def score(i, half, h, j):
        r0 = tab_ref[half, first + i, 2 * j]
        r1 = tab_ref[half, first + i, 2 * j + 1]
        bias = jnp.where(2 * j + 1 < tab_ref[half, first + i, cap], 0.0, NEG)
        cols = columns[h]
        q = q_ref[i, half * span : (half + 1) * span, cols]
        k = jnp.concatenate([k_ref[r0, :, cols], k_ref[r1, :, cols]], 0)
        v = jnp.concatenate([v_ref[r0, :, cols], v_ref[r1, :, cols]], 0)
        s = dot_nt(k, q) * SCALE
        return jnp.concatenate([s[:block], s[block:] + bias], 0), v

    def put(i, half, h, m, l, a):
        st_ref[i, half, h : h + 1, :] = m
        st_ref[i, half, 8 + h : 9 + h, :] = l
        acc_ref[i, half, columns[h], :] = a
        o_ref[i, half, columns[h], :] = a.astype(jnp.bfloat16)

    places = [(i, half) for i in range(group) for half in range(span_count)]
    def soften(i, half, h, s, v):
        m = jnp.max(s, axis=0, keepdims=True)
        p = jnp.exp2(s - m)
        l = jnp.sum(p, axis=0, keepdims=True)
        m = jnp.where(tab_ref[half, first + i, cap] > 0, m, NEG)
        return i, half, h, m, l, p.astype(jnp.bfloat16), v

    def weigh(i, half, h, m, l, p, v):
        return i, half, h, m, l, dot_tn(v, p)

    made = [[(i, half, h, *score(i, half, h, 0)) for h in range(heads)] for i, half in places]
    results = []
    for tiles in made:
        soft = [soften(*tile) for tile in tiles]
        results += [weigh(*tile) for tile in soft]
    for result in results:
        put(*result)

    def more(i, half, tiles):
        results = []
        for h, (s, v) in enumerate(tiles):
            old = st_ref[i, half, h : h + 1, :]
            m = jnp.maximum(jnp.max(s, axis=0, keepdims=True), old)
            decay = jnp.exp2(old - m)
            p = jnp.exp2(s - m)
            l = jnp.sum(p, axis=0, keepdims=True)
            l = l + st_ref[i, half, 8 + h : 9 + h, :] * decay
            a = dot_tn(v, p.astype(jnp.bfloat16))
            a = a + acc_ref[i, half, columns[h], :] * decay
            results.append((i, half, h, m, l, a))
        for result in results:
            put(*result)

    for i, half in places:
        n = tab_ref[half, first + i, cap]

        @pl.when(n > 2)
        def _(i=i, half=half, n=n):
            @pl.loop(1, (n + 1) // 2)
            def _(j):
                more(i, half, [score(i, half, h, j) for h in range(heads)])

    for i in range(group):

        @pl.when(tab_ref[0, first + i, cap + 1] > 0)
        def _(i=i):
            tiles = [
                (dot_nt(pk_ref[:, cols], q_ref[i, 0:span, cols]) * SCALE, pv_ref[:, cols])
                for cols in columns
            ]
            more(i, 0, tiles)


def owner_attention(table, q_all, cache_keys, cache_values, k, v, heads, cap):
    tokens, width = q_all.shape[2] - EXTRA, q_all.shape[3]
    span_count, devices = table.shape[:2]
    span = tokens // span_count
    q_all = q_all.reshape(devices, tokens + EXTRA, width)
    newest = pl.BlockSpec((span, width), lambda s, *_: (span_count - 1, 0))
    whole = pl.BlockSpec(cache_keys.shape, lambda s, *_: (0, 0, 0), pipeline_mode=pl.Buffered(1))
    return pl.pallas_call(
        functools.partial(owner_kernel, heads, cap),
        grid_spec=pltpu.PrefetchScalarGridSpec(
            num_scalar_prefetch=1,
            grid=(devices // GROUP,),
            in_specs=[
                pl.BlockSpec((GROUP, tokens, width), lambda s, *_: (s, 0, 0)),
                whole,
                whole,
                newest,
                newest,
            ],
            out_specs=[
                pl.BlockSpec((GROUP, span_count, width, span), lambda s, *_: (s, 0, 0, 0)),
                pl.BlockSpec((GROUP, span_count, 16, span), lambda s, *_: (s, 0, 0, 0)),
            ],
            scratch_shapes=[pltpu.VMEM((GROUP, span_count, width, span), jnp.float32)],
        ),
        out_shape=[
            jax.ShapeDtypeStruct((devices, span_count, width, span), jnp.bfloat16),
            jax.ShapeDtypeStruct((devices, span_count, 16, span), jnp.float32),
        ],
        name="owner_attention",
    )(table, q_all, cache_keys, cache_values, k, v)


def combine_kernel(
    heads,
    o_ref, st_ref, q_ref, k_ref, v_ref,
    out_ref,
    own, query, keys, values, st_own, relay, relay_st, got, got_st, mid, mid_st,
    relay2, relay2_st, got2, got2_st, acc, acc_st,
    load_sem, send, recv, recv_st,
):
    me = lax.axis_index("context")
    zpos, xpos = me // RING, lax.rem(me, RING)
    span = o_ref.shape[-1]
    token_count = k_ref.shape[0]
    cut = (heads + 1) // 2 * HDIM
    parts = ((0, cut), (cut, heads * HDIM - cut))
    order = (2, -1, 1, 0)

    def first_at(half, step):
        return wrap((xpos if half == 0 else zpos) + step)

    def second_at(half, step):
        return wrap((zpos if half == 0 else xpos) + step)

    def place(half, step, further):
        a, b = first_at(half, step), second_at(half, further)
        return (b, a, half) if half == 0 else (a, b, half)

    def way_of(further):
        return 1 if further in (2, 1) else -1

    def load(ref, dst, index):
        return pltpu.make_async_copy(ref, dst, load_sem.at[index])

    for kind in (0, 1):
        for further in order:
            for half in (0, 1):
                step = way_of(further) if kind == 0 else 0
                slot = (half, kind, order.index(further))
                load(o_ref.at[place(half, step, further)], own.at[slot], 0).start()
    query_load = load(q_ref.at[zpos, xpos, pl.ds(0, token_count)], query, 1)
    others = [load(k_ref, keys, 2), load(v_ref, values, 3), load(st_ref, st_own, 4)]
    for other in [query_load] + others:
        other.start()

    barrier = pltpu.get_barrier_semaphore()
    for other in (
        context_of(zpos + 1, xpos),
        context_of(zpos - 1, xpos),
        context_of(zpos, xpos + 1),
        context_of(zpos, xpos - 1),
    ):
        pl.semaphore_signal(barrier, inc=1, device_id={"context": other}, device_id_type=MESH)
    pl.semaphore_wait(barrier, 4)

    def copies(half, index, way, src, src_st, dst, dst_st):
        first = index < 8
        if (half == 0) == first:
            to = {"context": context_of(zpos, xpos + way)}
        else:
            to = {"context": context_of(zpos + way, xpos)}
        kind = 0 if first else 2
        return (
            remote(src, dst, (send.at[kind], recv, half * 11), index, to),
            remote(src_st, dst_st, (send.at[kind + 1], recv_st, half * 11), index, to),
        )

    def start(*args):
        for copy in copies(*args):
            copy.start()

    def arrive(half, index, dst, dst_st):
        for copy in copies(half, index, 1, dst, dst_st, dst, dst_st):
            copy.wait_recv()

    def merge(out, out_st, sources, head_range):
        results = []
        for h in head_range:
            rows = slice(h * HDIM, (h + 1) * HDIM)
            ms = [st[h : h + 1, :] for _, st in sources]
            m = functools.reduce(jnp.maximum, ms)
            ws = [jnp.exp2(x - m) for x in ms]
            ls = [st[8 + h : 9 + h, :] * w for (_, st), w in zip(sources, ws)]
            terms = [part[rows, :].astype(jnp.float32) * w for (part, _), w in zip(sources, ws)]
            total = functools.reduce(jnp.add, terms).astype(jnp.bfloat16)
            results.append((h, rows, m, functools.reduce(jnp.add, ls), total))
        for h, rows, m, l, total in results:
            out[rows, :] = total
            out_st[h : h + 1, :] = m
            out_st[8 + h : 9 + h, :] = l

    every = range(heads)

    def forward(half, further):
        i, at = order.index(further), place(half, 2, further)
        start(
            half, i, way_of(further), o_ref.at[at], st_ref.at[at],
            relay.at[half, i], relay_st.at[half, i],
        )

    def direct(half, further):
        way = -way_of(further)
        i, at, side = order.index(further), place(half, way, further), 0 if way == 1 else 1
        start(
            half, 4 + i, way, o_ref.at[at], st_ref.at[at],
            got.at[half, side, i], got_st.at[half, side, i],
        )

    def merged(half, further):
        way = way_of(further)
        i, at, side = order.index(further), place(half, way, further), 0 if way == 1 else 1
        part, st = relay.at[half, i], relay_st.at[half, i]
        arrive(half, i, part, st)
        merge(part, st, [(part, st), (own.at[half, 0, i], st_own.at[at])], every)
        start(
            half, 4 + i, way, part, st, got.at[half, side, i], got_st.at[half, side, i]
        )

    def collect(half, further):
        i = order.index(further)
        both = pl.ds(0, 2)
        arrive(half, 4 + i, got.at[half, both, i], got_st.at[half, both, i])
        merge(
            mid.at[half, i], mid_st.at[half, i],
            [(own.at[half, 1, i], st_own.at[place(half, 0, further)])]
            + [(got.at[half, n, i], got_st.at[half, n, i]) for n in (0, 1)],
            every,
        )

    halves = (0, 1)
    for further in order:
        for half in halves:
            forward(half, further)
    for further in (2, -1):
        for half in halves:
            direct(half, further)

    key = lax.broadcasted_iota(jnp.int32, (span, span), 0)
    row = lax.broadcasted_iota(jnp.int32, (span, span), 1)

    def local(half, keys_of, values_of, bias, first):
        results = []
        for h in every:
            cols = slice(h * HDIM, (h + 1) * HDIM)
            s = dot_nt(keys_of(cols), query[half * span : (half + 1) * span, cols]) * SCALE
            s = jnp.where(key <= row, s, NEG) if bias is None else s + bias
            m = jnp.max(s, axis=0, keepdims=True)
            if not first:
                old = acc_st[half, h : h + 1, :]
                m = jnp.maximum(m, old)
                decay = jnp.exp2(old - m)
            p = jnp.exp2(s - m)
            l = jnp.sum(p, axis=0, keepdims=True)
            a = dot_tn(values_of(cols), p.astype(jnp.bfloat16))
            if not first:
                l = l + acc_st[half, 8 + h : 9 + h, :] * decay
                a = a + acc[half, cols, :] * decay
            results.append((h, cols, m, l, a))
        for h, cols, m, l, a in results:
            acc_st[half, h : h + 1, :] = m
            acc_st[half, 8 + h : 9 + h, :] = l
            acc[half, cols, :] = a

    for other in [query_load] + others:
        other.wait()
    load(own, own, 0).wait()
    for half in halves:
        rows = slice(half * span, (half + 1) * span)
        local(half, lambda c, r=rows: keys[r, c], lambda c, r=rows: values[r, c], None, True)

    for further in (2, -1):
        for half in halves:
            merged(half, further)
    for further in (1, 0):
        for half in halves:
            direct(half, further)
    for further in (1, 0):
        for half in halves:
            merged(half, further)
    local(1, lambda c: keys[0:span, c], lambda c: values[0:span, c], 0.0, False)

    for half in halves:
        collect(half, 2)
        for side, way in ((0, 1), (1, -1)):
            rows = pl.ds(*parts[side])
            start(
                half, 8 + side, way, mid.at[half, 0, rows], mid_st.at[half, 0],
                relay2.at[half, rows], relay2_st.at[half, side],
            )
    for side, way in ((1, -1), (0, 1)):
        for half in halves:
            i = order.index(way)
            collect(half, way)
            other = pl.ds(*parts[1 - side])
            start(
                half, 10, way, mid.at[half, i, other], mid_st.at[half, i],
                got2.at[half, side, other], got2_st.at[half, side, 1 - side],
            )
    for half in halves:
        for side, way in ((0, 1), (1, -1)):
            i = order.index(way)
            rows = pl.ds(*parts[side])
            part, st = relay2.at[half], relay2_st.at[half, side]
            arrive(half, 8 + side, relay2.at[half, rows], st)
            merge(
                part, st, [(part, st), (mid.at[half, i], mid_st.at[half, i])],
                range(parts[side][0] // HDIM, sum(parts[side]) // HDIM),
            )
            start(
                half, 10, way, relay2.at[half, rows], st,
                got2.at[half, side, rows], got2_st.at[half, side, side],
            )

    last = order.index(0)
    for half in halves:
        collect(half, 0)
        part, st = mid.at[half, last], mid_st.at[half, last]
        results = []
        for h in every:
            cols = slice(h * HDIM, (h + 1) * HDIM)
            old, new = acc_st[half, h : h + 1, :], st[h : h + 1, :]
            m = jnp.maximum(old, new)
            decay, w = jnp.exp2(old - m), jnp.exp2(new - m)
            l = acc_st[half, 8 + h : 9 + h, :] * decay + st[8 + h : 9 + h, :] * w
            a = acc[half, cols, :] * decay + part[cols, :].astype(jnp.float32) * w
            results.append((h, cols, m, l, a))
        for h, cols, m, l, a in results:
            acc_st[half, h : h + 1, :] = m
            acc_st[half, 8 + h : 9 + h, :] = l
            acc[half, cols, :] = a
    for half in halves:
        arrive(half, 10, got2.at[half], got2_st.at[half])
        for h in every:
            cols = slice(h * HDIM, (h + 1) * HDIM)
            which = 0 if h * HDIM < cut else 1
            sources = [(got2.at[half, i], got2_st.at[half, i, which]) for i in (0, 1)]
            old = acc_st[half, h : h + 1, :]
            ms = [st[h : h + 1, :] for _, st in sources]
            m = functools.reduce(jnp.maximum, ms, old)
            decay = jnp.exp2(old - m)
            total = acc_st[half, 8 + h : 9 + h, :] * decay
            a = acc[half, cols, :] * decay
            for (part, st), x in zip(sources, ms):
                w = jnp.exp2(x - m)
                total = total + st[8 + h : 9 + h, :] * w
                a = a + part[cols, :].astype(jnp.float32) * w
            out_ref[half * span : (half + 1) * span, cols] = jnp.transpose(a / total).astype(
                out_ref.dtype
            )

    for index, ref in enumerate(
        (
            o_ref.at[pl.ds(0, 3)],
            st_ref.at[pl.ds(0, 3)],
            o_ref.at[pl.ds(0, 3), 0],
            st_ref.at[pl.ds(0, 3), pl.ds(0, 2)],
        )
    ):
        to = {"context": context_of(zpos, xpos + 1)}
        remote(ref, ref, (send.at[index], recv, 0), 0, to).wait_send()


def combine(o, st, q_all, k, v, heads):
    span_count, width, span = o.shape[1:]
    rows = st.shape[2]
    o = o.reshape(RING, RING, span_count, width, span)
    st = st.reshape(RING, RING, span_count, rows, span)
    vmem = pl.BlockSpec(memory_space=pltpu.VMEM)
    hbm = pl.BlockSpec(memory_space=pl.ANY)

    def part(*lead):
        return pltpu.VMEM(lead + (width, span), jnp.bfloat16)

    def stats(*lead):
        return pltpu.VMEM(lead + (rows, span), jnp.float32)

    return pl.pallas_call(
        functools.partial(combine_kernel, heads),
        in_specs=[hbm] * 5,
        out_specs=vmem,
        out_shape=jax.ShapeDtypeStruct(k.shape, jnp.bfloat16),
        scratch_shapes=[
            part(2, 2, RING),
            pltpu.VMEM(k.shape, jnp.bfloat16),
            pltpu.VMEM(k.shape, jnp.bfloat16),
            pltpu.VMEM(k.shape, jnp.bfloat16),
            stats(RING, RING, span_count),
            part(2, RING),
            stats(2, RING),
            part(2, 2, RING),
            stats(2, 2, RING),
            part(2, RING),
            stats(2, RING),
            part(2),
            stats(2, 2),
            part(2, 2),
            stats(2, 2, 2),
            pltpu.VMEM((2, width, span), jnp.float32),
            stats(2),
        ]
        + [pltpu.SemaphoreType.DMA((count,)) for count in (5, 4, 22, 22)],
        compiler_params=pltpu.CompilerParams(
            collective_id=1, has_side_effects=True, vmem_limit_bytes=60 << 20
        ),
        name="combine",
    )(o, st, q_all, k, v)


def shards(
    tokens,
    query_weight,
    key_weight,
    value_weight,
    cache_keys,
    cache_values,
    selected,
    counts,
    block_slot,
):
    heads = query_weight.shape[1] // HDIM
    span_count, select_count = selected.shape
    devices = lax.axis_size("context")
    cap = max(2, 2 * span_count * select_count // devices)

    stored = cache_keys.shape[0]
    q_all, k, v, table = gather_project(
        tokens, query_weight, key_weight, value_weight, selected, counts, block_slot, cap, stored
    )
    o, st = owner_attention(table, q_all, cache_keys, cache_values, k, v, heads, cap)
    return combine(o, st, q_all, k, v, heads)


def solution(mesh):
    placed = (
        P("context", "tensor"),
        P("context", "tensor"),
        P("context", "tensor"),
        P("context", "tensor"),
        P("context", None, "tensor"),
        P("context", None, "tensor"),
        P("context", None),
        P("context"),
        P(),
    )
    return jax.shard_map(
        shards, mesh=mesh, in_specs=placed, out_specs=P("context", "tensor"), check_vma=False
    )
```
